32 devices in a mesh: dp: 8 (over y, x, core), tensor: 4 (over z).
Axes of the slice: x: 2, y: 2, z: 4, core: 2. Of those that a mesh axis runs over, the one named last changes fastest.
Arguments:
- tokens: bfloat16 [8192, 2048], P(('dp', 'tensor')), may hold values from -6 to 6
- lengths: int32 [8], P('dp'), may hold values from 256 to 1024, as said below
- ln1_gain: bfloat16 [2048], P('dp'), may hold values from 0.5 to 1.5
- ln1_bias: bfloat16 [2048], P('dp'), may hold values from -4 to 4
- qkv_weight: bfloat16 [2048, 3, 2048], P('dp', None, 'tensor'), may hold values from -0.125 to 0.125
- qv_bias: bfloat16 [2, 16, 128], P(None, 'tensor', 'dp'), may hold values from -4 to 4
- out_weight: bfloat16 [2048, 2048], P('tensor', 'dp'), may hold values from -0.75 to 0.75
- out_bias: bfloat16 [2048], P('dp'), may hold values from -4 to 4
- ln2_gain: bfloat16 [2048], P('dp'), may hold values from 0.5 to 1.5
- ln2_bias: bfloat16 [2048], P('dp'), may hold values from -4 to 4
- up_weight: bfloat16 [2048, 8192], P('dp', 'tensor'), may hold values from -0.125 to 0.125
- up_bias: bfloat16 [512, 16], P('tensor', 'dp'), may hold values from -4 to 4
- down_weight: bfloat16 [8192, 2048], P('tensor', 'dp'), may hold values from -0.0625 to 0.0625
- down_bias: bfloat16 [2048], P('dp'), may hold values from -4 to 4
- cotangent: bfloat16 [8192, 2048], P(('dp', 'tensor')), may hold values from -6 to 6
Outputs:
- output: bfloat16 [8192, 2048], P(('dp', 'tensor'))
- tokens_grad: float32 [8192, 2048], P(('dp', 'tensor'))
- ln1_gain_grad: float32 [2048], P('dp')
- ln1_bias_grad: float32 [2048], P('dp')
- qkv_weight_grad: float32 [2048, 3, 2048], P('dp', None, 'tensor')
- qv_bias_grad: float32 [2, 16, 128], P(None, 'tensor', 'dp')
- out_weight_grad: float32 [2048, 2048], P('tensor', 'dp')
- out_bias_grad: float32 [2048], P('dp')
- ln2_gain_grad: float32 [2048], P('dp')
- ln2_bias_grad: float32 [2048], P('dp')
- up_weight_grad: float32 [2048, 8192], P('dp', 'tensor')
- up_bias_grad: float32 [512, 16], P('tensor', 'dp')
- down_weight_grad: float32 [8192, 2048], P('tensor', 'dp')
- down_bias_grad: float32 [2048], P('dp')
- stream_rms: float32 [5], replicated
The draws below stay inside these ranges and needn't reach their ends.
Inputs may be any that keep to these rules, and one draw needn't show every extreme that they name: `lengths`: each sequence's true token count.
All inputs are finite; a program needn't handle non-finite values.
Results may differ from the reference program's by a relative error of at most 0.02.
Values may be sent and summed in bfloat16 or wider, within the bound.
A program may use at most 256 MiB of HBM per device.

```python
from functools import partial
import jax
import jax.numpy as jnp
from jax import lax

D = 2048
H = 16
HD = 128
FF = 8192
LEN = 1024
SEQS = 8
TOKENS = 8192


def draw_lengths(key, part):
    seq_index = jnp.arange(SEQS, dtype=jnp.int32)
    last_index = max(SEQS - 1, 1)
    rising = LEN // 4 + (LEN - LEN // 4) * seq_index // last_index
    jitter = jax.random.randint(key, (SEQS,), 0, max(LEN // 32, 1), dtype=jnp.int32)
    middle = (seq_index > 0) & (seq_index < SEQS - 1)
    return jnp.maximum(jnp.where(middle, rising - jitter, rising), LEN // 4).astype(jnp.int32)


def level_of(own_key, shape, shards, low, largest):
    def one(position, shards_of):
        draws = jax.random.uniform(jax.random.fold_in(jax.random.fold_in(own_key, 6), position), (shards_of,), jnp.float32, low / len(shards), largest / len(shards))
        return jnp.repeat(jnp.exp(draws), shape[position] // shards_of).reshape((-1,) + (1,) * (len(shape) - position - 1))

    gain = one(*shards[0])
    for cut in shards[1:]:
        gain = gain * one(*cut)
    return gain


def bell_draw(own_key, dims, width, bound, shards=(), kind=jnp.bfloat16):
    gain = level_of(own_key, dims, shards, -0.22, 0.18) if shards else 1.0
    values = jax.random.normal(own_key, dims, jnp.float32) * width * gain
    return jnp.minimum(jnp.maximum(values, -bound), bound).astype(kind)


def setup_inputs(seed: int = 0) -> dict:
    splits = jax.random.split(jax.random.key(seed), 16)
    tokens = bell_draw(splits[0], (TOKENS, D), 1.0, 6.0, ((0, 32),))
    lengths = draw_lengths(jax.random.fold_in(splits[15], 71), 0)
    ln1_gain = jnp.clip(1.0 + 0.1 * jax.random.normal(splits[2], (D,), jnp.float32), 0.5, 1.5).astype(jnp.bfloat16)
    ln1_bias = bell_draw(splits[3], (D,), 0.3, 4.0, ((0, 8),))
    qkv_weight = bell_draw(splits[4], (D, 3, D), D ** -0.5, 0.125, ((0, 8), (2, 4)))
    qv_bias = bell_draw(splits[5], (2, H, HD), 0.3, 4.0, ((1, 4), (2, 8)))
    out_weight = bell_draw(splits[6], (D, D), (D // 32) ** -0.5, 0.75, ((0, 4), (1, 8)))
    out_bias = bell_draw(splits[7], (D,), 0.3, 4.0, ((0, 8),))
    ln2_gain = jnp.clip(1.0 + 0.1 * jax.random.normal(splits[8], (D,), jnp.float32), 0.5, 1.5).astype(jnp.bfloat16)
    ln2_bias = bell_draw(splits[9], (D,), 0.3, 4.0, ((0, 8),))
    up_weight = bell_draw(splits[10], (D, FF), D ** -0.5, 0.125, ((0, 8), (1, 4)))
    up_bias = bell_draw(splits[11], (FF // 16, 16), 0.3, 4.0, ((0, 4), (1, 8)))
    down_weight = bell_draw(splits[12], (FF, D), FF ** -0.5, 0.0625, ((0, 4), (1, 8)))
    down_bias = bell_draw(splits[13], (D,), 0.3, 4.0, ((0, 8),))
    cotangent = bell_draw(splits[14], (TOKENS, D), 1.0, 6.0, ((0, 32),))
    return {"tokens": tokens, "lengths": lengths, "ln1_gain": ln1_gain, "ln1_bias": ln1_bias, "qkv_weight": qkv_weight, "qv_bias": qv_bias, "out_weight": out_weight, "out_bias": out_bias, "ln2_gain": ln2_gain, "ln2_bias": ln2_bias, "up_weight": up_weight, "up_bias": up_bias, "down_weight": down_weight, "down_bias": down_bias, "cotangent": cotangent}


EPS = 1e-05
HIGHEST = lax.Precision.HIGHEST

@jax.custom_vjp
def low(v):
    return lax.optimization_barrier(v.astype(jnp.bfloat16)).astype(jnp.float32)

@jax.custom_vjp
def low_back(v):
    return v

def low_keep(v):
    return (low(v), None)

def low_pass(kept, grad):
    return (grad,)

def back_keep(v):
    return (v, None)

def back_low(kept, grad):
    return (low(grad),)
low.defvjp(low_keep, low_pass)
low_back.defvjp(back_keep, back_low)

def layer_norm(values, norm_gain, norm_shift):
    center = values - lax.optimization_barrier(jnp.mean(values, axis=-1, keepdims=True))
    normed = center * lax.rsqrt(lax.optimization_barrier(jnp.mean(center * center, axis=-1, keepdims=True)) + EPS)
    return normed * norm_gain + norm_shift

def attention(queries, key_rows, value_rows, length):
    block_size = min(512, LEN)
    positions = jnp.arange(LEN, dtype=jnp.int32)

    def one_block(block_index):
        first_row = block_index * block_size
        query_block = lax.dynamic_slice_in_dim(queries, first_row, block_size, 0)
        scores = jnp.einsum('qhd,khd->hqk', query_block, key_rows, precision=HIGHEST) * HD ** (-0.5)
        scores = low_back(scores)
        query_pos = first_row + jnp.arange(block_size, dtype=jnp.int32)
        allowed = (positions[None, :] <= query_pos[:, None]) & (positions[None, :] < length)
        scores = jnp.where(allowed[None], scores, -1e+30)
        row_max = lax.optimization_barrier(jnp.max(scores, axis=-1, keepdims=True))
        powers = jnp.exp(scores - row_max)
        shares = low(powers / lax.optimization_barrier(jnp.sum(powers, axis=-1, keepdims=True)))
        return jnp.einsum('hqk,khd->qhd', shares, value_rows, precision=HIGHEST)
    blocks_out = lax.map(jax.checkpoint(one_block), jnp.arange(LEN // block_size, dtype=jnp.int32))
    return blocks_out.reshape(LEN, H, HD)

def sequence_layer(params, inputs, length):
    ln1_gain, ln1_bias, qkv_weight, qv_bias, out_weight, out_bias, ln2_gain, ln2_bias, up_weight, up_bias, down_weight, down_bias = params
    positions = jnp.arange(LEN, dtype=jnp.int32)
    valid = (positions < length).astype(jnp.float32)[:, None]
    normed_a = low(layer_norm(inputs, ln1_gain, ln1_bias))
    projected = jnp.dot(normed_a, qkv_weight.reshape(D, 3 * D), precision=HIGHEST, preferred_element_type=jnp.float32).reshape(LEN, 3, H, HD)
    zero_bias = jnp.zeros((1, H, HD), jnp.float32)
    projected = projected + jnp.concatenate([qv_bias[0:1], zero_bias, qv_bias[1:2]], axis=0)[None]
    projected = low(low_back(projected))
    attended = attention(projected[:, 0], projected[:, 1], projected[:, 2], length)
    attended = low(low_back(attended.reshape(LEN, D)))
    attn_out = low_back(jnp.dot(attended, out_weight, precision=HIGHEST, preferred_element_type=jnp.float32)) + out_bias
    middle = inputs + attn_out
    normed_c = low(layer_norm(middle, ln2_gain, ln2_bias))
    hidden_pre = low_back(jnp.dot(normed_c, up_weight, precision=HIGHEST, preferred_element_type=jnp.float32) + up_bias.reshape(FF))
    hidden_act = low(jax.nn.gelu(hidden_pre, approximate=True))
    mlp_out = low_back(jnp.dot(hidden_act, down_weight, precision=HIGHEST, preferred_element_type=jnp.float32)) + down_bias
    result = middle + mlp_out
    squares = jnp.stack([jnp.sum(valid * stream * stream) for stream in (inputs, attn_out, middle, mlp_out, result)])
    return (result, squares)

def forward(lengths, token_values, params):

    def one_sequence(pair):
        return sequence_layer(params, pair[0], pair[1])
    results, squares = lax.map(jax.checkpoint(one_sequence), (token_values.reshape(SEQS, LEN, D), lengths))
    return (results.reshape(TOKENS, D), lax.optimization_barrier(jnp.sum(squares, axis=0)))

def reference(tokens, lengths, ln1_gain, ln1_bias, qkv_weight, qv_bias, out_weight, out_bias, ln2_gain, ln2_bias, up_weight, up_bias, down_weight, down_bias, cotangent):
    params = tuple((weight.astype(jnp.float32) for weight in (ln1_gain, ln1_bias, qkv_weight, qv_bias, out_weight, out_bias, ln2_gain, ln2_bias, up_weight, up_bias, down_weight, down_bias)))
    result, back_fn, squares = jax.vjp(partial(forward, lengths), tokens.astype(jnp.float32), params, has_aux=True)
    token_index = jnp.arange(TOKENS, dtype=jnp.int32)
    length_rows = lengths[token_index // LEN]
    valid = (token_index % LEN < length_rows).astype(jnp.float32)
    tokens_grad, grads = back_fn(cotangent.astype(jnp.float32) * valid[:, None])
    count = jnp.sum(lengths).astype(jnp.float32)
    stream_rms = jnp.sqrt(squares / (count * D))
    return (result.astype(jnp.bfloat16), tokens_grad, grads[0], grads[1], grads[2], grads[3], grads[4], grads[5], grads[6], grads[7], grads[8], grads[9], grads[10], grads[11], stream_rms)
```

```python
import functools

import jax
import jax.numpy as jnp
from jax import lax
from jax.experimental import pallas as pl
from jax.experimental.pallas import tpu as pltpu
from jax.sharding import PartitionSpec as P

HD = 128
LEN = 1024
EPS = 1e-05
MESH = pl.DeviceIdType.MESH
F32 = jnp.float32
BF16 = jnp.bfloat16
VMEM_CAP = 60 * 1024 * 1024
SUBS = 2
WHOLE = pl.BlockSpec(memory_space=pltpu.VMEM)


class Line:
    def __init__(self, size, rows):
        self.size, self.rows, self.t = size, rows, lax.axis_index("tensor")
        self.sub = rows // SUBS

    def barrier(self):
        sem = pltpu.get_barrier_semaphore()

        @pl.when(self.t > 0)
        def _():
            pl.semaphore_signal(sem, device_id={"tensor": self.t - 1}, device_id_type=MESH)

        @pl.when(self.t < self.size - 1)
        def _():
            pl.semaphore_signal(sem, device_id={"tensor": self.t + 1}, device_id_type=MESH)

        more = jnp.where(self.t > 0, 1, 0) + jnp.where(self.t < self.size - 1, 1, 0)
        pl.semaphore_wait(sem, more)

    def _copy(self, src, dst, sems, way, shard, part):
        send, recv = sems
        target = self.t + 1 if way == 0 else self.t - 1
        return pltpu.make_async_remote_copy(
            src_ref=src,
            dst_ref=dst.at[shard, pl.ds(part * self.sub, self.sub)],
            send_sem=send.at[way, shard, part],
            recv_sem=recv.at[way, shard, part],
            device_id={"tensor": target},
            device_id_type=MESH,
        )

    def _rows(self, ref, shard, part):
        return ref.at[shard, pl.ds(part * self.sub, self.sub)]

    def _edge(self, way):
        return self.t < self.size - 1 if way == 0 else self.t > 0

    def gather_step(self, way, k, part, buf, sems, first):
        t, last = self.t, self.size - 1
        shard = t - k if way == 0 else t + k
        inside = (t >= k) if way == 0 else (t + k <= last)

        @pl.when(inside)
        def _():
            held = self._rows(buf, shard, part)
            if k > 0:
                self._copy(held, buf, sems, way, shard, part).wait_recv()

            @pl.when(self._edge(way))
            def _():
                src = held
                if k == 0 and first is not None:
                    src = first.at[pl.ds(part * self.sub, self.sub)]
                self._copy(src, buf, sems, way, shard, part).start()

    def scatter_step(self, way, j, part, terms, buf, sems):
        t, last = self.t, self.size - 1
        shard = last - j if way == 0 else j
        beyond = (shard > t) if way == 0 else (shard < t)
        starts = (t == 0) if way == 0 else (t == last)

        @pl.when(beyond & starts)
        def _():
            self._copy(self._rows(terms, shard, part), buf, sems, way, shard, part).start()

        @pl.when(beyond & jnp.logical_not(starts))
        def _():
            held = self._rows(buf, shard, part)
            self._copy(held, buf, sems, way, shard, part).wait_recv()
            step = min(32, self.sub)

            def add(i, carry):
                rows = pl.ds(part * self.sub + i * step, step)
                total = buf[shard, rows, :].astype(F32) + terms[shard, rows, :].astype(F32)
                buf[shard, rows, :] = total.astype(BF16)
                return carry

            lax.fori_loop(0, self.sub // step, add, 0)
            self._copy(held, buf, sems, way, shard, part).start()

    def phase(self, gather=None, scatter=None, on_slot=None):
        n = self.size
        for k in range(n):
            for part in range(SUBS):
                for way in (0, 1):
                    if gather is not None:
                        self.gather_step(way, k, part, gather[0], gather[1], gather[2])
                    if scatter is not None:
                        if gather is None:
                            if k < n - 1:
                                self.scatter_step(way, k, part, scatter[0], scatter[1][way], scatter[2])
                        else:
                            behind = self.t if way == 0 else n - 1 - self.t
                            for b in range(k):

                                @pl.when(behind == b)
                                def _(b=b, k=k, part=part, way=way):
                                    self.scatter_step(
                                        way, k - 1 - b, part, scatter[0], scatter[1][way], scatter[2]
                                    )
            if on_slot is not None:
                on_slot(k)

    def own_wait(self, bufs, sems):
        for way in (0, 1):
            arrives = self.t > 0 if way == 0 else self.t < self.size - 1

            @pl.when(arrives)
            def _(way=way):
                for part in range(SUBS):
                    held = self._rows(bufs[way], self.t, part)
                    self._copy(held, bufs[way], sems, way, self.t, part).wait_recv()

    def own_sum(self, terms, bufs, rows):
        t = self.t
        zero = jnp.zeros((), F32)
        right = jnp.where(t > 0, bufs[0][t, rows, :].astype(F32), zero)
        left = jnp.where(t < self.size - 1, bufs[1][t, rows, :].astype(F32), zero)
        return terms[t, rows, :].astype(F32) + right + left

    def drain_gather(self, buf, sems):
        for way in (0, 1):
            for k in range(self.size):
                shard = self.t - k if way == 0 else self.t + k
                inside = (self.t >= k) if way == 0 else (self.t + k <= self.size - 1)

                @pl.when(inside & self._edge(way))
                def _(way=way, shard=shard):
                    for part in range(SUBS):
                        held = self._rows(buf, shard, part)
                        self._copy(held, buf, sems, way, shard, part).wait_send()

    def drain_scatter(self, bufs, sems):
        for way in (0, 1):
            for j in range(self.size - 1):
                shard = self.size - 1 - j if way == 0 else j
                beyond = (shard > self.t) if way == 0 else (shard < self.t)

                @pl.when(beyond)
                def _(way=way, shard=shard):
                    for part in range(SUBS):
                        held = self._rows(bufs[way], shard, part)
                        self._copy(held, bufs[way], sems, way, shard, part).wait_send()


def line_sems(size):
    return [pltpu.SemaphoreType.DMA((2, size, SUBS)), pltpu.SemaphoreType.DMA((2, size, SUBS))]


def fold(x):
    rows, width = x.shape
    return jnp.sum(x.reshape(rows // 8, 8, width), axis=0)


def normal(x):
    centre = x - jnp.mean(x, axis=-1, keepdims=True)
    spread = lax.rsqrt(jnp.mean(centre * centre, axis=-1, keepdims=True) + EPS)
    return centre * spread, spread


def normal_back(upstream, normed, spread, gain):
    scaled = upstream * gain
    mean_part = jnp.mean(scaled, axis=-1, keepdims=True)
    across = jnp.mean(scaled * normed, axis=-1, keepdims=True)
    return spread * (scaled - mean_part - normed * across)


def row_loop(rows, step, body):
    def one(i, carry):
        body(pl.ds(pl.multiple_of(i * step, step), step))
        return carry

    lax.fori_loop(0, rows // step, one, 0)


def params(collective_id=None):
    if collective_id is None:
        return pltpu.CompilerParams(vmem_limit_bytes=VMEM_CAP)
    return pltpu.CompilerParams(
        collective_id=collective_id, has_side_effects=True, vmem_limit_bytes=VMEM_CAP
    )


def gather_small_kernel(n_dp, small, out, send, recv):
    me = lax.axis_index("dp")
    sem = pltpu.get_barrier_semaphore()
    for p in range(1, n_dp):
        pl.semaphore_signal(
            sem, device_id={"dp": lax.rem(me + p, n_dp)}, device_id_type=MESH
        )
    pl.semaphore_wait(sem, n_dp - 1)
    for p in range(1, n_dp):
        pltpu.make_async_remote_copy(
            src_ref=small,
            dst_ref=out.at[me],
            send_sem=send.at[p],
            recv_sem=recv.at[me],
            device_id={"dp": lax.rem(me + p, n_dp)},
            device_id_type=MESH,
        ).start()
    out[pl.ds(me, 1)] = small[...][None]
    for p in range(1, n_dp):
        source = lax.rem(me + p, n_dp)
        done = pltpu.make_async_remote_copy(
            src_ref=small,
            dst_ref=out.at[source],
            send_sem=send.at[p],
            recv_sem=recv.at[source],
            device_id={"dp": source},
            device_id_type=MESH,
        )
        done.wait_recv()
        done.wait_send()


def gather_small(small, n_dp, cid):
    return pl.pallas_call(
        functools.partial(gather_small_kernel, n_dp),
        out_shape=jax.ShapeDtypeStruct((n_dp,) + small.shape, small.dtype),
        in_specs=[WHOLE],
        out_specs=WHOLE,
        scratch_shapes=[pltpu.SemaphoreType.DMA((n_dp,)), pltpu.SemaphoreType.DMA((n_dp,))],
        compiler_params=params(cid),
    )(small)


def gather_rows_kernel(size, own, out, send, recv):
    line = Line(size, own.shape[0])
    line.barrier()
    sems = (send, recv)
    line.phase(
        gather=(out, sems, own),
    )
    out[pl.ds(line.t, 1)] = own[...][None]
    line.drain_gather(out, sems)


def gather_rows(own, size, cid):
    rows, width = own.shape
    return pl.pallas_call(
        functools.partial(gather_rows_kernel, size),
        out_shape=jax.ShapeDtypeStruct((size, rows, width), own.dtype),
        in_specs=[WHOLE],
        out_specs=WHOLE,
        scratch_shapes=line_sems(size),
        compiler_params=params(cid),
        name="gather_tokens",
    )(own)


def middle_kernel(
    size, terms, cot, tok, valid, vecs, c_out, gm_out, mid_out, stats,
    right, left, gs, gr, ss, sr, cs, cr,
):
    line = Line(size, tok.shape[0])
    rows = tok.shape[0]
    step = min(32, rows)
    line.barrier()
    line.phase(gather=(gm_out, (gs, gr), cot), scatter=(terms, (right, left), (ss, sr)))
    gm_out[pl.ds(line.t, 1)] = cot[...][None]
    line.own_wait((right, left), (ss, sr))
    stats[...] = jnp.zeros_like(stats)

    def body(at):
        attn = line.own_sum(terms, (right, left), at) + vecs[2:3, :]
        x = tok[at, :].astype(F32)
        mid = x + attn
        normed, _ = normal(mid)
        c_out[line.t, at, :] = (normed * vecs[3:4, :] + vecs[4:5, :]).astype(BF16)
        mid_out[at, :] = mid
        ok = valid[at, 0:1]
        stats[0:8, :] += fold(ok * x * x)
        stats[8:16, :] += fold(ok * attn * attn)
        stats[16:24, :] += fold(ok * mid * mid)

    row_loop(rows, step, body)
    line.phase(gather=(c_out, (cs, cr), None))
    line.drain_gather(gm_out, (gs, gr))
    line.drain_scatter((right, left), (ss, sr))
    line.drain_gather(c_out, (cs, cr))


def middle(terms, cot, tok, valid, vecs, size, cid):
    rows, width = tok.shape
    full = (size, rows, width)
    return pl.pallas_call(
        functools.partial(middle_kernel, size),
        out_shape=(
            jax.ShapeDtypeStruct(full, BF16),
            jax.ShapeDtypeStruct(full, BF16),
            jax.ShapeDtypeStruct((rows, width), F32),
            jax.ShapeDtypeStruct((24, width), F32),
        ),
        in_specs=[WHOLE] * 5,
        out_specs=(WHOLE,) * 4,
        scratch_shapes=[pltpu.VMEM(full, BF16), pltpu.VMEM(full, BF16)]
        + line_sems(size)
        + line_sems(size)
        + line_sems(size),
        compiler_params=params(cid),
        name="middle",
    )(terms, cot, tok, valid, vecs)


def back_middle_kernel(
    size, terms, mlp, gm, mid, valid, vecs, gz_out, gmid_out, y_out, stats,
    right, left, right2, left2, ss, sr, ms, mr, gs, gr,
):
    line = Line(size, mid.shape[0])
    rows = mid.shape[0]
    step = min(32, rows)
    line.barrier()
    line.phase(scatter=(terms, (right, left), (ss, sr)))
    line.own_wait((right, left), (ss, sr))
    stats[...] = jnp.zeros_like(stats)

    def body(at):
        e = line.own_sum(terms, (right, left), at)
        normed, spread = normal(mid[at, :])
        gy = gm[at, :].astype(F32)
        gmid = gy + normal_back(e, normed, spread, vecs[3:4, :])
        gz_out[line.t, at, :] = gmid.astype(BF16)
        gmid_out[at, :] = gmid
        stats[0:8, :] += fold(e * normed)
        stats[8:16, :] += fold(e)
        stats[16:24, :] += fold(gmid)
        stats[24:32, :] += fold(gy)

    row_loop(rows, step, body)
    line.phase(gather=(gz_out, (gs, gr), None), scatter=(mlp, (right2, left2), (ms, mr)))
    line.own_wait((right2, left2), (ms, mr))

    def tail(at):
        out = line.own_sum(mlp, (right2, left2), at) + vecs[5:6, :]
        y = mid[at, :] + out
        y_out[at, :] = y.astype(BF16)
        ok = valid[at, 0:1]
        stats[32:40, :] += fold(ok * out * out)
        stats[40:48, :] += fold(ok * y * y)

    row_loop(rows, step, tail)
    line.drain_scatter((right, left), (ss, sr))
    line.drain_scatter((right2, left2), (ms, mr))
    line.drain_gather(gz_out, (gs, gr))


def back_middle(terms, mlp, gm, mid, valid, vecs, size, cid):
    rows, width = mid.shape
    full = (size, rows, width)
    return pl.pallas_call(
        functools.partial(back_middle_kernel, size),
        out_shape=(
            jax.ShapeDtypeStruct(full, BF16),
            jax.ShapeDtypeStruct((rows, width), F32),
            jax.ShapeDtypeStruct((rows, width), BF16),
            jax.ShapeDtypeStruct((48, width), F32),
        ),
        in_specs=[WHOLE] * 6,
        out_specs=(WHOLE,) * 4,
        scratch_shapes=[pltpu.VMEM(full, BF16)] * 4
        + line_sems(size)
        + line_sems(size)
        + line_sems(size),
        compiler_params=params(cid),
        name="back_middle",
    )(terms, mlp, gm, mid, valid, vecs)


def finish_kernel(size, terms, tok, gmid, vecs, grad_out, stats, right, left, ss, sr):
    line = Line(size, tok.shape[0])
    rows = tok.shape[0]
    step = min(32, rows)
    line.barrier()
    line.phase(scatter=(terms, (right, left), (ss, sr)))
    line.own_wait((right, left), (ss, sr))
    stats[...] = jnp.zeros_like(stats)

    def body(at):
        e = line.own_sum(terms, (right, left), at)
        normed, spread = normal(tok[at, :].astype(F32))
        grad_out[at, :] = gmid[at, :] + normal_back(e, normed, spread, vecs[0:1, :])
        stats[0:8, :] += fold(e * normed)
        stats[8:16, :] += fold(e)

    row_loop(rows, step, body)
    line.drain_scatter((right, left), (ss, sr))


def finish(terms, tok, gmid, vecs, size, cid):
    rows, width = tok.shape
    full = (size, rows, width)
    return pl.pallas_call(
        functools.partial(finish_kernel, size),
        out_shape=(
            jax.ShapeDtypeStruct((rows, width), F32),
            jax.ShapeDtypeStruct((16, width), F32),
        ),
        in_specs=[WHOLE] * 4,
        out_specs=(WHOLE,) * 2,
        scratch_shapes=[pltpu.VMEM(full, BF16)] * 2 + line_sems(size),
        compiler_params=params(cid),
        name="finish",
    )(terms, tok, gmid, vecs)


def reduce_small_kernel(n_dp, n_t, shared, blocks, out, land, sums, land2, s1, r1, s2, r2):
    me, t = lax.axis_index("dp"), lax.axis_index("tensor")
    sem = pltpu.get_barrier_semaphore()
    for p in range(1, n_dp):
        pl.semaphore_signal(sem, device_id={"dp": lax.rem(me + p, n_dp)}, device_id_type=MESH)
    for p in range(1, n_t):
        pl.semaphore_signal(sem, device_id={"tensor": lax.rem(t + p, n_t)}, device_id_type=MESH)
    pl.semaphore_wait(sem, n_dp + n_t - 2)

    def one(p):
        other = lax.rem(me + p, n_dp)
        return pltpu.make_async_remote_copy(
            src_ref=blocks.at[other],
            dst_ref=land.at[p],
            send_sem=s1.at[p],
            recv_sem=r1.at[p],
            device_id={"dp": other},
            device_id_type=MESH,
        )

    for p in range(1, n_dp):
        one(p).start()
    total = blocks[me]
    for p in range(1, n_dp):
        one(p).wait_recv()
        total = total + land[p]
    sums[...] = total

    def two(p):
        return pltpu.make_async_remote_copy(
            src_ref=sums.at[pl.ds(0, shared)],
            dst_ref=land2.at[p],
            send_sem=s2.at[p],
            recv_sem=r2.at[p],
            device_id={"tensor": lax.rem(t + p, n_t)},
            device_id_type=MESH,
        )

    for p in range(1, n_t):
        two(p).start()
    out[...] = total
    top = sums[pl.ds(0, shared), :]
    for p in range(1, n_t):
        two(p).wait_recv()
        top = top + land2[p]
    out[pl.ds(0, shared), :] = top
    for p in range(1, n_dp):
        one(p).wait_send()
    for p in range(1, n_t):
        two(p).wait_send()


def reduce_small(blocks, shared, n_dp, n_t, cid):
    _, rows, width = blocks.shape
    return pl.pallas_call(
        functools.partial(reduce_small_kernel, n_dp, n_t, shared),
        out_shape=jax.ShapeDtypeStruct((rows, width), F32),
        in_specs=[WHOLE],
        out_specs=WHOLE,
        scratch_shapes=[
            pltpu.VMEM((n_dp, rows, width), F32),
            pltpu.VMEM((rows, width), F32),
            pltpu.VMEM((n_t, shared, width), F32),
            pltpu.SemaphoreType.DMA((n_dp,)),
            pltpu.SemaphoreType.DMA((n_dp,)),
            pltpu.SemaphoreType.DMA((n_t,)),
            pltpu.SemaphoreType.DMA((n_t,)),
        ],
        compiler_params=params(cid),
        name="reduce_small",
    )(blocks)


BLOCK = 256
NEG = -1e30
SCALE = HD**-0.5


def dot(a, b):
    return jnp.dot(a, b, preferred_element_type=F32)


def dot_t(a, b):
    return lax.dot_general(a, b, (((1,), (1,)), ((), ())), preferred_element_type=F32)


def masked_scores(q, k, keys, first, bar):
    scores = dot_t(k, q) * SCALE + bar
    key_pos = lax.broadcasted_iota(jnp.int32, (keys, BLOCK), 0)
    query_pos = first + lax.broadcasted_iota(jnp.int32, (keys, BLOCK), 1)
    return jnp.where(key_pos <= query_pos, scores, NEG)


def attend_kernel(q, k, v, bar, out, log_totals):
    value_cols = v[...].T
    for block in range(LEN // BLOCK):
        first, keys = block * BLOCK, (block + 1) * BLOCK
        scores = masked_scores(
            q[first : first + BLOCK, :], k[0:keys, :], keys, first, bar[0:keys, 0:1]
        )
        top = jnp.max(scores, axis=0, keepdims=True)
        powers = jnp.exp(scores - top)
        total = jnp.sum(powers, axis=0, keepdims=True)
        shares = (powers * (1.0 / total)).astype(BF16)
        mixed = dot(value_cols[:, 0:keys], shares)
        out[first : first + BLOCK, :] = mixed.T.astype(BF16)
        log_totals[0, :, first : first + BLOCK] = jnp.broadcast_to(top + jnp.log(total), (8, BLOCK))


def attend(qkv, bar, heads):
    def column(part):
        return pl.BlockSpec((LEN, HD), lambda h: (0, part * heads + h))

    return pl.pallas_call(
        attend_kernel,
        grid=(heads,),
        out_shape=(
            jax.ShapeDtypeStruct((LEN, heads * HD), BF16),
            jax.ShapeDtypeStruct((heads, 8, LEN), F32),
        ),
        in_specs=[column(0), column(1), column(2), pl.BlockSpec((LEN, 128), lambda h: (0, 0))],
        out_specs=(
            pl.BlockSpec((LEN, HD), lambda h: (0, h)),
            pl.BlockSpec((1, 8, LEN), lambda h: (h, 0, 0)),
        ),
        compiler_params=params(),
        name="attend",
    )(qkv, qkv, qkv, bar)


def attend_back_kernel(heads, q, k, v, go, bar, log_totals, out, sums, key_grad, value_grad):
    h = pl.program_id(0)
    key_cols = k[...].T
    query_sum = jnp.zeros((1, HD), F32)
    width = heads * HD
    at_q = pl.ds(pl.multiple_of(h * HD, HD), HD)
    at_k = pl.ds(pl.multiple_of(width + h * HD, HD), HD)
    at_v = pl.ds(pl.multiple_of(2 * width + h * HD, HD), HD)
    for block in range(LEN // BLOCK - 1, -1, -1):
        first, keys = block * BLOCK, (block + 1) * BLOCK
        here = slice(first, first + BLOCK)
        scores = masked_scores(q[here, :], k[0:keys, :], keys, first, bar[0:keys, 0:1])
        shares = jnp.exp(scores - log_totals[0, 0:1, here])
        share_grad = dot_t(v[0:keys, :], go[here, :])
        centre = jnp.sum(shares * share_grad, axis=0, keepdims=True)
        score_grad = (shares * (share_grad - centre)).astype(BF16)
        values = dot(shares.astype(BF16), go[here, :])
        keyed = dot(score_grad, q[here, :])
        if block == LEN // BLOCK - 1:
            value_grad[...] = values
            key_grad[...] = keyed
        else:
            value_grad[0:keys, :] += values
            key_grad[0:keys, :] += keyed
        query_grad = ((dot(key_cols[:, 0:keys], score_grad)) * SCALE).T.astype(BF16)
        out[here, at_q] = query_grad
        query_sum = query_sum + jnp.sum(query_grad.astype(F32), axis=0, keepdims=True)
    out[:, at_k] = (key_grad[...] * SCALE).astype(BF16)
    rounded = value_grad[...].astype(BF16)
    out[:, at_v] = rounded
    value_sum = jnp.sum(rounded.astype(F32), axis=0, keepdims=True)
    sums[0, 0:8, :] = jnp.broadcast_to(query_sum, (8, HD))
    sums[0, 8:16, :] = jnp.broadcast_to(value_sum, (8, HD))


def attend_back(qkv, go, bar, log_totals, heads):
    def column(part):
        return pl.BlockSpec((LEN, HD), lambda h: (0, part * heads + h))

    return pl.pallas_call(
        functools.partial(attend_back_kernel, heads),
        grid=(heads,),
        out_shape=(
            jax.ShapeDtypeStruct((LEN, 3 * heads * HD), BF16),
            jax.ShapeDtypeStruct((heads, 16, HD), F32),
        ),
        in_specs=[
            column(0), column(1), column(2), column(0),
            pl.BlockSpec((LEN, 128), lambda h: (0, 0)),
            pl.BlockSpec((1, 8, LEN), lambda h: (h, 0, 0)),
        ],
        out_specs=(
            pl.BlockSpec((LEN, 3 * heads * HD), lambda h: (0, 0)),
            pl.BlockSpec((1, 16, HD), lambda h: (h, 0, 0)),
        ),
        scratch_shapes=[pltpu.VMEM((LEN, HD), F32), pltpu.VMEM((LEN, HD), F32)],
        compiler_params=params(),
        name="attend_back",
    )(qkv, qkv, qkv, go, bar, log_totals)


def gelu_both(u):
    inner = 0.7978845608028654 * (u + 0.044715 * (u * u * u))
    th = jnp.tanh(inner)
    half = 0.5 * (1.0 + th)
    slope = half + 0.5 * u * (1.0 - th * th) * (
        0.7978845608028654 * (1.0 + 3 * 0.044715 * (u * u))
    )
    return u * half, slope


def hidden_kernel(n_dp, c, gm, up, down, bias, act_out, gu_out, sums):
    width = down.shape[2]
    rows = c.shape[0]
    step = min(256, rows)
    sums[...] = jnp.zeros_like(sums)

    def body(at):
        u = dot(c[at, :], up[...]) + bias[0:1, :]
        grad = dot_t(gm[at, 0:width], down[0])
        for d in range(1, n_dp):
            grad = grad + dot_t(gm[at, d * width : (d + 1) * width], down[d])
        act, slope = gelu_both(u)
        act_out[at, :] = act.astype(BF16)
        gu = (grad * slope).astype(BF16)
        gu_out[at, :] = gu
        sums[...] += fold(gu.astype(F32))

    row_loop(rows, step, body)


def hidden(c, gm, up, down, bias):
    rows, width = c.shape
    n_dp, units, part = down.shape
    block = min(512, units)
    return pl.pallas_call(
        functools.partial(hidden_kernel, n_dp),
        grid=(units // block,),
        out_shape=(
            jax.ShapeDtypeStruct((rows, units), BF16),
            jax.ShapeDtypeStruct((rows, units), BF16),
            jax.ShapeDtypeStruct((8, units), F32),
        ),
        in_specs=[
            pl.BlockSpec((rows, width), lambda i: (0, 0), pipeline_mode=pl.Buffered(1)),
            pl.BlockSpec((rows, width), lambda i: (0, 0), pipeline_mode=pl.Buffered(1)),
            pl.BlockSpec((width, block), lambda i: (0, i)),
            pl.BlockSpec((n_dp, block, part), lambda i: (0, i, 0)),
            pl.BlockSpec((8, block), lambda i: (0, i)),
        ],
        out_specs=(
            pl.BlockSpec((rows, block), lambda i: (0, i)),
            pl.BlockSpec((rows, block), lambda i: (0, i)),
            pl.BlockSpec((8, block), lambda i: (0, i)),
        ),
        compiler_params=params(),
        name="hidden",
    )(c, gm, up, down, bias)


def pad_to(x, count):
    return jnp.pad(x, ((0, 0), (0, count - x.shape[1])))


def shards(
    tokens, lengths, ln1_gain, ln1_bias, qkv_weight, qv_bias, out_weight, out_bias,
    ln2_gain, ln2_bias, up_weight, up_bias, down_weight, down_bias, cotangent,
):
    n_dp, n_t = lax.axis_size("dp"), lax.axis_size("tensor")
    rows, width = tokens.shape
    part = ln1_gain.shape[0]
    local = qkv_weight.shape[2]
    heads = local // HD
    units = up_weight.shape[1]
    hd_part = qv_bias.shape[2]
    t = lax.axis_index("tensor")
    length = lengths[0]

    pieces = [
        ln1_gain, ln1_bias, out_bias, ln2_gain, ln2_bias, down_bias,
        qv_bias.reshape(-1), up_bias.reshape(-1),
    ]
    packed = jnp.concatenate(pieces)
    count = packed.shape[0]
    lanes = -(-count // 2048) * 2048
    small = jnp.pad(packed, (0, lanes - count)).reshape(lanes // 128, 128)
    smalls = gather_small(small, n_dp, 0).reshape(n_dp, lanes)
    vecs = jnp.stack([smalls[:, i * part : (i + 1) * part].reshape(width) for i in range(6)])
    vecs = jnp.pad(vecs, ((0, 2), (0, 0))).astype(F32)
    at = 6 * part
    qv_all = smalls[:, at : at + 2 * heads * hd_part].reshape(n_dp, 2, heads, hd_part)
    qv_all = qv_all.transpose(1, 2, 0, 3).reshape(2, local).astype(F32)
    at += 2 * heads * hd_part
    up_all = smalls[:, at : at + units // n_dp].reshape(n_dp, units // 16, 16 // n_dp)
    up_shift = up_all.transpose(1, 0, 2).reshape(1, units).astype(F32)
    qkv_shift = jnp.concatenate([qv_all[0], jnp.zeros_like(qv_all[0]), qv_all[1]])

    qkv_full = lax.all_gather(qkv_weight, "dp", axis=0, tiled=True).reshape(width, 3 * local)
    out_full = lax.all_gather(out_weight, "dp", axis=1, tiled=True)
    up_full = lax.all_gather(up_weight, "dp", axis=0, tiled=True)
    down_blocks = lax.all_gather(down_weight, "dp", axis=0, tiled=False)

    own_pos = t * rows + jnp.arange(rows, dtype=jnp.int32)
    valid_own = (own_pos < length).astype(F32)
    valid = jnp.broadcast_to(valid_own[:, None], (rows, 128))
    positions = jnp.arange(LEN, dtype=jnp.int32)
    bar = jnp.broadcast_to(jnp.where(positions < length, 0.0, NEG)[:, None], (LEN, 128))
    gm_own = (cotangent.astype(F32) * valid_own[:, None]).astype(BF16)

    all_tokens = gather_rows(tokens, n_t, 1).reshape(n_t * rows, width)
    normed_one, _ = normal(all_tokens.astype(F32))
    a = (normed_one * vecs[0:1] + vecs[1:2]).astype(BF16)
    qkv = (dot(a, qkv_full) + qkv_shift).astype(BF16)
    attended, log_totals = attend(qkv, bar, heads)
    terms = dot(attended, out_full).astype(BF16).reshape(n_t, rows, width)
    c, gm, mid, stats_a = middle(terms, gm_own, tokens, valid, vecs, n_t, 2)
    c, gm = c.reshape(-1, width), gm.reshape(-1, width)
    act, gu, up_sums = hidden(
        c, gm, up_full, down_blocks, jnp.broadcast_to(up_shift, (8, units))
    )
    down_mat = down_blocks.transpose(1, 0, 2).reshape(units, width)

    def rows_dot(left, right):
        return lax.dot_general(
            left, right, (((0,), (0,)), ((), ())), preferred_element_type=F32
        ).astype(BF16)

    down_grad = rows_dot(act, gm)
    down_out = lax.psum_scatter(down_grad, "dp", scatter_dimension=1, tiled=True)
    up_grad = rows_dot(c, gu)
    up_out = lax.psum_scatter(up_grad, "dp", scatter_dimension=0, tiled=True)
    back_terms = dot_t(gu, up_full).astype(BF16).reshape(n_t, rows, width)
    mlp = dot(act, down_mat).astype(BF16).reshape(n_t, rows, width)
    gz, gmid, output, stats_b = back_middle(back_terms, mlp, gm_own, mid, valid, vecs, n_t, 3)
    gz = gz.reshape(-1, width)
    go = dot_t(gz, out_full).astype(BF16)
    out_grad = rows_dot(attended, gz)
    out_out = lax.psum_scatter(out_grad, "dp", scatter_dimension=1, tiled=True)
    gqkv, head_sums = attend_back(qkv, go, bar, log_totals, heads)
    qkv_grad = rows_dot(a, gqkv).reshape(width, 3, local)
    qkv_out = lax.psum_scatter(qkv_grad, "dp", scatter_dimension=0, tiled=True)
    last_terms = dot_t(gqkv, qkv_full).astype(BF16).reshape(n_t, rows, width)
    tokens_grad, stats_c = finish(last_terms, tokens, gmid, vecs, n_t, 4)

    def vec_sum(stats, i):
        return jnp.sum(stats[8 * i : 8 * i + 8], axis=0)

    vectors = jnp.stack(
        [
            vec_sum(stats_c, 0), vec_sum(stats_c, 1), vec_sum(stats_b, 2),
            vec_sum(stats_b, 0), vec_sum(stats_b, 1), vec_sum(stats_b, 3),
        ]
    )
    squares = jnp.stack(
        [
            jnp.sum(stats_a[0:8]), jnp.sum(stats_a[8:16]), jnp.sum(stats_a[16:24]),
            jnp.sum(stats_b[32:40]), jnp.sum(stats_b[40:48]), jnp.sum(valid_own),
        ]
    )
    vector_blocks = vectors.reshape(6, n_dp, part).transpose(1, 0, 2).reshape(n_dp, 6 * part)
    scalar_blocks = jnp.broadcast_to(squares[None], (n_dp, 6))
    top = jnp.concatenate([vector_blocks, scalar_blocks], axis=1)
    top_len = -(-top.shape[1] // 1024) * 1024
    up_blocks = jnp.sum(up_sums, axis=0).reshape(units // 16, n_dp, 16 // n_dp)
    up_blocks = up_blocks.transpose(1, 0, 2).reshape(n_dp, units // n_dp)
    qv_sums = jnp.stack([head_sums[:, 0], head_sums[:, 8]])
    qv_blocks = qv_sums.reshape(2, heads, n_dp, hd_part).transpose(2, 0, 1, 3)
    qv_blocks = qv_blocks.reshape(n_dp, 2 * heads * hd_part)
    low = jnp.concatenate([up_blocks, qv_blocks], axis=1)
    low_len = -(-low.shape[1] // 1024) * 1024
    blocks = jnp.concatenate([pad_to(top, top_len), pad_to(low, low_len)], axis=1)
    blocks = blocks.reshape(n_dp, (top_len + low_len) // 128, 128)
    reduced = reduce_small(blocks, top_len // 128, n_dp, n_t, 5).reshape(-1)
    outs = [reduced[i * part : (i + 1) * part] for i in range(6)]
    totals = reduced[6 * part : 6 * part + 6]
    stream_rms = jnp.sqrt(totals[:5] / (totals[5] * width))
    at = top_len
    up_bias_out = reduced[at : at + units // n_dp].reshape(up_bias.shape)
    at += units // n_dp
    qv_bias_out = reduced[at : at + 2 * heads * hd_part].reshape(qv_bias.shape)

    return (
        output, tokens_grad, outs[0], outs[1],
        qkv_out.astype(F32), qv_bias_out, out_out.astype(F32), outs[2],
        outs[3], outs[4], up_out.astype(F32), up_bias_out,
        down_out.astype(F32), outs[5], stream_rms,
    )


def solution(mesh):
    vector = P("dp")
    rows = P(("dp", "tensor"), None)
    return jax.shard_map(
        shards,
        mesh=mesh,
        in_specs=(
            rows, vector, vector, vector, P("dp", None, "tensor"), P(None, "tensor", "dp"),
            P("tensor", "dp"), vector, vector, vector, P("dp", "tensor"), P("tensor", "dp"),
            P("tensor", "dp"), vector, rows,
        ),
        out_specs=(
            rows, rows, vector, vector, P("dp", None, "tensor"), P(None, "tensor", "dp"),
            P("tensor", "dp"), vector, vector, vector, P("dp", "tensor"), P("tensor", "dp"),
            P("tensor", "dp"), vector, P(),
        ),
        check_vma=False,
    )
```

```python
import functools

import jax
import jax.numpy as jnp
from jax import lax
from jax.experimental import pallas as pl
from jax.experimental.pallas import tpu as pltpu
from jax.sharding import PartitionSpec as P

HD = 128
LEN = 1024
EPS = 1e-05
MESH = pl.DeviceIdType.MESH
F32 = jnp.float32
BF16 = jnp.bfloat16
VMEM_CAP = 60 * 1024 * 1024
SUBS = 2
WHOLE = pl.BlockSpec(memory_space=pltpu.VMEM)


class Line:
    def __init__(self, size, rows):
        self.size, self.rows, self.t = size, rows, lax.axis_index("tensor")
        self.sub = rows // SUBS

    def barrier(self):
        sem = pltpu.get_barrier_semaphore()
        pl.semaphore_wait(sem, self.greet(sem))

    def greet(self, sem):
        @pl.when(self.t > 0)
        def _():
            pl.semaphore_signal(sem, device_id={"tensor": self.t - 1}, device_id_type=MESH)

        @pl.when(self.t < self.size - 1)
        def _():
            pl.semaphore_signal(sem, device_id={"tensor": self.t + 1}, device_id_type=MESH)

        return jnp.where(self.t > 0, 1, 0) + jnp.where(self.t < self.size - 1, 1, 0)

    def _copy(self, src, dst, sems, way, shard, part):
        send, recv = sems
        target = self.t + 1 if way == 0 else self.t - 1
        return pltpu.make_async_remote_copy(
            src_ref=src,
            dst_ref=dst.at[shard, pl.ds(part * self.sub, self.sub)],
            send_sem=send.at[way, shard, part],
            recv_sem=recv.at[way, shard, part],
            device_id={"tensor": target},
            device_id_type=MESH,
        )

    def _rows(self, ref, shard, part):
        return ref.at[shard, pl.ds(part * self.sub, self.sub)]

    def _edge(self, way):
        return self.t < self.size - 1 if way == 0 else self.t > 0

    def gather_step(self, way, k, part, buf, sems, first):
        t, last = self.t, self.size - 1
        shard = t - k if way == 0 else t + k
        inside = (t >= k) if way == 0 else (t + k <= last)

        @pl.when(inside)
        def _():
            held = self._rows(buf, shard, part)
            if k > 0:
                self._copy(held, buf, sems, way, shard, part).wait_recv()

            @pl.when(self._edge(way))
            def _():
                src = held
                if k == 0 and first is not None:
                    src = first.at[pl.ds(part * self.sub, self.sub)]
                self._copy(src, buf, sems, way, shard, part).start()

    def scatter_step(self, way, j, part, terms, buf, sems):
        t, last = self.t, self.size - 1
        shard = last - j if way == 0 else j
        beyond = (shard > t) if way == 0 else (shard < t)
        starts = (t == 0) if way == 0 else (t == last)

        @pl.when(beyond & starts)
        def _():
            self._copy(self._rows(terms, shard, part), buf, sems, way, shard, part).start()

        @pl.when(beyond & jnp.logical_not(starts))
        def _():
            held = self._rows(buf, shard, part)
            self._copy(held, buf, sems, way, shard, part).wait_recv()
            step = min(32, self.sub)

            def add(i, carry):
                rows = pl.ds(part * self.sub + i * step, step)
                total = buf[shard, rows, :].astype(F32) + terms[shard, rows, :].astype(F32)
                buf[shard, rows, :] = total.astype(BF16)
                return carry

            lax.fori_loop(0, self.sub // step, add, 0)
            self._copy(held, buf, sems, way, shard, part).start()

    def phase(self, gather=None, scatter=None, on_slot=None):
        n = self.size
        for k in range(n):
            for part in range(SUBS):
                for way in (0, 1):
                    if gather is not None:
                        self.gather_step(way, k, part, gather[0], gather[1], gather[2])
                    if scatter is not None:
                        if gather is None:
                            if k < n - 1:
                                self.scatter_step(way, k, part, scatter[0], scatter[1][way], scatter[2])
                        else:
                            behind = self.t if way == 0 else n - 1 - self.t
                            for b in range(k):

                                @pl.when(behind == b)
                                def _(b=b, k=k, part=part, way=way):
                                    self.scatter_step(
                                        way, k - 1 - b, part, scatter[0], scatter[1][way], scatter[2]
                                    )
            if on_slot is not None:
                on_slot(k)

    def own_wait(self, bufs, sems):
        for way in (0, 1):
            arrives = self.t > 0 if way == 0 else self.t < self.size - 1

            @pl.when(arrives)
            def _(way=way):
                for part in range(SUBS):
                    held = self._rows(bufs[way], self.t, part)
                    self._copy(held, bufs[way], sems, way, self.t, part).wait_recv()

    def own_sum(self, terms, bufs, rows):
        t = self.t
        zero = jnp.zeros((), F32)
        right = jnp.where(t > 0, bufs[0][t, rows, :].astype(F32), zero)
        left = jnp.where(t < self.size - 1, bufs[1][t, rows, :].astype(F32), zero)
        return terms[t, rows, :].astype(F32) + right + left

    def drain_gather(self, buf, sems):
        for way in (0, 1):
            for k in range(self.size):
                shard = self.t - k if way == 0 else self.t + k
                inside = (self.t >= k) if way == 0 else (self.t + k <= self.size - 1)

                @pl.when(inside & self._edge(way))
                def _(way=way, shard=shard):
                    for part in range(SUBS):
                        held = self._rows(buf, shard, part)
                        self._copy(held, buf, sems, way, shard, part).wait_send()

    def drain_scatter(self, bufs, sems):
        for way in (0, 1):
            for j in range(self.size - 1):
                shard = self.size - 1 - j if way == 0 else j
                beyond = (shard > self.t) if way == 0 else (shard < self.t)

                @pl.when(beyond)
                def _(way=way, shard=shard):
                    for part in range(SUBS):
                        held = self._rows(bufs[way], shard, part)
                        self._copy(held, bufs[way], sems, way, shard, part).wait_send()


def line_sems(size):
    return [pltpu.SemaphoreType.DMA((2, size, SUBS)), pltpu.SemaphoreType.DMA((2, size, SUBS))]


def fold(x):
    rows, width = x.shape
    return jnp.sum(x.reshape(rows // 8, 8, width), axis=0)


def normal(x):
    centre = x - jnp.mean(x, axis=-1, keepdims=True)
    spread = lax.rsqrt(jnp.mean(centre * centre, axis=-1, keepdims=True) + EPS)
    return centre * spread, spread


def normal_back(upstream, normed, spread, gain):
    scaled = upstream * gain
    mean_part = jnp.mean(scaled, axis=-1, keepdims=True)
    across = jnp.mean(scaled * normed, axis=-1, keepdims=True)
    return spread * (scaled - mean_part - normed * across)


def row_loop(rows, step, body):
    def one(i, carry):
        body(pl.ds(pl.multiple_of(i * step, step), step))
        return carry

    lax.fori_loop(0, rows // step, one, 0)


def params(collective_id=None):
    if collective_id is None:
        return pltpu.CompilerParams(vmem_limit_bytes=VMEM_CAP)
    return pltpu.CompilerParams(
        collective_id=collective_id, has_side_effects=True, vmem_limit_bytes=VMEM_CAP
    )


def first_kernel(n_dp, size, part, small, own, smalls, a_out, tok, send, recv, gs, gr):
    line = Line(size, own.shape[0])
    me = lax.axis_index("dp")
    rows, width = own.shape
    sem = pltpu.get_barrier_semaphore()
    for p in range(1, n_dp):
        pl.semaphore_signal(sem, device_id={"dp": lax.rem(me + p, n_dp)}, device_id_type=MESH)
    ends = line.greet(sem)
    pl.semaphore_wait(sem, ends + n_dp - 1)
    sems = (gs, gr)

    def small_copy(p, slot):
        return pltpu.make_async_remote_copy(
            src_ref=small,
            dst_ref=smalls.at[slot],
            send_sem=send.at[p],
            recv_sem=recv.at[slot],
            device_id={"dp": lax.rem(me + p, n_dp)},
            device_id_type=MESH,
        )

    for p in range(1, n_dp):
        small_copy(p, me).start()
    smalls[pl.ds(me, 1)] = small[...][None]
    step = min(32, rows)
    vec_rows = part // 128

    def normalise(source, shard):
        gain = jnp.concatenate(
            [smalls[d, r : r + 1, :] for d in range(n_dp) for r in range(vec_rows)], axis=1
        ).astype(F32)
        shift = jnp.concatenate(
            [smalls[d, r : r + 1, :] for d in range(n_dp) for r in range(vec_rows, 2 * vec_rows)],
            axis=1,
        ).astype(F32)

        def body(at):
            x = source[at, :] if shard is None else source[shard, at, :]
            normed, _ = normal(x.astype(F32))
            to = line.t if shard is None else shard
            a_out[to, at, :] = (normed * gain + shift).astype(BF16)

        row_loop(rows, step, body)

    def on_slot(k):
        if k == 0:
            for p in range(1, n_dp):
                small_copy(p, lax.rem(me + p, n_dp)).wait_recv()
            normalise(own, None)
        else:

            @pl.when(line.t >= k)
            def _():
                normalise(tok, line.t - k)

            @pl.when(line.t + k <= size - 1)
            def _():
                normalise(tok, line.t + k)

    line.phase(gather=(tok, sems, own), on_slot=on_slot)
    line.drain_gather(tok, sems)
    for p in range(1, n_dp):
        small_copy(p, me).wait_send()


def first(small, own, part, n_dp, size, cid):
    rows, width = own.shape
    return pl.pallas_call(
        functools.partial(first_kernel, n_dp, size, part),
        out_shape=(
            jax.ShapeDtypeStruct((n_dp,) + small.shape, small.dtype),
            jax.ShapeDtypeStruct((size, rows, width), BF16),
        ),
        in_specs=[WHOLE, WHOLE],
        out_specs=(WHOLE, WHOLE),
        scratch_shapes=[
            pltpu.VMEM((size, rows, width), BF16),
            pltpu.SemaphoreType.DMA((n_dp,)),
            pltpu.SemaphoreType.DMA((n_dp,)),
        ]
        + line_sems(size),
        compiler_params=params(cid),
        name="first",
    )(small, own)


def middle_kernel(
    size, terms, cot, tok, valid, vecs, c_out, gm_out, mid_out, stats,
    right, left, gs, gr, ss, sr, cs, cr,
):
    line = Line(size, tok.shape[0])
    rows = tok.shape[0]
    step = min(32, rows)
    line.barrier()
    line.phase(gather=(gm_out, (gs, gr), cot), scatter=(terms, (right, left), (ss, sr)))
    gm_out[pl.ds(line.t, 1)] = cot[...][None]
    line.own_wait((right, left), (ss, sr))
    stats[...] = jnp.zeros_like(stats)

    def body(at):
        attn = line.own_sum(terms, (right, left), at) + vecs[2:3, :]
        x = tok[at, :].astype(F32)
        mid = x + attn
        normed, _ = normal(mid)
        c_out[line.t, at, :] = (normed * vecs[3:4, :] + vecs[4:5, :]).astype(BF16)
        mid_out[at, :] = mid
        ok = valid[at, 0:1]
        stats[0:8, :] += fold(ok * x * x)
        stats[8:16, :] += fold(ok * attn * attn)
        stats[16:24, :] += fold(ok * mid * mid)

    row_loop(rows, step, body)
    line.phase(gather=(c_out, (cs, cr), None))
    line.drain_gather(gm_out, (gs, gr))
    line.drain_scatter((right, left), (ss, sr))
    line.drain_gather(c_out, (cs, cr))


def middle(terms, cot, tok, valid, vecs, size, cid):
    rows, width = tok.shape
    full = (size, rows, width)
    return pl.pallas_call(
        functools.partial(middle_kernel, size),
        out_shape=(
            jax.ShapeDtypeStruct(full, BF16),
            jax.ShapeDtypeStruct(full, BF16),
            jax.ShapeDtypeStruct((rows, width), F32),
            jax.ShapeDtypeStruct((24, width), F32),
        ),
        in_specs=[WHOLE] * 5,
        out_specs=(WHOLE,) * 4,
        scratch_shapes=[pltpu.VMEM(full, BF16), pltpu.VMEM(full, BF16)]
        + line_sems(size)
        + line_sems(size)
        + line_sems(size),
        compiler_params=params(cid),
        name="middle",
    )(terms, cot, tok, valid, vecs)


def back_middle_kernel(
    size, terms, mlp, gm, mid, valid, vecs, gz_out, gmid_out, y_out, stats,
    right, left, right2, left2, ss, sr, ms, mr, gs, gr,
):
    line = Line(size, mid.shape[0])
    rows = mid.shape[0]
    step = min(32, rows)
    line.barrier()
    line.phase(scatter=(terms, (right, left), (ss, sr)))
    line.own_wait((right, left), (ss, sr))
    stats[...] = jnp.zeros_like(stats)

    def body(at):
        e = line.own_sum(terms, (right, left), at)
        normed, spread = normal(mid[at, :])
        gy = gm[at, :].astype(F32)
        gmid = gy + normal_back(e, normed, spread, vecs[3:4, :])
        gz_out[line.t, at, :] = gmid.astype(BF16)
        gmid_out[at, :] = gmid
        stats[0:8, :] += fold(e * normed)
        stats[8:16, :] += fold(e)
        stats[16:24, :] += fold(gmid)
        stats[24:32, :] += fold(gy)

    row_loop(rows, step, body)
    line.phase(gather=(gz_out, (gs, gr), None), scatter=(mlp, (right2, left2), (ms, mr)))
    line.own_wait((right2, left2), (ms, mr))

    def tail(at):
        out = line.own_sum(mlp, (right2, left2), at) + vecs[5:6, :]
        y = mid[at, :] + out
        y_out[at, :] = y.astype(BF16)
        ok = valid[at, 0:1]
        stats[32:40, :] += fold(ok * out * out)
        stats[40:48, :] += fold(ok * y * y)

    row_loop(rows, step, tail)
    line.drain_scatter((right, left), (ss, sr))
    line.drain_scatter((right2, left2), (ms, mr))
    line.drain_gather(gz_out, (gs, gr))


def back_middle(terms, mlp, gm, mid, valid, vecs, size, cid):
    rows, width = mid.shape
    full = (size, rows, width)
    return pl.pallas_call(
        functools.partial(back_middle_kernel, size),
        out_shape=(
            jax.ShapeDtypeStruct(full, BF16),
            jax.ShapeDtypeStruct((rows, width), F32),
            jax.ShapeDtypeStruct((rows, width), BF16),
            jax.ShapeDtypeStruct((48, width), F32),
        ),
        in_specs=[WHOLE] * 6,
        out_specs=(WHOLE,) * 4,
        scratch_shapes=[pltpu.VMEM(full, BF16)] * 4
        + line_sems(size)
        + line_sems(size)
        + line_sems(size),
        compiler_params=params(cid),
        name="back_middle",
    )(terms, mlp, gm, mid, valid, vecs)


def finish_kernel(size, terms, tok, gmid, vecs, grad_out, stats, right, left, ss, sr):
    line = Line(size, tok.shape[0])
    rows = tok.shape[0]
    step = min(32, rows)
    line.barrier()
    line.phase(scatter=(terms, (right, left), (ss, sr)))
    line.own_wait((right, left), (ss, sr))
    stats[...] = jnp.zeros_like(stats)

    def body(at):
        e = line.own_sum(terms, (right, left), at)
        normed, spread = normal(tok[at, :].astype(F32))
        grad_out[at, :] = gmid[at, :] + normal_back(e, normed, spread, vecs[0:1, :])
        stats[0:8, :] += fold(e * normed)
        stats[8:16, :] += fold(e)

    row_loop(rows, step, body)
    line.drain_scatter((right, left), (ss, sr))


def finish(terms, tok, gmid, vecs, size, cid):
    rows, width = tok.shape
    full = (size, rows, width)
    return pl.pallas_call(
        functools.partial(finish_kernel, size),
        out_shape=(
            jax.ShapeDtypeStruct((rows, width), F32),
            jax.ShapeDtypeStruct((16, width), F32),
        ),
        in_specs=[WHOLE] * 4,
        out_specs=(WHOLE,) * 2,
        scratch_shapes=[pltpu.VMEM(full, BF16)] * 2 + line_sems(size),
        compiler_params=params(cid),
        name="finish",
    )(terms, tok, gmid, vecs)


def reduce_small_kernel(n_dp, n_t, shared, blocks, out, land, sums, land2, s1, r1, s2, r2):
    me, t = lax.axis_index("dp"), lax.axis_index("tensor")
    sem = pltpu.get_barrier_semaphore()
    for p in range(1, n_dp):
        pl.semaphore_signal(sem, device_id={"dp": lax.rem(me + p, n_dp)}, device_id_type=MESH)
    for p in range(1, n_t):
        pl.semaphore_signal(sem, device_id={"tensor": lax.rem(t + p, n_t)}, device_id_type=MESH)
    pl.semaphore_wait(sem, n_dp + n_t - 2)

    def one(p):
        other = lax.rem(me + p, n_dp)
        return pltpu.make_async_remote_copy(
            src_ref=blocks.at[other],
            dst_ref=land.at[p],
            send_sem=s1.at[p],
            recv_sem=r1.at[p],
            device_id={"dp": other},
            device_id_type=MESH,
        )

    for p in range(1, n_dp):
        one(p).start()
    total = blocks[me]
    for p in range(1, n_dp):
        one(p).wait_recv()
        total = total + land[p]
    sums[...] = total

    def two(p):
        return pltpu.make_async_remote_copy(
            src_ref=sums.at[pl.ds(0, shared)],
            dst_ref=land2.at[p],
            send_sem=s2.at[p],
            recv_sem=r2.at[p],
            device_id={"tensor": lax.rem(t + p, n_t)},
            device_id_type=MESH,
        )

    for p in range(1, n_t):
        two(p).start()
    out[...] = total
    top = sums[pl.ds(0, shared), :]
    for p in range(1, n_t):
        two(p).wait_recv()
        top = top + land2[p]
    out[pl.ds(0, shared), :] = top
    for p in range(1, n_dp):
        one(p).wait_send()
    for p in range(1, n_t):
        two(p).wait_send()


def reduce_small(blocks, shared, n_dp, n_t, cid):
    _, rows, width = blocks.shape
    return pl.pallas_call(
        functools.partial(reduce_small_kernel, n_dp, n_t, shared),
        out_shape=jax.ShapeDtypeStruct((rows, width), F32),
        in_specs=[WHOLE],
        out_specs=WHOLE,
        scratch_shapes=[
            pltpu.VMEM((n_dp, rows, width), F32),
            pltpu.VMEM((rows, width), F32),
            pltpu.VMEM((n_t, shared, width), F32),
            pltpu.SemaphoreType.DMA((n_dp,)),
            pltpu.SemaphoreType.DMA((n_dp,)),
            pltpu.SemaphoreType.DMA((n_t,)),
            pltpu.SemaphoreType.DMA((n_t,)),
        ],
        compiler_params=params(cid),
        name="reduce_small",
    )(blocks)


BLOCK = 256
NEG = -1e30
SCALE = HD**-0.5


def dot(a, b):
    return jnp.dot(a, b, preferred_element_type=F32)


def dot_t(a, b):
    return lax.dot_general(a, b, (((1,), (1,)), ((), ())), preferred_element_type=F32)


def masked_scores(q, k, keys, first, bar):
    scores = dot_t(k, q) * SCALE + bar
    key_pos = lax.broadcasted_iota(jnp.int32, (keys, BLOCK), 0)
    query_pos = first + lax.broadcasted_iota(jnp.int32, (keys, BLOCK), 1)
    return jnp.where(key_pos <= query_pos, scores, NEG)


def attend_kernel(q, k, v, bar, out, log_totals):
    value_cols = v[...].T
    for block in range(LEN // BLOCK):
        first, keys = block * BLOCK, (block + 1) * BLOCK
        scores = masked_scores(
            q[first : first + BLOCK, :], k[0:keys, :], keys, first, bar[0:keys, 0:1]
        )
        top = jnp.max(scores, axis=0, keepdims=True)
        powers = jnp.exp(scores - top)
        total = jnp.sum(powers, axis=0, keepdims=True)
        shares = (powers * (1.0 / total)).astype(BF16)
        mixed = dot(value_cols[:, 0:keys], shares)
        out[first : first + BLOCK, :] = mixed.T.astype(BF16)
        log_totals[0, :, first : first + BLOCK] = jnp.broadcast_to(top + jnp.log(total), (8, BLOCK))


def attend(qkv, bar, heads):
    def column(part):
        return pl.BlockSpec((LEN, HD), lambda h: (0, part * heads + h))

    return pl.pallas_call(
        attend_kernel,
        grid=(heads,),
        out_shape=(
            jax.ShapeDtypeStruct((LEN, heads * HD), BF16),
            jax.ShapeDtypeStruct((heads, 8, LEN), F32),
        ),
        in_specs=[column(0), column(1), column(2), pl.BlockSpec((LEN, 128), lambda h: (0, 0))],
        out_specs=(
            pl.BlockSpec((LEN, HD), lambda h: (0, h)),
            pl.BlockSpec((1, 8, LEN), lambda h: (h, 0, 0)),
        ),
        compiler_params=params(),
        name="attend",
    )(qkv, qkv, qkv, bar)


def attend_back_kernel(heads, q, k, v, go, bar, log_totals, out, sums, key_grad, value_grad):
    h = pl.program_id(0)
    key_cols = k[...].T
    query_sum = jnp.zeros((1, HD), F32)
    width = heads * HD
    at_q = pl.ds(pl.multiple_of(h * HD, HD), HD)
    at_k = pl.ds(pl.multiple_of(width + h * HD, HD), HD)
    at_v = pl.ds(pl.multiple_of(2 * width + h * HD, HD), HD)
    for block in range(LEN // BLOCK - 1, -1, -1):
        first, keys = block * BLOCK, (block + 1) * BLOCK
        here = slice(first, first + BLOCK)
        scores = masked_scores(q[here, :], k[0:keys, :], keys, first, bar[0:keys, 0:1])
        shares = jnp.exp(scores - log_totals[0, 0:1, here])
        share_grad = dot_t(v[0:keys, :], go[here, :])
        centre = jnp.sum(shares * share_grad, axis=0, keepdims=True)
        score_grad = (shares * (share_grad - centre)).astype(BF16)
        values = dot(shares.astype(BF16), go[here, :])
        keyed = dot(score_grad, q[here, :])
        if block == LEN // BLOCK - 1:
            value_grad[...] = values
            key_grad[...] = keyed
        else:
            value_grad[0:keys, :] += values
            key_grad[0:keys, :] += keyed
        query_grad = ((dot(key_cols[:, 0:keys], score_grad)) * SCALE).T.astype(BF16)
        out[here, at_q] = query_grad
        query_sum = query_sum + jnp.sum(query_grad.astype(F32), axis=0, keepdims=True)
    out[:, at_k] = (key_grad[...] * SCALE).astype(BF16)
    rounded = value_grad[...].astype(BF16)
    out[:, at_v] = rounded
    value_sum = jnp.sum(rounded.astype(F32), axis=0, keepdims=True)
    sums[0, 0:8, :] = jnp.broadcast_to(query_sum, (8, HD))
    sums[0, 8:16, :] = jnp.broadcast_to(value_sum, (8, HD))


def attend_back(qkv, go, bar, log_totals, heads):
    def column(part):
        return pl.BlockSpec((LEN, HD), lambda h: (0, part * heads + h))

    return pl.pallas_call(
        functools.partial(attend_back_kernel, heads),
        grid=(heads,),
        out_shape=(
            jax.ShapeDtypeStruct((LEN, 3 * heads * HD), BF16),
            jax.ShapeDtypeStruct((heads, 16, HD), F32),
        ),
        in_specs=[
            column(0), column(1), column(2), column(0),
            pl.BlockSpec((LEN, 128), lambda h: (0, 0)),
            pl.BlockSpec((1, 8, LEN), lambda h: (h, 0, 0)),
        ],
        out_specs=(
            pl.BlockSpec((LEN, 3 * heads * HD), lambda h: (0, 0)),
            pl.BlockSpec((1, 16, HD), lambda h: (h, 0, 0)),
        ),
        scratch_shapes=[pltpu.VMEM((LEN, HD), F32), pltpu.VMEM((LEN, HD), F32)],
        compiler_params=params(),
        name="attend_back",
    )(qkv, qkv, qkv, go, bar, log_totals)


def gelu_both(u):
    inner = 0.7978845608028654 * (u + 0.044715 * (u * u * u))
    th = jnp.tanh(inner)
    half = 0.5 * (1.0 + th)
    slope = half + 0.5 * u * (1.0 - th * th) * (
        0.7978845608028654 * (1.0 + 3 * 0.044715 * (u * u))
    )
    return u * half, slope


def hidden_kernel(n_dp, c, gm, up, down, bias, act_out, gu_out, sums):
    width = down.shape[2]
    rows = c.shape[0]
    step = min(256, rows)
    sums[...] = jnp.zeros_like(sums)

    def body(at):
        u = dot(c[at, :], up[...]) + bias[0:1, :]
        grad = dot_t(gm[at, 0:width], down[0])
        for d in range(1, n_dp):
            grad = grad + dot_t(gm[at, d * width : (d + 1) * width], down[d])
        act, slope = gelu_both(u)
        act_out[at, :] = act.astype(BF16)
        gu = (grad * slope).astype(BF16)
        gu_out[at, :] = gu
        sums[...] += fold(gu.astype(F32))

    row_loop(rows, step, body)


def hidden(c, gm, up, down, bias):
    rows, width = c.shape
    n_dp, units, part = down.shape
    block = min(512, units)
    return pl.pallas_call(
        functools.partial(hidden_kernel, n_dp),
        grid=(units // block,),
        out_shape=(
            jax.ShapeDtypeStruct((rows, units), BF16),
            jax.ShapeDtypeStruct((rows, units), BF16),
            jax.ShapeDtypeStruct((8, units), F32),
        ),
        in_specs=[
            pl.BlockSpec((rows, width), lambda i: (0, 0), pipeline_mode=pl.Buffered(1)),
            pl.BlockSpec((rows, width), lambda i: (0, 0), pipeline_mode=pl.Buffered(1)),
            pl.BlockSpec((width, block), lambda i: (0, i)),
            pl.BlockSpec((n_dp, block, part), lambda i: (0, i, 0)),
            pl.BlockSpec((8, block), lambda i: (0, i)),
        ],
        out_specs=(
            pl.BlockSpec((rows, block), lambda i: (0, i)),
            pl.BlockSpec((rows, block), lambda i: (0, i)),
            pl.BlockSpec((8, block), lambda i: (0, i)),
        ),
        compiler_params=params(),
        name="hidden",
    )(c, gm, up, down, bias)


def project_kernel(act, down, out):
    out[...] = dot(act[...], down[0]).astype(BF16)


def project(act, down):
    rows, units = act.shape
    n_dp, _, part = down.shape
    return pl.pallas_call(
        project_kernel,
        grid=(n_dp,),
        out_shape=jax.ShapeDtypeStruct((rows, n_dp * part), BF16),
        in_specs=[
            pl.BlockSpec((rows, units), lambda i: (0, 0), pipeline_mode=pl.Buffered(1)),
            pl.BlockSpec((1, units, part), lambda i: (i, 0, 0)),
        ],
        out_specs=pl.BlockSpec((rows, part), lambda i: (0, i)),
        compiler_params=params(),
        name="project",
    )(act, down)


def pad_to(x, count):
    return jnp.pad(x, ((0, 0), (0, count - x.shape[1])))


def shards(
    tokens, lengths, ln1_gain, ln1_bias, qkv_weight, qv_bias, out_weight, out_bias,
    ln2_gain, ln2_bias, up_weight, up_bias, down_weight, down_bias, cotangent,
):
    n_dp, n_t = lax.axis_size("dp"), lax.axis_size("tensor")
    rows, width = tokens.shape
    part = ln1_gain.shape[0]
    local = qkv_weight.shape[2]
    heads = local // HD
    units = up_weight.shape[1]
    hd_part = qv_bias.shape[2]
    t = lax.axis_index("tensor")
    length = lengths[0]

    pieces = [
        ln1_gain, ln1_bias, out_bias, ln2_gain, ln2_bias, down_bias,
        qv_bias.reshape(-1), up_bias.reshape(-1),
    ]
    packed = jnp.concatenate(pieces)
    count = packed.shape[0]
    lanes = -(-count // 2048) * 2048
    small = jnp.pad(packed, (0, lanes - count)).reshape(lanes // 128, 128)
    smalls, a = first(small, tokens, part, n_dp, n_t, 0)
    smalls, a = smalls.reshape(n_dp, lanes), a.reshape(n_t * rows, width)
    vecs = jnp.stack([smalls[:, i * part : (i + 1) * part].reshape(width) for i in range(6)])
    vecs = jnp.pad(vecs, ((0, 2), (0, 0))).astype(F32)
    at = 6 * part
    qv_all = smalls[:, at : at + 2 * heads * hd_part].reshape(n_dp, 2, heads, hd_part)
    qv_all = qv_all.transpose(1, 2, 0, 3).reshape(2, local).astype(F32)
    at += 2 * heads * hd_part
    up_all = smalls[:, at : at + units // n_dp].reshape(n_dp, units // 16, 16 // n_dp)
    up_shift = up_all.transpose(1, 0, 2).reshape(1, units).astype(F32)
    qkv_shift = jnp.concatenate([qv_all[0], jnp.zeros_like(qv_all[0]), qv_all[1]])

    qkv_full = lax.all_gather(qkv_weight, "dp", axis=0, tiled=True).reshape(width, 3 * local)
    out_full = lax.all_gather(out_weight, "dp", axis=1, tiled=True)
    up_full = lax.all_gather(up_weight, "dp", axis=0, tiled=True)
    down_blocks = lax.all_gather(down_weight, "dp", axis=0, tiled=False)

    own_pos = t * rows + jnp.arange(rows, dtype=jnp.int32)
    valid_own = (own_pos < length).astype(F32)
    valid = jnp.broadcast_to(valid_own[:, None], (rows, 128))
    positions = jnp.arange(LEN, dtype=jnp.int32)
    bar = jnp.broadcast_to(jnp.where(positions < length, 0.0, NEG)[:, None], (LEN, 128))
    gm_own = (cotangent.astype(F32) * valid_own[:, None]).astype(BF16)

    qkv = (dot(a, qkv_full) + qkv_shift).astype(BF16)
    attended, log_totals = attend(qkv, bar, heads)
    terms = dot(attended, out_full).astype(BF16).reshape(n_t, rows, width)
    c, gm, mid, stats_a = middle(terms, gm_own, tokens, valid, vecs, n_t, 2)
    c, gm = c.reshape(-1, width), gm.reshape(-1, width)
    act, gu, up_sums = hidden(
        c, gm, up_full, down_blocks, jnp.broadcast_to(up_shift, (8, units))
    )

    def rows_dot(left, right):
        return lax.dot_general(
            left, right, (((0,), (0,)), ((), ())), preferred_element_type=F32
        ).astype(BF16)

    down_grad = rows_dot(act, gm)
    up_grad = rows_dot(c, gu)
    back_terms = dot_t(gu, up_full).astype(BF16).reshape(n_t, rows, width)
    mlp = project(act, down_blocks).reshape(n_t, rows, width)
    back_terms, mlp, down_grad, up_grad = lax.optimization_barrier(
        (back_terms, mlp, down_grad, up_grad)
    )
    down_out = lax.psum_scatter(down_grad, "dp", scatter_dimension=1, tiled=True)
    up_out = lax.psum_scatter(up_grad, "dp", scatter_dimension=0, tiled=True)
    gz, gmid, output, stats_b = back_middle(back_terms, mlp, gm_own, mid, valid, vecs, n_t, 3)
    gz, down_out, up_out = lax.optimization_barrier((gz, down_out, up_out))
    gz = gz.reshape(-1, width)
    go = dot_t(gz, out_full).astype(BF16)
    out_grad = rows_dot(attended, gz)
    out_out = lax.psum_scatter(out_grad, "dp", scatter_dimension=1, tiled=True)
    gqkv, head_sums = attend_back(qkv, go, bar, log_totals, heads)
    qkv_grad = rows_dot(a, gqkv).reshape(width, 3, local)
    qkv_out = lax.psum_scatter(qkv_grad, "dp", scatter_dimension=0, tiled=True)
    last_terms = dot_t(gqkv, qkv_full).astype(BF16).reshape(n_t, rows, width)
    tokens_grad, stats_c = finish(last_terms, tokens, gmid, vecs, n_t, 4)

    def vec_sum(stats, i):
        return jnp.sum(stats[8 * i : 8 * i + 8], axis=0)

    vectors = jnp.stack(
        [
            vec_sum(stats_c, 0), vec_sum(stats_c, 1), vec_sum(stats_b, 2),
            vec_sum(stats_b, 0), vec_sum(stats_b, 1), vec_sum(stats_b, 3),
        ]
    )
    squares = jnp.stack(
        [
            jnp.sum(stats_a[0:8]), jnp.sum(stats_a[8:16]), jnp.sum(stats_a[16:24]),
            jnp.sum(stats_b[32:40]), jnp.sum(stats_b[40:48]), jnp.sum(valid_own),
        ]
    )
    vector_blocks = vectors.reshape(6, n_dp, part).transpose(1, 0, 2).reshape(n_dp, 6 * part)
    scalar_blocks = jnp.broadcast_to(squares[None], (n_dp, 6))
    top = jnp.concatenate([vector_blocks, scalar_blocks], axis=1)
    top_len = -(-top.shape[1] // 1024) * 1024
    up_blocks = jnp.sum(up_sums, axis=0).reshape(units // 16, n_dp, 16 // n_dp)
    up_blocks = up_blocks.transpose(1, 0, 2).reshape(n_dp, units // n_dp)
    qv_sums = jnp.stack([head_sums[:, 0], head_sums[:, 8]])
    qv_blocks = qv_sums.reshape(2, heads, n_dp, hd_part).transpose(2, 0, 1, 3)
    qv_blocks = qv_blocks.reshape(n_dp, 2 * heads * hd_part)
    low = jnp.concatenate([up_blocks, qv_blocks], axis=1)
    low_len = -(-low.shape[1] // 1024) * 1024
    blocks = jnp.concatenate([pad_to(top, top_len), pad_to(low, low_len)], axis=1)
    blocks = blocks.reshape(n_dp, (top_len + low_len) // 128, 128)
    reduced = reduce_small(blocks, top_len // 128, n_dp, n_t, 5).reshape(-1)
    outs = [reduced[i * part : (i + 1) * part] for i in range(6)]
    totals = reduced[6 * part : 6 * part + 6]
    stream_rms = jnp.sqrt(totals[:5] / (totals[5] * width))
    at = top_len
    up_bias_out = reduced[at : at + units // n_dp].reshape(up_bias.shape)
    at += units // n_dp
    qv_bias_out = reduced[at : at + 2 * heads * hd_part].reshape(qv_bias.shape)

    return (
        output, tokens_grad, outs[0], outs[1],
        qkv_out.astype(F32), qv_bias_out, out_out.astype(F32), outs[2],
        outs[3], outs[4], up_out.astype(F32), up_bias_out,
        down_out.astype(F32), outs[5], stream_rms,
    )


def solution(mesh):
    vector = P("dp")
    rows = P(("dp", "tensor"), None)
    return jax.shard_map(
        shards,
        mesh=mesh,
        in_specs=(
            rows, vector, vector, vector, P("dp", None, "tensor"), P(None, "tensor", "dp"),
            P("tensor", "dp"), vector, vector, vector, P("dp", "tensor"), P("tensor", "dp"),
            P("tensor", "dp"), vector, rows,
        ),
        out_specs=(
            rows, rows, vector, vector, P("dp", None, "tensor"), P(None, "tensor", "dp"),
            P("tensor", "dp"), vector, vector, vector, P("dp", "tensor"), P("tensor", "dp"),
            P("tensor", "dp"), vector, P(),
        ),
        check_vma=False,
    )
```

```python
import functools

import jax
import jax.numpy as jnp
from jax import lax
from jax.experimental import pallas as pl
from jax.experimental.pallas import tpu as pltpu
from jax.sharding import PartitionSpec as P

HD = 128
LEN = 1024
EPS = 1e-05
MESH = pl.DeviceIdType.MESH
F32 = jnp.float32
BF16 = jnp.bfloat16
VMEM_CAP = 60 * 1024 * 1024
SUBS = 2
WHOLE = pl.BlockSpec(memory_space=pltpu.VMEM)


class Line:
    def __init__(self, size, rows):
        self.size, self.rows, self.t = size, rows, lax.axis_index("tensor")
        self.sub = rows // SUBS

    def barrier(self):
        sem = pltpu.get_barrier_semaphore()
        pl.semaphore_wait(sem, self.greet(sem))

    def greet(self, sem):
        @pl.when(self.t > 0)
        def _():
            pl.semaphore_signal(sem, device_id={"tensor": self.t - 1}, device_id_type=MESH)

        @pl.when(self.t < self.size - 1)
        def _():
            pl.semaphore_signal(sem, device_id={"tensor": self.t + 1}, device_id_type=MESH)

        return jnp.where(self.t > 0, 1, 0) + jnp.where(self.t < self.size - 1, 1, 0)

    def _copy(self, src, dst, sems, way, shard, part):
        send, recv = sems
        target = self.t + 1 if way == 0 else self.t - 1
        return pltpu.make_async_remote_copy(
            src_ref=src,
            dst_ref=dst.at[shard, pl.ds(part * self.sub, self.sub)],
            send_sem=send.at[way, shard, part],
            recv_sem=recv.at[way, shard, part],
            device_id={"tensor": target},
            device_id_type=MESH,
        )

    def _rows(self, ref, shard, part):
        return ref.at[shard, pl.ds(part * self.sub, self.sub)]

    def _edge(self, way):
        return self.t < self.size - 1 if way == 0 else self.t > 0

    def gather_step(self, way, k, part, buf, sems, first):
        t, last = self.t, self.size - 1
        shard = t - k if way == 0 else t + k
        inside = (t >= k) if way == 0 else (t + k <= last)

        @pl.when(inside)
        def _():
            held = self._rows(buf, shard, part)
            if k > 0:
                self._copy(held, buf, sems, way, shard, part).wait_recv()

            @pl.when(self._edge(way))
            def _():
                src = held
                if k == 0 and first is not None:
                    src = first.at[pl.ds(part * self.sub, self.sub)]
                self._copy(src, buf, sems, way, shard, part).start()

    def relay(self, k, part, buf, sems):
        for way in (0, 1):
            shard = self.t - k if way == 0 else self.t + k
            inside = (self.t >= k) if way == 0 else (self.t + k <= self.size - 1)

            @pl.when(inside)
            def _(way=way, shard=shard):
                held = self._rows(buf, shard, part)
                self._copy(held, buf, sems, way, shard, part).wait_recv()

                @pl.when(self._edge(way))
                def _():
                    self._copy(held, buf, sems, way, shard, part).start()

    def walk(self, buf, sems, work):
        last_part = SUBS - 1

        def visit(m, carry):
            k = (m + 1) // 2
            shard = jnp.where(m % 2 == 1, self.t - k, self.t + k)

            @pl.when((shard >= 0) & (shard < self.size))
            def _():
                work(shard)

            @pl.when(m == 0)
            def _():
                for part in range(last_part):
                    self.relay(1, part, buf, sems)

            @pl.when(m % 2 == 0)
            def _():
                self.relay(k + 1, last_part, buf, sems)

            @pl.when(m % 2 == 1)
            def _():
                for part in range(last_part):
                    self.relay(k + 1, part, buf, sems)

            return carry

        lax.fori_loop(0, 2 * self.size - 1, visit, 0)

    def scatter_step(self, way, j, part, terms, buf, sems):
        t, last = self.t, self.size - 1
        shard = last - j if way == 0 else j
        beyond = (shard > t) if way == 0 else (shard < t)
        starts = (t == 0) if way == 0 else (t == last)

        @pl.when(beyond & starts)
        def _():
            self._copy(self._rows(terms, shard, part), buf, sems, way, shard, part).start()

        @pl.when(beyond & jnp.logical_not(starts))
        def _():
            held = self._rows(buf, shard, part)
            self._copy(held, buf, sems, way, shard, part).wait_recv()
            step = min(32, self.sub)

            def add(i, carry):
                rows = pl.ds(part * self.sub + i * step, step)
                total = buf[shard, rows, :].astype(F32) + terms[shard, rows, :].astype(F32)
                buf[shard, rows, :] = total.astype(BF16)
                return carry

            lax.fori_loop(0, self.sub // step, add, 0)
            self._copy(held, buf, sems, way, shard, part).start()

    def phase(self, gather=None, scatter=None, on_slot=None):
        n = self.size
        for k in range(n):
            for part in range(SUBS):
                for way in (0, 1):
                    if gather is not None:
                        self.gather_step(way, k, part, gather[0], gather[1], gather[2])
                    if scatter is not None:
                        if gather is None:
                            if k < n - 1:
                                self.scatter_step(way, k, part, scatter[0], scatter[1][way], scatter[2])
                        else:
                            behind = self.t if way == 0 else n - 1 - self.t
                            for b in range(k):

                                @pl.when(behind == b)
                                def _(b=b, k=k, part=part, way=way):
                                    self.scatter_step(
                                        way, k - 1 - b, part, scatter[0], scatter[1][way], scatter[2]
                                    )
            if on_slot is not None:
                on_slot(k)

    def own_wait(self, bufs, sems):
        for way in (0, 1):
            arrives = self.t > 0 if way == 0 else self.t < self.size - 1

            @pl.when(arrives)
            def _(way=way):
                for part in range(SUBS):
                    held = self._rows(bufs[way], self.t, part)
                    self._copy(held, bufs[way], sems, way, self.t, part).wait_recv()

    def own_sum(self, terms, bufs, rows):
        t = self.t
        zero = jnp.zeros((), F32)
        right = jnp.where(t > 0, bufs[0][t, rows, :].astype(F32), zero)
        left = jnp.where(t < self.size - 1, bufs[1][t, rows, :].astype(F32), zero)
        return terms[t, rows, :].astype(F32) + right + left

    def drain_gather(self, buf, sems):
        for way in (0, 1):
            for k in range(self.size):
                shard = self.t - k if way == 0 else self.t + k
                inside = (self.t >= k) if way == 0 else (self.t + k <= self.size - 1)

                @pl.when(inside & self._edge(way))
                def _(way=way, shard=shard):
                    for part in range(SUBS):
                        held = self._rows(buf, shard, part)
                        self._copy(held, buf, sems, way, shard, part).wait_send()

    def drain_scatter(self, bufs, sems):
        for way in (0, 1):
            for j in range(self.size - 1):
                shard = self.size - 1 - j if way == 0 else j
                beyond = (shard > self.t) if way == 0 else (shard < self.t)

                @pl.when(beyond)
                def _(way=way, shard=shard):
                    for part in range(SUBS):
                        held = self._rows(bufs[way], shard, part)
                        self._copy(held, bufs[way], sems, way, shard, part).wait_send()


def line_sems(size):
    return [pltpu.SemaphoreType.DMA((2, size, SUBS)), pltpu.SemaphoreType.DMA((2, size, SUBS))]


def fold(x):
    rows, width = x.shape
    return jnp.sum(x.reshape(rows // 8, 8, width), axis=0)


def normal(x):
    centre = x - jnp.mean(x, axis=-1, keepdims=True)
    spread = lax.rsqrt(jnp.mean(centre * centre, axis=-1, keepdims=True) + EPS)
    return centre * spread, spread


def normal_back(upstream, normed, spread, gain):
    scaled = upstream * gain
    mean_part = jnp.mean(scaled, axis=-1, keepdims=True)
    across = jnp.mean(scaled * normed, axis=-1, keepdims=True)
    return spread * (scaled - mean_part - normed * across)


def row_loop(rows, step, body):
    def one(i, carry):
        body(pl.ds(pl.multiple_of(i * step, step), step))
        return carry

    lax.fori_loop(0, rows // step, one, 0)


def params(collective_id=None):
    if collective_id is None:
        return pltpu.CompilerParams(vmem_limit_bytes=VMEM_CAP)
    return pltpu.CompilerParams(
        collective_id=collective_id, has_side_effects=True, vmem_limit_bytes=VMEM_CAP
    )


def first_kernel(n_dp, size, part, small, own, smalls, a_out, tok, send, recv, gs, gr):
    line = Line(size, own.shape[0])
    me = lax.axis_index("dp")
    rows, width = own.shape
    sem = pltpu.get_barrier_semaphore()
    for p in range(1, n_dp):
        pl.semaphore_signal(sem, device_id={"dp": lax.rem(me + p, n_dp)}, device_id_type=MESH)
    ends = line.greet(sem)
    pl.semaphore_wait(sem, ends + n_dp - 1)
    sems = (gs, gr)

    def small_copy(p, slot):
        return pltpu.make_async_remote_copy(
            src_ref=small,
            dst_ref=smalls.at[slot],
            send_sem=send.at[p],
            recv_sem=recv.at[slot],
            device_id={"dp": lax.rem(me + p, n_dp)},
            device_id_type=MESH,
        )

    for p in range(1, n_dp):
        small_copy(p, me).start()
    smalls[pl.ds(me, 1)] = small[...][None]
    step = min(32, rows)
    vec_rows = part // 128

    def normalise(source, shard):
        gain = jnp.concatenate(
            [smalls[d, r : r + 1, :] for d in range(n_dp) for r in range(vec_rows)], axis=1
        ).astype(F32)
        shift = jnp.concatenate(
            [smalls[d, r : r + 1, :] for d in range(n_dp) for r in range(vec_rows, 2 * vec_rows)],
            axis=1,
        ).astype(F32)

        def body(at):
            x = source[at, :] if shard is None else source[shard, at, :]
            normed, _ = normal(x.astype(F32))
            to = line.t if shard is None else shard
            a_out[to, at, :] = (normed * gain + shift).astype(BF16)

        row_loop(rows, step, body)

    def on_slot(k):
        if k == 0:
            for p in range(1, n_dp):
                small_copy(p, lax.rem(me + p, n_dp)).wait_recv()
            normalise(own, None)
        else:

            @pl.when(line.t >= k)
            def _():
                normalise(tok, line.t - k)

            @pl.when(line.t + k <= size - 1)
            def _():
                normalise(tok, line.t + k)

    line.phase(gather=(tok, sems, own), on_slot=on_slot)
    line.drain_gather(tok, sems)
    for p in range(1, n_dp):
        small_copy(p, me).wait_send()


def first(small, own, part, n_dp, size, cid):
    rows, width = own.shape
    return pl.pallas_call(
        functools.partial(first_kernel, n_dp, size, part),
        out_shape=(
            jax.ShapeDtypeStruct((n_dp,) + small.shape, small.dtype),
            jax.ShapeDtypeStruct((size, rows, width), BF16),
        ),
        in_specs=[WHOLE, WHOLE],
        out_specs=(WHOLE, WHOLE),
        scratch_shapes=[
            pltpu.VMEM((size, rows, width), BF16),
            pltpu.SemaphoreType.DMA((n_dp,)),
            pltpu.SemaphoreType.DMA((n_dp,)),
        ]
        + line_sems(size),
        compiler_params=params(cid),
        name="first",
    )(small, own)


def middle_kernel(
    size, terms, cot, tok, valid, vecs, c_out, gm_out, mid_out, stats,
    right, left, gs, gr, ss, sr,
):
    line = Line(size, tok.shape[0])
    rows = tok.shape[0]
    step = min(32, rows)
    line.barrier()
    line.phase(gather=(gm_out, (gs, gr), cot), scatter=(terms, (right, left), (ss, sr)))
    gm_out[pl.ds(line.t, 1)] = cot[...][None]
    line.own_wait((right, left), (ss, sr))
    stats[...] = jnp.zeros_like(stats)

    def body(at):
        attn = line.own_sum(terms, (right, left), at) + vecs[2:3, :]
        x = tok[at, :].astype(F32)
        mid = x + attn
        normed, _ = normal(mid)
        c_out[at, :] = (normed * vecs[3:4, :] + vecs[4:5, :]).astype(BF16)
        mid_out[at, :] = mid
        ok = valid[at, 0:1]
        stats[0:8, :] += fold(ok * x * x)
        stats[8:16, :] += fold(ok * attn * attn)
        stats[16:24, :] += fold(ok * mid * mid)

    row_loop(rows, step, body)
    line.drain_gather(gm_out, (gs, gr))
    line.drain_scatter((right, left), (ss, sr))


def middle(terms, cot, tok, valid, vecs, size, cid):
    rows, width = tok.shape
    full = (size, rows, width)
    return pl.pallas_call(
        functools.partial(middle_kernel, size),
        out_shape=(
            jax.ShapeDtypeStruct((rows, width), BF16),
            jax.ShapeDtypeStruct(full, BF16),
            jax.ShapeDtypeStruct((rows, width), F32),
            jax.ShapeDtypeStruct((24, width), F32),
        ),
        in_specs=[WHOLE] * 5,
        out_specs=(WHOLE,) * 4,
        scratch_shapes=[pltpu.VMEM(full, BF16), pltpu.VMEM(full, BF16)]
        + line_sems(size)
        + line_sems(size),
        compiler_params=params(cid),
        name="middle",
    )(terms, cot, tok, valid, vecs)


def back_middle_kernel(
    size, terms, mlp, gm, mid, valid, vecs, out_w, o_t, gz_out, gmid_out, y_out, stats,
    go_out, grad_out, right, left, right2, left2, grad, ss, sr, ms, mr, gs, gr,
):
    line = Line(size, mid.shape[0])
    rows = mid.shape[0]
    step = min(32, rows)
    line.barrier()
    line.phase(scatter=(terms, (right, left), (ss, sr)))
    line.own_wait((right, left), (ss, sr))
    stats[...] = jnp.zeros_like(stats)

    def body(at):
        e = line.own_sum(terms, (right, left), at)
        normed, spread = normal(mid[at, :])
        gy = gm[at, :].astype(F32)
        gmid = gy + normal_back(e, normed, spread, vecs[3:4, :])
        gz_out[line.t, at, :] = gmid.astype(BF16)
        gmid_out[at, :] = gmid
        stats[0:8, :] += fold(e * normed)
        stats[8:16, :] += fold(e)
        stats[16:24, :] += fold(gmid)
        stats[24:32, :] += fold(gy)

    row_loop(rows, step, body)
    width = mid.shape[1]
    block = min(512, width)

    def weigh(shard):
        go_out[shard] = dot_t(gz_out[shard], out_w[...]).astype(BF16)
        here = o_t[:, pl.ds(pl.multiple_of(shard * rows, rows), rows)]

        def column(j, carry):
            at = pl.ds(pl.multiple_of(j * block, block), block)
            grad[:, at] += dot(here, gz_out[shard, :, at])
            return carry

        lax.fori_loop(0, width // block, column, 0)

    def on_slot(k):
        def side(i, carry):
            shard = line.t + k * (2 * i - 1)

            @pl.when((shard >= 0) & (shard < size))
            def _():
                weigh(shard)

            return carry

        lax.fori_loop(0, 1 if k == 0 else 2, side, 0)

    grad[...] = jnp.zeros_like(grad)
    line.phase(
        gather=(gz_out, (gs, gr), None),
        scatter=(mlp, (right2, left2), (ms, mr)),
        on_slot=on_slot,
    )
    grad_out[...] = grad[...].astype(BF16)
    line.own_wait((right2, left2), (ms, mr))

    def tail(at):
        out = line.own_sum(mlp, (right2, left2), at) + vecs[5:6, :]
        y = mid[at, :] + out
        y_out[at, :] = y.astype(BF16)
        ok = valid[at, 0:1]
        stats[32:40, :] += fold(ok * out * out)
        stats[40:48, :] += fold(ok * y * y)

    row_loop(rows, step, tail)
    line.drain_scatter((right, left), (ss, sr))
    line.drain_scatter((right2, left2), (ms, mr))
    line.drain_gather(gz_out, (gs, gr))


def back_middle(terms, mlp, gm, mid, valid, vecs, out_w, o_t, size, cid):
    rows, width = mid.shape
    local = out_w.shape[0]
    full = (size, rows, width)
    return pl.pallas_call(
        functools.partial(back_middle_kernel, size),
        out_shape=(
            jax.ShapeDtypeStruct(full, BF16),
            jax.ShapeDtypeStruct((rows, width), F32),
            jax.ShapeDtypeStruct((rows, width), BF16),
            jax.ShapeDtypeStruct((48, width), F32),
            jax.ShapeDtypeStruct((size, rows, local), BF16),
            jax.ShapeDtypeStruct((local, width), BF16),
        ),
        in_specs=[WHOLE] * 8,
        out_specs=(WHOLE,) * 6,
        scratch_shapes=[pltpu.VMEM(full, BF16)] * 4
        + [pltpu.VMEM((local, width), F32)]
        + line_sems(size)
        + line_sems(size)
        + line_sems(size),
        compiler_params=params(cid),
        name="back_middle",
    )(terms, mlp, gm, mid, valid, vecs, out_w, o_t)


def finish_kernel(size, terms, tok, gmid, vecs, grad_out, stats, right, left, ss, sr):
    line = Line(size, tok.shape[0])
    rows = tok.shape[0]
    step = min(32, rows)
    line.barrier()
    line.phase(scatter=(terms, (right, left), (ss, sr)))
    line.own_wait((right, left), (ss, sr))
    stats[...] = jnp.zeros_like(stats)

    def body(at):
        e = line.own_sum(terms, (right, left), at)
        normed, spread = normal(tok[at, :].astype(F32))
        grad_out[at, :] = gmid[at, :] + normal_back(e, normed, spread, vecs[0:1, :])
        stats[0:8, :] += fold(e * normed)
        stats[8:16, :] += fold(e)

    row_loop(rows, step, body)
    line.drain_scatter((right, left), (ss, sr))


def finish(terms, tok, gmid, vecs, size, cid):
    rows, width = tok.shape
    full = (size, rows, width)
    return pl.pallas_call(
        functools.partial(finish_kernel, size),
        out_shape=(
            jax.ShapeDtypeStruct((rows, width), F32),
            jax.ShapeDtypeStruct((16, width), F32),
        ),
        in_specs=[WHOLE] * 4,
        out_specs=(WHOLE,) * 2,
        scratch_shapes=[pltpu.VMEM(full, BF16)] * 2 + line_sems(size),
        compiler_params=params(cid),
        name="finish",
    )(terms, tok, gmid, vecs)


def reduce_small_kernel(n_dp, n_t, shared, blocks, out, land, sums, land2, s1, r1, s2, r2):
    me, t = lax.axis_index("dp"), lax.axis_index("tensor")
    sem = pltpu.get_barrier_semaphore()
    for p in range(1, n_dp):
        pl.semaphore_signal(sem, device_id={"dp": lax.rem(me + p, n_dp)}, device_id_type=MESH)
    for p in range(1, n_t):
        pl.semaphore_signal(sem, device_id={"tensor": lax.rem(t + p, n_t)}, device_id_type=MESH)
    pl.semaphore_wait(sem, n_dp + n_t - 2)

    def one(p):
        other = lax.rem(me + p, n_dp)
        return pltpu.make_async_remote_copy(
            src_ref=blocks.at[other],
            dst_ref=land.at[p],
            send_sem=s1.at[p],
            recv_sem=r1.at[p],
            device_id={"dp": other},
            device_id_type=MESH,
        )

    for p in range(1, n_dp):
        one(p).start()
    total = blocks[me]
    for p in range(1, n_dp):
        one(p).wait_recv()
        total = total + land[p]
    sums[...] = total

    def two(p):
        return pltpu.make_async_remote_copy(
            src_ref=sums.at[pl.ds(0, shared)],
            dst_ref=land2.at[p],
            send_sem=s2.at[p],
            recv_sem=r2.at[p],
            device_id={"tensor": lax.rem(t + p, n_t)},
            device_id_type=MESH,
        )

    for p in range(1, n_t):
        two(p).start()
    out[...] = total
    top = sums[pl.ds(0, shared), :]
    for p in range(1, n_t):
        two(p).wait_recv()
        top = top + land2[p]
    out[pl.ds(0, shared), :] = top
    for p in range(1, n_dp):
        one(p).wait_send()
    for p in range(1, n_t):
        two(p).wait_send()


def reduce_small(blocks, shared, n_dp, n_t, cid):
    _, rows, width = blocks.shape
    return pl.pallas_call(
        functools.partial(reduce_small_kernel, n_dp, n_t, shared),
        out_shape=jax.ShapeDtypeStruct((rows, width), F32),
        in_specs=[WHOLE],
        out_specs=WHOLE,
        scratch_shapes=[
            pltpu.VMEM((n_dp, rows, width), F32),
            pltpu.VMEM((rows, width), F32),
            pltpu.VMEM((n_t, shared, width), F32),
            pltpu.SemaphoreType.DMA((n_dp,)),
            pltpu.SemaphoreType.DMA((n_dp,)),
            pltpu.SemaphoreType.DMA((n_t,)),
            pltpu.SemaphoreType.DMA((n_t,)),
        ],
        compiler_params=params(cid),
        name="reduce_small",
    )(blocks)


BLOCK = 256
NEG = -1e30
SCALE = HD**-0.5


def dot(a, b):
    return jnp.dot(a, b, preferred_element_type=F32)


def dot_t(a, b):
    return lax.dot_general(a, b, (((1,), (1,)), ((), ())), preferred_element_type=F32)


def masked_scores(q, k, keys, first, bar):
    scores = dot_t(k, q) * SCALE + bar
    key_pos = lax.broadcasted_iota(jnp.int32, (keys, BLOCK), 0)
    query_pos = first + lax.broadcasted_iota(jnp.int32, (keys, BLOCK), 1)
    return jnp.where(key_pos <= query_pos, scores, NEG)


def attend_kernel(q, k, v, bar, out, out_t, log_totals):
    value_cols = v[...].T
    for block in range(LEN // BLOCK):
        first, keys = block * BLOCK, (block + 1) * BLOCK
        scores = masked_scores(
            q[first : first + BLOCK, :], k[0:keys, :], keys, first, bar[0:keys, 0:1]
        )
        top = jnp.max(scores, axis=0, keepdims=True)
        powers = jnp.exp(scores - top)
        total = jnp.sum(powers, axis=0, keepdims=True)
        shares = (powers * (1.0 / total)).astype(BF16)
        mixed = dot(value_cols[:, 0:keys], shares)
        out[first : first + BLOCK, :] = mixed.T.astype(BF16)
        out_t[:, first : first + BLOCK] = mixed.astype(BF16)
        log_totals[0, :, first : first + BLOCK] = jnp.broadcast_to(top + jnp.log(total), (8, BLOCK))


def attend(qkv, bar, heads):
    def column(part):
        return pl.BlockSpec((LEN, HD), lambda h: (0, part * heads + h))

    return pl.pallas_call(
        attend_kernel,
        grid=(heads,),
        out_shape=(
            jax.ShapeDtypeStruct((LEN, heads * HD), BF16),
            jax.ShapeDtypeStruct((heads * HD, LEN), BF16),
            jax.ShapeDtypeStruct((heads, 8, LEN), F32),
        ),
        in_specs=[column(0), column(1), column(2), pl.BlockSpec((LEN, 128), lambda h: (0, 0))],
        out_specs=(
            pl.BlockSpec((LEN, HD), lambda h: (0, h)),
            pl.BlockSpec((HD, LEN), lambda h: (h, 0)),
            pl.BlockSpec((1, 8, LEN), lambda h: (h, 0, 0)),
        ),
        compiler_params=params(),
        name="attend",
    )(qkv, qkv, qkv, bar)


def attend_back_kernel(heads, q, k, v, go, bar, log_totals, out, sums, key_grad, value_grad):
    h = pl.program_id(0)
    key_cols = k[...].T
    query_sum = jnp.zeros((1, HD), F32)
    width = heads * HD
    at_q = pl.ds(pl.multiple_of(h * HD, HD), HD)
    at_k = pl.ds(pl.multiple_of(width + h * HD, HD), HD)
    at_v = pl.ds(pl.multiple_of(2 * width + h * HD, HD), HD)
    for block in range(LEN // BLOCK - 1, -1, -1):
        first, keys = block * BLOCK, (block + 1) * BLOCK
        here = slice(first, first + BLOCK)
        scores = masked_scores(q[here, :], k[0:keys, :], keys, first, bar[0:keys, 0:1])
        shares = jnp.exp(scores - log_totals[0, 0:1, here])
        share_grad = dot_t(v[0:keys, :], go[here, :])
        centre = jnp.sum(shares * share_grad, axis=0, keepdims=True)
        score_grad = (shares * (share_grad - centre)).astype(BF16)
        values = dot(shares.astype(BF16), go[here, :])
        keyed = dot(score_grad, q[here, :])
        if block == LEN // BLOCK - 1:
            value_grad[...] = values
            key_grad[...] = keyed
        else:
            value_grad[0:keys, :] += values
            key_grad[0:keys, :] += keyed
        query_grad = ((dot(key_cols[:, 0:keys], score_grad)) * SCALE).T.astype(BF16)
        out[here, at_q] = query_grad
        query_sum = query_sum + jnp.sum(query_grad.astype(F32), axis=0, keepdims=True)
    out[:, at_k] = (key_grad[...] * SCALE).astype(BF16)
    rounded = value_grad[...].astype(BF16)
    out[:, at_v] = rounded
    value_sum = jnp.sum(rounded.astype(F32), axis=0, keepdims=True)
    sums[0, 0:8, :] = jnp.broadcast_to(query_sum, (8, HD))
    sums[0, 8:16, :] = jnp.broadcast_to(value_sum, (8, HD))


def attend_back(qkv, go, bar, log_totals, heads):
    def column(part):
        return pl.BlockSpec((LEN, HD), lambda h: (0, part * heads + h))

    return pl.pallas_call(
        functools.partial(attend_back_kernel, heads),
        grid=(heads,),
        out_shape=(
            jax.ShapeDtypeStruct((LEN, 3 * heads * HD), BF16),
            jax.ShapeDtypeStruct((heads, 16, HD), F32),
        ),
        in_specs=[
            column(0), column(1), column(2), column(0),
            pl.BlockSpec((LEN, 128), lambda h: (0, 0)),
            pl.BlockSpec((1, 8, LEN), lambda h: (h, 0, 0)),
        ],
        out_specs=(
            pl.BlockSpec((LEN, 3 * heads * HD), lambda h: (0, 0)),
            pl.BlockSpec((1, 16, HD), lambda h: (h, 0, 0)),
        ),
        scratch_shapes=[pltpu.VMEM((LEN, HD), F32), pltpu.VMEM((LEN, HD), F32)],
        compiler_params=params(),
        name="attend_back",
    )(qkv, qkv, qkv, go, bar, log_totals)


def gelu_both(u):
    inner = 0.7978845608028654 * (u + 0.044715 * (u * u * u))
    th = jnp.tanh(inner)
    half = 0.5 * (1.0 + th)
    slope = half + 0.5 * u * (1.0 - th * th) * (
        0.7978845608028654 * (1.0 + 3 * 0.044715 * (u * u))
    )
    return u * half, slope


def hidden_kernel(
    n_dp, size, c_own, gm, up_in, down_in, bias, c_out, act_out, gu_out, mlp_out, back_out, sums,
    up, down, act, gu, mlp, back, gs, gr, in_sem, out_sem,
):
    line = Line(size, c_own.shape[0])
    rows, width = c_own.shape
    units, part = down.shape[1], down.shape[2]
    block = min(512, units)
    loads = [
        pltpu.make_async_copy(up_in, up, in_sem.at[0]),
        pltpu.make_async_copy(down_in, down, in_sem.at[1]),
    ]
    for load in loads:
        load.start()
    line.barrier()
    for piece in range(SUBS):
        for way in (0, 1):
            line.gather_step(way, 0, piece, c_out, (gs, gr), c_own)
    c_out[pl.ds(line.t, 1)] = c_own[...][None]
    sums[...] = jnp.zeros_like(sums)
    for load in loads:
        load.wait()

    def stores(shard):
        pairs = ((act, act_out), (gu, gu_out), (mlp, mlp_out), (back, back_out))
        return [
            pltpu.make_async_copy(src.at[shard], dst.at[shard], out_sem.at[i, shard])
            for i, (src, dst) in enumerate(pairs)
        ]

    def work(shard):
        def unit_block(j, carry):
            at = pl.ds(pl.multiple_of(j * block, block), block)
            u = dot(c_out[shard], up[:, at]) + bias[0:1, at]
            grad = dot_t(gm[shard, :, 0:part], down[0, at, :])
            for d in range(1, n_dp):
                grad = grad + dot_t(gm[shard, :, d * part : (d + 1) * part], down[d, at, :])
            value, slope = gelu_both(u)
            act[shard, :, at] = value.astype(BF16)
            rounded = (grad * slope).astype(BF16)
            gu[shard, :, at] = rounded
            sums[:, at] += fold(rounded.astype(F32))
            return carry

        lax.fori_loop(0, units // block, unit_block, 0)

        def feature_block(d, carry):
            at = pl.ds(pl.multiple_of(d * part, part), part)
            mlp[shard, :, at] = dot(act[shard], down[d]).astype(BF16)
            back[shard, :, at] = dot_t(gu[shard], up[at, :]).astype(BF16)
            return carry

        lax.fori_loop(0, n_dp, feature_block, 0)
        for store in stores(shard):
            store.start()

    line.walk(c_out, (gs, gr), work)
    line.drain_gather(c_out, (gs, gr))
    for shard in range(size):
        for store in stores(shard):
            store.wait()


def hidden(c_own, gm, up, down, bias, size, cid):
    rows, width = c_own.shape
    n_dp, units, part = down.shape
    full, wide = (size, rows, width), (size, rows, units)
    hbm = pl.BlockSpec(memory_space=pltpu.HBM)
    return pl.pallas_call(
        functools.partial(hidden_kernel, n_dp, size),
        out_shape=(
            jax.ShapeDtypeStruct(full, BF16),
            jax.ShapeDtypeStruct(wide, BF16),
            jax.ShapeDtypeStruct(wide, BF16),
            jax.ShapeDtypeStruct(full, BF16),
            jax.ShapeDtypeStruct(full, BF16),
            jax.ShapeDtypeStruct((8, units), F32),
        ),
        in_specs=[WHOLE, WHOLE, hbm, hbm, WHOLE],
        out_specs=(WHOLE, hbm, hbm, hbm, hbm, WHOLE),
        scratch_shapes=[
            pltpu.VMEM((width, units), BF16),
            pltpu.VMEM((n_dp, units, part), BF16),
            pltpu.VMEM(wide, BF16),
            pltpu.VMEM(wide, BF16),
            pltpu.VMEM(full, BF16),
            pltpu.VMEM(full, BF16),
        ]
        + line_sems(size)
        + [pltpu.SemaphoreType.DMA((2,)), pltpu.SemaphoreType.DMA((4, size))],
        compiler_params=params(cid),
        name="hidden",
    )(c_own, gm, up, down, bias)


def pad_to(x, count):
    return jnp.pad(x, ((0, 0), (0, count - x.shape[1])))


def shards(
    tokens, lengths, ln1_gain, ln1_bias, qkv_weight, qv_bias, out_weight, out_bias,
    ln2_gain, ln2_bias, up_weight, up_bias, down_weight, down_bias, cotangent,
):
    n_dp, n_t = lax.axis_size("dp"), lax.axis_size("tensor")
    rows, width = tokens.shape
    part = ln1_gain.shape[0]
    local = qkv_weight.shape[2]
    heads = local // HD
    units = up_weight.shape[1]
    hd_part = qv_bias.shape[2]
    t = lax.axis_index("tensor")
    length = lengths[0]

    pieces = [
        ln1_gain, ln1_bias, out_bias, ln2_gain, ln2_bias, down_bias,
        qv_bias.reshape(-1), up_bias.reshape(-1),
    ]
    packed = jnp.concatenate(pieces)
    count = packed.shape[0]
    lanes = -(-count // 2048) * 2048
    small = jnp.pad(packed, (0, lanes - count)).reshape(lanes // 128, 128)
    smalls, a = first(small, tokens, part, n_dp, n_t, 0)
    smalls, a = smalls.reshape(n_dp, lanes), a.reshape(n_t * rows, width)
    vecs = jnp.stack([smalls[:, i * part : (i + 1) * part].reshape(width) for i in range(6)])
    vecs = jnp.pad(vecs, ((0, 2), (0, 0))).astype(F32)
    at = 6 * part
    qv_all = smalls[:, at : at + 2 * heads * hd_part].reshape(n_dp, 2, heads, hd_part)
    qv_all = qv_all.transpose(1, 2, 0, 3).reshape(2, local).astype(F32)
    at += 2 * heads * hd_part
    up_all = smalls[:, at : at + units // n_dp].reshape(n_dp, units // 16, 16 // n_dp)
    up_shift = up_all.transpose(1, 0, 2).reshape(1, units).astype(F32)
    qkv_shift = jnp.concatenate([qv_all[0], jnp.zeros_like(qv_all[0]), qv_all[1]])

    qkv_full = lax.all_gather(qkv_weight.reshape(part, 3 * local), "dp", axis=0, tiled=True)
    out_full = lax.all_gather(out_weight, "dp", axis=1, tiled=True)
    up_full = lax.all_gather(up_weight, "dp", axis=0, tiled=True)
    down_blocks = lax.all_gather(down_weight, "dp", axis=0, tiled=False)

    own_pos = t * rows + jnp.arange(rows, dtype=jnp.int32)
    valid_own = (own_pos < length).astype(F32)
    valid = jnp.broadcast_to(valid_own[:, None], (rows, 128))
    positions = jnp.arange(LEN, dtype=jnp.int32)
    bar = jnp.broadcast_to(jnp.where(positions < length, 0.0, NEG)[:, None], (LEN, 128))
    gm_own = (cotangent.astype(F32) * valid_own[:, None]).astype(BF16)

    qkv = (dot(a, qkv_full) + qkv_shift).astype(BF16)
    attended, attended_t, log_totals = attend(qkv, bar, heads)
    terms = dot(attended, out_full).astype(BF16).reshape(n_t, rows, width)
    c_own, gm, mid, stats_a = middle(terms, gm_own, tokens, valid, vecs, n_t, 2)
    c, act, gu, mlp, back_terms, up_sums = hidden(
        c_own, gm, up_full, down_blocks, jnp.broadcast_to(up_shift, (8, units)), n_t, 6
    )
    c, gm = c.reshape(-1, width), gm.reshape(-1, width)
    act, gu = act.reshape(-1, units), gu.reshape(-1, units)

    def rows_dot(left, right):
        return lax.dot_general(
            left, right, (((0,), (0,)), ((), ())), preferred_element_type=F32
        ).astype(BF16)

    down_grad = rows_dot(act, gm)
    up_grad = rows_dot(c, gu)
    back_terms, mlp, down_grad, up_grad = lax.optimization_barrier(
        (back_terms, mlp, down_grad, up_grad)
    )
    down_out = lax.psum_scatter(down_grad, "dp", scatter_dimension=1, tiled=True)
    up_out = lax.psum_scatter(up_grad, "dp", scatter_dimension=0, tiled=True)
    _, gmid, output, stats_b, go, out_grad = back_middle(
        back_terms, mlp, gm_own, mid, valid, vecs, out_full, attended_t, n_t, 3
    )
    go, out_grad, down_out, up_out = lax.optimization_barrier((go, out_grad, down_out, up_out))
    out_out = lax.psum_scatter(out_grad, "dp", scatter_dimension=1, tiled=True)
    gqkv, head_sums = attend_back(qkv, go.reshape(-1, local), bar, log_totals, heads)
    qkv_grad = rows_dot(a, gqkv)
    qkv_out = lax.psum_scatter(qkv_grad, "dp", scatter_dimension=0, tiled=True)
    qkv_out = qkv_out.reshape(part, 3, local)
    last_terms = dot_t(gqkv, qkv_full).astype(BF16).reshape(n_t, rows, width)
    tokens_grad, stats_c = finish(last_terms, tokens, gmid, vecs, n_t, 4)

    def vec_sum(stats, i):
        return jnp.sum(stats[8 * i : 8 * i + 8], axis=0)

    vectors = jnp.stack(
        [
            vec_sum(stats_c, 0), vec_sum(stats_c, 1), vec_sum(stats_b, 2),
            vec_sum(stats_b, 0), vec_sum(stats_b, 1), vec_sum(stats_b, 3),
        ]
    )
    squares = jnp.stack(
        [
            jnp.sum(stats_a[0:8]), jnp.sum(stats_a[8:16]), jnp.sum(stats_a[16:24]),
            jnp.sum(stats_b[32:40]), jnp.sum(stats_b[40:48]), jnp.sum(valid_own),
        ]
    )
    vector_blocks = vectors.reshape(6, n_dp, part).transpose(1, 0, 2).reshape(n_dp, 6 * part)
    scalar_blocks = jnp.broadcast_to(squares[None], (n_dp, 6))
    top = jnp.concatenate([vector_blocks, scalar_blocks], axis=1)
    top_len = -(-top.shape[1] // 1024) * 1024
    up_blocks = jnp.sum(up_sums, axis=0).reshape(units // 16, n_dp, 16 // n_dp)
    up_blocks = up_blocks.transpose(1, 0, 2).reshape(n_dp, units // n_dp)
    qv_sums = jnp.stack([head_sums[:, 0], head_sums[:, 8]])
    qv_blocks = qv_sums.reshape(2, heads, n_dp, hd_part).transpose(2, 0, 1, 3)
    qv_blocks = qv_blocks.reshape(n_dp, 2 * heads * hd_part)
    low = jnp.concatenate([up_blocks, qv_blocks], axis=1)
    low_len = -(-low.shape[1] // 1024) * 1024
    blocks = jnp.concatenate([pad_to(top, top_len), pad_to(low, low_len)], axis=1)
    blocks = blocks.reshape(n_dp, (top_len + low_len) // 128, 128)
    reduced = reduce_small(blocks, top_len // 128, n_dp, n_t, 5).reshape(-1)
    outs = [reduced[i * part : (i + 1) * part] for i in range(6)]
    totals = reduced[6 * part : 6 * part + 6]
    stream_rms = jnp.sqrt(totals[:5] / (totals[5] * width))
    at = top_len
    up_bias_out = reduced[at : at + units // n_dp].reshape(up_bias.shape)
    at += units // n_dp
    qv_bias_out = reduced[at : at + 2 * heads * hd_part].reshape(qv_bias.shape)

    return (
        output, tokens_grad, outs[0], outs[1],
        qkv_out.astype(F32), qv_bias_out, out_out.astype(F32), outs[2],
        outs[3], outs[4], up_out.astype(F32), up_bias_out,
        down_out.astype(F32), outs[5], stream_rms,
    )


def solution(mesh):
    vector = P("dp")
    rows = P(("dp", "tensor"), None)
    return jax.shard_map(
        shards,
        mesh=mesh,
        in_specs=(
            rows, vector, vector, vector, P("dp", None, "tensor"), P(None, "tensor", "dp"),
            P("tensor", "dp"), vector, vector, vector, P("dp", "tensor"), P("tensor", "dp"),
            P("tensor", "dp"), vector, rows,
        ),
        out_specs=(
            rows, rows, vector, vector, P("dp", None, "tensor"), P(None, "tensor", "dp"),
            P("tensor", "dp"), vector, vector, vector, P("dp", "tensor"), P("tensor", "dp"),
            P("tensor", "dp"), vector, P(),
        ),
        check_vma=False,
    )
```

```python
import functools

import jax
import jax.numpy as jnp
from jax import lax
from jax.experimental import pallas as pl
from jax.experimental.pallas import tpu as pltpu
from jax.sharding import PartitionSpec as P

HD = 128
LEN = 1024
EPS = 1e-05
MESH = pl.DeviceIdType.MESH
F32 = jnp.float32
BF16 = jnp.bfloat16
VMEM_CAP = 60 * 1024 * 1024
SUBS = 2
WHOLE = pl.BlockSpec(memory_space=pltpu.VMEM)
HBM = pl.BlockSpec(memory_space=pltpu.HBM)


class Line:
    def __init__(self, size, rows):
        self.size, self.rows, self.t = size, rows, lax.axis_index("tensor")
        self.sub = rows // SUBS

    def barrier(self):
        sem = pltpu.get_barrier_semaphore()
        pl.semaphore_wait(sem, self.greet(sem))

    def greet(self, sem):
        @pl.when(self.t > 0)
        def _():
            pl.semaphore_signal(sem, device_id={"tensor": self.t - 1}, device_id_type=MESH)

        @pl.when(self.t < self.size - 1)
        def _():
            pl.semaphore_signal(sem, device_id={"tensor": self.t + 1}, device_id_type=MESH)

        return jnp.where(self.t > 0, 1, 0) + jnp.where(self.t < self.size - 1, 1, 0)

    def _copy(self, src, dst, sems, way, shard, part):
        send, recv = sems
        target = self.t + 1 if way == 0 else self.t - 1
        return pltpu.make_async_remote_copy(
            src_ref=src,
            dst_ref=dst.at[shard, pl.ds(part * self.sub, self.sub)],
            send_sem=send.at[way, shard, part],
            recv_sem=recv.at[way, shard, part],
            device_id={"tensor": target},
            device_id_type=MESH,
        )

    def _rows(self, ref, shard, part):
        return ref.at[shard, pl.ds(part * self.sub, self.sub)]

    def _edge(self, way):
        return self.t < self.size - 1 if way == 0 else self.t > 0

    def hop(self, way, src, dst, sems):
        return pltpu.make_async_remote_copy(
            src_ref=src,
            dst_ref=dst.at[way],
            send_sem=sems[0].at[way],
            recv_sem=sems[1].at[way],
            device_id={"tensor": self.t + 1 if way == 0 else self.t - 1},
            device_id_type=MESH,
        )

    def hop_start(self, srcs, dst, sems):
        for way in (0, 1):

            @pl.when(self._edge(way))
            def _(way=way):
                self.hop(way, srcs[way], dst, sems).start()

    def hop_wait(self, srcs, dst, sems):
        for way in (0, 1):

            @pl.when(self._edge(1 - way))
            def _(way=way):
                self.hop(way, srcs[way], dst, sems).wait_recv()

        for way in (0, 1):

            @pl.when(self._edge(way))
            def _(way=way):
                self.hop(way, srcs[way], dst, sems).wait_send()

    def gather_step(self, way, k, part, buf, sems, first, near=None):
        t, last = self.t, self.size - 1
        shard = t - k if way == 0 else t + k
        inside = (t >= k) if way == 0 else (t + k <= last)

        @pl.when(inside)
        def _():
            held = self._rows(buf, shard, part)
            if k > 1 or (k == 1 and near is None):
                self._copy(held, buf, sems, way, shard, part).wait_recv()

            @pl.when(self._edge(way))
            def _():
                src = held
                if k == 0 and first is not None:
                    src = first.at[pl.ds(part * self.sub, self.sub)]
                if k == 1 and near is not None:
                    src = near.at[way, pl.ds(part * self.sub, self.sub)]
                self._copy(src, buf, sems, way, shard, part).start()

    def relay(self, k, part, buf, sems):
        for way in (0, 1):
            shard = self.t - k if way == 0 else self.t + k
            inside = (self.t >= k) if way == 0 else (self.t + k <= self.size - 1)

            @pl.when(inside)
            def _(way=way, shard=shard):
                held = self._rows(buf, shard, part)
                self._copy(held, buf, sems, way, shard, part).wait_recv()

                @pl.when(self._edge(way))
                def _():
                    self._copy(held, buf, sems, way, shard, part).start()

    def walk(self, buf, sems, work):
        last_part = SUBS - 1

        def visit(m, carry):
            k = (m + 1) // 2
            shard = jnp.where(m % 2 == 1, self.t - k, self.t + k)

            @pl.when((shard >= 0) & (shard < self.size))
            def _():
                work(shard)

            @pl.when(m == 0)
            def _():
                for part in range(last_part):
                    self.relay(1, part, buf, sems)

            @pl.when(m % 2 == 0)
            def _():
                self.relay(k + 1, last_part, buf, sems)

            @pl.when(m % 2 == 1)
            def _():
                for part in range(last_part):
                    self.relay(k + 1, part, buf, sems)

            return carry

        lax.fori_loop(0, 2 * self.size - 1, visit, 0)

    def scatter_step(self, way, j, part, terms, buf, sems, ends=None):
        t, last = self.t, self.size - 1
        shard = last - j if way == 0 else j
        beyond = (shard > t) if way == 0 else (shard < t)
        starts = (t == 0) if way == 0 else (t == last)
        step = min(32, self.sub)
        if ends is None:
            goes, stays = beyond, None
        else:
            goes = (shard > t + 1) if way == 0 else (shard < t - 1)
            stays = (shard == t + 1) if way == 0 else (shard == t - 1)

        @pl.when(goes & starts)
        def _():
            self._copy(self._rows(terms, shard, part), buf, sems, way, shard, part).start()

        @pl.when(goes & jnp.logical_not(starts))
        def _():
            held = self._rows(buf, shard, part)
            self._copy(held, buf, sems, way, shard, part).wait_recv()

            def add(i, carry):
                rows = pl.ds(part * self.sub + i * step, step)
                total = buf[shard, rows, :].astype(F32) + terms[shard, rows, :].astype(F32)
                buf[shard, rows, :] = total.astype(BF16)
                return carry

            lax.fori_loop(0, self.sub // step, add, 0)
            self._copy(held, buf, sems, way, shard, part).start()

        if stays is None:
            return

        @pl.when(stays & starts)
        def _():
            rows = pl.ds(part * self.sub, self.sub)
            ends[way, rows, :] = terms[shard, rows, :]

        @pl.when(stays & jnp.logical_not(starts))
        def _():
            held = self._rows(buf, shard, part)
            self._copy(held, buf, sems, way, shard, part).wait_recv()

            def add(i, carry):
                rows = pl.ds(part * self.sub + i * step, step)
                total = buf[shard, rows, :].astype(F32) + terms[shard, rows, :].astype(F32)
                ends[way, rows, :] = total.astype(BF16)
                return carry

            lax.fori_loop(0, self.sub // step, add, 0)

    def phase(self, gather=None, scatter=None, on_slot=None, near=None, ends=None):
        n = self.size
        for k in range(0 if near is None else 1, n):
            for part in range(SUBS):
                for way in (0, 1):
                    if gather is not None:
                        self.gather_step(way, k, part, gather[0], gather[1], gather[2], near)
                    if scatter is not None:
                        if gather is None:
                            if k < n - 1:
                                self.scatter_step(way, k, part, scatter[0], scatter[1][way], scatter[2])
                        else:
                            behind = self.t if way == 0 else n - 1 - self.t
                            for b in range(k):

                                @pl.when(behind == b)
                                def _(b=b, k=k, part=part, way=way):
                                    self.scatter_step(
                                        way, k - 1 - b, part, scatter[0], scatter[1][way],
                                        scatter[2], ends,
                                    )
            if on_slot is not None:
                on_slot(k)

    def own_wait(self, bufs, sems):
        for way in (0, 1):
            arrives = self.t > 0 if way == 0 else self.t < self.size - 1

            @pl.when(arrives)
            def _(way=way):
                for part in range(SUBS):
                    held = self._rows(bufs[way], self.t, part)
                    self._copy(held, bufs[way], sems, way, self.t, part).wait_recv()

    def own_sum(self, terms, bufs, rows):
        t = self.t
        zero = jnp.zeros((), F32)
        right = jnp.where(t > 0, bufs[0][t, rows, :].astype(F32), zero)
        left = jnp.where(t < self.size - 1, bufs[1][t, rows, :].astype(F32), zero)
        return terms[t, rows, :].astype(F32) + right + left

    def drain_gather(self, buf, sems, first=0):
        for way in (0, 1):
            for k in range(first, self.size):
                shard = self.t - k if way == 0 else self.t + k
                inside = (self.t >= k) if way == 0 else (self.t + k <= self.size - 1)

                @pl.when(inside & self._edge(way))
                def _(way=way, shard=shard):
                    for part in range(SUBS):
                        held = self._rows(buf, shard, part)
                        self._copy(held, buf, sems, way, shard, part).wait_send()

    def drain_scatter(self, bufs, sems, margin=0):
        for way in (0, 1):
            for j in range(self.size - 1):
                shard = self.size - 1 - j if way == 0 else j
                beyond = (shard > self.t + margin) if way == 0 else (shard < self.t - margin)

                @pl.when(beyond)
                def _(way=way, shard=shard):
                    for part in range(SUBS):
                        held = self._rows(bufs[way], shard, part)
                        self._copy(held, bufs[way], sems, way, shard, part).wait_send()


def line_sems(size):
    return [pltpu.SemaphoreType.DMA((2, size, SUBS)), pltpu.SemaphoreType.DMA((2, size, SUBS))]


def fold(x):
    rows, width = x.shape
    return jnp.sum(x.reshape(rows // 8, 8, width), axis=0)


def normal(x):
    centre = x - jnp.mean(x, axis=-1, keepdims=True)
    spread = lax.rsqrt(jnp.mean(centre * centre, axis=-1, keepdims=True) + EPS)
    return centre * spread, spread


def normal_back(upstream, normed, spread, gain):
    scaled = upstream * gain
    mean_part = jnp.mean(scaled, axis=-1, keepdims=True)
    across = jnp.mean(scaled * normed, axis=-1, keepdims=True)
    return spread * (scaled - mean_part - normed * across)


def row_loop(rows, step, body):
    def one(i, carry):
        body(pl.ds(pl.multiple_of(i * step, step), step))
        return carry

    lax.fori_loop(0, rows // step, one, 0)


def params(collective_id=None):
    if collective_id is None:
        return pltpu.CompilerParams(vmem_limit_bytes=VMEM_CAP)
    return pltpu.CompilerParams(
        collective_id=collective_id, has_side_effects=True, vmem_limit_bytes=VMEM_CAP
    )


def first_kernel(n_dp, size, part, small, own, smalls, a_out, tok, send, recv, gs, gr):
    line = Line(size, own.shape[0])
    me = lax.axis_index("dp")
    rows, width = own.shape
    sem = pltpu.get_barrier_semaphore()
    for p in range(1, n_dp):
        pl.semaphore_signal(sem, device_id={"dp": lax.rem(me + p, n_dp)}, device_id_type=MESH)
    ends = line.greet(sem)
    pl.semaphore_wait(sem, ends + n_dp - 1)
    sems = (gs, gr)

    def small_copy(p, slot):
        return pltpu.make_async_remote_copy(
            src_ref=small,
            dst_ref=smalls.at[slot],
            send_sem=send.at[p],
            recv_sem=recv.at[slot],
            device_id={"dp": lax.rem(me + p, n_dp)},
            device_id_type=MESH,
        )

    for p in range(1, n_dp):
        small_copy(p, me).start()
    smalls[pl.ds(me, 1)] = small[...][None]
    step = min(32, rows)
    vec_rows = part // 128

    def normalise(source, shard):
        gain = jnp.concatenate(
            [smalls[d, r : r + 1, :] for d in range(n_dp) for r in range(vec_rows)], axis=1
        ).astype(F32)
        shift = jnp.concatenate(
            [smalls[d, r : r + 1, :] for d in range(n_dp) for r in range(vec_rows, 2 * vec_rows)],
            axis=1,
        ).astype(F32)

        def body(at):
            x = source[at, :] if shard is None else source[shard, at, :]
            normed, _ = normal(x.astype(F32))
            to = line.t if shard is None else shard
            a_out[to, at, :] = (normed * gain + shift).astype(BF16)

        row_loop(rows, step, body)

    def on_slot(k):
        if k == 0:
            for p in range(1, n_dp):
                small_copy(p, lax.rem(me + p, n_dp)).wait_recv()
            normalise(own, None)
        else:

            @pl.when(line.t >= k)
            def _():
                normalise(tok, line.t - k)

            @pl.when(line.t + k <= size - 1)
            def _():
                normalise(tok, line.t + k)

    line.phase(gather=(tok, sems, own), on_slot=on_slot)
    line.drain_gather(tok, sems)
    for p in range(1, n_dp):
        small_copy(p, me).wait_send()


def first(small, own, part, n_dp, size, cid):
    rows, width = own.shape
    return pl.pallas_call(
        functools.partial(first_kernel, n_dp, size, part),
        out_shape=(
            jax.ShapeDtypeStruct((n_dp,) + small.shape, small.dtype),
            jax.ShapeDtypeStruct((size, rows, width), BF16),
        ),
        in_specs=[WHOLE, WHOLE],
        out_specs=(WHOLE, WHOLE),
        scratch_shapes=[
            pltpu.VMEM((size, rows, width), BF16),
            pltpu.SemaphoreType.DMA((n_dp,)),
            pltpu.SemaphoreType.DMA((n_dp,)),
        ]
        + line_sems(size),
        compiler_params=params(cid),
        name="first",
    )(small, own)


def middle_kernel(
    size, terms, cot, near, tok, valid, vecs, c_out, gm_out, mid_out, stats,
    right, left, gs, gr, ss, sr, near_sem,
):
    line = Line(size, tok.shape[0])
    rows = tok.shape[0]
    step = min(32, rows)
    line.barrier()

    def keep(way):
        shard = line.t - 1 if way == 0 else line.t + 1
        return pltpu.make_async_copy(near.at[way], gm_out.at[shard], near_sem.at[way])

    def keep_all(act):
        for way in (0, 1):

            @pl.when(line._edge(1 - way))
            def _(way=way):
                act(keep(way))

    keep_all(lambda copy: copy.start())
    line.phase(
        gather=(gm_out, (gs, gr), None), scatter=(terms, (right, left), (ss, sr)), near=near
    )
    gm_out[pl.ds(line.t, 1)] = cot[...][None]
    keep_all(lambda copy: copy.wait())
    line.own_wait((right, left), (ss, sr))
    stats[...] = jnp.zeros_like(stats)

    def body(at):
        attn = line.own_sum(terms, (right, left), at) + vecs[2:3, :]
        x = tok[at, :].astype(F32)
        mid = x + attn
        normed, _ = normal(mid)
        c_out[at, :] = (normed * vecs[3:4, :] + vecs[4:5, :]).astype(BF16)
        mid_out[at, :] = mid
        ok = valid[at, 0:1]
        stats[0:8, :] += fold(ok * x * x)
        stats[8:16, :] += fold(ok * attn * attn)
        stats[16:24, :] += fold(ok * mid * mid)

    row_loop(rows, step, body)
    line.drain_gather(gm_out, (gs, gr), 1)
    line.drain_scatter((right, left), (ss, sr))


def middle(terms, cot, near, tok, valid, vecs, size, cid):
    rows, width = tok.shape
    full = (size, rows, width)
    return pl.pallas_call(
        functools.partial(middle_kernel, size),
        out_shape=(
            jax.ShapeDtypeStruct((rows, width), BF16),
            jax.ShapeDtypeStruct(full, BF16),
            jax.ShapeDtypeStruct((rows, width), F32),
            jax.ShapeDtypeStruct((24, width), F32),
        ),
        in_specs=[WHOLE, WHOLE, HBM, WHOLE, WHOLE, WHOLE],
        out_specs=(WHOLE,) * 4,
        scratch_shapes=[pltpu.VMEM(full, BF16), pltpu.VMEM(full, BF16)]
        + line_sems(size)
        + line_sems(size)
        + [pltpu.SemaphoreType.DMA((2,))],
        compiler_params=params(cid),
        name="middle",
    )(terms, cot, near, tok, valid, vecs)


def back_middle_kernel(
    size, terms, mlp, gm, mid, vecs, out_w, o_t, gz_out, gmid_out, ends, stats,
    go_out, grad_out, right, left, right2, left2, grad, ss, sr, ms, mr, gs, gr,
):
    line = Line(size, mid.shape[0])
    rows = mid.shape[0]
    step = min(32, rows)
    line.barrier()
    line.phase(scatter=(terms, (right, left), (ss, sr)))
    line.own_wait((right, left), (ss, sr))
    stats[...] = jnp.zeros_like(stats)

    def body(at):
        e = line.own_sum(terms, (right, left), at)
        normed, spread = normal(mid[at, :])
        gy = gm[at, :].astype(F32)
        gmid = gy + normal_back(e, normed, spread, vecs[3:4, :])
        gz_out[line.t, at, :] = gmid.astype(BF16)
        gmid_out[at, :] = gmid
        stats[0:8, :] += fold(e * normed)
        stats[8:16, :] += fold(e)
        stats[16:24, :] += fold(gmid)
        stats[24:32, :] += fold(gy)

    row_loop(rows, step, body)
    width = mid.shape[1]
    block = min(512, width)

    def weigh(shard):
        go_out[shard] = dot_t(gz_out[shard], out_w[...]).astype(BF16)
        here = o_t[:, pl.ds(pl.multiple_of(shard * rows, rows), rows)]

        def column(j, carry):
            at = pl.ds(pl.multiple_of(j * block, block), block)
            grad[:, at] += dot(here, gz_out[shard, :, at])
            return carry

        lax.fori_loop(0, width // block, column, 0)

    def on_slot(k):
        def side(i, carry):
            shard = line.t + k * (2 * i - 1)

            @pl.when((shard >= 0) & (shard < size))
            def _():
                weigh(shard)

            return carry

        lax.fori_loop(0, 1 if k == 0 else 2, side, 0)

    grad[...] = jnp.zeros_like(grad)
    line.phase(
        gather=(gz_out, (gs, gr), None),
        scatter=(mlp, (right2, left2), (ms, mr)),
        on_slot=on_slot,
        ends=ends,
    )
    grad_out[...] = grad[...].astype(BF16)
    line.drain_scatter((right, left), (ss, sr))
    line.drain_scatter((right2, left2), (ms, mr), 1)
    line.drain_gather(gz_out, (gs, gr))


def back_middle(terms, mlp, gm, mid, vecs, out_w, o_t, size, cid):
    rows, width = mid.shape
    local = out_w.shape[0]
    full = (size, rows, width)
    return pl.pallas_call(
        functools.partial(back_middle_kernel, size),
        out_shape=(
            jax.ShapeDtypeStruct(full, BF16),
            jax.ShapeDtypeStruct((rows, width), F32),
            jax.ShapeDtypeStruct((2, rows, width), BF16),
            jax.ShapeDtypeStruct((32, width), F32),
            jax.ShapeDtypeStruct((size, rows, local), BF16),
            jax.ShapeDtypeStruct((local, width), BF16),
        ),
        in_specs=[WHOLE] * 7,
        out_specs=(WHOLE,) * 6,
        scratch_shapes=[pltpu.VMEM(full, BF16)] * 4
        + [pltpu.VMEM((local, width), F32)]
        + line_sems(size)
        + line_sems(size)
        + line_sems(size),
        compiler_params=params(cid),
        name="back_middle",
    )(terms, mlp, gm, mid, vecs, out_w, o_t)


def finish_kernel(
    size, terms, tok, gmid, mlp, landed, mid, valid, vecs, grad_out, y_out, stats,
    right, left, own_mlp, ends, ss, sr, load_sem,
):
    line = Line(size, tok.shape[0])
    rows = tok.shape[0]
    step = min(32, rows)
    loads = [
        pltpu.make_async_copy(mlp.at[line.t], own_mlp, load_sem.at[0]),
        pltpu.make_async_copy(landed, ends, load_sem.at[1]),
    ]
    for load in loads:
        load.start()
    line.barrier()
    stats[...] = jnp.zeros_like(stats)

    def tail(at):
        zero = jnp.zeros((), F32)
        from_left = jnp.where(line.t > 0, ends[0, at, :].astype(F32), zero)
        from_right = jnp.where(line.t < size - 1, ends[1, at, :].astype(F32), zero)
        out = own_mlp[at, :].astype(F32) + from_left + from_right + vecs[5:6, :]
        y = mid[at, :] + out
        y_out[at, :] = y.astype(BF16)
        ok = valid[at, 0:1]
        stats[16:24, :] += fold(ok * out * out)
        stats[24:32, :] += fold(ok * y * y)

    for j in range(size - 1):
        for piece in range(SUBS):
            for way in (0, 1):
                line.scatter_step(way, j, piece, terms, (right, left)[way], (ss, sr))
        if j == 0:
            for load in loads:
                load.wait()
            row_loop(rows, step, tail)
    line.own_wait((right, left), (ss, sr))

    def body(at):
        e = line.own_sum(terms, (right, left), at)
        normed, spread = normal(tok[at, :].astype(F32))
        grad_out[at, :] = gmid[at, :] + normal_back(e, normed, spread, vecs[0:1, :])
        stats[0:8, :] += fold(e * normed)
        stats[8:16, :] += fold(e)

    row_loop(rows, step, body)
    line.drain_scatter((right, left), (ss, sr))


def finish(terms, tok, gmid, mlp, landed, mid, valid, vecs, size, cid):
    rows, width = tok.shape
    full = (size, rows, width)
    return pl.pallas_call(
        functools.partial(finish_kernel, size),
        out_shape=(
            jax.ShapeDtypeStruct((rows, width), F32),
            jax.ShapeDtypeStruct((rows, width), BF16),
            jax.ShapeDtypeStruct((32, width), F32),
        ),
        in_specs=[WHOLE, WHOLE, WHOLE, HBM, HBM, WHOLE, WHOLE, WHOLE],
        out_specs=(WHOLE,) * 3,
        scratch_shapes=[pltpu.VMEM(full, BF16)] * 2
        + [pltpu.VMEM((rows, width), BF16), pltpu.VMEM((2, rows, width), BF16)]
        + line_sems(size)
        + [pltpu.SemaphoreType.DMA((2,))],
        compiler_params=params(cid),
        name="finish",
    )(terms, tok, gmid, mlp, landed, mid, valid, vecs)


def reduce_small_kernel(n_dp, n_t, shared, blocks, out, land, sums, land2, s1, r1, s2, r2):
    me, t = lax.axis_index("dp"), lax.axis_index("tensor")
    sem = pltpu.get_barrier_semaphore()
    for p in range(1, n_dp):
        pl.semaphore_signal(sem, device_id={"dp": lax.rem(me + p, n_dp)}, device_id_type=MESH)
    for p in range(1, n_t):
        pl.semaphore_signal(sem, device_id={"tensor": lax.rem(t + p, n_t)}, device_id_type=MESH)
    pl.semaphore_wait(sem, n_dp + n_t - 2)

    def one(p):
        other = lax.rem(me + p, n_dp)
        return pltpu.make_async_remote_copy(
            src_ref=blocks.at[other],
            dst_ref=land.at[p],
            send_sem=s1.at[p],
            recv_sem=r1.at[p],
            device_id={"dp": other},
            device_id_type=MESH,
        )

    for p in range(1, n_dp):
        one(p).start()
    total = blocks[me]
    for p in range(1, n_dp):
        one(p).wait_recv()
        total = total + land[p]
    sums[...] = total

    def two(p):
        return pltpu.make_async_remote_copy(
            src_ref=sums.at[pl.ds(0, shared)],
            dst_ref=land2.at[p],
            send_sem=s2.at[p],
            recv_sem=r2.at[p],
            device_id={"tensor": lax.rem(t + p, n_t)},
            device_id_type=MESH,
        )

    for p in range(1, n_t):
        two(p).start()
    out[...] = total
    top = sums[pl.ds(0, shared), :]
    for p in range(1, n_t):
        two(p).wait_recv()
        top = top + land2[p]
    out[pl.ds(0, shared), :] = top
    for p in range(1, n_dp):
        one(p).wait_send()
    for p in range(1, n_t):
        two(p).wait_send()


def reduce_small(blocks, shared, n_dp, n_t, cid):
    _, rows, width = blocks.shape
    return pl.pallas_call(
        functools.partial(reduce_small_kernel, n_dp, n_t, shared),
        out_shape=jax.ShapeDtypeStruct((rows, width), F32),
        in_specs=[WHOLE],
        out_specs=WHOLE,
        scratch_shapes=[
            pltpu.VMEM((n_dp, rows, width), F32),
            pltpu.VMEM((rows, width), F32),
            pltpu.VMEM((n_t, shared, width), F32),
            pltpu.SemaphoreType.DMA((n_dp,)),
            pltpu.SemaphoreType.DMA((n_dp,)),
            pltpu.SemaphoreType.DMA((n_t,)),
            pltpu.SemaphoreType.DMA((n_t,)),
        ],
        compiler_params=params(cid),
        name="reduce_small",
    )(blocks)


BLOCK = 256
NEG = -1e30
SCALE = HD**-0.5


def dot(a, b):
    return jnp.dot(a, b, preferred_element_type=F32)


def dot_t(a, b):
    return lax.dot_general(a, b, (((1,), (1,)), ((), ())), preferred_element_type=F32)


def masked_scores(q, k, keys, first, bar):
    scores = dot_t(k, q) * SCALE + bar
    key_pos = lax.broadcasted_iota(jnp.int32, (keys, BLOCK), 0)
    query_pos = first + lax.broadcasted_iota(jnp.int32, (keys, BLOCK), 1)
    return jnp.where(key_pos <= query_pos, scores, NEG)


def head_cols(part, h, heads):
    return pl.ds(pl.multiple_of((part * heads + h) * HD, HD), HD)


def front_kernel(
    size, heads, a, weights, shift, bar, out_w, cot, qkv, out_t, log_totals, terms, near,
    cols, mixed_all, gs, gr, load_sem,
):
    h = pl.program_id(0)
    rows = cot.shape[0]
    local = heads * HD
    line = Line(size, rows)

    def load(part):
        at = pl.ds(part * local, local)
        return pltpu.make_async_copy(weights.at[:, at], cols.at[:, at], load_sem.at[part])

    @pl.when(h == 0)
    def _():
        for part in range(3):
            load(part).start()
        line.barrier()
        line.hop_start((cot, cot), near, (gs, gr))
        for part in range(3):
            load(part).wait()
            span = slice(part * local, (part + 1) * local)

            def product(at, span=span):
                qkv[at, span] = (dot(a[at, :], cols[:, span]) + shift[0:1, span]).astype(BF16)

            row_loop(LEN, min(256, LEN), product)

    at_q, at_k, at_v = (head_cols(part, h, heads) for part in range(3))
    value_cols = qkv[:, at_v].T
    for block in range(LEN // BLOCK):
        first, keys = block * BLOCK, (block + 1) * BLOCK
        here = slice(first, first + BLOCK)
        scores = masked_scores(qkv[here, at_q], qkv[0:keys, at_k], keys, first, bar[0:keys, 0:1])
        top = jnp.max(scores, axis=0, keepdims=True)
        powers = jnp.exp(scores - top)
        total = jnp.sum(powers, axis=0, keepdims=True)
        shares = (powers * (1.0 / total)).astype(BF16)
        mixed = dot(value_cols[:, 0:keys], shares)
        mixed_all[here, head_cols(0, h, heads)] = mixed.T.astype(BF16)
        out_t[:, here] = mixed.astype(BF16)
        log_totals[0, :, here] = jnp.broadcast_to(top + jnp.log(total), (8, BLOCK))

    @pl.when(h == heads - 1)
    def _():
        def project(at):
            terms[at, :] = dot(mixed_all[at, :], out_w[...]).astype(BF16)

        row_loop(LEN, min(256, LEN), project)
        line.hop_wait((cot, cot), near, (gs, gr))


def front(a, weights, shift, bar, out_w, cot, size, cid):
    width, local3 = weights.shape
    local = local3 // 3
    heads = local // HD
    return pl.pallas_call(
        functools.partial(front_kernel, size, heads),
        grid=(heads,),
        out_shape=(
            jax.ShapeDtypeStruct((LEN, local3), BF16),
            jax.ShapeDtypeStruct((local, LEN), BF16),
            jax.ShapeDtypeStruct((heads, 8, LEN), F32),
            jax.ShapeDtypeStruct((LEN, width), BF16),
            jax.ShapeDtypeStruct((2,) + cot.shape, BF16),
        ),
        in_specs=[WHOLE, HBM, WHOLE, WHOLE, WHOLE, HBM],
        out_specs=(
            pl.BlockSpec((LEN, local3), lambda h: (0, 0)),
            pl.BlockSpec((HD, LEN), lambda h: (h, 0)),
            pl.BlockSpec((1, 8, LEN), lambda h: (h, 0, 0)),
            pl.BlockSpec((LEN, width), lambda h: (0, 0)),
            HBM,
        ),
        scratch_shapes=[
            pltpu.VMEM((width, local3), BF16),
            pltpu.VMEM((LEN, local), BF16),
            pltpu.SemaphoreType.DMA((2,)),
            pltpu.SemaphoreType.DMA((2,)),
            pltpu.SemaphoreType.DMA((3,)),
        ],
        compiler_params=params(cid),
        name="front",
    )(a, weights, shift, bar, out_w, cot)


def attend_back_kernel(
    size, heads, q, k, v, go, bar, log_totals, weights, ends, out, sums, terms, landed,
    key_grad, value_grad, cols, gs, gr, load_sem,
):
    h = pl.program_id(0)
    line = Line(size, ends.shape[1])
    srcs = (ends.at[0], ends.at[1])
    load = pltpu.make_async_copy(weights, cols, load_sem.at[0])

    @pl.when(h == 0)
    def _():
        load.start()
        line.barrier()
        line.hop_start(srcs, landed, (gs, gr))

    key_cols = k[...].T
    query_sum = jnp.zeros((1, HD), F32)
    at_q, at_k, at_v = (head_cols(part, h, heads) for part in range(3))
    for block in range(LEN // BLOCK - 1, -1, -1):
        first, keys = block * BLOCK, (block + 1) * BLOCK
        here = slice(first, first + BLOCK)
        scores = masked_scores(q[here, :], k[0:keys, :], keys, first, bar[0:keys, 0:1])
        shares = jnp.exp(scores - log_totals[0, 0:1, here])
        share_grad = dot_t(v[0:keys, :], go[here, :])
        centre = jnp.sum(shares * share_grad, axis=0, keepdims=True)
        score_grad = (shares * (share_grad - centre)).astype(BF16)
        values = dot(shares.astype(BF16), go[here, :])
        keyed = dot(score_grad, q[here, :])
        if block == LEN // BLOCK - 1:
            value_grad[...] = values
            key_grad[...] = keyed
        else:
            value_grad[0:keys, :] += values
            key_grad[0:keys, :] += keyed
        query_grad = ((dot(key_cols[:, 0:keys], score_grad)) * SCALE).T.astype(BF16)
        out[here, at_q] = query_grad
        query_sum = query_sum + jnp.sum(query_grad.astype(F32), axis=0, keepdims=True)
    out[:, at_k] = (key_grad[...] * SCALE).astype(BF16)
    rounded = value_grad[...].astype(BF16)
    out[:, at_v] = rounded
    value_sum = jnp.sum(rounded.astype(F32), axis=0, keepdims=True)
    sums[0, 0:8, :] = jnp.broadcast_to(query_sum, (8, HD))
    sums[0, 8:16, :] = jnp.broadcast_to(value_sum, (8, HD))

    @pl.when(h == heads - 1)
    def _():
        load.wait()

        def product(at):
            terms[at, :] = dot_t(out[at, :], cols[...]).astype(BF16)

        row_loop(LEN, min(256, LEN), product)
        line.hop_wait(srcs, landed, (gs, gr))


def attend_back(qkv, go, bar, log_totals, weights, ends, size, cid):
    width, local3 = weights.shape
    heads = local3 // 3 // HD

    def column(part):
        return pl.BlockSpec((LEN, HD), lambda h: (0, part * heads + h))

    return pl.pallas_call(
        functools.partial(attend_back_kernel, size, heads),
        grid=(heads,),
        out_shape=(
            jax.ShapeDtypeStruct((LEN, local3), BF16),
            jax.ShapeDtypeStruct((heads, 16, HD), F32),
            jax.ShapeDtypeStruct((LEN, width), BF16),
            jax.ShapeDtypeStruct(ends.shape, BF16),
        ),
        in_specs=[
            column(0), column(1), column(2), column(0),
            pl.BlockSpec((LEN, 128), lambda h: (0, 0)),
            pl.BlockSpec((1, 8, LEN), lambda h: (h, 0, 0)),
            HBM, HBM,
        ],
        out_specs=(
            pl.BlockSpec((LEN, local3), lambda h: (0, 0)),
            pl.BlockSpec((1, 16, HD), lambda h: (h, 0, 0)),
            pl.BlockSpec((LEN, width), lambda h: (0, 0)),
            HBM,
        ),
        scratch_shapes=[
            pltpu.VMEM((LEN, HD), F32),
            pltpu.VMEM((LEN, HD), F32),
            pltpu.VMEM((width, local3), BF16),
            pltpu.SemaphoreType.DMA((2,)),
            pltpu.SemaphoreType.DMA((2,)),
            pltpu.SemaphoreType.DMA((1,)),
        ],
        compiler_params=params(cid),
        name="attend_back",
    )(qkv, qkv, qkv, go, bar, log_totals, weights, ends)


def gelu_both(u):
    inner = 0.7978845608028654 * (u + 0.044715 * (u * u * u))
    th = jnp.tanh(inner)
    half = 0.5 * (1.0 + th)
    slope = half + 0.5 * u * (1.0 - th * th) * (
        0.7978845608028654 * (1.0 + 3 * 0.044715 * (u * u))
    )
    return u * half, slope


def hidden_kernel(
    n_dp, size, c_own, gm, up_in, down_in, bias, c_out, act_out, gu_out, mlp_out, back_out, sums,
    up, down, act, gu, mlp, back, gs, gr, in_sem, out_sem,
):
    line = Line(size, c_own.shape[0])
    rows, width = c_own.shape
    units, part = down.shape[1], down.shape[2]
    block = min(512, units)
    loads = [
        pltpu.make_async_copy(up_in, up, in_sem.at[0]),
        pltpu.make_async_copy(down_in, down, in_sem.at[1]),
    ]
    for load in loads:
        load.start()
    line.barrier()
    for piece in range(SUBS):
        for way in (0, 1):
            line.gather_step(way, 0, piece, c_out, (gs, gr), c_own)
    c_out[pl.ds(line.t, 1)] = c_own[...][None]
    sums[...] = jnp.zeros_like(sums)
    for load in loads:
        load.wait()

    def stores(shard):
        pairs = ((act, act_out), (gu, gu_out), (mlp, mlp_out), (back, back_out))
        return [
            pltpu.make_async_copy(src.at[shard], dst.at[shard], out_sem.at[i, shard])
            for i, (src, dst) in enumerate(pairs)
        ]

    def work(shard):
        def unit_block(j, carry):
            at = pl.ds(pl.multiple_of(j * block, block), block)
            u = dot(c_out[shard], up[:, at]) + bias[0:1, at]
            grad = dot_t(gm[shard, :, 0:part], down[0, at, :])
            for d in range(1, n_dp):
                grad = grad + dot_t(gm[shard, :, d * part : (d + 1) * part], down[d, at, :])
            value, slope = gelu_both(u)
            act[shard, :, at] = value.astype(BF16)
            rounded = (grad * slope).astype(BF16)
            gu[shard, :, at] = rounded
            sums[:, at] += fold(rounded.astype(F32))
            return carry

        lax.fori_loop(0, units // block, unit_block, 0)

        def feature_block(d, carry):
            at = pl.ds(pl.multiple_of(d * part, part), part)
            mlp[shard, :, at] = dot(act[shard], down[d]).astype(BF16)
            back[shard, :, at] = dot_t(gu[shard], up[at, :]).astype(BF16)
            return carry

        lax.fori_loop(0, n_dp, feature_block, 0)
        for store in stores(shard):
            store.start()

    line.walk(c_out, (gs, gr), work)
    line.drain_gather(c_out, (gs, gr))
    for shard in range(size):
        for store in stores(shard):
            store.wait()


def hidden(c_own, gm, up, down, bias, size, cid):
    rows, width = c_own.shape
    n_dp, units, part = down.shape
    full, wide = (size, rows, width), (size, rows, units)
    return pl.pallas_call(
        functools.partial(hidden_kernel, n_dp, size),
        out_shape=(
            jax.ShapeDtypeStruct(full, BF16),
            jax.ShapeDtypeStruct(wide, BF16),
            jax.ShapeDtypeStruct(wide, BF16),
            jax.ShapeDtypeStruct(full, BF16),
            jax.ShapeDtypeStruct(full, BF16),
            jax.ShapeDtypeStruct((8, units), F32),
        ),
        in_specs=[WHOLE, WHOLE, HBM, HBM, WHOLE],
        out_specs=(WHOLE, HBM, HBM, HBM, HBM, WHOLE),
        scratch_shapes=[
            pltpu.VMEM((width, units), BF16),
            pltpu.VMEM((n_dp, units, part), BF16),
            pltpu.VMEM(wide, BF16),
            pltpu.VMEM(wide, BF16),
            pltpu.VMEM(full, BF16),
            pltpu.VMEM(full, BF16),
        ]
        + line_sems(size)
        + [pltpu.SemaphoreType.DMA((2,)), pltpu.SemaphoreType.DMA((4, size))],
        compiler_params=params(cid),
        name="hidden",
    )(c_own, gm, up, down, bias)


def pad_to(x, count):
    return jnp.pad(x, ((0, 0), (0, count - x.shape[1])))


def shards(
    tokens, lengths, ln1_gain, ln1_bias, qkv_weight, qv_bias, out_weight, out_bias,
    ln2_gain, ln2_bias, up_weight, up_bias, down_weight, down_bias, cotangent,
):
    n_dp, n_t = lax.axis_size("dp"), lax.axis_size("tensor")
    rows, width = tokens.shape
    part = ln1_gain.shape[0]
    local = qkv_weight.shape[2]
    heads = local // HD
    units = up_weight.shape[1]
    hd_part = qv_bias.shape[2]
    t = lax.axis_index("tensor")
    length = lengths[0]

    pieces = [
        ln1_gain, ln1_bias, out_bias, ln2_gain, ln2_bias, down_bias,
        qv_bias.reshape(-1), up_bias.reshape(-1),
    ]
    packed = jnp.concatenate(pieces)
    count = packed.shape[0]
    lanes = -(-count // 2048) * 2048
    small = jnp.pad(packed, (0, lanes - count)).reshape(lanes // 128, 128)
    smalls, a = first(small, tokens, part, n_dp, n_t, 0)
    smalls, a = smalls.reshape(n_dp, lanes), a.reshape(n_t * rows, width)
    vecs = jnp.stack([smalls[:, i * part : (i + 1) * part].reshape(width) for i in range(6)])
    vecs = jnp.pad(vecs, ((0, 2), (0, 0))).astype(F32)
    at = 6 * part
    qv_all = smalls[:, at : at + 2 * heads * hd_part].reshape(n_dp, 2, heads, hd_part)
    qv_all = qv_all.transpose(1, 2, 0, 3).reshape(2, local).astype(F32)
    at += 2 * heads * hd_part
    up_all = smalls[:, at : at + units // n_dp].reshape(n_dp, units // 16, 16 // n_dp)
    up_shift = up_all.transpose(1, 0, 2).reshape(1, units).astype(F32)
    qkv_shift = jnp.concatenate([qv_all[0], jnp.zeros_like(qv_all[0]), qv_all[1]])

    qkv_full = lax.all_gather(qkv_weight.reshape(part, 3 * local), "dp", axis=0, tiled=True)
    out_full = lax.all_gather(out_weight, "dp", axis=1, tiled=True)
    up_full = lax.all_gather(up_weight, "dp", axis=0, tiled=True)
    down_blocks = lax.all_gather(down_weight, "dp", axis=0, tiled=False)

    own_pos = t * rows + jnp.arange(rows, dtype=jnp.int32)
    valid_own = (own_pos < length).astype(F32)
    valid = jnp.broadcast_to(valid_own[:, None], (rows, 128))
    positions = jnp.arange(LEN, dtype=jnp.int32)
    bar = jnp.broadcast_to(jnp.where(positions < length, 0.0, NEG)[:, None], (LEN, 128))
    gm_own = (cotangent.astype(F32) * valid_own[:, None]).astype(BF16)

    shift = jnp.broadcast_to(qkv_shift, (8, 3 * local))
    qkv, attended_t, log_totals, terms, near = front(
        a, qkv_full, shift, bar, out_full, gm_own, n_t, 7
    )
    terms = terms.reshape(n_t, rows, width)
    c_own, gm, mid, stats_a = middle(terms, gm_own, near, tokens, valid, vecs, n_t, 2)
    c, act, gu, mlp, back_terms, up_sums = hidden(
        c_own, gm, up_full, down_blocks, jnp.broadcast_to(up_shift, (8, units)), n_t, 6
    )
    c, gm = c.reshape(-1, width), gm.reshape(-1, width)
    act, gu = act.reshape(-1, units), gu.reshape(-1, units)

    def rows_dot(left, right):
        return lax.dot_general(
            left, right, (((0,), (0,)), ((), ())), preferred_element_type=F32
        ).astype(BF16)

    down_grad = rows_dot(act, gm)
    up_grad = rows_dot(c, gu)
    back_terms, mlp, down_grad, up_grad = lax.optimization_barrier(
        (back_terms, mlp, down_grad, up_grad)
    )
    down_out = lax.psum_scatter(down_grad, "dp", scatter_dimension=1, tiled=True)
    up_out = lax.psum_scatter(up_grad, "dp", scatter_dimension=0, tiled=True)
    _, gmid, ends, stats_b, go, out_grad = back_middle(
        back_terms, mlp, gm_own, mid, vecs, out_full, attended_t, n_t, 3
    )
    go, out_grad, down_out, up_out = lax.optimization_barrier((go, out_grad, down_out, up_out))
    out_out = lax.psum_scatter(out_grad, "dp", scatter_dimension=1, tiled=True)
    gqkv, head_sums, last_terms, landed = attend_back(
        qkv, go.reshape(-1, local), bar, log_totals, qkv_full, ends, n_t, 8
    )
    qkv_grad = rows_dot(a, gqkv)
    last_terms, qkv_grad = lax.optimization_barrier((last_terms, qkv_grad))
    qkv_out = lax.psum_scatter(qkv_grad, "dp", scatter_dimension=0, tiled=True)
    qkv_out = qkv_out.reshape(part, 3, local)
    tokens_grad, output, stats_c = finish(
        last_terms.reshape(n_t, rows, width), tokens, gmid, mlp, landed, mid, valid, vecs, n_t, 4
    )

    def vec_sum(stats, i):
        return jnp.sum(stats[8 * i : 8 * i + 8], axis=0)

    vectors = jnp.stack(
        [
            vec_sum(stats_c, 0), vec_sum(stats_c, 1), vec_sum(stats_b, 2),
            vec_sum(stats_b, 0), vec_sum(stats_b, 1), vec_sum(stats_b, 3),
        ]
    )
    squares = jnp.stack(
        [
            jnp.sum(stats_a[0:8]), jnp.sum(stats_a[8:16]), jnp.sum(stats_a[16:24]),
            jnp.sum(stats_c[16:24]), jnp.sum(stats_c[24:32]), jnp.sum(valid_own),
        ]
    )
    vector_blocks = vectors.reshape(6, n_dp, part).transpose(1, 0, 2).reshape(n_dp, 6 * part)
    scalar_blocks = jnp.broadcast_to(squares[None], (n_dp, 6))
    top = jnp.concatenate([vector_blocks, scalar_blocks], axis=1)
    top_len = -(-top.shape[1] // 1024) * 1024
    up_blocks = jnp.sum(up_sums, axis=0).reshape(units // 16, n_dp, 16 // n_dp)
    up_blocks = up_blocks.transpose(1, 0, 2).reshape(n_dp, units // n_dp)
    qv_sums = jnp.stack([head_sums[:, 0], head_sums[:, 8]])
    qv_blocks = qv_sums.reshape(2, heads, n_dp, hd_part).transpose(2, 0, 1, 3)
    qv_blocks = qv_blocks.reshape(n_dp, 2 * heads * hd_part)
    low = jnp.concatenate([up_blocks, qv_blocks], axis=1)
    low_len = -(-low.shape[1] // 1024) * 1024
    blocks = jnp.concatenate([pad_to(top, top_len), pad_to(low, low_len)], axis=1)
    blocks = blocks.reshape(n_dp, (top_len + low_len) // 128, 128)
    reduced = reduce_small(blocks, top_len // 128, n_dp, n_t, 5).reshape(-1)
    outs = [reduced[i * part : (i + 1) * part] for i in range(6)]
    totals = reduced[6 * part : 6 * part + 6]
    stream_rms = jnp.sqrt(totals[:5] / (totals[5] * width))
    at = top_len
    up_bias_out = reduced[at : at + units // n_dp].reshape(up_bias.shape)
    at += units // n_dp
    qv_bias_out = reduced[at : at + 2 * heads * hd_part].reshape(qv_bias.shape)

    return (
        output, tokens_grad, outs[0], outs[1],
        qkv_out.astype(F32), qv_bias_out, out_out.astype(F32), outs[2],
        outs[3], outs[4], up_out.astype(F32), up_bias_out,
        down_out.astype(F32), outs[5], stream_rms,
    )


def solution(mesh):
    vector = P("dp")
    rows = P(("dp", "tensor"), None)
    return jax.shard_map(
        shards,
        mesh=mesh,
        in_specs=(
            rows, vector, vector, vector, P("dp", None, "tensor"), P(None, "tensor", "dp"),
            P("tensor", "dp"), vector, vector, vector, P("dp", "tensor"), P("tensor", "dp"),
            P("tensor", "dp"), vector, rows,
        ),
        out_specs=(
            rows, rows, vector, vector, P("dp", None, "tensor"), P(None, "tensor", "dp"),
            P("tensor", "dp"), vector, vector, vector, P("dp", "tensor"), P("tensor", "dp"),
            P("tensor", "dp"), vector, P(),
        ),
        check_vma=False,
    )
```

```python
import functools

import jax
import jax.numpy as jnp
from jax import lax
from jax.experimental import pallas as pl
from jax.experimental.pallas import tpu as pltpu
from jax.sharding import PartitionSpec as P

HD = 128
LEN = 1024
EPS = 1e-05
MESH = pl.DeviceIdType.MESH
F32 = jnp.float32
BF16 = jnp.bfloat16
VMEM_CAP = 60 * 1024 * 1024
SUBS = 2
WHOLE = pl.BlockSpec(memory_space=pltpu.VMEM)
HBM = pl.BlockSpec(memory_space=pltpu.HBM)


class Line:
    def __init__(self, size, rows):
        self.size, self.rows, self.t = size, rows, lax.axis_index("tensor")
        self.sub = rows // SUBS

    def barrier(self):
        sem = pltpu.get_barrier_semaphore()
        pl.semaphore_wait(sem, self.greet(sem))

    def greet(self, sem):
        @pl.when(self.t > 0)
        def _():
            pl.semaphore_signal(sem, device_id={"tensor": self.t - 1}, device_id_type=MESH)

        @pl.when(self.t < self.size - 1)
        def _():
            pl.semaphore_signal(sem, device_id={"tensor": self.t + 1}, device_id_type=MESH)

        return jnp.where(self.t > 0, 1, 0) + jnp.where(self.t < self.size - 1, 1, 0)

    def _copy(self, src, dst, sems, way, shard, part):
        send, recv = sems
        target = self.t + 1 if way == 0 else self.t - 1
        return pltpu.make_async_remote_copy(
            src_ref=src,
            dst_ref=dst.at[shard, pl.ds(part * self.sub, self.sub)],
            send_sem=send.at[way, shard, part],
            recv_sem=recv.at[way, shard, part],
            device_id={"tensor": target},
            device_id_type=MESH,
        )

    def _rows(self, ref, shard, part):
        return ref.at[shard, pl.ds(part * self.sub, self.sub)]

    def _edge(self, way):
        return self.t < self.size - 1 if way == 0 else self.t > 0

    def hop(self, way, src, dst, sems):
        return pltpu.make_async_remote_copy(
            src_ref=src,
            dst_ref=dst.at[way],
            send_sem=sems[0].at[way],
            recv_sem=sems[1].at[way],
            device_id={"tensor": self.t + 1 if way == 0 else self.t - 1},
            device_id_type=MESH,
        )

    def hop_start(self, srcs, dst, sems):
        for way in (0, 1):

            @pl.when(self._edge(way))
            def _(way=way):
                self.hop(way, srcs[way], dst, sems).start()

    def hop_wait(self, srcs, dst, sems):
        for way in (0, 1):

            @pl.when(self._edge(1 - way))
            def _(way=way):
                self.hop(way, srcs[way], dst, sems).wait_recv()

        for way in (0, 1):

            @pl.when(self._edge(way))
            def _(way=way):
                self.hop(way, srcs[way], dst, sems).wait_send()

    def gather_step(self, way, k, part, buf, sems, first, near=None):
        t, last = self.t, self.size - 1
        shard = t - k if way == 0 else t + k
        inside = (t >= k) if way == 0 else (t + k <= last)

        @pl.when(inside)
        def _():
            held = self._rows(buf, shard, part)
            if k > 1 or (k == 1 and near is None):
                self._copy(held, buf, sems, way, shard, part).wait_recv()

            @pl.when(self._edge(way))
            def _():
                src = held
                if k == 0 and first is not None:
                    src = first.at[pl.ds(part * self.sub, self.sub)]
                if k == 1 and near is not None:
                    src = near.at[way, pl.ds(part * self.sub, self.sub)]
                self._copy(src, buf, sems, way, shard, part).start()

    def relay(self, k, part, buf, sems):
        for way in (0, 1):
            shard = self.t - k if way == 0 else self.t + k
            inside = (self.t >= k) if way == 0 else (self.t + k <= self.size - 1)

            @pl.when(inside)
            def _(way=way, shard=shard):
                held = self._rows(buf, shard, part)
                self._copy(held, buf, sems, way, shard, part).wait_recv()

                @pl.when(self._edge(way))
                def _():
                    self._copy(held, buf, sems, way, shard, part).start()

    def walk(self, buf, sems, work):
        last_part = SUBS - 1

        def visit(m, carry):
            k = (m + 1) // 2
            shard = jnp.where(m % 2 == 1, self.t - k, self.t + k)

            @pl.when((shard >= 0) & (shard < self.size))
            def _():
                work(shard)

            @pl.when(m == 0)
            def _():
                for part in range(last_part):
                    self.relay(1, part, buf, sems)

            @pl.when(m % 2 == 0)
            def _():
                self.relay(k + 1, last_part, buf, sems)

            @pl.when(m % 2 == 1)
            def _():
                for part in range(last_part):
                    self.relay(k + 1, part, buf, sems)

            return carry

        lax.fori_loop(0, 2 * self.size - 1, visit, 0)

    def scatter_step(self, way, j, part, terms, buf, sems, ends=None, early=None):
        t, last = self.t, self.size - 1
        shard = last - j if way == 0 else j
        beyond = (shard > t) if way == 0 else (shard < t)
        starts = (t == 0) if way == 0 else (t == last)
        step = min(32, self.sub)
        if ends is None:
            goes, stays = beyond, None
        else:
            goes = (shard > t + 1) if way == 0 else (shard < t - 1)
            stays = (shard == t + 1) if way == 0 else (shard == t - 1)

        second = (t == 1) if way == 0 else (t == last - 1)
        done = early is not None and j == 0

        if not done:

            @pl.when(goes & starts)
            def _():
                self._copy(self._rows(terms, shard, part), buf, sems, way, shard, part).start()

        @pl.when(goes & jnp.logical_not(starts))
        def _():
            held = self._rows(buf, shard, part)
            arrival = self._copy(held, buf, sems, way, shard, part)
            if not done:
                arrival.wait_recv()
            else:

                @pl.when(jnp.logical_not(second))
                def _():
                    arrival.wait_recv()

                if part == 0:

                    @pl.when(second)
                    def _():
                        early[way].wait()

            def add(i, carry):
                rows = pl.ds(part * self.sub + i * step, step)
                total = buf[shard, rows, :].astype(F32) + terms[shard, rows, :].astype(F32)
                buf[shard, rows, :] = total.astype(BF16)
                return carry

            lax.fori_loop(0, self.sub // step, add, 0)
            self._copy(held, buf, sems, way, shard, part).start()

        if stays is None:
            return

        @pl.when(stays & starts)
        def _():
            rows = pl.ds(part * self.sub, self.sub)
            ends[way, rows, :] = terms[shard, rows, :]

        @pl.when(stays & jnp.logical_not(starts))
        def _():
            held = self._rows(buf, shard, part)
            self._copy(held, buf, sems, way, shard, part).wait_recv()

            def add(i, carry):
                rows = pl.ds(part * self.sub + i * step, step)
                total = buf[shard, rows, :].astype(F32) + terms[shard, rows, :].astype(F32)
                ends[way, rows, :] = total.astype(BF16)
                return carry

            lax.fori_loop(0, self.sub // step, add, 0)

    def phase(self, gather=None, scatter=None, on_slot=None, near=None, ends=None):
        n = self.size
        for k in range(0 if near is None else 1, n):
            for part in range(SUBS):
                for way in (0, 1):
                    if gather is not None:
                        self.gather_step(way, k, part, gather[0], gather[1], gather[2], near)
                    if scatter is not None:
                        if gather is None:
                            if k < n - 1:
                                self.scatter_step(way, k, part, scatter[0], scatter[1][way], scatter[2])
                        else:
                            behind = self.t if way == 0 else n - 1 - self.t
                            for b in range(k):

                                @pl.when(behind == b)
                                def _(b=b, k=k, part=part, way=way):
                                    self.scatter_step(
                                        way, k - 1 - b, part, scatter[0], scatter[1][way],
                                        scatter[2], ends,
                                    )
            if on_slot is not None:
                on_slot(k)

    def own_wait(self, bufs, sems):
        for way in (0, 1):
            arrives = self.t > 0 if way == 0 else self.t < self.size - 1

            @pl.when(arrives)
            def _(way=way):
                for part in range(SUBS):
                    held = self._rows(bufs[way], self.t, part)
                    self._copy(held, bufs[way], sems, way, self.t, part).wait_recv()

    def own_sum(self, terms, bufs, rows):
        t = self.t
        zero = jnp.zeros((), F32)
        right = jnp.where(t > 0, bufs[0][t, rows, :].astype(F32), zero)
        left = jnp.where(t < self.size - 1, bufs[1][t, rows, :].astype(F32), zero)
        return terms[t, rows, :].astype(F32) + right + left

    def drain_gather(self, buf, sems, first=0):
        for way in (0, 1):
            for k in range(first, self.size):
                shard = self.t - k if way == 0 else self.t + k
                inside = (self.t >= k) if way == 0 else (self.t + k <= self.size - 1)

                @pl.when(inside & self._edge(way))
                def _(way=way, shard=shard):
                    for part in range(SUBS):
                        held = self._rows(buf, shard, part)
                        self._copy(held, buf, sems, way, shard, part).wait_send()

    def drain_scatter(self, bufs, sems, margin=0, early=False):
        for way in (0, 1):
            for j in range(self.size - 1):
                shard = self.size - 1 - j if way == 0 else j
                beyond = (shard > self.t + margin) if way == 0 else (shard < self.t - margin)
                if early and j == 0:
                    beyond = beyond & self._edge(1 - way)

                @pl.when(beyond)
                def _(way=way, shard=shard):
                    for part in range(SUBS):
                        held = self._rows(bufs[way], shard, part)
                        self._copy(held, bufs[way], sems, way, shard, part).wait_send()


def line_sems(size):
    return [pltpu.SemaphoreType.DMA((2, size, SUBS)), pltpu.SemaphoreType.DMA((2, size, SUBS))]


def fold(x):
    rows, width = x.shape
    return jnp.sum(x.reshape(rows // 8, 8, width), axis=0)


def normal(x):
    centre = x - jnp.mean(x, axis=-1, keepdims=True)
    spread = lax.rsqrt(jnp.mean(centre * centre, axis=-1, keepdims=True) + EPS)
    return centre * spread, spread


def normal_back(upstream, normed, spread, gain):
    scaled = upstream * gain
    mean_part = jnp.mean(scaled, axis=-1, keepdims=True)
    across = jnp.mean(scaled * normed, axis=-1, keepdims=True)
    return spread * (scaled - mean_part - normed * across)


def row_loop(rows, step, body):
    def one(i, carry):
        body(pl.ds(pl.multiple_of(i * step, step), step))
        return carry

    lax.fori_loop(0, rows // step, one, 0)


def params(collective_id=None):
    if collective_id is None:
        return pltpu.CompilerParams(vmem_limit_bytes=VMEM_CAP)
    return pltpu.CompilerParams(
        collective_id=collective_id, has_side_effects=True, vmem_limit_bytes=VMEM_CAP
    )


def first_kernel(n_dp, size, part, small, own, smalls, a_out, tok, send, recv, gs, gr):
    line = Line(size, own.shape[0])
    me = lax.axis_index("dp")
    rows, width = own.shape
    sem = pltpu.get_barrier_semaphore()
    for p in range(1, n_dp):
        pl.semaphore_signal(sem, device_id={"dp": lax.rem(me + p, n_dp)}, device_id_type=MESH)
    ends = line.greet(sem)
    pl.semaphore_wait(sem, ends + n_dp - 1)
    sems = (gs, gr)

    def small_copy(p, slot):
        return pltpu.make_async_remote_copy(
            src_ref=small,
            dst_ref=smalls.at[slot],
            send_sem=send.at[p],
            recv_sem=recv.at[slot],
            device_id={"dp": lax.rem(me + p, n_dp)},
            device_id_type=MESH,
        )

    for p in range(1, n_dp):
        small_copy(p, me).start()
    smalls[pl.ds(me, 1)] = small[...][None]
    step = min(32, rows)
    vec_rows = part // 128

    def normalise(source, shard):
        gain = jnp.concatenate(
            [smalls[d, r : r + 1, :] for d in range(n_dp) for r in range(vec_rows)], axis=1
        ).astype(F32)
        shift = jnp.concatenate(
            [smalls[d, r : r + 1, :] for d in range(n_dp) for r in range(vec_rows, 2 * vec_rows)],
            axis=1,
        ).astype(F32)

        def body(at):
            x = source[at, :] if shard is None else source[shard, at, :]
            normed, _ = normal(x.astype(F32))
            to = line.t if shard is None else shard
            a_out[to, at, :] = (normed * gain + shift).astype(BF16)

        row_loop(rows, step, body)

    def on_slot(k):
        if k == 0:
            for p in range(1, n_dp):
                small_copy(p, lax.rem(me + p, n_dp)).wait_recv()
            normalise(own, None)
        else:

            @pl.when(line.t >= k)
            def _():
                normalise(tok, line.t - k)

            @pl.when(line.t + k <= size - 1)
            def _():
                normalise(tok, line.t + k)

    line.phase(gather=(tok, sems, own), on_slot=on_slot)
    line.drain_gather(tok, sems)
    for p in range(1, n_dp):
        small_copy(p, me).wait_send()


def first(small, own, part, n_dp, size, cid):
    rows, width = own.shape
    return pl.pallas_call(
        functools.partial(first_kernel, n_dp, size, part),
        out_shape=(
            jax.ShapeDtypeStruct((n_dp,) + small.shape, small.dtype),
            jax.ShapeDtypeStruct((size, rows, width), BF16),
        ),
        in_specs=[WHOLE, WHOLE],
        out_specs=(WHOLE, WHOLE),
        scratch_shapes=[
            pltpu.VMEM((size, rows, width), BF16),
            pltpu.SemaphoreType.DMA((n_dp,)),
            pltpu.SemaphoreType.DMA((n_dp,)),
        ]
        + line_sems(size),
        compiler_params=params(cid),
        name="first",
    )(small, own)


def middle_kernel(
    size, terms, cot, near, tok, valid, vecs, c_out, gm_out, mid_out, stats,
    right, left, gs, gr, ss, sr, near_sem,
):
    line = Line(size, tok.shape[0])
    rows = tok.shape[0]
    step = min(32, rows)
    line.barrier()

    def keep(way):
        shard = line.t - 1 if way == 0 else line.t + 1
        return pltpu.make_async_copy(near.at[way], gm_out.at[shard], near_sem.at[way])

    def keep_all(act):
        for way in (0, 1):

            @pl.when(line._edge(1 - way))
            def _(way=way):
                act(keep(way))

    keep_all(lambda copy: copy.start())
    line.phase(
        gather=(gm_out, (gs, gr), None), scatter=(terms, (right, left), (ss, sr)), near=near
    )
    gm_out[pl.ds(line.t, 1)] = cot[...][None]
    keep_all(lambda copy: copy.wait())
    line.own_wait((right, left), (ss, sr))
    stats[...] = jnp.zeros_like(stats)

    def body(at):
        attn = line.own_sum(terms, (right, left), at) + vecs[2:3, :]
        x = tok[at, :].astype(F32)
        mid = x + attn
        normed, _ = normal(mid)
        c_out[at, :] = (normed * vecs[3:4, :] + vecs[4:5, :]).astype(BF16)
        mid_out[at, :] = mid
        ok = valid[at, 0:1]
        stats[0:8, :] += fold(ok * x * x)
        stats[8:16, :] += fold(ok * attn * attn)
        stats[16:24, :] += fold(ok * mid * mid)

    row_loop(rows, step, body)
    line.drain_gather(gm_out, (gs, gr), 1)
    line.drain_scatter((right, left), (ss, sr))


def middle(terms, cot, near, tok, valid, vecs, size, cid):
    rows, width = tok.shape
    full = (size, rows, width)
    return pl.pallas_call(
        functools.partial(middle_kernel, size),
        out_shape=(
            jax.ShapeDtypeStruct((rows, width), BF16),
            jax.ShapeDtypeStruct(full, BF16),
            jax.ShapeDtypeStruct((rows, width), F32),
            jax.ShapeDtypeStruct((24, width), F32),
        ),
        in_specs=[WHOLE, WHOLE, HBM, WHOLE, WHOLE, WHOLE],
        out_specs=(WHOLE,) * 4,
        scratch_shapes=[pltpu.VMEM(full, BF16), pltpu.VMEM(full, BF16)]
        + line_sems(size)
        + line_sems(size)
        + [pltpu.SemaphoreType.DMA((2,))],
        compiler_params=params(cid),
        name="middle",
    )(terms, cot, near, tok, valid, vecs)


def back_middle_kernel(
    size, terms, landed, mlp, gm, mid, vecs, out_w, o_t, gz_out, gmid_out, ends, stats,
    go_out, grad_out, right, left, right2, left2, grad, ss, sr, ms, mr, gs, gr, early_sem,
):
    line = Line(size, mid.shape[0])
    rows = mid.shape[0]
    step = min(32, rows)
    early = (
        pltpu.make_async_copy(landed.at[0], right.at[size - 1], early_sem.at[0]),
        pltpu.make_async_copy(landed.at[1], left.at[0], early_sem.at[1]),
    )
    for copy, holder in zip(early, (1, size - 2)):

        @pl.when(line.t == holder)
        def _(copy=copy):
            copy.start()

    line.barrier()
    for j in range(size - 1):
        for piece in range(SUBS):
            for way in (0, 1):
                line.scatter_step(
                    way, j, piece, terms, (right, left)[way], (ss, sr), None, early
                )
    line.own_wait((right, left), (ss, sr))
    stats[...] = jnp.zeros_like(stats)

    def body(at):
        e = line.own_sum(terms, (right, left), at)
        normed, spread = normal(mid[at, :])
        gy = gm[at, :].astype(F32)
        gmid = gy + normal_back(e, normed, spread, vecs[3:4, :])
        gz_out[line.t, at, :] = gmid.astype(BF16)
        gmid_out[at, :] = gmid
        stats[0:8, :] += fold(e * normed)
        stats[8:16, :] += fold(e)
        stats[16:24, :] += fold(gmid)
        stats[24:32, :] += fold(gy)

    row_loop(rows, step, body)
    width = mid.shape[1]
    block = min(512, width)

    def weigh(shard):
        go_out[shard] = dot_t(gz_out[shard], out_w[...]).astype(BF16)
        here = o_t[:, pl.ds(pl.multiple_of(shard * rows, rows), rows)]

        def column(j, carry):
            at = pl.ds(pl.multiple_of(j * block, block), block)
            grad[:, at] += dot(here, gz_out[shard, :, at])
            return carry

        lax.fori_loop(0, width // block, column, 0)

    def on_slot(k):
        def side(i, carry):
            shard = line.t + k * (2 * i - 1)

            @pl.when((shard >= 0) & (shard < size))
            def _():
                weigh(shard)

            return carry

        lax.fori_loop(0, 1 if k == 0 else 2, side, 0)

    grad[...] = jnp.zeros_like(grad)
    line.phase(
        gather=(gz_out, (gs, gr), None),
        scatter=(mlp, (right2, left2), (ms, mr)),
        on_slot=on_slot,
        ends=ends,
    )
    grad_out[...] = grad[...].astype(BF16)
    line.drain_scatter((right, left), (ss, sr), 0, True)
    line.drain_scatter((right2, left2), (ms, mr), 1)
    line.drain_gather(gz_out, (gs, gr))


def back_middle(terms, landed, mlp, gm, mid, vecs, out_w, o_t, size, cid):
    rows, width = mid.shape
    local = out_w.shape[0]
    full = (size, rows, width)
    return pl.pallas_call(
        functools.partial(back_middle_kernel, size),
        out_shape=(
            jax.ShapeDtypeStruct(full, BF16),
            jax.ShapeDtypeStruct((rows, width), F32),
            jax.ShapeDtypeStruct((2, rows, width), BF16),
            jax.ShapeDtypeStruct((32, width), F32),
            jax.ShapeDtypeStruct((size, rows, local), BF16),
            jax.ShapeDtypeStruct((local, width), BF16),
        ),
        in_specs=[WHOLE, HBM] + [WHOLE] * 6,
        out_specs=(WHOLE,) * 6,
        scratch_shapes=[pltpu.VMEM(full, BF16)] * 4
        + [pltpu.VMEM((local, width), F32)]
        + line_sems(size)
        + line_sems(size)
        + line_sems(size)
        + [pltpu.SemaphoreType.DMA((2,))],
        compiler_params=params(cid),
        name="back_middle",
    )(terms, landed, mlp, gm, mid, vecs, out_w, o_t)


def finish_kernel(
    size, terms, tok, gmid, mlp, landed, mid, valid, vecs, grad_out, y_out, stats,
    right, left, own_mlp, ends, ss, sr, load_sem,
):
    line = Line(size, tok.shape[0])
    rows = tok.shape[0]
    step = min(32, rows)
    loads = [
        pltpu.make_async_copy(mlp.at[line.t], own_mlp, load_sem.at[0]),
        pltpu.make_async_copy(landed, ends, load_sem.at[1]),
    ]
    for load in loads:
        load.start()
    line.barrier()
    stats[...] = jnp.zeros_like(stats)

    def tail(at):
        zero = jnp.zeros((), F32)
        from_left = jnp.where(line.t > 0, ends[0, at, :].astype(F32), zero)
        from_right = jnp.where(line.t < size - 1, ends[1, at, :].astype(F32), zero)
        out = own_mlp[at, :].astype(F32) + from_left + from_right + vecs[5:6, :]
        y = mid[at, :] + out
        y_out[at, :] = y.astype(BF16)
        ok = valid[at, 0:1]
        stats[16:24, :] += fold(ok * out * out)
        stats[24:32, :] += fold(ok * y * y)

    for j in range(size - 1):
        for piece in range(SUBS):
            for way in (0, 1):
                line.scatter_step(way, j, piece, terms, (right, left)[way], (ss, sr))
        if j == 0:
            for load in loads:
                load.wait()
            row_loop(rows, step, tail)
    line.own_wait((right, left), (ss, sr))

    def body(at):
        e = line.own_sum(terms, (right, left), at)
        normed, spread = normal(tok[at, :].astype(F32))
        grad_out[at, :] = gmid[at, :] + normal_back(e, normed, spread, vecs[0:1, :])
        stats[0:8, :] += fold(e * normed)
        stats[8:16, :] += fold(e)

    row_loop(rows, step, body)
    line.drain_scatter((right, left), (ss, sr))


def finish(terms, tok, gmid, mlp, landed, mid, valid, vecs, size, cid):
    rows, width = tok.shape
    full = (size, rows, width)
    return pl.pallas_call(
        functools.partial(finish_kernel, size),
        out_shape=(
            jax.ShapeDtypeStruct((rows, width), F32),
            jax.ShapeDtypeStruct((rows, width), BF16),
            jax.ShapeDtypeStruct((32, width), F32),
        ),
        in_specs=[WHOLE, WHOLE, WHOLE, HBM, HBM, WHOLE, WHOLE, WHOLE],
        out_specs=(WHOLE,) * 3,
        scratch_shapes=[pltpu.VMEM(full, BF16)] * 2
        + [pltpu.VMEM((rows, width), BF16), pltpu.VMEM((2, rows, width), BF16)]
        + line_sems(size)
        + [pltpu.SemaphoreType.DMA((2,))],
        compiler_params=params(cid),
        name="finish",
    )(terms, tok, gmid, mlp, landed, mid, valid, vecs)


def reduce_small_kernel(n_dp, n_t, shared, blocks, out, land, sums, land2, s1, r1, s2, r2):
    me, t = lax.axis_index("dp"), lax.axis_index("tensor")
    sem = pltpu.get_barrier_semaphore()
    for p in range(1, n_dp):
        pl.semaphore_signal(sem, device_id={"dp": lax.rem(me + p, n_dp)}, device_id_type=MESH)
    for p in range(1, n_t):
        pl.semaphore_signal(sem, device_id={"tensor": lax.rem(t + p, n_t)}, device_id_type=MESH)
    pl.semaphore_wait(sem, n_dp + n_t - 2)

    def one(p):
        other = lax.rem(me + p, n_dp)
        return pltpu.make_async_remote_copy(
            src_ref=blocks.at[other],
            dst_ref=land.at[p],
            send_sem=s1.at[p],
            recv_sem=r1.at[p],
            device_id={"dp": other},
            device_id_type=MESH,
        )

    for p in range(1, n_dp):
        one(p).start()
    total = blocks[me]
    for p in range(1, n_dp):
        one(p).wait_recv()
        total = total + land[p]
    sums[...] = total

    def two(p):
        return pltpu.make_async_remote_copy(
            src_ref=sums.at[pl.ds(0, shared)],
            dst_ref=land2.at[p],
            send_sem=s2.at[p],
            recv_sem=r2.at[p],
            device_id={"tensor": lax.rem(t + p, n_t)},
            device_id_type=MESH,
        )

    for p in range(1, n_t):
        two(p).start()
    out[...] = total
    top = sums[pl.ds(0, shared), :]
    for p in range(1, n_t):
        two(p).wait_recv()
        top = top + land2[p]
    out[pl.ds(0, shared), :] = top
    for p in range(1, n_dp):
        one(p).wait_send()
    for p in range(1, n_t):
        two(p).wait_send()


def reduce_small(blocks, shared, n_dp, n_t, cid):
    _, rows, width = blocks.shape
    return pl.pallas_call(
        functools.partial(reduce_small_kernel, n_dp, n_t, shared),
        out_shape=jax.ShapeDtypeStruct((rows, width), F32),
        in_specs=[WHOLE],
        out_specs=WHOLE,
        scratch_shapes=[
            pltpu.VMEM((n_dp, rows, width), F32),
            pltpu.VMEM((rows, width), F32),
            pltpu.VMEM((n_t, shared, width), F32),
            pltpu.SemaphoreType.DMA((n_dp,)),
            pltpu.SemaphoreType.DMA((n_dp,)),
            pltpu.SemaphoreType.DMA((n_t,)),
            pltpu.SemaphoreType.DMA((n_t,)),
        ],
        compiler_params=params(cid),
        name="reduce_small",
    )(blocks)


BLOCK = 256
NEG = -1e30
SCALE = HD**-0.5


def dot(a, b):
    return jnp.dot(a, b, preferred_element_type=F32)


def dot_t(a, b):
    return lax.dot_general(a, b, (((1,), (1,)), ((), ())), preferred_element_type=F32)


def masked_scores(q, k, keys, first, bar):
    scores = dot_t(k, q) * SCALE + bar
    key_pos = lax.broadcasted_iota(jnp.int32, (keys, BLOCK), 0)
    query_pos = first + lax.broadcasted_iota(jnp.int32, (keys, BLOCK), 1)
    return jnp.where(key_pos <= query_pos, scores, NEG)


def head_cols(part, h, heads):
    return pl.ds(pl.multiple_of((part * heads + h) * HD, HD), HD)


def front_kernel(
    size, heads, a, weights, shift, bar, out_w, cot, qkv, out_t, log_totals, terms, near,
    cols, mixed_all, gs, gr, load_sem,
):
    h = pl.program_id(0)
    rows = cot.shape[0]
    local = heads * HD
    line = Line(size, rows)

    def load(part):
        at = pl.ds(part * local, local)
        return pltpu.make_async_copy(weights.at[:, at], cols.at[:, at], load_sem.at[part])

    @pl.when(h == 0)
    def _():
        for part in range(3):
            load(part).start()
        line.barrier()
        line.hop_start((cot, cot), near, (gs, gr))
        for part in range(3):
            load(part).wait()
            span = slice(part * local, (part + 1) * local)

            def product(at, span=span):
                qkv[at, span] = (dot(a[at, :], cols[:, span]) + shift[0:1, span]).astype(BF16)

            row_loop(LEN, min(256, LEN), product)

    at_q, at_k, at_v = (head_cols(part, h, heads) for part in range(3))
    value_cols = qkv[:, at_v].T
    for block in range(LEN // BLOCK):
        first, keys = block * BLOCK, (block + 1) * BLOCK
        here = slice(first, first + BLOCK)
        scores = masked_scores(qkv[here, at_q], qkv[0:keys, at_k], keys, first, bar[0:keys, 0:1])
        top = jnp.max(scores, axis=0, keepdims=True)
        powers = jnp.exp(scores - top)
        total = jnp.sum(powers, axis=0, keepdims=True)
        shares = (powers * (1.0 / total)).astype(BF16)
        mixed = dot(value_cols[:, 0:keys], shares)
        mixed_all[here, head_cols(0, h, heads)] = mixed.T.astype(BF16)
        out_t[:, here] = mixed.astype(BF16)
        log_totals[0, :, here] = jnp.broadcast_to(top + jnp.log(total), (8, BLOCK))

    @pl.when(h == heads - 1)
    def _():
        def project(at):
            terms[at, :] = dot(mixed_all[at, :], out_w[...]).astype(BF16)

        row_loop(LEN, min(256, LEN), project)
        line.hop_wait((cot, cot), near, (gs, gr))


def front(a, weights, shift, bar, out_w, cot, size, cid):
    width, local3 = weights.shape
    local = local3 // 3
    heads = local // HD
    return pl.pallas_call(
        functools.partial(front_kernel, size, heads),
        grid=(heads,),
        out_shape=(
            jax.ShapeDtypeStruct((LEN, local3), BF16),
            jax.ShapeDtypeStruct((local, LEN), BF16),
            jax.ShapeDtypeStruct((heads, 8, LEN), F32),
            jax.ShapeDtypeStruct((LEN, width), BF16),
            jax.ShapeDtypeStruct((2,) + cot.shape, BF16),
        ),
        in_specs=[WHOLE, HBM, WHOLE, WHOLE, WHOLE, HBM],
        out_specs=(
            pl.BlockSpec((LEN, local3), lambda h: (0, 0)),
            pl.BlockSpec((HD, LEN), lambda h: (h, 0)),
            pl.BlockSpec((1, 8, LEN), lambda h: (h, 0, 0)),
            pl.BlockSpec((LEN, width), lambda h: (0, 0)),
            HBM,
        ),
        scratch_shapes=[
            pltpu.VMEM((width, local3), BF16),
            pltpu.VMEM((LEN, local), BF16),
            pltpu.SemaphoreType.DMA((2,)),
            pltpu.SemaphoreType.DMA((2,)),
            pltpu.SemaphoreType.DMA((3,)),
        ],
        compiler_params=params(cid),
        name="front",
    )(a, weights, shift, bar, out_w, cot)


def attend_back_kernel(
    size, heads, q, k, v, go, bar, log_totals, weights, ends, out, sums, terms, landed,
    key_grad, value_grad, cols, gs, gr, load_sem,
):
    h = pl.program_id(0)
    line = Line(size, ends.shape[1])
    srcs = (ends.at[0], ends.at[1])
    load = pltpu.make_async_copy(weights, cols, load_sem.at[0])

    @pl.when(h == 0)
    def _():
        load.start()
        line.barrier()
        line.hop_start(srcs, landed, (gs, gr))

    key_cols = k[...].T
    query_sum = jnp.zeros((1, HD), F32)
    at_q, at_k, at_v = (head_cols(part, h, heads) for part in range(3))
    for block in range(LEN // BLOCK - 1, -1, -1):
        first, keys = block * BLOCK, (block + 1) * BLOCK
        here = slice(first, first + BLOCK)
        scores = masked_scores(q[here, :], k[0:keys, :], keys, first, bar[0:keys, 0:1])
        shares = jnp.exp(scores - log_totals[0, 0:1, here])
        share_grad = dot_t(v[0:keys, :], go[here, :])
        centre = jnp.sum(shares * share_grad, axis=0, keepdims=True)
        score_grad = (shares * (share_grad - centre)).astype(BF16)
        values = dot(shares.astype(BF16), go[here, :])
        keyed = dot(score_grad, q[here, :])
        if block == LEN // BLOCK - 1:
            value_grad[...] = values
            key_grad[...] = keyed
        else:
            value_grad[0:keys, :] += values
            key_grad[0:keys, :] += keyed
        query_grad = ((dot(key_cols[:, 0:keys], score_grad)) * SCALE).T.astype(BF16)
        out[here, at_q] = query_grad
        query_sum = query_sum + jnp.sum(query_grad.astype(F32), axis=0, keepdims=True)
    out[:, at_k] = (key_grad[...] * SCALE).astype(BF16)
    rounded = value_grad[...].astype(BF16)
    out[:, at_v] = rounded
    value_sum = jnp.sum(rounded.astype(F32), axis=0, keepdims=True)
    sums[0, 0:8, :] = jnp.broadcast_to(query_sum, (8, HD))
    sums[0, 8:16, :] = jnp.broadcast_to(value_sum, (8, HD))

    @pl.when(h == heads - 1)
    def _():
        load.wait()

        def product(at):
            terms[at, :] = dot_t(out[at, :], cols[...]).astype(BF16)

        row_loop(LEN, min(256, LEN), product)
        line.hop_wait(srcs, landed, (gs, gr))


def attend_back(qkv, go, bar, log_totals, weights, ends, size, cid):
    width, local3 = weights.shape
    heads = local3 // 3 // HD

    def column(part):
        return pl.BlockSpec((LEN, HD), lambda h: (0, part * heads + h))

    return pl.pallas_call(
        functools.partial(attend_back_kernel, size, heads),
        grid=(heads,),
        out_shape=(
            jax.ShapeDtypeStruct((LEN, local3), BF16),
            jax.ShapeDtypeStruct((heads, 16, HD), F32),
            jax.ShapeDtypeStruct((LEN, width), BF16),
            jax.ShapeDtypeStruct(ends.shape, BF16),
        ),
        in_specs=[
            column(0), column(1), column(2), column(0),
            pl.BlockSpec((LEN, 128), lambda h: (0, 0)),
            pl.BlockSpec((1, 8, LEN), lambda h: (h, 0, 0)),
            HBM, HBM,
        ],
        out_specs=(
            pl.BlockSpec((LEN, local3), lambda h: (0, 0)),
            pl.BlockSpec((1, 16, HD), lambda h: (h, 0, 0)),
            pl.BlockSpec((LEN, width), lambda h: (0, 0)),
            HBM,
        ),
        scratch_shapes=[
            pltpu.VMEM((LEN, HD), F32),
            pltpu.VMEM((LEN, HD), F32),
            pltpu.VMEM((width, local3), BF16),
            pltpu.SemaphoreType.DMA((2,)),
            pltpu.SemaphoreType.DMA((2,)),
            pltpu.SemaphoreType.DMA((1,)),
        ],
        compiler_params=params(cid),
        name="attend_back",
    )(qkv, qkv, qkv, go, bar, log_totals, weights, ends)


def gelu_both(u):
    inner = 0.7978845608028654 * (u + 0.044715 * (u * u * u))
    th = jnp.tanh(inner)
    half = 0.5 * (1.0 + th)
    slope = half + 0.5 * u * (1.0 - th * th) * (
        0.7978845608028654 * (1.0 + 3 * 0.044715 * (u * u))
    )
    return u * half, slope


def hidden_kernel(
    n_dp, size, c_own, gm, up_in, down_in, bias, c_out, act_out, gu_out, mlp_out, back_out, sums,
    up, down, act, gu, mlp, back, gs, gr, in_sem, out_sem,
):
    line = Line(size, c_own.shape[0])
    rows, width = c_own.shape
    units, part = down.shape[1], down.shape[2]
    block = min(512, units)
    loads = [
        pltpu.make_async_copy(up_in, up, in_sem.at[0]),
        pltpu.make_async_copy(down_in, down, in_sem.at[1]),
    ]
    for load in loads:
        load.start()
    line.barrier()
    for piece in range(SUBS):
        for way in (0, 1):
            line.gather_step(way, 0, piece, c_out, (gs, gr), c_own)
    c_out[pl.ds(line.t, 1)] = c_own[...][None]
    sums[...] = jnp.zeros_like(sums)
    for load in loads:
        load.wait()

    def stores(shard):
        pairs = ((act, act_out), (gu, gu_out), (mlp, mlp_out), (back, back_out))
        return [
            pltpu.make_async_copy(src.at[shard], dst.at[shard], out_sem.at[i, shard])
            for i, (src, dst) in enumerate(pairs)
        ]

    def work(shard):
        def unit_block(j, carry):
            at = pl.ds(pl.multiple_of(j * block, block), block)
            u = dot(c_out[shard], up[:, at]) + bias[0:1, at]
            grad = dot_t(gm[shard, :, 0:part], down[0, at, :])
            for d in range(1, n_dp):
                grad = grad + dot_t(gm[shard, :, d * part : (d + 1) * part], down[d, at, :])
            value, slope = gelu_both(u)
            act[shard, :, at] = value.astype(BF16)
            rounded = (grad * slope).astype(BF16)
            gu[shard, :, at] = rounded
            sums[:, at] += fold(rounded.astype(F32))
            return carry

        lax.fori_loop(0, units // block, unit_block, 0)

        def feature_block(d, carry):
            at = pl.ds(pl.multiple_of(d * part, part), part)
            mlp[shard, :, at] = dot(act[shard], down[d]).astype(BF16)
            back[shard, :, at] = dot_t(gu[shard], up[at, :]).astype(BF16)
            return carry

        lax.fori_loop(0, n_dp, feature_block, 0)
        for store in stores(shard):
            store.start()

    line.walk(c_out, (gs, gr), work)
    line.drain_gather(c_out, (gs, gr))
    for shard in range(size):
        for store in stores(shard):
            store.wait()


def hidden(c_own, gm, up, down, bias, size, cid):
    rows, width = c_own.shape
    n_dp, units, part = down.shape
    full, wide = (size, rows, width), (size, rows, units)
    return pl.pallas_call(
        functools.partial(hidden_kernel, n_dp, size),
        out_shape=(
            jax.ShapeDtypeStruct(full, BF16),
            jax.ShapeDtypeStruct(wide, BF16),
            jax.ShapeDtypeStruct(wide, BF16),
            jax.ShapeDtypeStruct(full, BF16),
            jax.ShapeDtypeStruct(full, BF16),
            jax.ShapeDtypeStruct((8, units), F32),
        ),
        in_specs=[WHOLE, WHOLE, HBM, HBM, WHOLE],
        out_specs=(WHOLE, HBM, HBM, HBM, HBM, WHOLE),
        scratch_shapes=[
            pltpu.VMEM((width, units), BF16),
            pltpu.VMEM((n_dp, units, part), BF16),
            pltpu.VMEM(wide, BF16),
            pltpu.VMEM(wide, BF16),
            pltpu.VMEM(full, BF16),
            pltpu.VMEM(full, BF16),
        ]
        + line_sems(size)
        + [pltpu.SemaphoreType.DMA((2,)), pltpu.SemaphoreType.DMA((4, size))],
        compiler_params=params(cid),
        name="hidden",
    )(c_own, gm, up, down, bias)


def cross(left, right):
    return lax.dot_general(left, right, (((0,), (0,)), ((), ())), preferred_element_type=F32)


def products_kernel(
    size, steps, act, gm, c, gu_in, terms, down_out, up_out, landed, gu, gs, gr, load_sem
):
    i = pl.program_id(0)
    last = size - 1
    line = Line(size, terms.shape[1])
    load = pltpu.make_async_copy(gu_in, gu, load_sem.at[0])
    hops = [
        (line.t == sender, line.t == taker, line.hop(way, terms.at[shard], landed, (gs, gr)))
        for way, sender, taker, shard in ((0, 0, 1, last), (1, last, last - 1, 0))
    ]

    @pl.when(i == 0)
    def _():
        load.start()
        line.barrier()
        for sends, _, copy in hops:

            @pl.when(sends)
            def _(copy=copy):
                copy.start()

    @pl.when(i < steps)
    def _():
        down_out[...] = cross(act[...], gm[...]).astype(BF16)

    @pl.when(i == steps)
    def _():
        load.wait()

    @pl.when(i >= steps)
    def _():
        up_out[...] = cross(c[...], gu[...]).astype(BF16)

    @pl.when(i == pl.num_programs(0) - 1)
    def _():
        for sends, takes, copy in hops:

            @pl.when(sends)
            def _(copy=copy):
                copy.wait_send()

            @pl.when(takes)
            def _(copy=copy):
                copy.wait_recv()


def products(act, gm, c, gu, terms, size, cid):
    rows, units = act.shape
    width = gm.shape[1]
    steps, more = units // BLOCK, width // BLOCK
    return pl.pallas_call(
        functools.partial(products_kernel, size, steps),
        grid=(steps + more,),
        out_shape=(
            jax.ShapeDtypeStruct((units, width), BF16),
            jax.ShapeDtypeStruct((width, units), BF16),
            jax.ShapeDtypeStruct((2,) + terms.shape[1:], BF16),
        ),
        in_specs=[
            pl.BlockSpec((rows, BLOCK), lambda i: (0, jnp.minimum(i, steps - 1))),
            WHOLE,
            pl.BlockSpec((rows, BLOCK), lambda i: (0, jnp.maximum(i - steps, 0))),
            HBM,
            HBM,
        ],
        out_specs=(
            pl.BlockSpec((BLOCK, width), lambda i: (jnp.minimum(i, steps - 1), 0)),
            pl.BlockSpec((BLOCK, units), lambda i: (jnp.maximum(i - steps, 0), 0)),
            HBM,
        ),
        scratch_shapes=[
            pltpu.VMEM((rows, units), BF16),
            pltpu.SemaphoreType.DMA((2,)),
            pltpu.SemaphoreType.DMA((2,)),
            pltpu.SemaphoreType.DMA((1,)),
        ],
        compiler_params=params(cid),
        name="products",
    )(act, gm, c, gu, terms)


def pad_to(x, count):
    return jnp.pad(x, ((0, 0), (0, count - x.shape[1])))


def shards(
    tokens, lengths, ln1_gain, ln1_bias, qkv_weight, qv_bias, out_weight, out_bias,
    ln2_gain, ln2_bias, up_weight, up_bias, down_weight, down_bias, cotangent,
):
    n_dp, n_t = lax.axis_size("dp"), lax.axis_size("tensor")
    rows, width = tokens.shape
    part = ln1_gain.shape[0]
    local = qkv_weight.shape[2]
    heads = local // HD
    units = up_weight.shape[1]
    hd_part = qv_bias.shape[2]
    t = lax.axis_index("tensor")
    length = lengths[0]

    pieces = [
        ln1_gain, ln1_bias, out_bias, ln2_gain, ln2_bias, down_bias,
        qv_bias.reshape(-1), up_bias.reshape(-1),
    ]
    packed = jnp.concatenate(pieces)
    count = packed.shape[0]
    lanes = -(-count // 2048) * 2048
    small = jnp.pad(packed, (0, lanes - count)).reshape(lanes // 128, 128)
    smalls, a = first(small, tokens, part, n_dp, n_t, 0)
    smalls, a = smalls.reshape(n_dp, lanes), a.reshape(n_t * rows, width)
    vecs = jnp.stack([smalls[:, i * part : (i + 1) * part].reshape(width) for i in range(6)])
    vecs = jnp.pad(vecs, ((0, 2), (0, 0))).astype(F32)
    at = 6 * part
    qv_all = smalls[:, at : at + 2 * heads * hd_part].reshape(n_dp, 2, heads, hd_part)
    qv_all = qv_all.transpose(1, 2, 0, 3).reshape(2, local).astype(F32)
    at += 2 * heads * hd_part
    up_all = smalls[:, at : at + units // n_dp].reshape(n_dp, units // 16, 16 // n_dp)
    up_shift = up_all.transpose(1, 0, 2).reshape(1, units).astype(F32)
    qkv_shift = jnp.concatenate([qv_all[0], jnp.zeros_like(qv_all[0]), qv_all[1]])

    qkv_full = lax.all_gather(qkv_weight.reshape(part, 3 * local), "dp", axis=0, tiled=True)
    out_full = lax.all_gather(out_weight, "dp", axis=1, tiled=True)
    up_full = lax.all_gather(up_weight, "dp", axis=0, tiled=True)
    down_blocks = lax.all_gather(down_weight, "dp", axis=0, tiled=False)

    own_pos = t * rows + jnp.arange(rows, dtype=jnp.int32)
    valid_own = (own_pos < length).astype(F32)
    valid = jnp.broadcast_to(valid_own[:, None], (rows, 128))
    positions = jnp.arange(LEN, dtype=jnp.int32)
    bar = jnp.broadcast_to(jnp.where(positions < length, 0.0, NEG)[:, None], (LEN, 128))
    gm_own = (cotangent.astype(F32) * valid_own[:, None]).astype(BF16)

    shift = jnp.broadcast_to(qkv_shift, (8, 3 * local))
    qkv, attended_t, log_totals, terms, near = front(
        a, qkv_full, shift, bar, out_full, gm_own, n_t, 7
    )
    terms = terms.reshape(n_t, rows, width)
    c_own, gm, mid, stats_a = middle(terms, gm_own, near, tokens, valid, vecs, n_t, 2)
    c, act, gu, mlp, back_terms, up_sums = hidden(
        c_own, gm, up_full, down_blocks, jnp.broadcast_to(up_shift, (8, units)), n_t, 6
    )
    c, gm = c.reshape(-1, width), gm.reshape(-1, width)
    act, gu = act.reshape(-1, units), gu.reshape(-1, units)

    def rows_dot(left, right):
        return lax.dot_general(
            left, right, (((0,), (0,)), ((), ())), preferred_element_type=F32
        ).astype(BF16)

    down_grad, up_grad, early = products(act, gm, c, gu, back_terms, n_t, 9)
    down_out = lax.psum_scatter(down_grad, "dp", scatter_dimension=1, tiled=True)
    up_out = lax.psum_scatter(up_grad, "dp", scatter_dimension=0, tiled=True)
    _, gmid, ends, stats_b, go, out_grad = back_middle(
        back_terms, early, mlp, gm_own, mid, vecs, out_full, attended_t, n_t, 3
    )
    go, out_grad, down_out, up_out = lax.optimization_barrier((go, out_grad, down_out, up_out))
    out_out = lax.psum_scatter(out_grad, "dp", scatter_dimension=1, tiled=True)
    gqkv, head_sums, last_terms, landed = attend_back(
        qkv, go.reshape(-1, local), bar, log_totals, qkv_full, ends, n_t, 8
    )
    qkv_grad = rows_dot(a, gqkv)
    last_terms, qkv_grad = lax.optimization_barrier((last_terms, qkv_grad))
    qkv_out = lax.psum_scatter(qkv_grad, "dp", scatter_dimension=0, tiled=True)
    qkv_out = qkv_out.reshape(part, 3, local)
    tokens_grad, output, stats_c = finish(
        last_terms.reshape(n_t, rows, width), tokens, gmid, mlp, landed, mid, valid, vecs, n_t, 4
    )

    def vec_sum(stats, i):
        return jnp.sum(stats[8 * i : 8 * i + 8], axis=0)

    vectors = jnp.stack(
        [
            vec_sum(stats_c, 0), vec_sum(stats_c, 1), vec_sum(stats_b, 2),
            vec_sum(stats_b, 0), vec_sum(stats_b, 1), vec_sum(stats_b, 3),
        ]
    )
    def squares(stats, i):
        return jnp.sum(stats[8 * i : 8 * i + 8].reshape(8, n_dp, part), axis=(0, 1))

    sums = jnp.concatenate(
        [
            squares(stats_a, 0), squares(stats_a, 1), squares(stats_a, 2),
            squares(stats_c, 2), squares(stats_c, 3),
        ]
    )
    count = jnp.clip(length - t * rows, 0, rows).astype(F32)
    vector_blocks = vectors.reshape(6, n_dp, part).transpose(1, 0, 2).reshape(n_dp, 6 * part)
    top = jnp.concatenate(
        [vector_blocks, jnp.broadcast_to(sums[None], (n_dp, 5 * part)), jnp.full((n_dp, 1), count)],
        axis=1,
    )
    top_len = -(-top.shape[1] // 1024) * 1024
    up_blocks = jnp.sum(up_sums, axis=0).reshape(units // 16, n_dp, 16 // n_dp)
    up_blocks = up_blocks.transpose(1, 0, 2).reshape(n_dp, units // n_dp)
    qv_sums = jnp.stack([head_sums[:, 0], head_sums[:, 8]])
    qv_blocks = qv_sums.reshape(2, heads, n_dp, hd_part).transpose(2, 0, 1, 3)
    qv_blocks = qv_blocks.reshape(n_dp, 2 * heads * hd_part)
    low = jnp.concatenate([up_blocks, qv_blocks], axis=1)
    low_len = -(-low.shape[1] // 1024) * 1024
    blocks = jnp.concatenate([pad_to(top, top_len), pad_to(low, low_len)], axis=1)
    blocks = blocks.reshape(n_dp, (top_len + low_len) // 128, 128)
    reduced = reduce_small(blocks, top_len // 128, n_dp, n_t, 5).reshape(-1)
    outs = [reduced[i * part : (i + 1) * part] for i in range(6)]
    totals = jnp.sum(reduced[6 * part : 11 * part].reshape(5, part), axis=1)
    stream_rms = jnp.sqrt(totals / (reduced[11 * part] * width))
    at = top_len
    up_bias_out = reduced[at : at + units // n_dp].reshape(up_bias.shape)
    at += units // n_dp
    qv_bias_out = reduced[at : at + 2 * heads * hd_part].reshape(qv_bias.shape)

    return (
        output, tokens_grad, outs[0], outs[1],
        qkv_out.astype(F32), qv_bias_out, out_out.astype(F32), outs[2],
        outs[3], outs[4], up_out.astype(F32), up_bias_out,
        down_out.astype(F32), outs[5], stream_rms,
    )


def solution(mesh):
    vector = P("dp")
    rows = P(("dp", "tensor"), None)
    return jax.shard_map(
        shards,
        mesh=mesh,
        in_specs=(
            rows, vector, vector, vector, P("dp", None, "tensor"), P(None, "tensor", "dp"),
            P("tensor", "dp"), vector, vector, vector, P("dp", "tensor"), P("tensor", "dp"),
            P("tensor", "dp"), vector, rows,
        ),
        out_specs=(
            rows, rows, vector, vector, P("dp", None, "tensor"), P(None, "tensor", "dp"),
            P("tensor", "dp"), vector, vector, vector, P("dp", "tensor"), P("tensor", "dp"),
            P("tensor", "dp"), vector, P(),
        ),
        check_vma=False,
    )
```

```python
import functools

import jax
import jax.numpy as jnp
from jax import lax
from jax.experimental import pallas as pl
from jax.experimental.pallas import tpu as pltpu
from jax.sharding import PartitionSpec as P

HD = 128
LEN = 1024
EPS = 1e-05
MESH = pl.DeviceIdType.MESH
F32 = jnp.float32
BF16 = jnp.bfloat16
VMEM_CAP = 60 * 1024 * 1024
SUBS = 2
WHOLE = pl.BlockSpec(memory_space=pltpu.VMEM)
HBM = pl.BlockSpec(memory_space=pltpu.HBM)


class Line:
    def __init__(self, size, rows):
        self.size, self.rows, self.t = size, rows, lax.axis_index("tensor")
        self.sub = rows // SUBS

    def barrier(self):
        sem = pltpu.get_barrier_semaphore()
        pl.semaphore_wait(sem, self.greet(sem))

    def greet(self, sem):
        @pl.when(self.t > 0)
        def _():
            pl.semaphore_signal(sem, device_id={"tensor": self.t - 1}, device_id_type=MESH)

        @pl.when(self.t < self.size - 1)
        def _():
            pl.semaphore_signal(sem, device_id={"tensor": self.t + 1}, device_id_type=MESH)

        return jnp.where(self.t > 0, 1, 0) + jnp.where(self.t < self.size - 1, 1, 0)

    def _copy(self, src, dst, sems, way, shard, part):
        send, recv = sems
        target = self.t + 1 if way == 0 else self.t - 1
        return pltpu.make_async_remote_copy(
            src_ref=src,
            dst_ref=dst.at[shard, pl.ds(part * self.sub, self.sub)],
            send_sem=send.at[way, shard, part],
            recv_sem=recv.at[way, shard, part],
            device_id={"tensor": target},
            device_id_type=MESH,
        )

    def _rows(self, ref, shard, part):
        return ref.at[shard, pl.ds(part * self.sub, self.sub)]

    def _edge(self, way):
        return self.t < self.size - 1 if way == 0 else self.t > 0

    def hop(self, way, src, dst, sems):
        return pltpu.make_async_remote_copy(
            src_ref=src,
            dst_ref=dst.at[way],
            send_sem=sems[0].at[way],
            recv_sem=sems[1].at[way],
            device_id={"tensor": self.t + 1 if way == 0 else self.t - 1},
            device_id_type=MESH,
        )

    def hop_start(self, srcs, dst, sems):
        for way in (0, 1):

            @pl.when(self._edge(way))
            def _(way=way):
                self.hop(way, srcs[way], dst, sems).start()

    def hop_wait(self, srcs, dst, sems):
        for way in (0, 1):

            @pl.when(self._edge(1 - way))
            def _(way=way):
                self.hop(way, srcs[way], dst, sems).wait_recv()

        for way in (0, 1):

            @pl.when(self._edge(way))
            def _(way=way):
                self.hop(way, srcs[way], dst, sems).wait_send()

    def first_hops(self, terms, landed, sems):
        last = self.size - 1
        return [
            (self.t == sender, self.t == taker, self.hop(way, terms.at[shard], landed, sems))
            for way, sender, taker, shard in ((0, 0, 1, last), (1, last, last - 1, 0))
        ]

    def hops_start(self, hops):
        for sends, _, copy in hops:

            @pl.when(sends)
            def _(copy=copy):
                copy.start()

    def hops_wait(self, hops):
        for sends, takes, copy in hops:

            @pl.when(sends)
            def _(copy=copy):
                copy.wait_send()

            @pl.when(takes)
            def _(copy=copy):
                copy.wait_recv()

    def early_start(self, landed, bufs, sem):
        last = self.size - 1
        early = (
            pltpu.make_async_copy(landed.at[0], bufs[0].at[last], sem.at[0]),
            pltpu.make_async_copy(landed.at[1], bufs[1].at[0], sem.at[1]),
        )
        for copy, holder in zip(early, (1, last - 1)):

            @pl.when(self.t == holder)
            def _(copy=copy):
                copy.start()

        return early

    def gather_step(self, way, k, part, buf, sems, first, near=None):
        t, last = self.t, self.size - 1
        shard = t - k if way == 0 else t + k
        inside = (t >= k) if way == 0 else (t + k <= last)

        @pl.when(inside)
        def _():
            held = self._rows(buf, shard, part)
            if k > 1 or (k == 1 and near is None):
                self._copy(held, buf, sems, way, shard, part).wait_recv()

            @pl.when(self._edge(way))
            def _():
                src = held
                if k == 0 and first is not None:
                    src = first.at[pl.ds(part * self.sub, self.sub)]
                if k == 1 and near is not None:
                    src = near.at[way, pl.ds(part * self.sub, self.sub)]
                self._copy(src, buf, sems, way, shard, part).start()

    def relay(self, k, part, buf, sems):
        for way in (0, 1):
            shard = self.t - k if way == 0 else self.t + k
            inside = (self.t >= k) if way == 0 else (self.t + k <= self.size - 1)

            @pl.when(inside)
            def _(way=way, shard=shard):
                held = self._rows(buf, shard, part)
                self._copy(held, buf, sems, way, shard, part).wait_recv()

                @pl.when(self._edge(way))
                def _():
                    self._copy(held, buf, sems, way, shard, part).start()

    def walk(self, buf, sems, work):
        last_part = SUBS - 1

        def visit(m, carry):
            k = (m + 1) // 2
            shard = jnp.where(m % 2 == 1, self.t - k, self.t + k)

            @pl.when((shard >= 0) & (shard < self.size))
            def _():
                work(shard)

            @pl.when(m == 0)
            def _():
                for part in range(last_part):
                    self.relay(1, part, buf, sems)

            @pl.when(m % 2 == 0)
            def _():
                self.relay(k + 1, last_part, buf, sems)

            @pl.when(m % 2 == 1)
            def _():
                for part in range(last_part):
                    self.relay(k + 1, part, buf, sems)

            return carry

        lax.fori_loop(0, 2 * self.size - 1, visit, 0)

    def scatter_step(self, way, j, part, terms, buf, sems, ends=None, early=None):
        t, last = self.t, self.size - 1
        shard = last - j if way == 0 else j
        beyond = (shard > t) if way == 0 else (shard < t)
        starts = (t == 0) if way == 0 else (t == last)
        step = min(32, self.sub)
        if ends is None:
            goes, stays = beyond, None
        else:
            goes = (shard > t + 1) if way == 0 else (shard < t - 1)
            stays = (shard == t + 1) if way == 0 else (shard == t - 1)

        second = (t == 1) if way == 0 else (t == last - 1)
        done = early is not None and j == 0

        if not done:

            @pl.when(goes & starts)
            def _():
                self._copy(self._rows(terms, shard, part), buf, sems, way, shard, part).start()

        @pl.when(goes & jnp.logical_not(starts))
        def _():
            held = self._rows(buf, shard, part)
            arrival = self._copy(held, buf, sems, way, shard, part)
            if not done:
                arrival.wait_recv()
            else:

                @pl.when(jnp.logical_not(second))
                def _():
                    arrival.wait_recv()

                if part == 0:

                    @pl.when(second)
                    def _():
                        early[way].wait()

            def add(i, carry):
                rows = pl.ds(part * self.sub + i * step, step)
                total = buf[shard, rows, :].astype(F32) + terms[shard, rows, :].astype(F32)
                buf[shard, rows, :] = total.astype(BF16)
                return carry

            lax.fori_loop(0, self.sub // step, add, 0)
            self._copy(held, buf, sems, way, shard, part).start()

        if stays is None:
            return

        @pl.when(stays & starts)
        def _():
            rows = pl.ds(part * self.sub, self.sub)
            ends[way, rows, :] = terms[shard, rows, :]

        @pl.when(stays & jnp.logical_not(starts))
        def _():
            held = self._rows(buf, shard, part)
            self._copy(held, buf, sems, way, shard, part).wait_recv()

            def add(i, carry):
                rows = pl.ds(part * self.sub + i * step, step)
                total = buf[shard, rows, :].astype(F32) + terms[shard, rows, :].astype(F32)
                ends[way, rows, :] = total.astype(BF16)
                return carry

            lax.fori_loop(0, self.sub // step, add, 0)

    def phase(self, gather=None, scatter=None, on_slot=None, near=None, ends=None):
        n = self.size
        for k in range(0 if near is None else 1, n):
            for part in range(SUBS):
                for way in (0, 1):
                    if gather is not None:
                        self.gather_step(way, k, part, gather[0], gather[1], gather[2], near)
                    if scatter is not None:
                        if gather is None:
                            if k < n - 1:
                                self.scatter_step(way, k, part, scatter[0], scatter[1][way], scatter[2])
                        else:
                            behind = self.t if way == 0 else n - 1 - self.t
                            for b in range(k):

                                @pl.when(behind == b)
                                def _(b=b, k=k, part=part, way=way):
                                    self.scatter_step(
                                        way, k - 1 - b, part, scatter[0], scatter[1][way],
                                        scatter[2], ends,
                                    )
            if on_slot is not None:
                on_slot(k)

    def own_wait(self, bufs, sems):
        for way in (0, 1):
            arrives = self.t > 0 if way == 0 else self.t < self.size - 1

            @pl.when(arrives)
            def _(way=way):
                for part in range(SUBS):
                    held = self._rows(bufs[way], self.t, part)
                    self._copy(held, bufs[way], sems, way, self.t, part).wait_recv()

    def own_sum(self, terms, bufs, rows):
        t = self.t
        zero = jnp.zeros((), F32)
        right = jnp.where(t > 0, bufs[0][t, rows, :].astype(F32), zero)
        left = jnp.where(t < self.size - 1, bufs[1][t, rows, :].astype(F32), zero)
        return terms[t, rows, :].astype(F32) + right + left

    def drain_gather(self, buf, sems, first=0):
        for way in (0, 1):
            for k in range(first, self.size):
                shard = self.t - k if way == 0 else self.t + k
                inside = (self.t >= k) if way == 0 else (self.t + k <= self.size - 1)

                @pl.when(inside & self._edge(way))
                def _(way=way, shard=shard):
                    for part in range(SUBS):
                        held = self._rows(buf, shard, part)
                        self._copy(held, buf, sems, way, shard, part).wait_send()

    def drain_scatter(self, bufs, sems, margin=0, early=False):
        for way in (0, 1):
            for j in range(self.size - 1):
                shard = self.size - 1 - j if way == 0 else j
                beyond = (shard > self.t + margin) if way == 0 else (shard < self.t - margin)
                if early and j == 0:
                    beyond = beyond & self._edge(1 - way)

                @pl.when(beyond)
                def _(way=way, shard=shard):
                    for part in range(SUBS):
                        held = self._rows(bufs[way], shard, part)
                        self._copy(held, bufs[way], sems, way, shard, part).wait_send()


def line_sems(size):
    return [pltpu.SemaphoreType.DMA((2, size, SUBS)), pltpu.SemaphoreType.DMA((2, size, SUBS))]


def fold(x):
    rows, width = x.shape
    return jnp.sum(x.reshape(rows // 8, 8, width), axis=0)


def normal(x):
    centre = x - jnp.mean(x, axis=-1, keepdims=True)
    spread = lax.rsqrt(jnp.mean(centre * centre, axis=-1, keepdims=True) + EPS)
    return centre * spread, spread


def normal_back(upstream, normed, spread, gain):
    scaled = upstream * gain
    mean_part = jnp.mean(scaled, axis=-1, keepdims=True)
    across = jnp.mean(scaled * normed, axis=-1, keepdims=True)
    return spread * (scaled - mean_part - normed * across)


def row_loop(rows, step, body):
    def one(i, carry):
        body(pl.ds(pl.multiple_of(i * step, step), step))
        return carry

    lax.fori_loop(0, rows // step, one, 0)


def params(collective_id=None):
    if collective_id is None:
        return pltpu.CompilerParams(vmem_limit_bytes=VMEM_CAP)
    return pltpu.CompilerParams(
        collective_id=collective_id, has_side_effects=True, vmem_limit_bytes=VMEM_CAP
    )


def first_kernel(n_dp, size, part, small, own, smalls, a_out, tok, send, recv, gs, gr):
    line = Line(size, own.shape[0])
    me = lax.axis_index("dp")
    rows, width = own.shape
    sem = pltpu.get_barrier_semaphore()
    for p in range(1, n_dp):
        pl.semaphore_signal(sem, device_id={"dp": lax.rem(me + p, n_dp)}, device_id_type=MESH)
    ends = line.greet(sem)
    pl.semaphore_wait(sem, ends + n_dp - 1)
    sems = (gs, gr)

    def small_copy(p, slot):
        return pltpu.make_async_remote_copy(
            src_ref=small,
            dst_ref=smalls.at[slot],
            send_sem=send.at[p],
            recv_sem=recv.at[slot],
            device_id={"dp": lax.rem(me + p, n_dp)},
            device_id_type=MESH,
        )

    for p in range(1, n_dp):
        small_copy(p, me).start()
    smalls[pl.ds(me, 1)] = small[...][None]
    step = min(32, rows)
    vec_rows = part // 128

    def normalise(source, shard):
        gain = jnp.concatenate(
            [smalls[d, r : r + 1, :] for d in range(n_dp) for r in range(vec_rows)], axis=1
        ).astype(F32)
        shift = jnp.concatenate(
            [smalls[d, r : r + 1, :] for d in range(n_dp) for r in range(vec_rows, 2 * vec_rows)],
            axis=1,
        ).astype(F32)

        def body(at):
            x = source[at, :] if shard is None else source[shard, at, :]
            normed, _ = normal(x.astype(F32))
            to = line.t if shard is None else shard
            a_out[to, at, :] = (normed * gain + shift).astype(BF16)

        row_loop(rows, step, body)

    def on_slot(k):
        if k == 0:
            for p in range(1, n_dp):
                small_copy(p, lax.rem(me + p, n_dp)).wait_recv()
            normalise(own, None)
        else:

            @pl.when(line.t >= k)
            def _():
                normalise(tok, line.t - k)

            @pl.when(line.t + k <= size - 1)
            def _():
                normalise(tok, line.t + k)

    line.phase(gather=(tok, sems, own), on_slot=on_slot)
    line.drain_gather(tok, sems)
    for p in range(1, n_dp):
        small_copy(p, me).wait_send()


def first(small, own, part, n_dp, size, cid):
    rows, width = own.shape
    return pl.pallas_call(
        functools.partial(first_kernel, n_dp, size, part),
        out_shape=(
            jax.ShapeDtypeStruct((n_dp,) + small.shape, small.dtype),
            jax.ShapeDtypeStruct((size, rows, width), BF16),
        ),
        in_specs=[WHOLE, WHOLE],
        out_specs=(WHOLE, WHOLE),
        scratch_shapes=[
            pltpu.VMEM((size, rows, width), BF16),
            pltpu.SemaphoreType.DMA((n_dp,)),
            pltpu.SemaphoreType.DMA((n_dp,)),
        ]
        + line_sems(size),
        compiler_params=params(cid),
        name="first",
    )(small, own)


def middle_kernel(
    size, terms, cot, near, tok, valid, vecs, c_out, gm_out, mid_out, stats,
    right, left, gs, gr, ss, sr, near_sem,
):
    line = Line(size, tok.shape[0])
    rows = tok.shape[0]
    step = min(32, rows)
    line.barrier()

    def keep(way):
        shard = line.t - 1 if way == 0 else line.t + 1
        return pltpu.make_async_copy(near.at[way], gm_out.at[shard], near_sem.at[way])

    def keep_all(act):
        for way in (0, 1):

            @pl.when(line._edge(1 - way))
            def _(way=way):
                act(keep(way))

    keep_all(lambda copy: copy.start())
    line.phase(
        gather=(gm_out, (gs, gr), None), scatter=(terms, (right, left), (ss, sr)), near=near
    )
    gm_out[pl.ds(line.t, 1)] = cot[...][None]
    keep_all(lambda copy: copy.wait())
    line.own_wait((right, left), (ss, sr))
    stats[...] = jnp.zeros_like(stats)

    def body(at):
        attn = line.own_sum(terms, (right, left), at) + vecs[2:3, :]
        x = tok[at, :].astype(F32)
        mid = x + attn
        normed, _ = normal(mid)
        c_out[at, :] = (normed * vecs[3:4, :] + vecs[4:5, :]).astype(BF16)
        mid_out[at, :] = mid
        ok = valid[at, 0:1]
        stats[0:8, :] += fold(ok * x * x)
        stats[8:16, :] += fold(ok * attn * attn)
        stats[16:24, :] += fold(ok * mid * mid)

    row_loop(rows, step, body)
    line.drain_gather(gm_out, (gs, gr), 1)
    line.drain_scatter((right, left), (ss, sr))


def middle(terms, cot, near, tok, valid, vecs, size, cid):
    rows, width = tok.shape
    full = (size, rows, width)
    return pl.pallas_call(
        functools.partial(middle_kernel, size),
        out_shape=(
            jax.ShapeDtypeStruct((rows, width), BF16),
            jax.ShapeDtypeStruct(full, BF16),
            jax.ShapeDtypeStruct((rows, width), F32),
            jax.ShapeDtypeStruct((24, width), F32),
        ),
        in_specs=[WHOLE, WHOLE, HBM, WHOLE, WHOLE, WHOLE],
        out_specs=(WHOLE,) * 4,
        scratch_shapes=[pltpu.VMEM(full, BF16), pltpu.VMEM(full, BF16)]
        + line_sems(size)
        + line_sems(size)
        + [pltpu.SemaphoreType.DMA((2,))],
        compiler_params=params(cid),
        name="middle",
    )(terms, cot, near, tok, valid, vecs)


def back_middle_kernel(
    size, terms, landed, mlp, gm, mid, vecs, out_w, gz_out, gmid_out, ends, stats,
    go_out, right, left, right2, left2, ss, sr, ms, mr, gs, gr, early_sem,
):
    line = Line(size, mid.shape[0])
    rows = mid.shape[0]
    step = min(32, rows)
    early = line.early_start(landed, (right, left), early_sem)
    line.barrier()
    for j in range(size - 1):
        for piece in range(SUBS):
            for way in (0, 1):
                line.scatter_step(
                    way, j, piece, terms, (right, left)[way], (ss, sr), None, early
                )
    line.own_wait((right, left), (ss, sr))
    stats[...] = jnp.zeros_like(stats)

    def body(at):
        e = line.own_sum(terms, (right, left), at)
        normed, spread = normal(mid[at, :])
        gy = gm[at, :].astype(F32)
        gmid = gy + normal_back(e, normed, spread, vecs[3:4, :])
        gz_out[line.t, at, :] = gmid.astype(BF16)
        gmid_out[at, :] = gmid
        stats[0:8, :] += fold(e * normed)
        stats[8:16, :] += fold(e)
        stats[16:24, :] += fold(gmid)
        stats[24:32, :] += fold(gy)

    row_loop(rows, step, body)
    def weigh(shard):
        go_out[shard] = dot_t(gz_out[shard], out_w[...]).astype(BF16)

    def on_slot(k):
        def side(i, carry):
            shard = line.t + k * (2 * i - 1)

            @pl.when((shard >= 0) & (shard < size))
            def _():
                weigh(shard)

            return carry

        lax.fori_loop(0, 1 if k == 0 else 2, side, 0)

    line.phase(
        gather=(gz_out, (gs, gr), None),
        scatter=(mlp, (right2, left2), (ms, mr)),
        on_slot=on_slot,
        ends=ends,
    )
    line.drain_scatter((right, left), (ss, sr), 0, True)
    line.drain_scatter((right2, left2), (ms, mr), 1)
    line.drain_gather(gz_out, (gs, gr))


def back_middle(terms, landed, mlp, gm, mid, vecs, out_w, size, cid):
    rows, width = mid.shape
    local = out_w.shape[0]
    full = (size, rows, width)
    return pl.pallas_call(
        functools.partial(back_middle_kernel, size),
        out_shape=(
            jax.ShapeDtypeStruct(full, BF16),
            jax.ShapeDtypeStruct((rows, width), F32),
            jax.ShapeDtypeStruct((2, rows, width), BF16),
            jax.ShapeDtypeStruct((32, width), F32),
            jax.ShapeDtypeStruct((size, rows, local), BF16),
        ),
        in_specs=[WHOLE, HBM] + [WHOLE] * 5,
        out_specs=(WHOLE,) * 5,
        scratch_shapes=[pltpu.VMEM(full, BF16)] * 4
        + line_sems(size)
        + line_sems(size)
        + line_sems(size)
        + [pltpu.SemaphoreType.DMA((2,))],
        compiler_params=params(cid),
        name="back_middle",
    )(terms, landed, mlp, gm, mid, vecs, out_w)


def finish_kernel(
    size, terms, first_landed, tok, gmid, mlp, landed, mid, valid, vecs, grad_out, y_out, stats,
    right, left, own_mlp, ends, ss, sr, load_sem, early_sem,
):
    line = Line(size, tok.shape[0])
    rows = tok.shape[0]
    step = min(32, rows)
    loads = [
        pltpu.make_async_copy(mlp.at[line.t], own_mlp, load_sem.at[0]),
        pltpu.make_async_copy(landed, ends, load_sem.at[1]),
    ]
    early = line.early_start(first_landed, (right, left), early_sem)
    for load in loads:
        load.start()
    line.barrier()
    stats[...] = jnp.zeros_like(stats)

    def tail(at):
        zero = jnp.zeros((), F32)
        from_left = jnp.where(line.t > 0, ends[0, at, :].astype(F32), zero)
        from_right = jnp.where(line.t < size - 1, ends[1, at, :].astype(F32), zero)
        out = own_mlp[at, :].astype(F32) + from_left + from_right + vecs[5:6, :]
        y = mid[at, :] + out
        y_out[at, :] = y.astype(BF16)
        ok = valid[at, 0:1]
        stats[16:24, :] += fold(ok * out * out)
        stats[24:32, :] += fold(ok * y * y)

    for j in range(size - 1):
        for piece in range(SUBS):
            for way in (0, 1):
                line.scatter_step(
                    way, j, piece, terms, (right, left)[way], (ss, sr), None, early
                )
        if j == 0:
            for load in loads:
                load.wait()
            row_loop(rows, step, tail)
    line.own_wait((right, left), (ss, sr))

    def body(at):
        e = line.own_sum(terms, (right, left), at)
        normed, spread = normal(tok[at, :].astype(F32))
        grad_out[at, :] = gmid[at, :] + normal_back(e, normed, spread, vecs[0:1, :])
        stats[0:8, :] += fold(e * normed)
        stats[8:16, :] += fold(e)

    row_loop(rows, step, body)
    line.drain_scatter((right, left), (ss, sr), 0, True)


def finish(terms, first_landed, tok, gmid, mlp, landed, mid, valid, vecs, size, cid):
    rows, width = tok.shape
    full = (size, rows, width)
    return pl.pallas_call(
        functools.partial(finish_kernel, size),
        out_shape=(
            jax.ShapeDtypeStruct((rows, width), F32),
            jax.ShapeDtypeStruct((rows, width), BF16),
            jax.ShapeDtypeStruct((32, width), F32),
        ),
        in_specs=[WHOLE, HBM, WHOLE, WHOLE, HBM, HBM, WHOLE, WHOLE, WHOLE],
        out_specs=(WHOLE,) * 3,
        scratch_shapes=[pltpu.VMEM(full, BF16)] * 2
        + [pltpu.VMEM((rows, width), BF16), pltpu.VMEM((2, rows, width), BF16)]
        + line_sems(size)
        + [pltpu.SemaphoreType.DMA((2,)), pltpu.SemaphoreType.DMA((2,))],
        compiler_params=params(cid),
        name="finish",
    )(terms, first_landed, tok, gmid, mlp, landed, mid, valid, vecs)


def reduce_small_kernel(n_dp, n_t, shared, blocks, out, land, sums, land2, s1, r1, s2, r2):
    me, t = lax.axis_index("dp"), lax.axis_index("tensor")
    sem = pltpu.get_barrier_semaphore()
    for p in range(1, n_dp):
        pl.semaphore_signal(sem, device_id={"dp": lax.rem(me + p, n_dp)}, device_id_type=MESH)
    for p in range(1, n_t):
        pl.semaphore_signal(sem, device_id={"tensor": lax.rem(t + p, n_t)}, device_id_type=MESH)
    pl.semaphore_wait(sem, n_dp + n_t - 2)

    def one(p):
        other = lax.rem(me + p, n_dp)
        return pltpu.make_async_remote_copy(
            src_ref=blocks.at[other],
            dst_ref=land.at[p],
            send_sem=s1.at[p],
            recv_sem=r1.at[p],
            device_id={"dp": other},
            device_id_type=MESH,
        )

    for p in range(1, n_dp):
        one(p).start()
    total = blocks[me]
    for p in range(1, n_dp):
        one(p).wait_recv()
        total = total + land[p]
    sums[...] = total

    def two(p):
        return pltpu.make_async_remote_copy(
            src_ref=sums.at[pl.ds(0, shared)],
            dst_ref=land2.at[p],
            send_sem=s2.at[p],
            recv_sem=r2.at[p],
            device_id={"tensor": lax.rem(t + p, n_t)},
            device_id_type=MESH,
        )

    for p in range(1, n_t):
        two(p).start()
    out[...] = total
    top = sums[pl.ds(0, shared), :]
    for p in range(1, n_t):
        two(p).wait_recv()
        top = top + land2[p]
    out[pl.ds(0, shared), :] = top
    for p in range(1, n_dp):
        one(p).wait_send()
    for p in range(1, n_t):
        two(p).wait_send()


def reduce_small(blocks, shared, n_dp, n_t, cid):
    _, rows, width = blocks.shape
    return pl.pallas_call(
        functools.partial(reduce_small_kernel, n_dp, n_t, shared),
        out_shape=jax.ShapeDtypeStruct((rows, width), F32),
        in_specs=[WHOLE],
        out_specs=WHOLE,
        scratch_shapes=[
            pltpu.VMEM((n_dp, rows, width), F32),
            pltpu.VMEM((rows, width), F32),
            pltpu.VMEM((n_t, shared, width), F32),
            pltpu.SemaphoreType.DMA((n_dp,)),
            pltpu.SemaphoreType.DMA((n_dp,)),
            pltpu.SemaphoreType.DMA((n_t,)),
            pltpu.SemaphoreType.DMA((n_t,)),
        ],
        compiler_params=params(cid),
        name="reduce_small",
    )(blocks)


BLOCK = 256
NEG = -1e30
SCALE = HD**-0.5


def dot(a, b):
    return jnp.dot(a, b, preferred_element_type=F32)


def dot_t(a, b):
    return lax.dot_general(a, b, (((1,), (1,)), ((), ())), preferred_element_type=F32)


def masked_scores(q, k, keys, first, bar):
    scores = dot_t(k, q) * SCALE + bar
    key_pos = lax.broadcasted_iota(jnp.int32, (keys, BLOCK), 0)
    query_pos = first + lax.broadcasted_iota(jnp.int32, (keys, BLOCK), 1)
    return jnp.where(key_pos <= query_pos, scores, NEG)


def head_cols(part, h, heads):
    return pl.ds(pl.multiple_of((part * heads + h) * HD, HD), HD)


def front_kernel(
    size, heads, a, weights, shift, bar, out_w, cot, qkv, mixed_all, log_totals, terms, near,
    cols, gs, gr, load_sem,
):
    h = pl.program_id(0)
    rows = cot.shape[0]
    local = heads * HD
    line = Line(size, rows)

    def load(part):
        at = pl.ds(part * local, local)
        return pltpu.make_async_copy(weights.at[:, at], cols.at[:, at], load_sem.at[part])

    @pl.when(h == 0)
    def _():
        for part in range(3):
            load(part).start()
        line.barrier()
        line.hop_start((cot, cot), near, (gs, gr))
        for part in range(3):
            load(part).wait()
            span = slice(part * local, (part + 1) * local)

            def product(at, span=span):
                qkv[at, span] = (dot(a[at, :], cols[:, span]) + shift[0:1, span]).astype(BF16)

            row_loop(LEN, min(256, LEN), product)

    at_q, at_k, at_v = (head_cols(part, h, heads) for part in range(3))
    value_cols = qkv[:, at_v].T
    for block in range(LEN // BLOCK):
        first, keys = block * BLOCK, (block + 1) * BLOCK
        here = slice(first, first + BLOCK)
        scores = masked_scores(qkv[here, at_q], qkv[0:keys, at_k], keys, first, bar[0:keys, 0:1])
        top = jnp.max(scores, axis=0, keepdims=True)
        powers = jnp.exp(scores - top)
        total = jnp.sum(powers, axis=0, keepdims=True)
        shares = (powers * (1.0 / total)).astype(BF16)
        mixed = dot(value_cols[:, 0:keys], shares)
        mixed_all[here, head_cols(0, h, heads)] = mixed.T.astype(BF16)
        log_totals[0, :, here] = jnp.broadcast_to(top + jnp.log(total), (8, BLOCK))

    @pl.when(h == heads - 1)
    def _():
        def project(at):
            terms[at, :] = dot(mixed_all[at, :], out_w[...]).astype(BF16)

        row_loop(LEN, min(256, LEN), project)
        line.hop_wait((cot, cot), near, (gs, gr))


def front(a, weights, shift, bar, out_w, cot, size, cid):
    width, local3 = weights.shape
    local = local3 // 3
    heads = local // HD
    return pl.pallas_call(
        functools.partial(front_kernel, size, heads),
        grid=(heads,),
        out_shape=(
            jax.ShapeDtypeStruct((LEN, local3), BF16),
            jax.ShapeDtypeStruct((LEN, local), BF16),
            jax.ShapeDtypeStruct((heads, 8, LEN), F32),
            jax.ShapeDtypeStruct((LEN, width), BF16),
            jax.ShapeDtypeStruct((2,) + cot.shape, BF16),
        ),
        in_specs=[WHOLE, HBM, WHOLE, WHOLE, WHOLE, HBM],
        out_specs=(
            pl.BlockSpec((LEN, local3), lambda h: (0, 0)),
            pl.BlockSpec((LEN, local), lambda h: (0, 0)),
            pl.BlockSpec((1, 8, LEN), lambda h: (h, 0, 0)),
            pl.BlockSpec((LEN, width), lambda h: (0, 0)),
            HBM,
        ),
        scratch_shapes=[
            pltpu.VMEM((width, local3), BF16),
            pltpu.SemaphoreType.DMA((2,)),
            pltpu.SemaphoreType.DMA((2,)),
            pltpu.SemaphoreType.DMA((3,)),
        ],
        compiler_params=params(cid),
        name="front",
    )(a, weights, shift, bar, out_w, cot)


def attend_back_kernel(
    size, heads, q, k, v, go, bar, log_totals, weights, ends, out, sums, terms, landed,
    key_grad, value_grad, cols, gs, gr, load_sem,
):
    h = pl.program_id(0)
    line = Line(size, ends.shape[1])
    srcs = (ends.at[0], ends.at[1])
    load = pltpu.make_async_copy(weights, cols, load_sem.at[0])

    @pl.when(h == 0)
    def _():
        load.start()
        line.barrier()
        line.hop_start(srcs, landed, (gs, gr))

    key_cols = k[...].T
    query_sum = jnp.zeros((1, HD), F32)
    at_q, at_k, at_v = (head_cols(part, h, heads) for part in range(3))
    for block in range(LEN // BLOCK - 1, -1, -1):
        first, keys = block * BLOCK, (block + 1) * BLOCK
        here = slice(first, first + BLOCK)
        scores = masked_scores(q[here, :], k[0:keys, :], keys, first, bar[0:keys, 0:1])
        shares = jnp.exp(scores - log_totals[0, 0:1, here])
        share_grad = dot_t(v[0:keys, :], go[here, :])
        centre = jnp.sum(shares * share_grad, axis=0, keepdims=True)
        score_grad = (shares * (share_grad - centre)).astype(BF16)
        values = dot(shares.astype(BF16), go[here, :])
        keyed = dot(score_grad, q[here, :])
        if block == LEN // BLOCK - 1:
            value_grad[...] = values
            key_grad[...] = keyed
        else:
            value_grad[0:keys, :] += values
            key_grad[0:keys, :] += keyed
        query_grad = ((dot(key_cols[:, 0:keys], score_grad)) * SCALE).T.astype(BF16)
        out[here, at_q] = query_grad
        query_sum = query_sum + jnp.sum(query_grad.astype(F32), axis=0, keepdims=True)
    out[:, at_k] = (key_grad[...] * SCALE).astype(BF16)
    rounded = value_grad[...].astype(BF16)
    out[:, at_v] = rounded
    value_sum = jnp.sum(rounded.astype(F32), axis=0, keepdims=True)
    sums[0, 0:8, :] = jnp.broadcast_to(query_sum, (8, HD))
    sums[0, 8:16, :] = jnp.broadcast_to(value_sum, (8, HD))

    @pl.when(h == heads - 1)
    def _():
        load.wait()

        def product(at):
            terms[at, :] = dot_t(out[at, :], cols[...]).astype(BF16)

        row_loop(LEN, min(256, LEN), product)
        line.hop_wait(srcs, landed, (gs, gr))


def attend_back(qkv, go, bar, log_totals, weights, ends, size, cid):
    width, local3 = weights.shape
    heads = local3 // 3 // HD

    def column(part):
        return pl.BlockSpec((LEN, HD), lambda h: (0, part * heads + h))

    return pl.pallas_call(
        functools.partial(attend_back_kernel, size, heads),
        grid=(heads,),
        out_shape=(
            jax.ShapeDtypeStruct((LEN, local3), BF16),
            jax.ShapeDtypeStruct((heads, 16, HD), F32),
            jax.ShapeDtypeStruct((LEN, width), BF16),
            jax.ShapeDtypeStruct(ends.shape, BF16),
        ),
        in_specs=[
            column(0), column(1), column(2), column(0),
            pl.BlockSpec((LEN, 128), lambda h: (0, 0)),
            pl.BlockSpec((1, 8, LEN), lambda h: (h, 0, 0)),
            HBM, HBM,
        ],
        out_specs=(
            pl.BlockSpec((LEN, local3), lambda h: (0, 0)),
            pl.BlockSpec((1, 16, HD), lambda h: (h, 0, 0)),
            pl.BlockSpec((LEN, width), lambda h: (0, 0)),
            HBM,
        ),
        scratch_shapes=[
            pltpu.VMEM((LEN, HD), F32),
            pltpu.VMEM((LEN, HD), F32),
            pltpu.VMEM((width, local3), BF16),
            pltpu.SemaphoreType.DMA((2,)),
            pltpu.SemaphoreType.DMA((2,)),
            pltpu.SemaphoreType.DMA((1,)),
        ],
        compiler_params=params(cid),
        name="attend_back",
    )(qkv, qkv, qkv, go, bar, log_totals, weights, ends)


def gelu_both(u):
    inner = 0.7978845608028654 * (u + 0.044715 * (u * u * u))
    th = jnp.tanh(inner)
    half = 0.5 * (1.0 + th)
    slope = half + 0.5 * u * (1.0 - th * th) * (
        0.7978845608028654 * (1.0 + 3 * 0.044715 * (u * u))
    )
    return u * half, slope


def hidden_kernel(
    n_dp, size, c_own, gm, up_in, down_in, bias, c_out, act_out, gu_out, mlp_out, back_out, sums,
    up, down, act, gu, mlp, back, gs, gr, in_sem, out_sem,
):
    line = Line(size, c_own.shape[0])
    rows, width = c_own.shape
    units, part = down.shape[1], down.shape[2]
    block = min(512, units)
    loads = [
        pltpu.make_async_copy(up_in, up, in_sem.at[0]),
        pltpu.make_async_copy(down_in, down, in_sem.at[1]),
    ]
    for load in loads:
        load.start()
    line.barrier()
    for piece in range(SUBS):
        for way in (0, 1):
            line.gather_step(way, 0, piece, c_out, (gs, gr), c_own)
    c_out[pl.ds(line.t, 1)] = c_own[...][None]
    sums[...] = jnp.zeros_like(sums)
    for load in loads:
        load.wait()

    def stores(shard):
        pairs = ((act, act_out), (gu, gu_out), (mlp, mlp_out), (back, back_out))
        return [
            pltpu.make_async_copy(src.at[shard], dst.at[shard], out_sem.at[i, shard])
            for i, (src, dst) in enumerate(pairs)
        ]

    def work(shard):
        def unit_block(j, carry):
            at = pl.ds(pl.multiple_of(j * block, block), block)
            u = dot(c_out[shard], up[:, at]) + bias[0:1, at]
            grad = dot_t(gm[shard, :, 0:part], down[0, at, :])
            for d in range(1, n_dp):
                grad = grad + dot_t(gm[shard, :, d * part : (d + 1) * part], down[d, at, :])
            value, slope = gelu_both(u)
            act[shard, :, at] = value.astype(BF16)
            rounded = (grad * slope).astype(BF16)
            gu[shard, :, at] = rounded
            sums[:, at] += fold(rounded.astype(F32))
            return carry

        lax.fori_loop(0, units // block, unit_block, 0)

        def feature_block(d, carry):
            at = pl.ds(pl.multiple_of(d * part, part), part)
            mlp[shard, :, at] = dot(act[shard], down[d]).astype(BF16)
            back[shard, :, at] = dot_t(gu[shard], up[at, :]).astype(BF16)
            return carry

        lax.fori_loop(0, n_dp, feature_block, 0)
        for store in stores(shard):
            store.start()

    line.walk(c_out, (gs, gr), work)
    line.drain_gather(c_out, (gs, gr))
    for shard in range(size):
        for store in stores(shard):
            store.wait()


def hidden(c_own, gm, up, down, bias, size, cid):
    rows, width = c_own.shape
    n_dp, units, part = down.shape
    full, wide = (size, rows, width), (size, rows, units)
    return pl.pallas_call(
        functools.partial(hidden_kernel, n_dp, size),
        out_shape=(
            jax.ShapeDtypeStruct(full, BF16),
            jax.ShapeDtypeStruct(wide, BF16),
            jax.ShapeDtypeStruct(wide, BF16),
            jax.ShapeDtypeStruct(full, BF16),
            jax.ShapeDtypeStruct(full, BF16),
            jax.ShapeDtypeStruct((8, units), F32),
        ),
        in_specs=[WHOLE, WHOLE, HBM, HBM, WHOLE],
        out_specs=(WHOLE, HBM, HBM, HBM, HBM, WHOLE),
        scratch_shapes=[
            pltpu.VMEM((width, units), BF16),
            pltpu.VMEM((n_dp, units, part), BF16),
            pltpu.VMEM(wide, BF16),
            pltpu.VMEM(wide, BF16),
            pltpu.VMEM(full, BF16),
            pltpu.VMEM(full, BF16),
        ]
        + line_sems(size)
        + [pltpu.SemaphoreType.DMA((2,)), pltpu.SemaphoreType.DMA((4, size))],
        compiler_params=params(cid),
        name="hidden",
    )(c_own, gm, up, down, bias)


def cross(left, right):
    return lax.dot_general(left, right, (((0,), (0,)), ((), ())), preferred_element_type=F32)


def products_kernel(
    size, steps, act, gm, c, gu_in, terms, down_out, up_out, landed, gu, gs, gr, load_sem
):
    i = pl.program_id(0)
    line = Line(size, terms.shape[1])
    load = pltpu.make_async_copy(gu_in, gu, load_sem.at[0])
    hops = line.first_hops(terms, landed, (gs, gr))

    @pl.when(i == 0)
    def _():
        load.start()
        line.barrier()
        line.hops_start(hops)

    @pl.when(i < steps)
    def _():
        down_out[...] = cross(act[...], gm[...]).astype(BF16)

    @pl.when(i == steps)
    def _():
        load.wait()

    @pl.when(i >= steps)
    def _():
        up_out[...] = cross(c[...], gu[...]).astype(BF16)

    @pl.when(i == pl.num_programs(0) - 1)
    def _():
        line.hops_wait(hops)


def products(act, gm, c, gu, terms, size, cid):
    rows, units = act.shape
    width = gm.shape[1]
    steps, more = units // BLOCK, width // BLOCK
    return pl.pallas_call(
        functools.partial(products_kernel, size, steps),
        grid=(steps + more,),
        out_shape=(
            jax.ShapeDtypeStruct((units, width), BF16),
            jax.ShapeDtypeStruct((width, units), BF16),
            jax.ShapeDtypeStruct((2,) + terms.shape[1:], BF16),
        ),
        in_specs=[
            pl.BlockSpec((rows, BLOCK), lambda i: (0, jnp.minimum(i, steps - 1))),
            WHOLE,
            pl.BlockSpec((rows, BLOCK), lambda i: (0, jnp.maximum(i - steps, 0))),
            HBM,
            HBM,
        ],
        out_specs=(
            pl.BlockSpec((BLOCK, width), lambda i: (jnp.minimum(i, steps - 1), 0)),
            pl.BlockSpec((BLOCK, units), lambda i: (jnp.maximum(i - steps, 0), 0)),
            HBM,
        ),
        scratch_shapes=[
            pltpu.VMEM((rows, units), BF16),
            pltpu.SemaphoreType.DMA((2,)),
            pltpu.SemaphoreType.DMA((2,)),
            pltpu.SemaphoreType.DMA((1,)),
        ],
        compiler_params=params(cid),
        name="products",
    )(act, gm, c, gu, terms)


def head_products_kernel(size, gz, a, o, gqkv, terms, out, landed, gs, gr):
    i = pl.program_id(0)
    line = Line(size, terms.shape[1])
    hops = line.first_hops(terms, landed, (gs, gr))
    local = o.shape[1]

    @pl.when(i == 0)
    def _():
        line.barrier()
        line.hops_start(hops)

    out[:, 0:local] = cross(gz[...], o[...]).astype(BF16)
    out[:, local:] = cross(a[...], gqkv[...]).astype(BF16)

    @pl.when(i == pl.num_programs(0) - 1)
    def _():
        line.hops_wait(hops)


def head_products(gz, a, o, gqkv, terms, size, cid):
    rows, width = a.shape
    columns = o.shape[1] + gqkv.shape[1]
    return pl.pallas_call(
        functools.partial(head_products_kernel, size),
        grid=(width // BLOCK,),
        out_shape=(
            jax.ShapeDtypeStruct((width, columns), BF16),
            jax.ShapeDtypeStruct((2,) + terms.shape[1:], BF16),
        ),
        in_specs=[
            pl.BlockSpec((rows, BLOCK), lambda i: (0, i)),
            pl.BlockSpec((rows, BLOCK), lambda i: (0, i)),
            WHOLE,
            WHOLE,
            HBM,
        ],
        out_specs=(pl.BlockSpec((BLOCK, columns), lambda i: (i, 0)), HBM),
        scratch_shapes=[pltpu.SemaphoreType.DMA((2,)), pltpu.SemaphoreType.DMA((2,))],
        compiler_params=params(cid),
        name="head_products",
    )(gz, a, o, gqkv, terms)


def pad_to(x, count):
    return jnp.pad(x, ((0, 0), (0, count - x.shape[1])))


def shards(
    tokens, lengths, ln1_gain, ln1_bias, qkv_weight, qv_bias, out_weight, out_bias,
    ln2_gain, ln2_bias, up_weight, up_bias, down_weight, down_bias, cotangent,
):
    n_dp, n_t = lax.axis_size("dp"), lax.axis_size("tensor")
    rows, width = tokens.shape
    part = ln1_gain.shape[0]
    local = qkv_weight.shape[2]
    heads = local // HD
    units = up_weight.shape[1]
    hd_part = qv_bias.shape[2]
    t = lax.axis_index("tensor")
    length = lengths[0]

    pieces = [
        ln1_gain, ln1_bias, out_bias, ln2_gain, ln2_bias, down_bias,
        qv_bias.reshape(-1), up_bias.reshape(-1),
    ]
    packed = jnp.concatenate(pieces)
    count = packed.shape[0]
    lanes = -(-count // 2048) * 2048
    small = jnp.pad(packed, (0, lanes - count)).reshape(lanes // 128, 128)
    smalls, a = first(small, tokens, part, n_dp, n_t, 0)
    smalls, a = smalls.reshape(n_dp, lanes), a.reshape(n_t * rows, width)
    vecs = jnp.stack([smalls[:, i * part : (i + 1) * part].reshape(width) for i in range(6)])
    vecs = jnp.pad(vecs, ((0, 2), (0, 0))).astype(F32)
    at = 6 * part
    qv_all = smalls[:, at : at + 2 * heads * hd_part].reshape(n_dp, 2, heads, hd_part)
    qv_all = qv_all.transpose(1, 2, 0, 3).reshape(2, local).astype(F32)
    at += 2 * heads * hd_part
    up_all = smalls[:, at : at + units // n_dp].reshape(n_dp, units // 16, 16 // n_dp)
    up_shift = up_all.transpose(1, 0, 2).reshape(1, units).astype(F32)
    qkv_shift = jnp.concatenate([qv_all[0], jnp.zeros_like(qv_all[0]), qv_all[1]])

    qkv_full = lax.all_gather(qkv_weight.reshape(part, 3 * local), "dp", axis=0, tiled=True)
    out_full = lax.all_gather(out_weight, "dp", axis=1, tiled=True)
    up_full = lax.all_gather(up_weight, "dp", axis=0, tiled=True)
    down_blocks = lax.all_gather(down_weight, "dp", axis=0, tiled=False)

    own_pos = t * rows + jnp.arange(rows, dtype=jnp.int32)
    valid_own = (own_pos < length).astype(F32)
    valid = jnp.broadcast_to(valid_own[:, None], (rows, 128))
    positions = jnp.arange(LEN, dtype=jnp.int32)
    bar = jnp.broadcast_to(jnp.where(positions < length, 0.0, NEG)[:, None], (LEN, 128))
    gm_own = (cotangent.astype(F32) * valid_own[:, None]).astype(BF16)

    shift = jnp.broadcast_to(qkv_shift, (8, 3 * local))
    qkv, attended, log_totals, terms, near = front(
        a, qkv_full, shift, bar, out_full, gm_own, n_t, 7
    )
    terms = terms.reshape(n_t, rows, width)
    c_own, gm, mid, stats_a = middle(terms, gm_own, near, tokens, valid, vecs, n_t, 2)
    c, act, gu, mlp, back_terms, up_sums = hidden(
        c_own, gm, up_full, down_blocks, jnp.broadcast_to(up_shift, (8, units)), n_t, 6
    )
    c, gm = c.reshape(-1, width), gm.reshape(-1, width)
    act, gu = act.reshape(-1, units), gu.reshape(-1, units)

    down_grad, up_grad, early = products(act, gm, c, gu, back_terms, n_t, 9)
    down_out = lax.psum_scatter(down_grad, "dp", scatter_dimension=1, tiled=True)
    up_out = lax.psum_scatter(up_grad, "dp", scatter_dimension=0, tiled=True)
    gz, gmid, ends, stats_b, go = back_middle(
        back_terms, early, mlp, gm_own, mid, vecs, out_full, n_t, 3
    )
    gqkv, head_sums, last_terms, landed = attend_back(
        qkv, go.reshape(-1, local), bar, log_totals, qkv_full, ends, n_t, 8
    )
    last_terms = last_terms.reshape(n_t, rows, width)
    head_grad, last_early = head_products(
        gz.reshape(-1, width), a, attended, gqkv, last_terms, n_t, 10
    )
    last_early, head_grad, down_out, up_out = lax.optimization_barrier(
        (last_early, head_grad, down_out, up_out)
    )
    head_out = lax.psum_scatter(head_grad, "dp", scatter_dimension=0, tiled=True)
    out_out = head_out[:, :local].T
    qkv_out = head_out[:, local:].reshape(part, 3, local)
    tokens_grad, output, stats_c = finish(
        last_terms, last_early, tokens, gmid, mlp, landed, mid, valid, vecs, n_t, 4
    )

    def vec_sum(stats, i):
        return jnp.sum(stats[8 * i : 8 * i + 8], axis=0)

    vectors = jnp.stack(
        [
            vec_sum(stats_c, 0), vec_sum(stats_c, 1), vec_sum(stats_b, 2),
            vec_sum(stats_b, 0), vec_sum(stats_b, 1), vec_sum(stats_b, 3),
        ]
    )
    def squares(stats, i):
        return jnp.sum(stats[8 * i : 8 * i + 8].reshape(8, n_dp, part), axis=(0, 1))

    sums = jnp.concatenate(
        [
            squares(stats_a, 0), squares(stats_a, 1), squares(stats_a, 2),
            squares(stats_c, 2), squares(stats_c, 3),
        ]
    )
    count = jnp.clip(length - t * rows, 0, rows).astype(F32)
    vector_blocks = vectors.reshape(6, n_dp, part).transpose(1, 0, 2).reshape(n_dp, 6 * part)
    top = jnp.concatenate(
        [vector_blocks, jnp.broadcast_to(sums[None], (n_dp, 5 * part)), jnp.full((n_dp, 1), count)],
        axis=1,
    )
    top_len = -(-top.shape[1] // 1024) * 1024
    up_blocks = jnp.sum(up_sums, axis=0).reshape(units // 16, n_dp, 16 // n_dp)
    up_blocks = up_blocks.transpose(1, 0, 2).reshape(n_dp, units // n_dp)
    qv_sums = jnp.stack([head_sums[:, 0], head_sums[:, 8]])
    qv_blocks = qv_sums.reshape(2, heads, n_dp, hd_part).transpose(2, 0, 1, 3)
    qv_blocks = qv_blocks.reshape(n_dp, 2 * heads * hd_part)
    low = jnp.concatenate([up_blocks, qv_blocks], axis=1)
    low_len = -(-low.shape[1] // 1024) * 1024
    blocks = jnp.concatenate([pad_to(top, top_len), pad_to(low, low_len)], axis=1)
    blocks = blocks.reshape(n_dp, (top_len + low_len) // 128, 128)
    reduced = reduce_small(blocks, top_len // 128, n_dp, n_t, 5).reshape(-1)
    outs = [reduced[i * part : (i + 1) * part] for i in range(6)]
    totals = jnp.sum(reduced[6 * part : 11 * part].reshape(5, part), axis=1)
    stream_rms = jnp.sqrt(totals / (reduced[11 * part] * width))
    at = top_len
    up_bias_out = reduced[at : at + units // n_dp].reshape(up_bias.shape)
    at += units // n_dp
    qv_bias_out = reduced[at : at + 2 * heads * hd_part].reshape(qv_bias.shape)

    return (
        output, tokens_grad, outs[0], outs[1],
        qkv_out.astype(F32), qv_bias_out, out_out.astype(F32), outs[2],
        outs[3], outs[4], up_out.astype(F32), up_bias_out,
        down_out.astype(F32), outs[5], stream_rms,
    )


def solution(mesh):
    vector = P("dp")
    rows = P(("dp", "tensor"), None)
    return jax.shard_map(
        shards,
        mesh=mesh,
        in_specs=(
            rows, vector, vector, vector, P("dp", None, "tensor"), P(None, "tensor", "dp"),
            P("tensor", "dp"), vector, vector, vector, P("dp", "tensor"), P("tensor", "dp"),
            P("tensor", "dp"), vector, rows,
        ),
        out_specs=(
            rows, rows, vector, vector, P("dp", None, "tensor"), P(None, "tensor", "dp"),
            P("tensor", "dp"), vector, vector, vector, P("dp", "tensor"), P("tensor", "dp"),
            P("tensor", "dp"), vector, P(),
        ),
        check_vma=False,
    )
```

```python
import functools

import jax
import jax.numpy as jnp
from jax import lax
from jax.experimental import pallas as pl
from jax.experimental.pallas import tpu as pltpu
from jax.sharding import PartitionSpec as P

HD = 128
LEN = 1024
EPS = 1e-05
MESH = pl.DeviceIdType.MESH
F32 = jnp.float32
BF16 = jnp.bfloat16
VMEM_CAP = 60 * 1024 * 1024
SUBS = 2
WHOLE = pl.BlockSpec(memory_space=pltpu.VMEM)
HBM = pl.BlockSpec(memory_space=pltpu.HBM)


class Line:
    def __init__(self, size, rows):
        self.size, self.rows, self.t = size, rows, lax.axis_index("tensor")
        self.sub = rows // SUBS

    def barrier(self):
        sem = pltpu.get_barrier_semaphore()
        pl.semaphore_wait(sem, self.greet(sem))

    def greet(self, sem):
        @pl.when(self.t > 0)
        def _():
            pl.semaphore_signal(sem, device_id={"tensor": self.t - 1}, device_id_type=MESH)

        @pl.when(self.t < self.size - 1)
        def _():
            pl.semaphore_signal(sem, device_id={"tensor": self.t + 1}, device_id_type=MESH)

        return jnp.where(self.t > 0, 1, 0) + jnp.where(self.t < self.size - 1, 1, 0)

    def _copy(self, src, dst, sems, way, shard, part):
        send, recv = sems
        target = self.t + 1 if way == 0 else self.t - 1
        return pltpu.make_async_remote_copy(
            src_ref=src,
            dst_ref=dst.at[shard, pl.ds(part * self.sub, self.sub)],
            send_sem=send.at[way, shard, part],
            recv_sem=recv.at[way, shard, part],
            device_id={"tensor": target},
            device_id_type=MESH,
        )

    def _rows(self, ref, shard, part):
        return ref.at[shard, pl.ds(part * self.sub, self.sub)]

    def _edge(self, way):
        return self.t < self.size - 1 if way == 0 else self.t > 0

    def hop(self, way, src, dst, sems):
        return pltpu.make_async_remote_copy(
            src_ref=src,
            dst_ref=dst.at[way],
            send_sem=sems[0].at[way],
            recv_sem=sems[1].at[way],
            device_id={"tensor": self.t + 1 if way == 0 else self.t - 1},
            device_id_type=MESH,
        )

    def hop_start(self, srcs, dst, sems):
        for way in (0, 1):

            @pl.when(self._edge(way))
            def _(way=way):
                self.hop(way, srcs[way], dst, sems).start()

    def hop_wait(self, srcs, dst, sems):
        for way in (0, 1):

            @pl.when(self._edge(1 - way))
            def _(way=way):
                self.hop(way, srcs[way], dst, sems).wait_recv()

        for way in (0, 1):

            @pl.when(self._edge(way))
            def _(way=way):
                self.hop(way, srcs[way], dst, sems).wait_send()

    def first_hops(self, terms, landed, sems):
        last = self.size - 1
        return [
            (self.t == sender, self.t == taker, self.hop(way, terms.at[shard], landed, sems))
            for way, sender, taker, shard in ((0, 0, 1, last), (1, last, last - 1, 0))
        ]

    def hops_start(self, hops):
        for sends, _, copy in hops:

            @pl.when(sends)
            def _(copy=copy):
                copy.start()

    def hops_wait(self, hops):
        for sends, takes, copy in hops:

            @pl.when(sends)
            def _(copy=copy):
                copy.wait_send()

            @pl.when(takes)
            def _(copy=copy):
                copy.wait_recv()

    def early_start(self, landed, bufs, sem):
        last = self.size - 1
        early = (
            pltpu.make_async_copy(landed.at[0], bufs[0].at[last], sem.at[0]),
            pltpu.make_async_copy(landed.at[1], bufs[1].at[0], sem.at[1]),
        )
        for copy, holder in zip(early, (1, last - 1)):

            @pl.when(self.t == holder)
            def _(copy=copy):
                copy.start()

        return early

    def gather_step(self, way, k, part, buf, sems, first, near=None):
        t, last = self.t, self.size - 1
        shard = t - k if way == 0 else t + k
        inside = (t >= k) if way == 0 else (t + k <= last)

        @pl.when(inside)
        def _():
            held = self._rows(buf, shard, part)
            if k > 1 or (k == 1 and near is None):
                self._copy(held, buf, sems, way, shard, part).wait_recv()

            @pl.when(self._edge(way))
            def _():
                src = held
                if k == 0 and first is not None:
                    src = first.at[pl.ds(part * self.sub, self.sub)]
                if k == 1 and near is not None:
                    src = near.at[way, pl.ds(part * self.sub, self.sub)]
                self._copy(src, buf, sems, way, shard, part).start()

    def relay(self, k, part, buf, sems):
        for way in (0, 1):
            shard = self.t - k if way == 0 else self.t + k
            inside = (self.t >= k) if way == 0 else (self.t + k <= self.size - 1)

            @pl.when(inside)
            def _(way=way, shard=shard):
                held = self._rows(buf, shard, part)
                self._copy(held, buf, sems, way, shard, part).wait_recv()

                @pl.when(self._edge(way))
                def _():
                    self._copy(held, buf, sems, way, shard, part).start()

    def walk(self, buf, sems, work):
        last_part = SUBS - 1

        def visit(m, carry):
            k = (m + 1) // 2
            shard = jnp.where(m % 2 == 1, self.t - k, self.t + k)

            @pl.when((shard >= 0) & (shard < self.size))
            def _():
                work(shard)

            @pl.when(m == 0)
            def _():
                for part in range(last_part):
                    self.relay(1, part, buf, sems)

            @pl.when(m % 2 == 0)
            def _():
                self.relay(k + 1, last_part, buf, sems)

            @pl.when(m % 2 == 1)
            def _():
                for part in range(last_part):
                    self.relay(k + 1, part, buf, sems)

            return carry

        lax.fori_loop(0, 2 * self.size - 1, visit, 0)

    def _second(self, way):
        return self.t == (1 if way == 0 else self.size - 2)

    def send_sum(self, way, shard, part, terms, buf, sems):
        step = min(32, self.sub)

        def add(i, carry):
            rows = pl.ds(part * self.sub + i * step, step)
            total = buf[shard, rows, :].astype(F32) + terms[shard, rows, :].astype(F32)
            buf[shard, rows, :] = total.astype(BF16)
            return carry

        lax.fori_loop(0, self.sub // step, add, 0)
        held = self._rows(buf, shard, part)
        self._copy(held, buf, sems, way, shard, part).start()

    def early_sends(self, terms, bufs, sems, early):
        for way in (0, 1):

            @pl.when(self._second(way))
            def _(way=way):
                early[way].wait()
                for part in range(SUBS):
                    shard = self.size - 1 if way == 0 else 0
                    self.send_sum(way, shard, part, terms, bufs[way], sems)

    def scatter_step(self, way, j, part, terms, buf, sems, ends=None, early=False):
        t, last = self.t, self.size - 1
        shard = last - j if way == 0 else j
        beyond = (shard > t) if way == 0 else (shard < t)
        starts = (t == 0) if way == 0 else (t == last)
        step = min(32, self.sub)
        if ends is None:
            goes, stays = beyond, None
        else:
            goes = (shard > t + 1) if way == 0 else (shard < t - 1)
            stays = (shard == t + 1) if way == 0 else (shard == t - 1)

        done = early and j == 0

        if not done:

            @pl.when(goes & starts)
            def _():
                self._copy(self._rows(terms, shard, part), buf, sems, way, shard, part).start()

        relays = goes & jnp.logical_not(starts)
        if done:
            relays = relays & jnp.logical_not(self._second(way))

        @pl.when(relays)
        def _():
            held = self._rows(buf, shard, part)
            self._copy(held, buf, sems, way, shard, part).wait_recv()
            self.send_sum(way, shard, part, terms, buf, sems)

        if stays is None:
            return

        @pl.when(stays & starts)
        def _():
            rows = pl.ds(part * self.sub, self.sub)
            ends[way, rows, :] = terms[shard, rows, :]

        @pl.when(stays & jnp.logical_not(starts))
        def _():
            held = self._rows(buf, shard, part)
            self._copy(held, buf, sems, way, shard, part).wait_recv()

            def add(i, carry):
                rows = pl.ds(part * self.sub + i * step, step)
                total = buf[shard, rows, :].astype(F32) + terms[shard, rows, :].astype(F32)
                ends[way, rows, :] = total.astype(BF16)
                return carry

            lax.fori_loop(0, self.sub // step, add, 0)

    def phase(self, gather=None, scatter=None, on_slot=None, near=None, ends=None, start=0):
        n = self.size
        for k in range(start, n):
            for part in range(SUBS):
                for way in (0, 1):
                    if gather is not None:
                        self.gather_step(way, k, part, gather[0], gather[1], gather[2], near)
                    if scatter is not None:
                        if gather is None:
                            if k < n - 1:
                                self.scatter_step(way, k, part, scatter[0], scatter[1][way], scatter[2])
                        else:
                            behind = self.t if way == 0 else n - 1 - self.t
                            for b in range(k):

                                @pl.when(behind == b)
                                def _(b=b, k=k, part=part, way=way):
                                    self.scatter_step(
                                        way, k - 1 - b, part, scatter[0], scatter[1][way],
                                        scatter[2], ends,
                                    )
            if on_slot is not None:
                on_slot(k)

    def own_wait(self, bufs, sems, part):
        for way in (0, 1):
            arrives = self.t > 0 if way == 0 else self.t < self.size - 1

            @pl.when(arrives)
            def _(way=way):
                held = self._rows(bufs[way], self.t, part)
                self._copy(held, bufs[way], sems, way, self.t, part).wait_recv()

    def own_sum(self, terms, bufs, rows):
        t = self.t
        zero = jnp.zeros((), F32)
        right = jnp.where(t > 0, bufs[0][t, rows, :].astype(F32), zero)
        left = jnp.where(t < self.size - 1, bufs[1][t, rows, :].astype(F32), zero)
        return terms[t, rows, :].astype(F32) + right + left

    def drain_gather(self, buf, sems, first=0):
        for way in (0, 1):
            for k in range(first, self.size):
                shard = self.t - k if way == 0 else self.t + k
                inside = (self.t >= k) if way == 0 else (self.t + k <= self.size - 1)

                @pl.when(inside & self._edge(way))
                def _(way=way, shard=shard):
                    for part in range(SUBS):
                        held = self._rows(buf, shard, part)
                        self._copy(held, buf, sems, way, shard, part).wait_send()

    def drain_scatter(self, bufs, sems, margin=0, early=False):
        for way in (0, 1):
            for j in range(self.size - 1):
                shard = self.size - 1 - j if way == 0 else j
                beyond = (shard > self.t + margin) if way == 0 else (shard < self.t - margin)
                if early and j == 0:
                    beyond = beyond & self._edge(1 - way)

                @pl.when(beyond)
                def _(way=way, shard=shard):
                    for part in range(SUBS):
                        held = self._rows(bufs[way], shard, part)
                        self._copy(held, bufs[way], sems, way, shard, part).wait_send()


def line_sems(size):
    return [pltpu.SemaphoreType.DMA((2, size, SUBS)), pltpu.SemaphoreType.DMA((2, size, SUBS))]


def fold(x):
    rows, width = x.shape
    return jnp.sum(x.reshape(rows // 8, 8, width), axis=0)


def normal(x):
    centre = x - jnp.mean(x, axis=-1, keepdims=True)
    spread = lax.rsqrt(jnp.mean(centre * centre, axis=-1, keepdims=True) + EPS)
    return centre * spread, spread


def normal_back(upstream, normed, spread, gain):
    scaled = upstream * gain
    mean_part = jnp.mean(scaled, axis=-1, keepdims=True)
    across = jnp.mean(scaled * normed, axis=-1, keepdims=True)
    return spread * (scaled - mean_part - normed * across)


def row_loop(rows, step, body, base=0):
    def one(i, carry):
        body(pl.ds(pl.multiple_of(base + i * step, step), step))
        return carry

    lax.fori_loop(0, rows // step, one, 0)


def params(collective_id=None):
    if collective_id is None:
        return pltpu.CompilerParams(vmem_limit_bytes=VMEM_CAP)
    return pltpu.CompilerParams(
        collective_id=collective_id, has_side_effects=True, vmem_limit_bytes=VMEM_CAP
    )


def first_kernel(n_dp, size, part, small, own, smalls, a_out, tok, send, recv, gs, gr):
    line = Line(size, own.shape[0])
    me = lax.axis_index("dp")
    rows, width = own.shape
    sem = pltpu.get_barrier_semaphore()
    for p in range(1, n_dp):
        pl.semaphore_signal(sem, device_id={"dp": lax.rem(me + p, n_dp)}, device_id_type=MESH)
    ends = line.greet(sem)
    pl.semaphore_wait(sem, ends + n_dp - 1)
    sems = (gs, gr)

    def small_copy(p, slot):
        return pltpu.make_async_remote_copy(
            src_ref=small,
            dst_ref=smalls.at[slot],
            send_sem=send.at[p],
            recv_sem=recv.at[slot],
            device_id={"dp": lax.rem(me + p, n_dp)},
            device_id_type=MESH,
        )

    for p in range(1, n_dp):
        small_copy(p, me).start()
    smalls[pl.ds(me, 1)] = small[...][None]
    step = min(32, rows)
    vec_rows = part // 128

    def normalise(source, shard):
        gain = jnp.concatenate(
            [smalls[d, r : r + 1, :] for d in range(n_dp) for r in range(vec_rows)], axis=1
        ).astype(F32)
        shift = jnp.concatenate(
            [smalls[d, r : r + 1, :] for d in range(n_dp) for r in range(vec_rows, 2 * vec_rows)],
            axis=1,
        ).astype(F32)

        def body(at):
            x = source[at, :] if shard is None else source[shard, at, :]
            normed, _ = normal(x.astype(F32))
            to = line.t if shard is None else shard
            a_out[to, at, :] = (normed * gain + shift).astype(BF16)

        row_loop(rows, step, body)

    def on_slot(k):
        if k == 0:
            for p in range(1, n_dp):
                small_copy(p, lax.rem(me + p, n_dp)).wait_recv()
            normalise(own, None)
        else:

            @pl.when(line.t >= k)
            def _():
                normalise(tok, line.t - k)

            @pl.when(line.t + k <= size - 1)
            def _():
                normalise(tok, line.t + k)

    line.phase(gather=(tok, sems, own), on_slot=on_slot)
    line.drain_gather(tok, sems)
    for p in range(1, n_dp):
        small_copy(p, me).wait_send()


def first(small, own, part, n_dp, size, cid):
    rows, width = own.shape
    return pl.pallas_call(
        functools.partial(first_kernel, n_dp, size, part),
        out_shape=(
            jax.ShapeDtypeStruct((n_dp,) + small.shape, small.dtype),
            jax.ShapeDtypeStruct((size, rows, width), BF16),
        ),
        in_specs=[WHOLE, WHOLE],
        out_specs=(WHOLE, WHOLE),
        scratch_shapes=[
            pltpu.VMEM((size, rows, width), BF16),
            pltpu.SemaphoreType.DMA((n_dp,)),
            pltpu.SemaphoreType.DMA((n_dp,)),
        ]
        + line_sems(size),
        compiler_params=params(cid),
        name="first",
    )(small, own)


def middle_kernel(
    size, terms, cot, near, tok, valid, vecs, c_out, gm_out, mid_out, stats,
    right, left, gs, gr, ss, sr, near_sem,
):
    line = Line(size, tok.shape[0])
    rows = tok.shape[0]
    step = min(32, line.sub)
    own = pltpu.make_async_copy(cot, gm_out.at[line.t], near_sem.at[2])
    own.start()
    line.barrier()

    def keep(way):
        shard = line.t - 1 if way == 0 else line.t + 1
        return pltpu.make_async_copy(near.at[way], gm_out.at[shard], near_sem.at[way])

    def keep_all(act):
        for way in (0, 1):

            @pl.when(line._edge(1 - way))
            def _(way=way):
                act(keep(way))

    keep_all(lambda copy: copy.start())
    line.phase(
        gather=(gm_out, (gs, gr), None),
        scatter=(terms, (right, left), (ss, sr)),
        near=near,
        start=1,
    )
    stats[...] = jnp.zeros_like(stats)

    def body(at):
        attn = line.own_sum(terms, (right, left), at) + vecs[2:3, :]
        x = tok[at, :].astype(F32)
        mid = x + attn
        normed, _ = normal(mid)
        c_out[at, :] = (normed * vecs[3:4, :] + vecs[4:5, :]).astype(BF16)
        mid_out[at, :] = mid
        ok = valid[at, 0:1]
        stats[0:8, :] += fold(ok * x * x)
        stats[8:16, :] += fold(ok * attn * attn)
        stats[16:24, :] += fold(ok * mid * mid)

    for piece in range(SUBS):
        line.own_wait((right, left), (ss, sr), piece)
        row_loop(line.sub, step, body, piece * line.sub)
    own.wait()
    keep_all(lambda copy: copy.wait())
    line.drain_gather(gm_out, (gs, gr), 1)
    line.drain_scatter((right, left), (ss, sr))


def middle(terms, cot, near, tok, valid, vecs, size, cid):
    rows, width = tok.shape
    full = (size, rows, width)
    return pl.pallas_call(
        functools.partial(middle_kernel, size),
        out_shape=(
            jax.ShapeDtypeStruct((rows, width), BF16),
            jax.ShapeDtypeStruct(full, BF16),
            jax.ShapeDtypeStruct((rows, width), F32),
            jax.ShapeDtypeStruct((24, width), F32),
        ),
        in_specs=[WHOLE, HBM, HBM, WHOLE, WHOLE, WHOLE],
        out_specs=(WHOLE,) * 4,
        scratch_shapes=[pltpu.VMEM(full, BF16), pltpu.VMEM(full, BF16)]
        + line_sems(size)
        + line_sems(size)
        + [pltpu.SemaphoreType.DMA((3,))],
        compiler_params=params(cid),
        name="middle",
    )(terms, cot, near, tok, valid, vecs)


def back_middle_kernel(
    size, terms, landed, mlp_in, gm_in, mid_in, vecs, out_in, gz_out, gmid_out, ends, stats,
    go_out, right, left, right2, left2, mlp, gm, mid, out_w,
    ss, sr, ms, mr, gs, gr, early_sem, load_sem,
):
    rows = mid.shape[0]
    line = Line(size, rows)
    step = min(32, line.sub)
    early = line.early_start(landed, (right, left), early_sem)
    loads = [
        pltpu.make_async_copy(src, dst, load_sem.at[i])
        for i, (src, dst) in enumerate(
            ((gm_in, gm), (mid_in, mid), (mlp_in, mlp), (out_in, out_w))
        )
    ]
    for load in loads:
        load.start()
    line.barrier()
    line.early_sends(terms, (right, left), (ss, sr), early)
    for j in range(size - 1):
        for piece in range(SUBS):
            for way in (0, 1):
                line.scatter_step(
                    way, j, piece, terms, (right, left)[way], (ss, sr), None, True
                )
    for load in loads:
        load.wait()
    stats[...] = jnp.zeros_like(stats)

    def body(at):
        e = line.own_sum(terms, (right, left), at)
        normed, spread = normal(mid[at, :])
        gy = gm[at, :].astype(F32)
        gmid = gy + normal_back(e, normed, spread, vecs[3:4, :])
        gz_out[line.t, at, :] = gmid.astype(BF16)
        gmid_out[at, :] = gmid
        stats[0:8, :] += fold(e * normed)
        stats[8:16, :] += fold(e)
        stats[16:24, :] += fold(gmid)
        stats[24:32, :] += fold(gy)

    for piece in range(SUBS):
        line.own_wait((right, left), (ss, sr), piece)
        row_loop(line.sub, step, body, piece * line.sub)
        for way in (0, 1):
            line.gather_step(way, 0, piece, gz_out, (gs, gr), None)
    def weigh(shard):
        go_out[shard] = dot_t(gz_out[shard], out_w[...]).astype(BF16)

    def on_slot(k):
        def side(i, carry):
            shard = line.t + k * (2 * i - 1)

            @pl.when((shard >= 0) & (shard < size))
            def _():
                weigh(shard)

            return carry

        lax.fori_loop(0, 1 if k == 0 else 2, side, 0)

    on_slot(0)
    line.phase(
        gather=(gz_out, (gs, gr), None),
        scatter=(mlp, (right2, left2), (ms, mr)),
        on_slot=on_slot,
        ends=ends,
        start=1,
    )
    line.drain_scatter((right, left), (ss, sr), 0, True)
    line.drain_scatter((right2, left2), (ms, mr), 1)
    line.drain_gather(gz_out, (gs, gr))


def back_middle(terms, landed, mlp, gm, mid, vecs, out_w, size, cid):
    rows, width = mid.shape
    local = out_w.shape[0]
    full = (size, rows, width)
    return pl.pallas_call(
        functools.partial(back_middle_kernel, size),
        out_shape=(
            jax.ShapeDtypeStruct(full, BF16),
            jax.ShapeDtypeStruct((rows, width), F32),
            jax.ShapeDtypeStruct((2, rows, width), BF16),
            jax.ShapeDtypeStruct((32, width), F32),
            jax.ShapeDtypeStruct((size, rows, local), BF16),
        ),
        in_specs=[WHOLE, HBM, HBM, HBM, HBM, WHOLE, HBM],
        out_specs=(WHOLE,) * 5,
        scratch_shapes=[pltpu.VMEM(full, BF16)] * 5
        + [
            pltpu.VMEM((rows, width), BF16),
            pltpu.VMEM((rows, width), F32),
            pltpu.VMEM((local, width), BF16),
        ]
        + line_sems(size)
        + line_sems(size)
        + line_sems(size)
        + [pltpu.SemaphoreType.DMA((2,)), pltpu.SemaphoreType.DMA((4,))],
        compiler_params=params(cid),
        name="back_middle",
    )(terms, landed, mlp, gm, mid, vecs, out_w)


def finish_kernel(
    size, terms, first_landed, tok_in, gmid_in, mlp, landed, mid_in, valid, vecs,
    grad_out, y_out, stats, right, left, own_mlp, tok, ends, gmid, mid,
    ss, sr, load_sem, early_sem,
):
    rows = tok.shape[0]
    line = Line(size, rows)
    step = min(32, line.sub)
    loads = [
        pltpu.make_async_copy(src, dst, load_sem.at[i])
        for i, (src, dst) in enumerate(
            (
                (mlp.at[line.t], own_mlp), (landed, ends), (mid_in, mid),
                (tok_in, tok), (gmid_in, gmid),
            )
        )
    ]
    early = line.early_start(first_landed, (right, left), early_sem)
    for load in loads:
        load.start()
    line.barrier()
    line.early_sends(terms, (right, left), (ss, sr), early)
    stats[...] = jnp.zeros_like(stats)

    def tail(at):
        zero = jnp.zeros((), F32)
        from_left = jnp.where(line.t > 0, ends[0, at, :].astype(F32), zero)
        from_right = jnp.where(line.t < size - 1, ends[1, at, :].astype(F32), zero)
        out = own_mlp[at, :].astype(F32) + from_left + from_right + vecs[5:6, :]
        y = mid[at, :] + out
        y_out[at, :] = y.astype(BF16)
        ok = valid[at, 0:1]
        stats[16:24, :] += fold(ok * out * out)
        stats[24:32, :] += fold(ok * y * y)

    for j in range(size - 1):
        for piece in range(SUBS):
            for way in (0, 1):
                line.scatter_step(
                    way, j, piece, terms, (right, left)[way], (ss, sr), None, True
                )
        if j == 0:
            for load in loads:
                load.wait()
            row_loop(rows, step, tail)

    def body(at):
        e = line.own_sum(terms, (right, left), at)
        normed, spread = normal(tok[at, :].astype(F32))
        grad_out[at, :] = gmid[at, :] + normal_back(e, normed, spread, vecs[0:1, :])
        stats[0:8, :] += fold(e * normed)
        stats[8:16, :] += fold(e)

    for piece in range(SUBS):
        line.own_wait((right, left), (ss, sr), piece)
        row_loop(line.sub, step, body, piece * line.sub)
    line.drain_scatter((right, left), (ss, sr), 0, True)


def finish(terms, first_landed, tok, gmid, mlp, landed, mid, valid, vecs, size, cid):
    rows, width = tok.shape
    full = (size, rows, width)
    return pl.pallas_call(
        functools.partial(finish_kernel, size),
        out_shape=(
            jax.ShapeDtypeStruct((rows, width), F32),
            jax.ShapeDtypeStruct((rows, width), BF16),
            jax.ShapeDtypeStruct((32, width), F32),
        ),
        in_specs=[WHOLE] + [HBM] * 6 + [WHOLE, WHOLE],
        out_specs=(WHOLE,) * 3,
        scratch_shapes=[pltpu.VMEM(full, BF16)] * 2
        + [pltpu.VMEM((rows, width), BF16)] * 2
        + [pltpu.VMEM((2, rows, width), BF16)]
        + [pltpu.VMEM((rows, width), F32)] * 2
        + line_sems(size)
        + [pltpu.SemaphoreType.DMA((5,)), pltpu.SemaphoreType.DMA((2,))],
        compiler_params=params(cid),
        name="finish",
    )(terms, first_landed, tok, gmid, mlp, landed, mid, valid, vecs)


def reduce_small_kernel(n_dp, n_t, shared, blocks, out, land, sums, land2, s1, r1, s2, r2):
    me, t = lax.axis_index("dp"), lax.axis_index("tensor")
    sem = pltpu.get_barrier_semaphore()
    for p in range(1, n_dp):
        pl.semaphore_signal(sem, device_id={"dp": lax.rem(me + p, n_dp)}, device_id_type=MESH)
    for p in range(1, n_t):
        pl.semaphore_signal(sem, device_id={"tensor": lax.rem(t + p, n_t)}, device_id_type=MESH)
    pl.semaphore_wait(sem, n_dp + n_t - 2)

    def one(p):
        other = lax.rem(me + p, n_dp)
        return pltpu.make_async_remote_copy(
            src_ref=blocks.at[other],
            dst_ref=land.at[p],
            send_sem=s1.at[p],
            recv_sem=r1.at[p],
            device_id={"dp": other},
            device_id_type=MESH,
        )

    for p in range(1, n_dp):
        one(p).start()
    total = blocks[me]
    for p in range(1, n_dp):
        one(p).wait_recv()
        total = total + land[p]
    sums[...] = total

    def two(p):
        return pltpu.make_async_remote_copy(
            src_ref=sums.at[pl.ds(0, shared)],
            dst_ref=land2.at[p],
            send_sem=s2.at[p],
            recv_sem=r2.at[p],
            device_id={"tensor": lax.rem(t + p, n_t)},
            device_id_type=MESH,
        )

    for p in range(1, n_t):
        two(p).start()
    out[...] = total
    top = sums[pl.ds(0, shared), :]
    for p in range(1, n_t):
        two(p).wait_recv()
        top = top + land2[p]
    out[pl.ds(0, shared), :] = top
    for p in range(1, n_dp):
        one(p).wait_send()
    for p in range(1, n_t):
        two(p).wait_send()


def reduce_small(blocks, shared, n_dp, n_t, cid):
    _, rows, width = blocks.shape
    return pl.pallas_call(
        functools.partial(reduce_small_kernel, n_dp, n_t, shared),
        out_shape=jax.ShapeDtypeStruct((rows, width), F32),
        in_specs=[WHOLE],
        out_specs=WHOLE,
        scratch_shapes=[
            pltpu.VMEM((n_dp, rows, width), F32),
            pltpu.VMEM((rows, width), F32),
            pltpu.VMEM((n_t, shared, width), F32),
            pltpu.SemaphoreType.DMA((n_dp,)),
            pltpu.SemaphoreType.DMA((n_dp,)),
            pltpu.SemaphoreType.DMA((n_t,)),
            pltpu.SemaphoreType.DMA((n_t,)),
        ],
        compiler_params=params(cid),
        name="reduce_small",
    )(blocks)


BLOCK = 256
NEG = -1e30
SCALE = HD**-0.5


def dot(a, b):
    return jnp.dot(a, b, preferred_element_type=F32)


def dot_t(a, b):
    return lax.dot_general(a, b, (((1,), (1,)), ((), ())), preferred_element_type=F32)


def masked_scores(q, k, keys, first, bar):
    scores = dot_t(k, q) * SCALE + bar
    key_pos = lax.broadcasted_iota(jnp.int32, (keys, BLOCK), 0)
    query_pos = first + lax.broadcasted_iota(jnp.int32, (keys, BLOCK), 1)
    return jnp.where(key_pos <= query_pos, scores, NEG)


def head_cols(part, h, heads):
    return pl.ds(pl.multiple_of((part * heads + h) * HD, HD), HD)


def weight_loads(weights, cols, sem, part):
    n_dp, _, rows, local = weights.shape
    return [
        pltpu.make_async_copy(
            weights.at[d, part],
            cols.at[pl.ds(d * rows, rows), pl.ds(part * local, local)],
            sem.at[part, d],
        )
        for d in range(n_dp)
    ]


def front_kernel(
    size, heads, a, weights, shift, bar, out_w, cot, qkv, mixed_all, log_totals, terms, near,
    cols, gs, gr, load_sem,
):
    h = pl.program_id(0)
    rows = cot.shape[0]
    local = heads * HD
    line = Line(size, rows)

    @pl.when(h == 0)
    def _():
        for part in range(3):
            for load in weight_loads(weights, cols, load_sem, part):
                load.start()
        line.barrier()
        line.hop_start((cot, cot), near, (gs, gr))
        for part in range(3):
            for load in weight_loads(weights, cols, load_sem, part):
                load.wait()
            span = slice(part * local, (part + 1) * local)

            def product(at, span=span):
                qkv[at, span] = (dot(a[at, :], cols[:, span]) + shift[0:1, span]).astype(BF16)

            row_loop(LEN, min(256, LEN), product)

    at_q, at_k, at_v = (head_cols(part, h, heads) for part in range(3))
    value_cols = qkv[:, at_v].T
    for block in range(LEN // BLOCK):
        first, keys = block * BLOCK, (block + 1) * BLOCK
        here = slice(first, first + BLOCK)
        scores = masked_scores(qkv[here, at_q], qkv[0:keys, at_k], keys, first, bar[0:keys, 0:1])
        top = jnp.max(scores, axis=0, keepdims=True)
        powers = jnp.exp(scores - top)
        total = jnp.sum(powers, axis=0, keepdims=True)
        shares = (powers * (1.0 / total)).astype(BF16)
        mixed = dot(value_cols[:, 0:keys], shares)
        mixed_all[here, head_cols(0, h, heads)] = mixed.T.astype(BF16)
        log_totals[0, :, here] = jnp.broadcast_to(top + jnp.log(total), (8, BLOCK))

    @pl.when(h == heads - 1)
    def _():
        def project(at):
            terms[at, :] = dot(mixed_all[at, :], out_w[...]).astype(BF16)

        row_loop(LEN, min(256, LEN), project)
        line.hop_wait((cot, cot), near, (gs, gr))


def front(a, weights, shift, bar, out_w, cot, size, cid):
    n_dp, _, part, local = weights.shape
    width, local3 = n_dp * part, 3 * local
    heads = local // HD
    return pl.pallas_call(
        functools.partial(front_kernel, size, heads),
        grid=(heads,),
        out_shape=(
            jax.ShapeDtypeStruct((LEN, local3), BF16),
            jax.ShapeDtypeStruct((LEN, local), BF16),
            jax.ShapeDtypeStruct((heads, 8, LEN), F32),
            jax.ShapeDtypeStruct((LEN, width), BF16),
            jax.ShapeDtypeStruct((2,) + cot.shape, BF16),
        ),
        in_specs=[WHOLE, HBM, WHOLE, WHOLE, WHOLE, HBM],
        out_specs=(
            pl.BlockSpec((LEN, local3), lambda h: (0, 0)),
            pl.BlockSpec((LEN, local), lambda h: (0, 0)),
            pl.BlockSpec((1, 8, LEN), lambda h: (h, 0, 0)),
            pl.BlockSpec((LEN, width), lambda h: (0, 0)),
            HBM,
        ),
        scratch_shapes=[
            pltpu.VMEM((width, local3), BF16),
            pltpu.SemaphoreType.DMA((2,)),
            pltpu.SemaphoreType.DMA((2,)),
            pltpu.SemaphoreType.DMA((3, n_dp)),
        ],
        compiler_params=params(cid),
        name="front",
    )(a, weights, shift, bar, out_w, cot)


def attend_back_kernel(
    size, heads, q, k, v, go, bar, log_totals, weights, ends, out, sums, terms, landed,
    key_grad, value_grad, cols, gs, gr, load_sem,
):
    h = pl.program_id(0)
    line = Line(size, ends.shape[1])
    srcs = (ends.at[0], ends.at[1])
    loads = [load for part in range(3) for load in weight_loads(weights, cols, load_sem, part)]

    @pl.when(h == 0)
    def _():
        for load in loads:
            load.start()
        line.barrier()
        line.hop_start(srcs, landed, (gs, gr))

    key_cols = k[...].T
    query_sum = jnp.zeros((1, HD), F32)
    at_q, at_k, at_v = (head_cols(part, h, heads) for part in range(3))
    for block in range(LEN // BLOCK - 1, -1, -1):
        first, keys = block * BLOCK, (block + 1) * BLOCK
        here = slice(first, first + BLOCK)
        scores = masked_scores(q[here, :], k[0:keys, :], keys, first, bar[0:keys, 0:1])
        shares = jnp.exp(scores - log_totals[0, 0:1, here])
        share_grad = dot_t(v[0:keys, :], go[here, :])
        centre = jnp.sum(shares * share_grad, axis=0, keepdims=True)
        score_grad = (shares * (share_grad - centre)).astype(BF16)
        values = dot(shares.astype(BF16), go[here, :])
        keyed = dot(score_grad, q[here, :])
        if block == LEN // BLOCK - 1:
            value_grad[...] = values
            key_grad[...] = keyed
        else:
            value_grad[0:keys, :] += values
            key_grad[0:keys, :] += keyed
        query_grad = ((dot(key_cols[:, 0:keys], score_grad)) * SCALE).T.astype(BF16)
        out[here, at_q] = query_grad
        query_sum = query_sum + jnp.sum(query_grad.astype(F32), axis=0, keepdims=True)
    out[:, at_k] = (key_grad[...] * SCALE).astype(BF16)
    rounded = value_grad[...].astype(BF16)
    out[:, at_v] = rounded
    value_sum = jnp.sum(rounded.astype(F32), axis=0, keepdims=True)
    sums[0, 0:8, :] = jnp.broadcast_to(query_sum, (8, HD))
    sums[0, 8:16, :] = jnp.broadcast_to(value_sum, (8, HD))

    @pl.when(h == heads - 1)
    def _():
        for load in loads:
            load.wait()

        def product(at):
            terms[at, :] = dot_t(out[at, :], cols[...]).astype(BF16)

        row_loop(LEN, min(256, LEN), product)
        line.hop_wait(srcs, landed, (gs, gr))


def attend_back(qkv, go, bar, log_totals, weights, ends, size, cid):
    n_dp, _, part, local = weights.shape
    width, local3 = n_dp * part, 3 * local
    heads = local // HD

    def column(place):
        return pl.BlockSpec((LEN, HD), lambda h: (0, place * heads + h))

    return pl.pallas_call(
        functools.partial(attend_back_kernel, size, heads),
        grid=(heads,),
        out_shape=(
            jax.ShapeDtypeStruct((LEN, local3), BF16),
            jax.ShapeDtypeStruct((heads, 16, HD), F32),
            jax.ShapeDtypeStruct((LEN, width), BF16),
            jax.ShapeDtypeStruct(ends.shape, BF16),
        ),
        in_specs=[
            column(0), column(1), column(2), column(0),
            pl.BlockSpec((LEN, 128), lambda h: (0, 0)),
            pl.BlockSpec((1, 8, LEN), lambda h: (h, 0, 0)),
            HBM, HBM,
        ],
        out_specs=(
            pl.BlockSpec((LEN, local3), lambda h: (0, 0)),
            pl.BlockSpec((1, 16, HD), lambda h: (h, 0, 0)),
            pl.BlockSpec((LEN, width), lambda h: (0, 0)),
            HBM,
        ),
        scratch_shapes=[
            pltpu.VMEM((LEN, HD), F32),
            pltpu.VMEM((LEN, HD), F32),
            pltpu.VMEM((width, local3), BF16),
            pltpu.SemaphoreType.DMA((2,)),
            pltpu.SemaphoreType.DMA((2,)),
            pltpu.SemaphoreType.DMA((3, n_dp)),
        ],
        compiler_params=params(cid),
        name="attend_back",
    )(qkv, qkv, qkv, go, bar, log_totals, weights, ends)


def gelu_both(u):
    inner = 0.7978845608028654 * (u + 0.044715 * (u * u * u))
    th = jnp.tanh(inner)
    half = 0.5 * (1.0 + th)
    slope = half + 0.5 * u * (1.0 - th * th) * (
        0.7978845608028654 * (1.0 + 3 * 0.044715 * (u * u))
    )
    return u * half, slope


def hidden_kernel(
    n_dp, size, c_own, gm_in, up_in, down_in, bias,
    c_out, act_out, gu_out, mlp_out, back_out, sums, gm, up, down, act, gu, mlp, back, gs, gr, in_sem, out_sem,
):
    line = Line(size, c_own.shape[0])
    rows, width = c_own.shape
    units, part = down.shape[1], down.shape[2]
    block = min(512, units)
    loads = [
        pltpu.make_async_copy(up_in, up, in_sem.at[0]),
        pltpu.make_async_copy(down_in, down, in_sem.at[1]),
        pltpu.make_async_copy(gm_in, gm, in_sem.at[2]),
    ]
    for load in loads:
        load.start()
    line.barrier()
    for piece in range(SUBS):
        for way in (0, 1):
            line.gather_step(way, 0, piece, c_out, (gs, gr), c_own)
    c_out[pl.ds(line.t, 1)] = c_own[...][None]
    sums[...] = jnp.zeros_like(sums)
    for load in loads:
        load.wait()

    def stores(shard):
        pairs = ((act, act_out), (gu, gu_out), (mlp, mlp_out), (back, back_out))
        return [
            pltpu.make_async_copy(src.at[shard], dst.at[shard], out_sem.at[i, shard])
            for i, (src, dst) in enumerate(pairs)
        ]

    def work(shard):
        def unit_block(j, carry):
            at = pl.ds(pl.multiple_of(j * block, block), block)
            u = dot(c_out[shard], up[:, at]) + bias[0:1, at]
            grad = dot_t(gm[shard, :, 0:part], down[0, at, :])
            for d in range(1, n_dp):
                grad = grad + dot_t(gm[shard, :, d * part : (d + 1) * part], down[d, at, :])
            value, slope = gelu_both(u)
            act[shard, :, at] = value.astype(BF16)
            rounded = (grad * slope).astype(BF16)
            gu[shard, :, at] = rounded
            sums[:, at] += fold(rounded.astype(F32))
            return carry

        lax.fori_loop(0, units // block, unit_block, 0)

        def feature_block(d, carry):
            at = pl.ds(pl.multiple_of(d * part, part), part)
            mlp[shard, :, at] = dot(act[shard], down[d]).astype(BF16)
            back[shard, :, at] = dot_t(gu[shard], up[at, :]).astype(BF16)
            return carry

        lax.fori_loop(0, n_dp, feature_block, 0)
        for store in stores(shard):
            store.start()

    line.walk(c_out, (gs, gr), work)
    line.drain_gather(c_out, (gs, gr))
    for shard in range(size):
        for store in stores(shard):
            store.wait()


def hidden(c_own, gm, up, down, bias, size, cid):
    rows, width = c_own.shape
    n_dp, units, part = down.shape
    full, wide = (size, rows, width), (size, rows, units)
    return pl.pallas_call(
        functools.partial(hidden_kernel, n_dp, size),
        out_shape=(
            jax.ShapeDtypeStruct(full, BF16),
            jax.ShapeDtypeStruct(wide, BF16),
            jax.ShapeDtypeStruct(wide, BF16),
            jax.ShapeDtypeStruct(full, BF16),
            jax.ShapeDtypeStruct(full, BF16),
            jax.ShapeDtypeStruct((8, units), F32),
        ),
        in_specs=[WHOLE, HBM, HBM, HBM, WHOLE],
        out_specs=(WHOLE, HBM, HBM, HBM, HBM, WHOLE),
        scratch_shapes=[
            pltpu.VMEM(full, BF16),
            pltpu.VMEM((width, units), BF16),
            pltpu.VMEM((n_dp, units, part), BF16),
            pltpu.VMEM(wide, BF16),
            pltpu.VMEM(wide, BF16),
            pltpu.VMEM(full, BF16),
            pltpu.VMEM(full, BF16),
        ]
        + line_sems(size)
        + [pltpu.SemaphoreType.DMA((3,)), pltpu.SemaphoreType.DMA((4, size))],
        compiler_params=params(cid),
        name="hidden",
    )(c_own, gm, up, down, bias)


def cross(left, right):
    return lax.dot_general(left, right, (((0,), (0,)), ((), ())), preferred_element_type=F32)


def products_kernel(
    size, steps, act, gm, c, gu_in, terms, down_out, up_out, landed, gu, gs, gr, load_sem
):
    i = pl.program_id(0)
    line = Line(size, terms.shape[1])
    load = pltpu.make_async_copy(gu_in, gu, load_sem.at[0])
    hops = line.first_hops(terms, landed, (gs, gr))

    @pl.when(i == 0)
    def _():
        load.start()
        line.barrier()
        line.hops_start(hops)

    @pl.when(i < steps)
    def _():
        down_out[...] = cross(act[...], gm[...]).astype(BF16)

    @pl.when(i == steps)
    def _():
        load.wait()

    @pl.when(i >= steps)
    def _():
        up_out[...] = cross(c[...], gu[...]).astype(BF16)

    @pl.when(i == pl.num_programs(0) - 1)
    def _():
        line.hops_wait(hops)


def products(act, gm, c, gu, terms, size, cid):
    rows, units = act.shape
    width = gm.shape[1]
    steps, more = units // BLOCK, width // BLOCK
    return pl.pallas_call(
        functools.partial(products_kernel, size, steps),
        grid=(steps + more,),
        out_shape=(
            jax.ShapeDtypeStruct((units, width), BF16),
            jax.ShapeDtypeStruct((width, units), BF16),
            jax.ShapeDtypeStruct((2,) + terms.shape[1:], BF16),
        ),
        in_specs=[
            pl.BlockSpec((rows, BLOCK), lambda i: (0, jnp.minimum(i, steps - 1))),
            WHOLE,
            pl.BlockSpec((rows, BLOCK), lambda i: (0, jnp.maximum(i - steps, 0))),
            HBM,
            HBM,
        ],
        out_specs=(
            pl.BlockSpec((BLOCK, width), lambda i: (jnp.minimum(i, steps - 1), 0)),
            pl.BlockSpec((BLOCK, units), lambda i: (jnp.maximum(i - steps, 0), 0)),
            HBM,
        ),
        scratch_shapes=[
            pltpu.VMEM((rows, units), BF16),
            pltpu.SemaphoreType.DMA((2,)),
            pltpu.SemaphoreType.DMA((2,)),
            pltpu.SemaphoreType.DMA((1,)),
        ],
        compiler_params=params(cid),
        name="products",
    )(act, gm, c, gu, terms)


def head_products_kernel(size, gz, a, o, gqkv, terms, out, landed, gs, gr):
    i = pl.program_id(0)
    line = Line(size, terms.shape[1])
    hops = line.first_hops(terms, landed, (gs, gr))
    local = o.shape[1]

    @pl.when(i == 0)
    def _():
        line.barrier()
        line.hops_start(hops)

    out[:, 0:local] = cross(gz[...], o[...]).astype(BF16)
    out[:, local:] = cross(a[...], gqkv[...]).astype(BF16)

    @pl.when(i == pl.num_programs(0) - 1)
    def _():
        line.hops_wait(hops)


def head_products(gz, a, o, gqkv, terms, size, cid):
    rows, width = a.shape
    columns = o.shape[1] + gqkv.shape[1]
    return pl.pallas_call(
        functools.partial(head_products_kernel, size),
        grid=(width // BLOCK,),
        out_shape=(
            jax.ShapeDtypeStruct((width, columns), BF16),
            jax.ShapeDtypeStruct((2,) + terms.shape[1:], BF16),
        ),
        in_specs=[
            pl.BlockSpec((rows, BLOCK), lambda i: (0, i)),
            pl.BlockSpec((rows, BLOCK), lambda i: (0, i)),
            WHOLE,
            WHOLE,
            HBM,
        ],
        out_specs=(pl.BlockSpec((BLOCK, columns), lambda i: (i, 0)), HBM),
        scratch_shapes=[pltpu.SemaphoreType.DMA((2,)), pltpu.SemaphoreType.DMA((2,))],
        compiler_params=params(cid),
        name="head_products",
    )(gz, a, o, gqkv, terms)


def pad_to(x, count):
    return jnp.pad(x, ((0, 0), (0, count - x.shape[1])))


def shards(
    tokens, lengths, ln1_gain, ln1_bias, qkv_weight, qv_bias, out_weight, out_bias,
    ln2_gain, ln2_bias, up_weight, up_bias, down_weight, down_bias, cotangent,
):
    n_dp, n_t = lax.axis_size("dp"), lax.axis_size("tensor")
    rows, width = tokens.shape
    part = ln1_gain.shape[0]
    local = qkv_weight.shape[2]
    heads = local // HD
    units = up_weight.shape[1]
    hd_part = qv_bias.shape[2]
    t = lax.axis_index("tensor")
    length = lengths[0]

    pieces = [
        ln1_gain, ln1_bias, out_bias, ln2_gain, ln2_bias, down_bias,
        qv_bias.reshape(-1), up_bias.reshape(-1),
    ]
    packed = jnp.concatenate(pieces)
    count = packed.shape[0]
    lanes = -(-count // 2048) * 2048
    small = jnp.pad(packed, (0, lanes - count)).reshape(lanes // 128, 128)
    smalls, a = first(small, tokens, part, n_dp, n_t, 0)
    smalls, a = smalls.reshape(n_dp, lanes), a.reshape(n_t * rows, width)
    vecs = jnp.stack([smalls[:, i * part : (i + 1) * part].reshape(width) for i in range(6)])
    vecs = jnp.pad(vecs, ((0, 2), (0, 0))).astype(F32)
    at = 6 * part
    qv_all = smalls[:, at : at + 2 * heads * hd_part].reshape(n_dp, 2, heads, hd_part)
    qv_all = qv_all.transpose(1, 2, 0, 3).reshape(2, local).astype(F32)
    at += 2 * heads * hd_part
    up_all = smalls[:, at : at + units // n_dp].reshape(n_dp, units // 16, 16 // n_dp)
    up_shift = up_all.transpose(1, 0, 2).reshape(1, units).astype(F32)
    qkv_shift = jnp.concatenate([qv_all[0], jnp.zeros_like(qv_all[0]), qv_all[1]])

    qkv_full = lax.all_gather(
        qkv_weight.transpose(1, 0, 2).reshape(3 * part, local), "dp", axis=0, tiled=False
    ).reshape(n_dp, 3, part, local)
    out_full = lax.all_gather(out_weight, "dp", axis=1, tiled=True)
    up_full = lax.all_gather(up_weight, "dp", axis=0, tiled=True)
    down_blocks = lax.all_gather(down_weight, "dp", axis=0, tiled=False)

    own_pos = t * rows + jnp.arange(rows, dtype=jnp.int32)
    valid_own = (own_pos < length).astype(F32)
    valid = jnp.broadcast_to(valid_own[:, None], (rows, 128))
    positions = jnp.arange(LEN, dtype=jnp.int32)
    bar = jnp.broadcast_to(jnp.where(positions < length, 0.0, NEG)[:, None], (LEN, 128))
    gm_own = (cotangent.astype(F32) * valid_own[:, None]).astype(BF16)

    shift = jnp.broadcast_to(qkv_shift, (8, 3 * local))
    qkv, attended, log_totals, terms, near = front(
        a, qkv_full, shift, bar, out_full, gm_own, n_t, 7
    )
    terms = terms.reshape(n_t, rows, width)
    c_own, gm, mid, stats_a = middle(terms, gm_own, near, tokens, valid, vecs, n_t, 2)
    c, act, gu, mlp, back_terms, up_sums = hidden(
        c_own, gm, up_full, down_blocks, jnp.broadcast_to(up_shift, (8, units)), n_t, 6
    )
    c, gm = c.reshape(-1, width), gm.reshape(-1, width)
    act, gu = act.reshape(-1, units), gu.reshape(-1, units)

    down_grad, up_grad, early = products(act, gm, c, gu, back_terms, n_t, 9)
    down_out = lax.psum_scatter(down_grad, "dp", scatter_dimension=1, tiled=True)
    up_out = lax.psum_scatter(up_grad, "dp", scatter_dimension=0, tiled=True)
    gz, gmid, ends, stats_b, go = back_middle(
        back_terms, early, mlp, gm_own, mid, vecs, out_full, n_t, 3
    )
    gqkv, head_sums, last_terms, landed = attend_back(
        qkv, go.reshape(-1, local), bar, log_totals, qkv_full, ends, n_t, 8
    )
    last_terms = last_terms.reshape(n_t, rows, width)
    head_grad, last_early = head_products(
        gz.reshape(-1, width), a, attended, gqkv, last_terms, n_t, 10
    )
    last_early, head_grad, down_out, up_out = lax.optimization_barrier(
        (last_early, head_grad, down_out, up_out)
    )
    head_out = lax.psum_scatter(head_grad, "dp", scatter_dimension=0, tiled=True)
    out_out = head_out[:, :local].T
    qkv_out = head_out[:, local:].reshape(part, 3, local)
    tokens_grad, output, stats_c = finish(
        last_terms, last_early, tokens, gmid, mlp, landed, mid, valid, vecs, n_t, 4
    )

    def vec_sum(stats, i):
        return jnp.sum(stats[8 * i : 8 * i + 8], axis=0)

    vectors = jnp.stack(
        [
            vec_sum(stats_c, 0), vec_sum(stats_c, 1), vec_sum(stats_b, 2),
            vec_sum(stats_b, 0), vec_sum(stats_b, 1), vec_sum(stats_b, 3),
        ]
    )
    def squares(stats, i):
        return jnp.sum(stats[8 * i : 8 * i + 8].reshape(8, n_dp, part), axis=(0, 1))

    sums = jnp.concatenate(
        [
            squares(stats_a, 0), squares(stats_a, 1), squares(stats_a, 2),
            squares(stats_c, 2), squares(stats_c, 3),
        ]
    )
    count = jnp.clip(length - t * rows, 0, rows).astype(F32)
    vector_blocks = vectors.reshape(6, n_dp, part).transpose(1, 0, 2).reshape(n_dp, 6 * part)
    top = jnp.concatenate(
        [vector_blocks, jnp.broadcast_to(sums[None], (n_dp, 5 * part)), jnp.full((n_dp, 1), count)],
        axis=1,
    )
    top_len = -(-top.shape[1] // 1024) * 1024
    up_blocks = jnp.sum(up_sums, axis=0).reshape(units // 16, n_dp, 16 // n_dp)
    up_blocks = up_blocks.transpose(1, 0, 2).reshape(n_dp, units // n_dp)
    qv_sums = jnp.stack([head_sums[:, 0], head_sums[:, 8]])
    qv_blocks = qv_sums.reshape(2, heads, n_dp, hd_part).transpose(2, 0, 1, 3)
    qv_blocks = qv_blocks.reshape(n_dp, 2 * heads * hd_part)
    low = jnp.concatenate([up_blocks, qv_blocks], axis=1)
    low_len = -(-low.shape[1] // 1024) * 1024
    blocks = jnp.concatenate([pad_to(top, top_len), pad_to(low, low_len)], axis=1)
    blocks = blocks.reshape(n_dp, (top_len + low_len) // 128, 128)
    reduced = reduce_small(blocks, top_len // 128, n_dp, n_t, 5).reshape(-1)
    outs = [reduced[i * part : (i + 1) * part] for i in range(6)]
    totals = jnp.sum(reduced[6 * part : 11 * part].reshape(5, part), axis=1)
    stream_rms = jnp.sqrt(totals / (reduced[11 * part] * width))
    at = top_len
    up_bias_out = reduced[at : at + units // n_dp].reshape(up_bias.shape)
    at += units // n_dp
    qv_bias_out = reduced[at : at + 2 * heads * hd_part].reshape(qv_bias.shape)

    return (
        output, tokens_grad, outs[0], outs[1],
        qkv_out.astype(F32), qv_bias_out, out_out.astype(F32), outs[2],
        outs[3], outs[4], up_out.astype(F32), up_bias_out,
        down_out.astype(F32), outs[5], stream_rms,
    )


def solution(mesh):
    vector = P("dp")
    rows = P(("dp", "tensor"), None)
    return jax.shard_map(
        shards,
        mesh=mesh,
        in_specs=(
            rows, vector, vector, vector, P("dp", None, "tensor"), P(None, "tensor", "dp"),
            P("tensor", "dp"), vector, vector, vector, P("dp", "tensor"), P("tensor", "dp"),
            P("tensor", "dp"), vector, rows,
        ),
        out_specs=(
            rows, rows, vector, vector, P("dp", None, "tensor"), P(None, "tensor", "dp"),
            P("tensor", "dp"), vector, vector, vector, P("dp", "tensor"), P("tensor", "dp"),
            P("tensor", "dp"), vector, P(),
        ),
        check_vma=False,
    )
```

```python
import functools

import jax
import jax.numpy as jnp
from jax import lax
from jax.experimental import pallas as pl
from jax.experimental.pallas import tpu as pltpu
from jax.sharding import PartitionSpec as P

HD = 128
LEN = 1024
EPS = 1e-05
MESH = pl.DeviceIdType.MESH
F32 = jnp.float32
BF16 = jnp.bfloat16
VMEM_CAP = 60 * 1024 * 1024
SUBS = 2
WHOLE = pl.BlockSpec(memory_space=pltpu.VMEM)
HBM = pl.BlockSpec(memory_space=pltpu.HBM)


class Line:
    def __init__(self, size, rows):
        self.size, self.rows, self.t = size, rows, lax.axis_index("tensor")
        self.sub = rows // SUBS

    def barrier(self):
        sem = pltpu.get_barrier_semaphore()
        pl.semaphore_wait(sem, self.greet(sem))

    def greet(self, sem):
        @pl.when(self.t > 0)
        def _():
            pl.semaphore_signal(sem, device_id={"tensor": self.t - 1}, device_id_type=MESH)

        @pl.when(self.t < self.size - 1)
        def _():
            pl.semaphore_signal(sem, device_id={"tensor": self.t + 1}, device_id_type=MESH)

        return jnp.where(self.t > 0, 1, 0) + jnp.where(self.t < self.size - 1, 1, 0)

    def _copy(self, src, dst, sems, way, shard, part):
        send, recv = sems
        target = self.t + 1 if way == 0 else self.t - 1
        return pltpu.make_async_remote_copy(
            src_ref=src,
            dst_ref=dst.at[shard, pl.ds(part * self.sub, self.sub)],
            send_sem=send.at[way, shard, part],
            recv_sem=recv.at[way, shard, part],
            device_id={"tensor": target},
            device_id_type=MESH,
        )

    def _rows(self, ref, shard, part):
        return ref.at[shard, pl.ds(part * self.sub, self.sub)]

    def _edge(self, way):
        return self.t < self.size - 1 if way == 0 else self.t > 0

    def hop(self, way, src, dst, sems):
        return pltpu.make_async_remote_copy(
            src_ref=src,
            dst_ref=dst.at[way],
            send_sem=sems[0].at[way],
            recv_sem=sems[1].at[way],
            device_id={"tensor": self.t + 1 if way == 0 else self.t - 1},
            device_id_type=MESH,
        )

    def hop_start(self, srcs, dst, sems):
        for way in (0, 1):

            @pl.when(self._edge(way))
            def _(way=way):
                self.hop(way, srcs[way], dst, sems).start()

    def hop_wait(self, srcs, dst, sems):
        for way in (0, 1):

            @pl.when(self._edge(1 - way))
            def _(way=way):
                self.hop(way, srcs[way], dst, sems).wait_recv()

        for way in (0, 1):

            @pl.when(self._edge(way))
            def _(way=way):
                self.hop(way, srcs[way], dst, sems).wait_send()

    def first_hops(self, terms, landed, sems):
        last = self.size - 1
        return [
            (self.t == sender, self.t == taker, self.hop(way, terms.at[shard], landed, sems))
            for way, sender, taker, shard in ((0, 0, 1, last), (1, last, last - 1, 0))
        ]

    def hops_start(self, hops):
        for sends, _, copy in hops:

            @pl.when(sends)
            def _(copy=copy):
                copy.start()

    def hops_wait(self, hops):
        for sends, takes, copy in hops:

            @pl.when(sends)
            def _(copy=copy):
                copy.wait_send()

            @pl.when(takes)
            def _(copy=copy):
                copy.wait_recv()

    def early_start(self, landed, bufs, sem):
        last = self.size - 1
        early = (
            pltpu.make_async_copy(landed.at[0], bufs[0].at[last], sem.at[0]),
            pltpu.make_async_copy(landed.at[1], bufs[1].at[0], sem.at[1]),
        )
        for copy, holder in zip(early, (1, last - 1)):

            @pl.when(self.t == holder)
            def _(copy=copy):
                copy.start()

        return early

    def gather_step(self, way, k, part, buf, sems, first, near=None):
        t, last = self.t, self.size - 1
        shard = t - k if way == 0 else t + k
        inside = (t >= k) if way == 0 else (t + k <= last)

        @pl.when(inside)
        def _():
            held = self._rows(buf, shard, part)
            if k > 1 or (k == 1 and near is None):
                self._copy(held, buf, sems, way, shard, part).wait_recv()

            @pl.when(self._edge(way))
            def _():
                src = held
                if k == 0 and first is not None:
                    src = first.at[pl.ds(part * self.sub, self.sub)]
                if k == 1 and near is not None:
                    src = near.at[way, pl.ds(part * self.sub, self.sub)]
                self._copy(src, buf, sems, way, shard, part).start()

    def relay(self, k, part, buf, sems):
        for way in (0, 1):
            shard = self.t - k if way == 0 else self.t + k
            inside = (self.t >= k) if way == 0 else (self.t + k <= self.size - 1)

            @pl.when(inside)
            def _(way=way, shard=shard):
                held = self._rows(buf, shard, part)
                self._copy(held, buf, sems, way, shard, part).wait_recv()

                @pl.when(self._edge(way))
                def _():
                    self._copy(held, buf, sems, way, shard, part).start()

    def walk(self, buf, sems, work):
        last_part = SUBS - 1

        def visit(m, carry):
            k = (m + 1) // 2
            shard = jnp.where(m % 2 == 1, self.t - k, self.t + k)

            @pl.when((shard >= 0) & (shard < self.size))
            def _():
                work(shard)

            @pl.when(m == 0)
            def _():
                for part in range(last_part):
                    self.relay(1, part, buf, sems)

            @pl.when(m % 2 == 0)
            def _():
                self.relay(k + 1, last_part, buf, sems)

            @pl.when(m % 2 == 1)
            def _():
                for part in range(last_part):
                    self.relay(k + 1, part, buf, sems)

            return carry

        lax.fori_loop(0, 2 * self.size - 1, visit, 0)

    def _second(self, way):
        return self.t == (1 if way == 0 else self.size - 2)

    def send_sum(self, way, shard, part, terms, buf, sems):
        step = min(32, self.sub)

        def add(i, carry):
            rows = pl.ds(part * self.sub + i * step, step)
            total = buf[shard, rows, :].astype(F32) + terms[shard, rows, :].astype(F32)
            buf[shard, rows, :] = total.astype(BF16)
            return carry

        lax.fori_loop(0, self.sub // step, add, 0)
        held = self._rows(buf, shard, part)
        self._copy(held, buf, sems, way, shard, part).start()

    def early_sends(self, terms, bufs, sems, early):
        for way in (0, 1):

            @pl.when(self._second(way))
            def _(way=way):
                early[way].wait()
                for part in range(SUBS):
                    shard = self.size - 1 if way == 0 else 0
                    self.send_sum(way, shard, part, terms, bufs[way], sems)

    def scatter_step(self, way, j, part, terms, buf, sems, ends=None, early=False):
        t, last = self.t, self.size - 1
        shard = last - j if way == 0 else j
        beyond = (shard > t) if way == 0 else (shard < t)
        starts = (t == 0) if way == 0 else (t == last)
        step = min(32, self.sub)
        if ends is None:
            goes, stays = beyond, None
        else:
            goes = (shard > t + 1) if way == 0 else (shard < t - 1)
            stays = (shard == t + 1) if way == 0 else (shard == t - 1)

        done = early and j == 0

        if not done:

            @pl.when(goes & starts)
            def _():
                self._copy(self._rows(terms, shard, part), buf, sems, way, shard, part).start()

        relays = goes & jnp.logical_not(starts)
        if done:
            relays = relays & jnp.logical_not(self._second(way))

        @pl.when(relays)
        def _():
            held = self._rows(buf, shard, part)
            self._copy(held, buf, sems, way, shard, part).wait_recv()
            self.send_sum(way, shard, part, terms, buf, sems)

        if stays is None:
            return

        @pl.when(stays & starts)
        def _():
            rows = pl.ds(part * self.sub, self.sub)
            ends[way, rows, :] = terms[shard, rows, :]

        @pl.when(stays & jnp.logical_not(starts))
        def _():
            held = self._rows(buf, shard, part)
            self._copy(held, buf, sems, way, shard, part).wait_recv()

            def add(i, carry):
                rows = pl.ds(part * self.sub + i * step, step)
                total = buf[shard, rows, :].astype(F32) + terms[shard, rows, :].astype(F32)
                ends[way, rows, :] = total.astype(BF16)
                return carry

            lax.fori_loop(0, self.sub // step, add, 0)

    def phase(self, gather=None, scatter=None, on_slot=None, near=None, ends=None, start=0):
        n = self.size
        for k in range(start, n):
            for part in range(SUBS):
                for way in (0, 1):
                    if gather is not None:
                        self.gather_step(way, k, part, gather[0], gather[1], gather[2], near)
                    if scatter is not None:
                        if gather is None:
                            if k < n - 1:
                                self.scatter_step(way, k, part, scatter[0], scatter[1][way], scatter[2])
                        else:
                            behind = self.t if way == 0 else n - 1 - self.t
                            for b in range(k):

                                @pl.when(behind == b)
                                def _(b=b, k=k, part=part, way=way):
                                    self.scatter_step(
                                        way, k - 1 - b, part, scatter[0], scatter[1][way],
                                        scatter[2], ends,
                                    )
            if on_slot is not None:
                on_slot(k)

    def own_wait(self, bufs, sems, part):
        for way in (0, 1):
            arrives = self.t > 0 if way == 0 else self.t < self.size - 1

            @pl.when(arrives)
            def _(way=way):
                held = self._rows(bufs[way], self.t, part)
                self._copy(held, bufs[way], sems, way, self.t, part).wait_recv()

    def own_sum(self, terms, bufs, rows):
        t = self.t
        zero = jnp.zeros((), F32)
        right = jnp.where(t > 0, bufs[0][t, rows, :].astype(F32), zero)
        left = jnp.where(t < self.size - 1, bufs[1][t, rows, :].astype(F32), zero)
        return terms[t, rows, :].astype(F32) + right + left

    def drain_gather(self, buf, sems, first=0):
        for way in (0, 1):
            for k in range(first, self.size):
                shard = self.t - k if way == 0 else self.t + k
                inside = (self.t >= k) if way == 0 else (self.t + k <= self.size - 1)

                @pl.when(inside & self._edge(way))
                def _(way=way, shard=shard):
                    for part in range(SUBS):
                        held = self._rows(buf, shard, part)
                        self._copy(held, buf, sems, way, shard, part).wait_send()

    def drain_scatter(self, bufs, sems, margin=0, early=False):
        for way in (0, 1):
            for j in range(self.size - 1):
                shard = self.size - 1 - j if way == 0 else j
                beyond = (shard > self.t + margin) if way == 0 else (shard < self.t - margin)
                if early and j == 0:
                    beyond = beyond & self._edge(1 - way)

                @pl.when(beyond)
                def _(way=way, shard=shard):
                    for part in range(SUBS):
                        held = self._rows(bufs[way], shard, part)
                        self._copy(held, bufs[way], sems, way, shard, part).wait_send()


def line_sems(size):
    return [pltpu.SemaphoreType.DMA((2, size, SUBS)), pltpu.SemaphoreType.DMA((2, size, SUBS))]


def fold(x):
    rows, width = x.shape
    return jnp.sum(x.reshape(rows // 8, 8, width), axis=0)


def normal(x):
    centre = x - jnp.mean(x, axis=-1, keepdims=True)
    spread = lax.rsqrt(jnp.mean(centre * centre, axis=-1, keepdims=True) + EPS)
    return centre * spread, spread


def normal_back(upstream, normed, spread, gain):
    scaled = upstream * gain
    mean_part = jnp.mean(scaled, axis=-1, keepdims=True)
    across = jnp.mean(scaled * normed, axis=-1, keepdims=True)
    return spread * (scaled - mean_part - normed * across)


def row_loop(rows, step, body, base=0):
    def one(i, carry):
        body(pl.ds(pl.multiple_of(base + i * step, step), step))
        return carry

    lax.fori_loop(0, rows // step, one, 0)


def params(collective_id=None):
    if collective_id is None:
        return pltpu.CompilerParams(vmem_limit_bytes=VMEM_CAP)
    return pltpu.CompilerParams(
        collective_id=collective_id, has_side_effects=True, vmem_limit_bytes=VMEM_CAP
    )


def first_kernel(n_dp, size, part, small, own, smalls, a_out, tok, send, recv, gs, gr):
    line = Line(size, own.shape[0])
    me = lax.axis_index("dp")
    rows, width = own.shape
    sem = pltpu.get_barrier_semaphore()
    for p in range(1, n_dp):
        pl.semaphore_signal(sem, device_id={"dp": lax.rem(me + p, n_dp)}, device_id_type=MESH)
    ends = line.greet(sem)
    pl.semaphore_wait(sem, ends + n_dp - 1)
    sems = (gs, gr)

    def small_copy(p, slot):
        return pltpu.make_async_remote_copy(
            src_ref=small,
            dst_ref=smalls.at[slot],
            send_sem=send.at[p],
            recv_sem=recv.at[slot],
            device_id={"dp": lax.rem(me + p, n_dp)},
            device_id_type=MESH,
        )

    for p in range(1, n_dp):
        small_copy(p, me).start()
    smalls[pl.ds(me, 1)] = small[...][None]
    step = min(32, rows)
    vec_rows = part // 128

    def normalise(source, shard):
        gain = jnp.concatenate(
            [smalls[d, r : r + 1, :] for d in range(n_dp) for r in range(vec_rows)], axis=1
        ).astype(F32)
        shift = jnp.concatenate(
            [smalls[d, r : r + 1, :] for d in range(n_dp) for r in range(vec_rows, 2 * vec_rows)],
            axis=1,
        ).astype(F32)

        def body(at):
            x = source[at, :] if shard is None else source[shard, at, :]
            normed, _ = normal(x.astype(F32))
            to = line.t if shard is None else shard
            a_out[to, at, :] = (normed * gain + shift).astype(BF16)

        row_loop(rows, step, body)

    def on_slot(k):
        if k == 0:
            for p in range(1, n_dp):
                small_copy(p, lax.rem(me + p, n_dp)).wait_recv()
            normalise(own, None)
        else:

            @pl.when(line.t >= k)
            def _():
                normalise(tok, line.t - k)

            @pl.when(line.t + k <= size - 1)
            def _():
                normalise(tok, line.t + k)

    line.phase(gather=(tok, sems, own), on_slot=on_slot)
    line.drain_gather(tok, sems)
    for p in range(1, n_dp):
        small_copy(p, me).wait_send()


def first(small, own, part, n_dp, size, cid):
    rows, width = own.shape
    return pl.pallas_call(
        functools.partial(first_kernel, n_dp, size, part),
        out_shape=(
            jax.ShapeDtypeStruct((n_dp,) + small.shape, small.dtype),
            jax.ShapeDtypeStruct((size, rows, width), BF16),
        ),
        in_specs=[WHOLE, WHOLE],
        out_specs=(WHOLE, WHOLE),
        scratch_shapes=[
            pltpu.VMEM((size, rows, width), BF16),
            pltpu.SemaphoreType.DMA((n_dp,)),
            pltpu.SemaphoreType.DMA((n_dp,)),
        ]
        + line_sems(size),
        compiler_params=params(cid),
        name="first",
    )(small, own)


def middle_kernel(
    size, terms, cot, near, tok, valid, vecs, c_out, gm_out, mid_out, stats,
    right, left, gs, gr, ss, sr, near_sem,
):
    line = Line(size, tok.shape[0])
    rows = tok.shape[0]
    step = min(32, line.sub)
    own = pltpu.make_async_copy(cot, gm_out.at[line.t], near_sem.at[2])
    own.start()
    line.barrier()

    def keep(way):
        shard = line.t - 1 if way == 0 else line.t + 1
        return pltpu.make_async_copy(near.at[way], gm_out.at[shard], near_sem.at[way])

    def keep_all(act):
        for way in (0, 1):

            @pl.when(line._edge(1 - way))
            def _(way=way):
                act(keep(way))

    keep_all(lambda copy: copy.start())
    line.phase(
        gather=(gm_out, (gs, gr), None),
        scatter=(terms, (right, left), (ss, sr)),
        near=near,
        start=1,
    )
    stats[...] = jnp.zeros_like(stats)

    def body(at):
        attn = line.own_sum(terms, (right, left), at) + vecs[2:3, :]
        x = tok[at, :].astype(F32)
        mid = x + attn
        normed, _ = normal(mid)
        c_out[at, :] = (normed * vecs[3:4, :] + vecs[4:5, :]).astype(BF16)
        mid_out[at, :] = mid
        ok = valid[at, 0:1]
        stats[0:8, :] += fold(ok * x * x)
        stats[8:16, :] += fold(ok * attn * attn)
        stats[16:24, :] += fold(ok * mid * mid)

    for piece in range(SUBS):
        line.own_wait((right, left), (ss, sr), piece)
        row_loop(line.sub, step, body, piece * line.sub)
    own.wait()
    keep_all(lambda copy: copy.wait())
    line.drain_gather(gm_out, (gs, gr), 1)
    line.drain_scatter((right, left), (ss, sr))


def middle(terms, cot, near, tok, valid, vecs, size, cid):
    rows, width = tok.shape
    full = (size, rows, width)
    return pl.pallas_call(
        functools.partial(middle_kernel, size),
        out_shape=(
            jax.ShapeDtypeStruct((rows, width), BF16),
            jax.ShapeDtypeStruct(full, BF16),
            jax.ShapeDtypeStruct((rows, width), F32),
            jax.ShapeDtypeStruct((24, width), F32),
        ),
        in_specs=[WHOLE, HBM, HBM, WHOLE, WHOLE, WHOLE],
        out_specs=(WHOLE,) * 4,
        scratch_shapes=[pltpu.VMEM(full, BF16), pltpu.VMEM(full, BF16)]
        + line_sems(size)
        + line_sems(size)
        + [pltpu.SemaphoreType.DMA((3,))],
        compiler_params=params(cid),
        name="middle",
    )(terms, cot, near, tok, valid, vecs)


def back_middle_kernel(
    size, terms, landed, mlp_in, gm_in, mid_in, vecs, out_in, gz_out, gmid_out, ends, stats,
    go_out, right, left, right2, left2, mlp, gm, mid, out_w,
    ss, sr, ms, mr, gs, gr, early_sem, load_sem,
):
    rows = mid.shape[0]
    line = Line(size, rows)
    step = min(32, line.sub)
    early = line.early_start(landed, (right, left), early_sem)
    loads = [
        pltpu.make_async_copy(src, dst, load_sem.at[i])
        for i, (src, dst) in enumerate(
            ((gm_in, gm), (mid_in, mid), (mlp_in, mlp), (out_in, out_w))
        )
    ]
    for load in loads:
        load.start()
    line.barrier()
    line.early_sends(terms, (right, left), (ss, sr), early)
    for j in range(size - 1):
        for piece in range(SUBS):
            for way in (0, 1):
                line.scatter_step(
                    way, j, piece, terms, (right, left)[way], (ss, sr), None, True
                )
    for load in loads:
        load.wait()
    stats[...] = jnp.zeros_like(stats)

    def body(at):
        e = line.own_sum(terms, (right, left), at)
        normed, spread = normal(mid[at, :])
        gy = gm[at, :].astype(F32)
        gmid = gy + normal_back(e, normed, spread, vecs[3:4, :])
        gz_out[line.t, at, :] = gmid.astype(BF16)
        gmid_out[at, :] = gmid
        stats[0:8, :] += fold(e * normed)
        stats[8:16, :] += fold(e)
        stats[16:24, :] += fold(gmid)
        stats[24:32, :] += fold(gy)

    for piece in range(SUBS):
        line.own_wait((right, left), (ss, sr), piece)
        row_loop(line.sub, step, body, piece * line.sub)
        for way in (0, 1):
            line.gather_step(way, 0, piece, gz_out, (gs, gr), None)
    def weigh(shard):
        go_out[shard] = dot_t(gz_out[shard], out_w[...]).astype(BF16)

    def on_slot(k):
        def side(i, carry):
            shard = line.t + k * (2 * i - 1)

            @pl.when((shard >= 0) & (shard < size))
            def _():
                weigh(shard)

            return carry

        lax.fori_loop(0, 1 if k == 0 else 2, side, 0)

    on_slot(0)
    line.phase(
        gather=(gz_out, (gs, gr), None),
        scatter=(mlp, (right2, left2), (ms, mr)),
        on_slot=on_slot,
        ends=ends,
        start=1,
    )
    line.drain_scatter((right, left), (ss, sr), 0, True)
    line.drain_scatter((right2, left2), (ms, mr), 1)
    line.drain_gather(gz_out, (gs, gr))


def back_middle(terms, landed, mlp, gm, mid, vecs, out_w, size, cid):
    rows, width = mid.shape
    local = out_w.shape[0]
    full = (size, rows, width)
    return pl.pallas_call(
        functools.partial(back_middle_kernel, size),
        out_shape=(
            jax.ShapeDtypeStruct(full, BF16),
            jax.ShapeDtypeStruct((rows, width), F32),
            jax.ShapeDtypeStruct((2, rows, width), BF16),
            jax.ShapeDtypeStruct((32, width), F32),
            jax.ShapeDtypeStruct((size, rows, local), BF16),
        ),
        in_specs=[WHOLE, HBM, HBM, HBM, HBM, WHOLE, HBM],
        out_specs=(WHOLE,) * 5,
        scratch_shapes=[pltpu.VMEM(full, BF16)] * 5
        + [
            pltpu.VMEM((rows, width), BF16),
            pltpu.VMEM((rows, width), F32),
            pltpu.VMEM((local, width), BF16),
        ]
        + line_sems(size)
        + line_sems(size)
        + line_sems(size)
        + [pltpu.SemaphoreType.DMA((2,)), pltpu.SemaphoreType.DMA((4,))],
        compiler_params=params(cid),
        name="back_middle",
    )(terms, landed, mlp, gm, mid, vecs, out_w)


def finish_kernel(
    n_dp, size, shared, terms, first_landed, tok_in, gmid_in, mlp, landed, mid_in, valid, vecs, given,
    grad_out, y_out, reduced, rms, right, left, own_mlp, tok, ends, gmid, mid,
    stats, blocks, land, sums, land2, ss, sr, load_sem, early_sem, s1, r1, s2, r2,
):
    rows = tok.shape[0]
    line = Line(size, rows)
    step = min(32, line.sub)
    loads = [
        pltpu.make_async_copy(src, dst, load_sem.at[i])
        for i, (src, dst) in enumerate(
            (
                (mlp.at[line.t], own_mlp), (landed, ends), (mid_in, mid),
                (tok_in, tok), (gmid_in, gmid),
            )
        )
    ]
    early = line.early_start(first_landed, (right, left), early_sem)
    for load in loads:
        load.start()
    me = lax.axis_index("dp")
    entry = pltpu.get_barrier_semaphore()
    for p in range(1, n_dp):
        pl.semaphore_signal(entry, device_id={"dp": lax.rem(me + p, n_dp)}, device_id_type=MESH)
    for p in range(1, size):
        pl.semaphore_signal(
            entry, device_id={"tensor": lax.rem(line.t + p, size)}, device_id_type=MESH
        )
    pl.semaphore_wait(entry, n_dp + size - 2)
    line.early_sends(terms, (right, left), (ss, sr), early)
    stats[...] = jnp.zeros_like(stats)

    def tail(at):
        zero = jnp.zeros((), F32)
        from_left = jnp.where(line.t > 0, ends[0, at, :].astype(F32), zero)
        from_right = jnp.where(line.t < size - 1, ends[1, at, :].astype(F32), zero)
        out = own_mlp[at, :].astype(F32) + from_left + from_right + vecs[5:6, :]
        y = mid[at, :] + out
        y_out[at, :] = y.astype(BF16)
        ok = valid[at, 0:1]
        stats[16:24, :] += fold(ok * out * out)
        stats[24:32, :] += fold(ok * y * y)

    for j in range(size - 1):
        for piece in range(SUBS):
            for way in (0, 1):
                line.scatter_step(
                    way, j, piece, terms, (right, left)[way], (ss, sr), None, True
                )
        if j == 0:
            for load in loads:
                load.wait()
            row_loop(rows, step, tail)

    def body(at):
        e = line.own_sum(terms, (right, left), at)
        normed, spread = normal(tok[at, :].astype(F32))
        grad_out[at, :] = gmid[at, :] + normal_back(e, normed, spread, vecs[0:1, :])
        stats[0:8, :] += fold(e * normed)
        stats[8:16, :] += fold(e)

    for piece in range(SUBS):
        line.own_wait((right, left), (ss, sr), piece)
        row_loop(line.sub, step, body, piece * line.sub)
    per = tok.shape[1] // n_dp // 128
    blocks[...] = given[...]

    def lanes(total, chunk):
        return total[:, chunk * 128 : (chunk + 1) * 128]

    for place, group in ((0, 0), (1, 1)):
        total = jnp.sum(stats[8 * group : 8 * group + 8, :], axis=0, keepdims=True)
        for d in range(n_dp):
            for r in range(per):
                row = place * per + r
                blocks[d, row : row + 1, :] = lanes(total, d * per + r)
    for place, group in ((9, 2), (10, 3)):
        total = jnp.sum(stats[8 * group : 8 * group + 8, :], axis=0, keepdims=True)
        short = lanes(total, 0)
        for chunk in range(1, n_dp * per):
            short = short + lanes(total, chunk)
        for d in range(n_dp):
            row = place * per
            blocks[d, row : row + 1, :] = short

    def one(p):
        other = lax.rem(me + p, n_dp)
        return pltpu.make_async_remote_copy(
            src_ref=blocks.at[other],
            dst_ref=land.at[p],
            send_sem=s1.at[p],
            recv_sem=r1.at[p],
            device_id={"dp": other},
            device_id_type=MESH,
        )

    for p in range(1, n_dp):
        one(p).start()
    total = blocks[me]
    for p in range(1, n_dp):
        one(p).wait_recv()
        total = total + land[p]
    sums[...] = total

    def two(p):
        return pltpu.make_async_remote_copy(
            src_ref=sums.at[pl.ds(0, shared)],
            dst_ref=land2.at[p],
            send_sem=s2.at[p],
            recv_sem=r2.at[p],
            device_id={"tensor": lax.rem(line.t + p, size)},
            device_id_type=MESH,
        )

    for p in range(1, size):
        two(p).start()
    reduced[...] = total
    top = sums[pl.ds(0, shared), :]
    for p in range(1, size):
        two(p).wait_recv()
        top = top + land2[p]
    reduced[pl.ds(0, shared), :] = top
    count = reduced[11 * per : 11 * per + 1, :] * jnp.float32(tok.shape[1])
    for i in range(5):
        row = (6 + i) * per
        square = jnp.sum(reduced[row : row + per, :], keepdims=True)
        rms[i : i + 1, :] = jnp.sqrt(square / count)
    line.drain_scatter((right, left), (ss, sr), 0, True)
    for p in range(1, n_dp):
        one(p).wait_send()
    for p in range(1, size):
        two(p).wait_send()


def finish(
    terms, first_landed, tok, gmid, mlp, landed, mid, valid, vecs, given, shared, size, cid
):
    rows, width = tok.shape
    n_dp, lines, _ = given.shape
    full = (size, rows, width)
    return pl.pallas_call(
        functools.partial(finish_kernel, n_dp, size, shared),
        out_shape=(
            jax.ShapeDtypeStruct((rows, width), F32),
            jax.ShapeDtypeStruct((rows, width), BF16),
            jax.ShapeDtypeStruct((lines, 128), F32),
            jax.ShapeDtypeStruct((8, 128), F32),
        ),
        in_specs=[WHOLE] + [HBM] * 6 + [WHOLE] * 3,
        out_specs=(WHOLE,) * 4,
        scratch_shapes=[pltpu.VMEM(full, BF16)] * 2
        + [pltpu.VMEM((rows, width), BF16)] * 2
        + [pltpu.VMEM((2, rows, width), BF16)]
        + [pltpu.VMEM((rows, width), F32)] * 2
        + [
            pltpu.VMEM((32, width), F32),
            pltpu.VMEM((n_dp, lines, 128), F32),
            pltpu.VMEM((n_dp, lines, 128), F32),
            pltpu.VMEM((lines, 128), F32),
            pltpu.VMEM((size, shared, 128), F32),
        ]
        + line_sems(size)
        + [
            pltpu.SemaphoreType.DMA((5,)),
            pltpu.SemaphoreType.DMA((2,)),
            pltpu.SemaphoreType.DMA((n_dp,)),
            pltpu.SemaphoreType.DMA((n_dp,)),
            pltpu.SemaphoreType.DMA((size,)),
            pltpu.SemaphoreType.DMA((size,)),
        ],
        compiler_params=params(cid),
        name="finish",
    )(terms, first_landed, tok, gmid, mlp, landed, mid, valid, vecs, given)


BLOCK = 256
NEG = -1e30
SCALE = HD**-0.5


def dot(a, b):
    return jnp.dot(a, b, preferred_element_type=F32)


def dot_t(a, b):
    return lax.dot_general(a, b, (((1,), (1,)), ((), ())), preferred_element_type=F32)


def masked_scores(q, k, keys, first, bar):
    scores = dot_t(k, q) * SCALE + bar
    key_pos = lax.broadcasted_iota(jnp.int32, (keys, BLOCK), 0)
    query_pos = first + lax.broadcasted_iota(jnp.int32, (keys, BLOCK), 1)
    return jnp.where(key_pos <= query_pos, scores, NEG)


def head_cols(part, h, heads):
    return pl.ds(pl.multiple_of((part * heads + h) * HD, HD), HD)


def weight_loads(weights, cols, sem, part):
    n_dp, _, rows, local = weights.shape
    return [
        pltpu.make_async_copy(
            weights.at[d, part],
            cols.at[pl.ds(d * rows, rows), pl.ds(part * local, local)],
            sem.at[part, d],
        )
        for d in range(n_dp)
    ]


def front_kernel(
    size, heads, a, weights, shift, bar, out_w, cot, qkv, mixed_all, log_totals, terms, near,
    cols, gs, gr, load_sem,
):
    h = pl.program_id(0)
    rows = cot.shape[0]
    local = heads * HD
    line = Line(size, rows)

    @pl.when(h == 0)
    def _():
        for part in range(3):
            for load in weight_loads(weights, cols, load_sem, part):
                load.start()
        line.barrier()
        line.hop_start((cot, cot), near, (gs, gr))
        for part in range(3):
            for load in weight_loads(weights, cols, load_sem, part):
                load.wait()
            span = slice(part * local, (part + 1) * local)

            def product(at, span=span):
                qkv[at, span] = (dot(a[at, :], cols[:, span]) + shift[0:1, span]).astype(BF16)

            row_loop(LEN, min(256, LEN), product)

    at_q, at_k, at_v = (head_cols(part, h, heads) for part in range(3))
    value_cols = qkv[:, at_v].T
    for block in range(LEN // BLOCK):
        first, keys = block * BLOCK, (block + 1) * BLOCK
        here = slice(first, first + BLOCK)
        scores = masked_scores(qkv[here, at_q], qkv[0:keys, at_k], keys, first, bar[0:keys, 0:1])
        top = jnp.max(scores, axis=0, keepdims=True)
        powers = jnp.exp(scores - top)
        total = jnp.sum(powers, axis=0, keepdims=True)
        shares = (powers * (1.0 / total)).astype(BF16)
        mixed = dot(value_cols[:, 0:keys], shares)
        mixed_all[here, head_cols(0, h, heads)] = mixed.T.astype(BF16)
        log_totals[0, :, here] = jnp.broadcast_to(top + jnp.log(total), (8, BLOCK))

    @pl.when(h == heads - 1)
    def _():
        def project(at):
            terms[at, :] = dot(mixed_all[at, :], out_w[...]).astype(BF16)

        row_loop(LEN, min(256, LEN), project)
        line.hop_wait((cot, cot), near, (gs, gr))


def front(a, weights, shift, bar, out_w, cot, size, cid):
    n_dp, _, part, local = weights.shape
    width, local3 = n_dp * part, 3 * local
    heads = local // HD
    return pl.pallas_call(
        functools.partial(front_kernel, size, heads),
        grid=(heads,),
        out_shape=(
            jax.ShapeDtypeStruct((LEN, local3), BF16),
            jax.ShapeDtypeStruct((LEN, local), BF16),
            jax.ShapeDtypeStruct((heads, 8, LEN), F32),
            jax.ShapeDtypeStruct((LEN, width), BF16),
            jax.ShapeDtypeStruct((2,) + cot.shape, BF16),
        ),
        in_specs=[WHOLE, HBM, WHOLE, WHOLE, WHOLE, HBM],
        out_specs=(
            pl.BlockSpec((LEN, local3), lambda h: (0, 0)),
            pl.BlockSpec((LEN, local), lambda h: (0, 0)),
            pl.BlockSpec((1, 8, LEN), lambda h: (h, 0, 0)),
            pl.BlockSpec((LEN, width), lambda h: (0, 0)),
            HBM,
        ),
        scratch_shapes=[
            pltpu.VMEM((width, local3), BF16),
            pltpu.SemaphoreType.DMA((2,)),
            pltpu.SemaphoreType.DMA((2,)),
            pltpu.SemaphoreType.DMA((3, n_dp)),
        ],
        compiler_params=params(cid),
        name="front",
    )(a, weights, shift, bar, out_w, cot)


def attend_back_kernel(
    size, heads, q, k, v, go, bar, log_totals, weights, ends, out, sums, terms, landed,
    key_grad, value_grad, cols, gs, gr, load_sem,
):
    h = pl.program_id(0)
    line = Line(size, ends.shape[1])
    srcs = (ends.at[0], ends.at[1])
    loads = [load for part in range(3) for load in weight_loads(weights, cols, load_sem, part)]

    @pl.when(h == 0)
    def _():
        for load in loads:
            load.start()
        line.barrier()
        line.hop_start(srcs, landed, (gs, gr))

    key_cols = k[...].T
    query_sum = jnp.zeros((1, HD), F32)
    at_q, at_k, at_v = (head_cols(part, h, heads) for part in range(3))
    for block in range(LEN // BLOCK - 1, -1, -1):
        first, keys = block * BLOCK, (block + 1) * BLOCK
        here = slice(first, first + BLOCK)
        scores = masked_scores(q[here, :], k[0:keys, :], keys, first, bar[0:keys, 0:1])
        shares = jnp.exp(scores - log_totals[0, 0:1, here])
        share_grad = dot_t(v[0:keys, :], go[here, :])
        centre = jnp.sum(shares * share_grad, axis=0, keepdims=True)
        score_grad = (shares * (share_grad - centre)).astype(BF16)
        values = dot(shares.astype(BF16), go[here, :])
        keyed = dot(score_grad, q[here, :])
        if block == LEN // BLOCK - 1:
            value_grad[...] = values
            key_grad[...] = keyed
        else:
            value_grad[0:keys, :] += values
            key_grad[0:keys, :] += keyed
        query_grad = ((dot(key_cols[:, 0:keys], score_grad)) * SCALE).T.astype(BF16)
        out[here, at_q] = query_grad
        query_sum = query_sum + jnp.sum(query_grad.astype(F32), axis=0, keepdims=True)
    out[:, at_k] = (key_grad[...] * SCALE).astype(BF16)
    rounded = value_grad[...].astype(BF16)
    out[:, at_v] = rounded
    value_sum = jnp.sum(rounded.astype(F32), axis=0, keepdims=True)
    sums[0, 0:8, :] = jnp.broadcast_to(query_sum, (8, HD))
    sums[0, 8:16, :] = jnp.broadcast_to(value_sum, (8, HD))

    @pl.when(h == heads - 1)
    def _():
        for load in loads:
            load.wait()

        def product(at):
            terms[at, :] = dot_t(out[at, :], cols[...]).astype(BF16)

        row_loop(LEN, min(256, LEN), product)
        line.hop_wait(srcs, landed, (gs, gr))


def attend_back(qkv, go, bar, log_totals, weights, ends, size, cid):
    n_dp, _, part, local = weights.shape
    width, local3 = n_dp * part, 3 * local
    heads = local // HD

    def column(place):
        return pl.BlockSpec((LEN, HD), lambda h: (0, place * heads + h))

    return pl.pallas_call(
        functools.partial(attend_back_kernel, size, heads),
        grid=(heads,),
        out_shape=(
            jax.ShapeDtypeStruct((LEN, local3), BF16),
            jax.ShapeDtypeStruct((heads, 16, HD), F32),
            jax.ShapeDtypeStruct((LEN, width), BF16),
            jax.ShapeDtypeStruct(ends.shape, BF16),
        ),
        in_specs=[
            column(0), column(1), column(2), column(0),
            pl.BlockSpec((LEN, 128), lambda h: (0, 0)),
            pl.BlockSpec((1, 8, LEN), lambda h: (h, 0, 0)),
            HBM, HBM,
        ],
        out_specs=(
            pl.BlockSpec((LEN, local3), lambda h: (0, 0)),
            pl.BlockSpec((1, 16, HD), lambda h: (h, 0, 0)),
            pl.BlockSpec((LEN, width), lambda h: (0, 0)),
            HBM,
        ),
        scratch_shapes=[
            pltpu.VMEM((LEN, HD), F32),
            pltpu.VMEM((LEN, HD), F32),
            pltpu.VMEM((width, local3), BF16),
            pltpu.SemaphoreType.DMA((2,)),
            pltpu.SemaphoreType.DMA((2,)),
            pltpu.SemaphoreType.DMA((3, n_dp)),
        ],
        compiler_params=params(cid),
        name="attend_back",
    )(qkv, qkv, qkv, go, bar, log_totals, weights, ends)


def gelu_both(u):
    inner = 0.7978845608028654 * (u + 0.044715 * (u * u * u))
    th = jnp.tanh(inner)
    half = 0.5 * (1.0 + th)
    slope = half + 0.5 * u * (1.0 - th * th) * (
        0.7978845608028654 * (1.0 + 3 * 0.044715 * (u * u))
    )
    return u * half, slope


def hidden_kernel(
    n_dp, size, c_own, gm_in, up_in, down_in, bias,
    c_out, act_out, gu_out, mlp_out, back_out, sums, gm, up, down, act, gu, mlp, back, gs, gr, in_sem, out_sem,
):
    line = Line(size, c_own.shape[0])
    rows, width = c_own.shape
    units, part = down.shape[1], down.shape[2]
    block = min(512, units)
    loads = [
        pltpu.make_async_copy(up_in, up, in_sem.at[0]),
        pltpu.make_async_copy(down_in, down, in_sem.at[1]),
        pltpu.make_async_copy(gm_in, gm, in_sem.at[2]),
    ]
    for load in loads:
        load.start()
    line.barrier()
    for piece in range(SUBS):
        for way in (0, 1):
            line.gather_step(way, 0, piece, c_out, (gs, gr), c_own)
    c_out[pl.ds(line.t, 1)] = c_own[...][None]
    sums[...] = jnp.zeros_like(sums)
    for load in loads:
        load.wait()

    def stores(shard):
        pairs = ((act, act_out), (gu, gu_out), (mlp, mlp_out), (back, back_out))
        return [
            pltpu.make_async_copy(src.at[shard], dst.at[shard], out_sem.at[i, shard])
            for i, (src, dst) in enumerate(pairs)
        ]

    def work(shard):
        def unit_block(j, carry):
            at = pl.ds(pl.multiple_of(j * block, block), block)
            u = dot(c_out[shard], up[:, at]) + bias[0:1, at]
            grad = dot_t(gm[shard, :, 0:part], down[0, at, :])
            for d in range(1, n_dp):
                grad = grad + dot_t(gm[shard, :, d * part : (d + 1) * part], down[d, at, :])
            value, slope = gelu_both(u)
            act[shard, :, at] = value.astype(BF16)
            rounded = (grad * slope).astype(BF16)
            gu[shard, :, at] = rounded
            sums[:, at] += fold(rounded.astype(F32))
            return carry

        lax.fori_loop(0, units // block, unit_block, 0)

        def feature_block(d, carry):
            at = pl.ds(pl.multiple_of(d * part, part), part)
            mlp[shard, :, at] = dot(act[shard], down[d]).astype(BF16)
            back[shard, :, at] = dot_t(gu[shard], up[at, :]).astype(BF16)
            return carry

        lax.fori_loop(0, n_dp, feature_block, 0)
        for store in stores(shard):
            store.start()

    line.walk(c_out, (gs, gr), work)
    line.drain_gather(c_out, (gs, gr))
    for shard in range(size):
        for store in stores(shard):
            store.wait()


def hidden(c_own, gm, up, down, bias, size, cid):
    rows, width = c_own.shape
    n_dp, units, part = down.shape
    full, wide = (size, rows, width), (size, rows, units)
    return pl.pallas_call(
        functools.partial(hidden_kernel, n_dp, size),
        out_shape=(
            jax.ShapeDtypeStruct(full, BF16),
            jax.ShapeDtypeStruct(wide, BF16),
            jax.ShapeDtypeStruct(wide, BF16),
            jax.ShapeDtypeStruct(full, BF16),
            jax.ShapeDtypeStruct(full, BF16),
            jax.ShapeDtypeStruct((8, units), F32),
        ),
        in_specs=[WHOLE, HBM, HBM, HBM, WHOLE],
        out_specs=(WHOLE, HBM, HBM, HBM, HBM, WHOLE),
        scratch_shapes=[
            pltpu.VMEM(full, BF16),
            pltpu.VMEM((width, units), BF16),
            pltpu.VMEM((n_dp, units, part), BF16),
            pltpu.VMEM(wide, BF16),
            pltpu.VMEM(wide, BF16),
            pltpu.VMEM(full, BF16),
            pltpu.VMEM(full, BF16),
        ]
        + line_sems(size)
        + [pltpu.SemaphoreType.DMA((3,)), pltpu.SemaphoreType.DMA((4, size))],
        compiler_params=params(cid),
        name="hidden",
    )(c_own, gm, up, down, bias)


def cross(left, right):
    return lax.dot_general(left, right, (((0,), (0,)), ((), ())), preferred_element_type=F32)


def products_kernel(
    size, steps, act, gm, c, gu_in, terms, down_out, up_out, landed, gu, gs, gr, load_sem
):
    i = pl.program_id(0)
    line = Line(size, terms.shape[1])
    load = pltpu.make_async_copy(gu_in, gu, load_sem.at[0])
    hops = line.first_hops(terms, landed, (gs, gr))

    @pl.when(i == 0)
    def _():
        load.start()
        line.barrier()
        line.hops_start(hops)

    @pl.when(i < steps)
    def _():
        down_out[...] = cross(act[...], gm[...]).astype(BF16)

    @pl.when(i == steps)
    def _():
        load.wait()

    @pl.when(i >= steps)
    def _():
        up_out[...] = cross(c[...], gu[...]).astype(BF16)

    @pl.when(i == pl.num_programs(0) - 1)
    def _():
        line.hops_wait(hops)


def products(act, gm, c, gu, terms, size, cid):
    rows, units = act.shape
    width = gm.shape[1]
    steps, more = units // BLOCK, width // BLOCK
    return pl.pallas_call(
        functools.partial(products_kernel, size, steps),
        grid=(steps + more,),
        out_shape=(
            jax.ShapeDtypeStruct((units, width), BF16),
            jax.ShapeDtypeStruct((width, units), BF16),
            jax.ShapeDtypeStruct((2,) + terms.shape[1:], BF16),
        ),
        in_specs=[
            pl.BlockSpec((rows, BLOCK), lambda i: (0, jnp.minimum(i, steps - 1))),
            WHOLE,
            pl.BlockSpec((rows, BLOCK), lambda i: (0, jnp.maximum(i - steps, 0))),
            HBM,
            HBM,
        ],
        out_specs=(
            pl.BlockSpec((BLOCK, width), lambda i: (jnp.minimum(i, steps - 1), 0)),
            pl.BlockSpec((BLOCK, units), lambda i: (jnp.maximum(i - steps, 0), 0)),
            HBM,
        ),
        scratch_shapes=[
            pltpu.VMEM((rows, units), BF16),
            pltpu.SemaphoreType.DMA((2,)),
            pltpu.SemaphoreType.DMA((2,)),
            pltpu.SemaphoreType.DMA((1,)),
        ],
        compiler_params=params(cid),
        name="products",
    )(act, gm, c, gu, terms)


def head_products_kernel(size, gz, a, o, gqkv, terms, out, landed, gs, gr):
    i = pl.program_id(0)
    line = Line(size, terms.shape[1])
    hops = line.first_hops(terms, landed, (gs, gr))
    local = o.shape[1]

    @pl.when(i == 0)
    def _():
        line.barrier()
        line.hops_start(hops)

    out[:, 0:local] = cross(gz[...], o[...]).astype(BF16)
    out[:, local:] = cross(a[...], gqkv[...]).astype(BF16)

    @pl.when(i == pl.num_programs(0) - 1)
    def _():
        line.hops_wait(hops)


def head_products(gz, a, o, gqkv, terms, size, cid):
    rows, width = a.shape
    columns = o.shape[1] + gqkv.shape[1]
    return pl.pallas_call(
        functools.partial(head_products_kernel, size),
        grid=(width // BLOCK,),
        out_shape=(
            jax.ShapeDtypeStruct((width, columns), BF16),
            jax.ShapeDtypeStruct((2,) + terms.shape[1:], BF16),
        ),
        in_specs=[
            pl.BlockSpec((rows, BLOCK), lambda i: (0, i)),
            pl.BlockSpec((rows, BLOCK), lambda i: (0, i)),
            WHOLE,
            WHOLE,
            HBM,
        ],
        out_specs=(pl.BlockSpec((BLOCK, columns), lambda i: (i, 0)), HBM),
        scratch_shapes=[pltpu.SemaphoreType.DMA((2,)), pltpu.SemaphoreType.DMA((2,))],
        compiler_params=params(cid),
        name="head_products",
    )(gz, a, o, gqkv, terms)


def pad_to(x, count):
    return jnp.pad(x, ((0, 0), (0, count - x.shape[1])))


def shards(
    tokens, lengths, ln1_gain, ln1_bias, qkv_weight, qv_bias, out_weight, out_bias,
    ln2_gain, ln2_bias, up_weight, up_bias, down_weight, down_bias, cotangent,
):
    n_dp, n_t = lax.axis_size("dp"), lax.axis_size("tensor")
    rows, width = tokens.shape
    part = ln1_gain.shape[0]
    local = qkv_weight.shape[2]
    heads = local // HD
    units = up_weight.shape[1]
    hd_part = qv_bias.shape[2]
    t = lax.axis_index("tensor")
    length = lengths[0]

    pieces = [
        ln1_gain, ln1_bias, out_bias, ln2_gain, ln2_bias, down_bias,
        qv_bias.reshape(-1), up_bias.reshape(-1),
    ]
    packed = jnp.concatenate(pieces)
    count = packed.shape[0]
    lanes = -(-count // 2048) * 2048
    small = jnp.pad(packed, (0, lanes - count)).reshape(lanes // 128, 128)
    smalls, a = first(small, tokens, part, n_dp, n_t, 0)
    smalls, a = smalls.reshape(n_dp, lanes), a.reshape(n_t * rows, width)
    vecs = jnp.stack([smalls[:, i * part : (i + 1) * part].reshape(width) for i in range(6)])
    vecs = jnp.pad(vecs, ((0, 2), (0, 0))).astype(F32)
    at = 6 * part
    qv_all = smalls[:, at : at + 2 * heads * hd_part].reshape(n_dp, 2, heads, hd_part)
    qv_all = qv_all.transpose(1, 2, 0, 3).reshape(2, local).astype(F32)
    at += 2 * heads * hd_part
    up_all = smalls[:, at : at + units // n_dp].reshape(n_dp, units // 16, 16 // n_dp)
    up_shift = up_all.transpose(1, 0, 2).reshape(1, units).astype(F32)
    qkv_shift = jnp.concatenate([qv_all[0], jnp.zeros_like(qv_all[0]), qv_all[1]])

    qkv_full = lax.all_gather(
        qkv_weight.transpose(1, 0, 2).reshape(3 * part, local), "dp", axis=0, tiled=False
    ).reshape(n_dp, 3, part, local)
    out_full = lax.all_gather(out_weight, "dp", axis=1, tiled=True)
    up_full = lax.all_gather(up_weight, "dp", axis=0, tiled=True)
    down_blocks = lax.all_gather(down_weight, "dp", axis=0, tiled=False)

    own_pos = t * rows + jnp.arange(rows, dtype=jnp.int32)
    valid_own = (own_pos < length).astype(F32)
    valid = jnp.broadcast_to(valid_own[:, None], (rows, 128))
    positions = jnp.arange(LEN, dtype=jnp.int32)
    bar = jnp.broadcast_to(jnp.where(positions < length, 0.0, NEG)[:, None], (LEN, 128))
    gm_own = (cotangent.astype(F32) * valid_own[:, None]).astype(BF16)

    shift = jnp.broadcast_to(qkv_shift, (8, 3 * local))
    qkv, attended, log_totals, terms, near = front(
        a, qkv_full, shift, bar, out_full, gm_own, n_t, 7
    )
    terms = terms.reshape(n_t, rows, width)
    c_own, gm, mid, stats_a = middle(terms, gm_own, near, tokens, valid, vecs, n_t, 2)
    c, act, gu, mlp, back_terms, up_sums = hidden(
        c_own, gm, up_full, down_blocks, jnp.broadcast_to(up_shift, (8, units)), n_t, 6
    )
    c, gm = c.reshape(-1, width), gm.reshape(-1, width)
    act, gu = act.reshape(-1, units), gu.reshape(-1, units)

    down_grad, up_grad, early = products(act, gm, c, gu, back_terms, n_t, 9)
    down_out = lax.psum_scatter(down_grad, "dp", scatter_dimension=1, tiled=True)
    up_out = lax.psum_scatter(up_grad, "dp", scatter_dimension=0, tiled=True)
    gz, gmid, ends, stats_b, go = back_middle(
        back_terms, early, mlp, gm_own, mid, vecs, out_full, n_t, 3
    )
    gqkv, head_sums, last_terms, landed = attend_back(
        qkv, go.reshape(-1, local), bar, log_totals, qkv_full, ends, n_t, 8
    )
    last_terms = last_terms.reshape(n_t, rows, width)
    head_grad, last_early = head_products(
        gz.reshape(-1, width), a, attended, gqkv, last_terms, n_t, 10
    )
    last_early, head_grad, down_out, up_out = lax.optimization_barrier(
        (last_early, head_grad, down_out, up_out)
    )
    head_out = lax.psum_scatter(head_grad, "dp", scatter_dimension=0, tiled=True)
    out_out = head_out[:, :local].T
    qkv_out = head_out[:, local:].reshape(part, 3, local)
    def vec_sum(stats, i):
        return jnp.sum(stats[8 * i : 8 * i + 8], axis=0)

    def squares(stats, i):
        return jnp.sum(stats[8 * i : 8 * i + 8].reshape(8, n_dp, part), axis=(0, 1))

    vectors = jnp.concatenate(
        [jnp.zeros((2, width), F32), jnp.stack([vec_sum(stats_b, i) for i in (2, 0, 1, 3)])]
    )
    sums = jnp.concatenate([squares(stats_a, i) for i in range(3)] + [jnp.zeros((2 * part,), F32)])
    count = jnp.clip(length - t * rows, 0, rows).astype(F32)
    vector_blocks = vectors.reshape(6, n_dp, part).transpose(1, 0, 2).reshape(n_dp, 6 * part)
    top = jnp.concatenate(
        [
            vector_blocks,
            jnp.broadcast_to(sums[None], (n_dp, 5 * part)),
            jnp.full((n_dp, 128), count),
        ],
        axis=1,
    )
    top_len = -(-top.shape[1] // 1024) * 1024
    up_blocks = jnp.sum(up_sums, axis=0).reshape(units // 16, n_dp, 16 // n_dp)
    up_blocks = up_blocks.transpose(1, 0, 2).reshape(n_dp, units // n_dp)
    qv_sums = jnp.stack([head_sums[:, 0], head_sums[:, 8]])
    qv_blocks = qv_sums.reshape(2, heads, n_dp, hd_part).transpose(2, 0, 1, 3)
    qv_blocks = qv_blocks.reshape(n_dp, 2 * heads * hd_part)
    low = jnp.concatenate([up_blocks, qv_blocks], axis=1)
    low_len = -(-low.shape[1] // 1024) * 1024
    given = jnp.concatenate([pad_to(top, top_len), pad_to(low, low_len)], axis=1)
    given = given.reshape(n_dp, (top_len + low_len) // 128, 128)
    tokens_grad, output, reduced, rms = finish(
        last_terms, last_early, tokens, gmid, mlp, landed, mid, valid, vecs, given,
        top_len // 128, n_t, 4,
    )
    reduced = reduced.reshape(-1)
    outs = [reduced[i * part : (i + 1) * part] for i in range(6)]
    stream_rms = rms[:5, 0]
    at = top_len
    up_bias_out = reduced[at : at + units // n_dp].reshape(up_bias.shape)
    at += units // n_dp
    qv_bias_out = reduced[at : at + 2 * heads * hd_part].reshape(qv_bias.shape)

    return (
        output, tokens_grad, outs[0], outs[1],
        qkv_out.astype(F32), qv_bias_out, out_out.astype(F32), outs[2],
        outs[3], outs[4], up_out.astype(F32), up_bias_out,
        down_out.astype(F32), outs[5], stream_rms,
    )


def solution(mesh):
    vector = P("dp")
    rows = P(("dp", "tensor"), None)
    return jax.shard_map(
        shards,
        mesh=mesh,
        in_specs=(
            rows, vector, vector, vector, P("dp", None, "tensor"), P(None, "tensor", "dp"),
            P("tensor", "dp"), vector, vector, vector, P("dp", "tensor"), P("tensor", "dp"),
            P("tensor", "dp"), vector, rows,
        ),
        out_specs=(
            rows, rows, vector, vector, P("dp", None, "tensor"), P(None, "tensor", "dp"),
            P("tensor", "dp"), vector, vector, vector, P("dp", "tensor"), P("tensor", "dp"),
            P("tensor", "dp"), vector, P(),
        ),
        check_vma=False,
    )
```

```python
import functools

import jax
import jax.numpy as jnp
from jax import lax
from jax.experimental import pallas as pl
from jax.experimental.pallas import tpu as pltpu
from jax.sharding import PartitionSpec as P

HD = 128
LEN = 1024
EPS = 1e-05
MESH = pl.DeviceIdType.MESH
F32 = jnp.float32
BF16 = jnp.bfloat16
VMEM_CAP = 60 * 1024 * 1024
SUBS = 2
WHOLE = pl.BlockSpec(memory_space=pltpu.VMEM)
HBM = pl.BlockSpec(memory_space=pltpu.HBM)


class Line:
    def __init__(self, size, rows):
        self.size, self.rows, self.t = size, rows, lax.axis_index("tensor")
        self.sub = rows // SUBS

    def barrier(self):
        sem = pltpu.get_barrier_semaphore()
        pl.semaphore_wait(sem, self.greet(sem))

    def greet(self, sem):
        @pl.when(self.t > 0)
        def _():
            pl.semaphore_signal(sem, device_id={"tensor": self.t - 1}, device_id_type=MESH)

        @pl.when(self.t < self.size - 1)
        def _():
            pl.semaphore_signal(sem, device_id={"tensor": self.t + 1}, device_id_type=MESH)

        return jnp.where(self.t > 0, 1, 0) + jnp.where(self.t < self.size - 1, 1, 0)

    def _copy(self, src, dst, sems, way, shard, part):
        send, recv = sems
        target = self.t + 1 if way == 0 else self.t - 1
        return pltpu.make_async_remote_copy(
            src_ref=src,
            dst_ref=dst.at[shard, pl.ds(part * self.sub, self.sub)],
            send_sem=send.at[way, shard, part],
            recv_sem=recv.at[way, shard, part],
            device_id={"tensor": target},
            device_id_type=MESH,
        )

    def _rows(self, ref, shard, part):
        return ref.at[shard, pl.ds(part * self.sub, self.sub)]

    def _edge(self, way):
        return self.t < self.size - 1 if way == 0 else self.t > 0

    def hop(self, way, src, dst, sems):
        return pltpu.make_async_remote_copy(
            src_ref=src,
            dst_ref=dst.at[way],
            send_sem=sems[0].at[way],
            recv_sem=sems[1].at[way],
            device_id={"tensor": self.t + 1 if way == 0 else self.t - 1},
            device_id_type=MESH,
        )

    def hop_start(self, srcs, dst, sems):
        for way in (0, 1):

            @pl.when(self._edge(way))
            def _(way=way):
                self.hop(way, srcs[way], dst, sems).start()

    def hop_wait(self, srcs, dst, sems):
        for way in (0, 1):

            @pl.when(self._edge(1 - way))
            def _(way=way):
                self.hop(way, srcs[way], dst, sems).wait_recv()

        for way in (0, 1):

            @pl.when(self._edge(way))
            def _(way=way):
                self.hop(way, srcs[way], dst, sems).wait_send()

    def first_hops(self, terms, landed, sems):
        last = self.size - 1
        return [
            (self.t == sender, self.t == taker, self.hop(way, terms.at[shard], landed, sems))
            for way, sender, taker, shard in ((0, 0, 1, last), (1, last, last - 1, 0))
        ]

    def hops_start(self, hops):
        for sends, _, copy in hops:

            @pl.when(sends)
            def _(copy=copy):
                copy.start()

    def hops_wait(self, hops):
        for sends, takes, copy in hops:

            @pl.when(sends)
            def _(copy=copy):
                copy.wait_send()

            @pl.when(takes)
            def _(copy=copy):
                copy.wait_recv()

    def early_start(self, landed, bufs, sem):
        last = self.size - 1
        early = (
            pltpu.make_async_copy(landed.at[0], bufs[0].at[last], sem.at[0]),
            pltpu.make_async_copy(landed.at[1], bufs[1].at[0], sem.at[1]),
        )
        for copy, holder in zip(early, (1, last - 1)):

            @pl.when(self.t == holder)
            def _(copy=copy):
                copy.start()

        return early

    def gather_step(self, way, k, part, buf, sems, first, near=None):
        t, last = self.t, self.size - 1
        shard = t - k if way == 0 else t + k
        inside = (t >= k) if way == 0 else (t + k <= last)

        @pl.when(inside)
        def _():
            held = self._rows(buf, shard, part)
            if k > 1 or (k == 1 and near is None):
                self._copy(held, buf, sems, way, shard, part).wait_recv()

            @pl.when(self._edge(way))
            def _():
                src = held
                if k == 0 and first is not None:
                    src = first.at[pl.ds(part * self.sub, self.sub)]
                if k == 1 and near is not None:
                    src = near.at[way, pl.ds(part * self.sub, self.sub)]
                self._copy(src, buf, sems, way, shard, part).start()

    def relay(self, k, part, buf, sems):
        for way in (0, 1):
            shard = self.t - k if way == 0 else self.t + k
            inside = (self.t >= k) if way == 0 else (self.t + k <= self.size - 1)

            @pl.when(inside)
            def _(way=way, shard=shard):
                held = self._rows(buf, shard, part)
                self._copy(held, buf, sems, way, shard, part).wait_recv()

                @pl.when(self._edge(way))
                def _():
                    self._copy(held, buf, sems, way, shard, part).start()

    def walk(self, buf, sems, work):
        last_part = SUBS - 1

        def visit(m, carry):
            k = (m + 1) // 2
            shard = jnp.where(m % 2 == 1, self.t - k, self.t + k)

            @pl.when((shard >= 0) & (shard < self.size))
            def _():
                work(shard)

            @pl.when(m == 0)
            def _():
                for part in range(last_part):
                    self.relay(1, part, buf, sems)

            @pl.when(m % 2 == 0)
            def _():
                self.relay(k + 1, last_part, buf, sems)

            @pl.when(m % 2 == 1)
            def _():
                for part in range(last_part):
                    self.relay(k + 1, part, buf, sems)

            return carry

        lax.fori_loop(0, 2 * self.size - 1, visit, 0)

    def _second(self, way):
        return self.t == (1 if way == 0 else self.size - 2)

    def send_sum(self, way, shard, part, terms, buf, sems):
        step = min(32, self.sub)

        def add(i, carry):
            rows = pl.ds(part * self.sub + i * step, step)
            total = buf[shard, rows, :].astype(F32) + terms[shard, rows, :].astype(F32)
            buf[shard, rows, :] = total.astype(BF16)
            return carry

        lax.fori_loop(0, self.sub // step, add, 0)
        held = self._rows(buf, shard, part)
        self._copy(held, buf, sems, way, shard, part).start()

    def early_sends(self, terms, bufs, sems, early):
        for way in (0, 1):

            @pl.when(self._second(way))
            def _(way=way):
                early[way].wait()
                for part in range(SUBS):
                    shard = self.size - 1 if way == 0 else 0
                    self.send_sum(way, shard, part, terms, bufs[way], sems)

    def scatter_step(self, way, j, part, terms, buf, sems, ends=None, early=False):
        t, last = self.t, self.size - 1
        shard = last - j if way == 0 else j
        beyond = (shard > t) if way == 0 else (shard < t)
        starts = (t == 0) if way == 0 else (t == last)
        step = min(32, self.sub)
        if ends is None:
            goes, stays = beyond, None
        else:
            goes = (shard > t + 1) if way == 0 else (shard < t - 1)
            stays = (shard == t + 1) if way == 0 else (shard == t - 1)

        done = early and j == 0

        if not done:

            @pl.when(goes & starts)
            def _():
                self._copy(self._rows(terms, shard, part), buf, sems, way, shard, part).start()

        relays = goes & jnp.logical_not(starts)
        if done:
            relays = relays & jnp.logical_not(self._second(way))

        @pl.when(relays)
        def _():
            held = self._rows(buf, shard, part)
            self._copy(held, buf, sems, way, shard, part).wait_recv()
            self.send_sum(way, shard, part, terms, buf, sems)

        if stays is None:
            return

        @pl.when(stays & starts)
        def _():
            rows = pl.ds(part * self.sub, self.sub)
            ends[way, rows, :] = terms[shard, rows, :]

        @pl.when(stays & jnp.logical_not(starts))
        def _():
            held = self._rows(buf, shard, part)
            self._copy(held, buf, sems, way, shard, part).wait_recv()

            def add(i, carry):
                rows = pl.ds(part * self.sub + i * step, step)
                total = buf[shard, rows, :].astype(F32) + terms[shard, rows, :].astype(F32)
                ends[way, rows, :] = total.astype(BF16)
                return carry

            lax.fori_loop(0, self.sub // step, add, 0)

    def phase(
        self, gather=None, scatter=None, on_slot=None, near=None, ends=None, start=0, on_part=None
    ):
        n = self.size
        for k in range(start, n):
            for part in range(SUBS):
                for way in (0, 1):
                    if gather is not None:
                        self.gather_step(way, k, part, gather[0], gather[1], gather[2], near)
                    if scatter is not None:
                        if gather is None:
                            if k < n - 1:
                                self.scatter_step(way, k, part, scatter[0], scatter[1][way], scatter[2])
                        else:
                            behind = self.t if way == 0 else n - 1 - self.t
                            for b in range(k):

                                @pl.when(behind == b)
                                def _(b=b, k=k, part=part, way=way):
                                    self.scatter_step(
                                        way, k - 1 - b, part, scatter[0], scatter[1][way],
                                        scatter[2], ends,
                                    )
                if on_part is not None:
                    on_part(k, part)
            if on_slot is not None:
                on_slot(k)

    def own_wait(self, bufs, sems, part):
        for way in (0, 1):
            arrives = self.t > 0 if way == 0 else self.t < self.size - 1

            @pl.when(arrives)
            def _(way=way):
                held = self._rows(bufs[way], self.t, part)
                self._copy(held, bufs[way], sems, way, self.t, part).wait_recv()

    def own_sum(self, terms, bufs, rows):
        t = self.t
        zero = jnp.zeros((), F32)
        right = jnp.where(t > 0, bufs[0][t, rows, :].astype(F32), zero)
        left = jnp.where(t < self.size - 1, bufs[1][t, rows, :].astype(F32), zero)
        return terms[t, rows, :].astype(F32) + right + left

    def drain_gather(self, buf, sems, first=0):
        for way in (0, 1):
            for k in range(first, self.size):
                shard = self.t - k if way == 0 else self.t + k
                inside = (self.t >= k) if way == 0 else (self.t + k <= self.size - 1)

                @pl.when(inside & self._edge(way))
                def _(way=way, shard=shard):
                    for part in range(SUBS):
                        held = self._rows(buf, shard, part)
                        self._copy(held, buf, sems, way, shard, part).wait_send()

    def drain_scatter(self, bufs, sems, margin=0, early=False):
        for way in (0, 1):
            for j in range(self.size - 1):
                shard = self.size - 1 - j if way == 0 else j
                beyond = (shard > self.t + margin) if way == 0 else (shard < self.t - margin)
                if early and j == 0:
                    beyond = beyond & self._edge(1 - way)

                @pl.when(beyond)
                def _(way=way, shard=shard):
                    for part in range(SUBS):
                        held = self._rows(bufs[way], shard, part)
                        self._copy(held, bufs[way], sems, way, shard, part).wait_send()


def line_sems(size):
    return [pltpu.SemaphoreType.DMA((2, size, SUBS)), pltpu.SemaphoreType.DMA((2, size, SUBS))]


def fold(x):
    rows, width = x.shape
    return jnp.sum(x.reshape(rows // 8, 8, width), axis=0)


def normal(x):
    centre = x - jnp.mean(x, axis=-1, keepdims=True)
    spread = lax.rsqrt(jnp.mean(centre * centre, axis=-1, keepdims=True) + EPS)
    return centre * spread, spread


def normal_back(upstream, normed, spread, gain):
    scaled = upstream * gain
    mean_part = jnp.mean(scaled, axis=-1, keepdims=True)
    across = jnp.mean(scaled * normed, axis=-1, keepdims=True)
    return spread * (scaled - mean_part - normed * across)


def row_loop(rows, step, body, base=0):
    def one(i, carry):
        body(pl.ds(pl.multiple_of(base + i * step, step), step))
        return carry

    lax.fori_loop(0, rows // step, one, 0)


def params(collective_id=None):
    if collective_id is None:
        return pltpu.CompilerParams(vmem_limit_bytes=VMEM_CAP)
    return pltpu.CompilerParams(
        collective_id=collective_id, has_side_effects=True, vmem_limit_bytes=VMEM_CAP
    )


def first_kernel(n_dp, size, part, small, own, smalls, a_out, tok, send, recv, gs, gr):
    line = Line(size, own.shape[0])
    me = lax.axis_index("dp")
    rows, width = own.shape
    sem = pltpu.get_barrier_semaphore()
    for p in range(1, n_dp):
        pl.semaphore_signal(sem, device_id={"dp": lax.rem(me + p, n_dp)}, device_id_type=MESH)
    ends = line.greet(sem)
    pl.semaphore_wait(sem, ends + n_dp - 1)
    sems = (gs, gr)

    def small_copy(p, slot):
        return pltpu.make_async_remote_copy(
            src_ref=small,
            dst_ref=smalls.at[slot],
            send_sem=send.at[p],
            recv_sem=recv.at[slot],
            device_id={"dp": lax.rem(me + p, n_dp)},
            device_id_type=MESH,
        )

    for p in range(1, n_dp):
        small_copy(p, me).start()
    smalls[pl.ds(me, 1)] = small[...][None]
    step = min(32, line.sub)
    vec_rows = part // 128

    def normalise(source, shard, piece):
        gain = jnp.concatenate(
            [smalls[d, r : r + 1, :] for d in range(n_dp) for r in range(vec_rows)], axis=1
        ).astype(F32)
        shift = jnp.concatenate(
            [smalls[d, r : r + 1, :] for d in range(n_dp) for r in range(vec_rows, 2 * vec_rows)],
            axis=1,
        ).astype(F32)

        def body(at):
            x = source[at, :] if shard is None else source[shard, at, :]
            normed, _ = normal(x.astype(F32))
            to = line.t if shard is None else shard
            a_out[to, at, :] = (normed * gain + shift).astype(BF16)

        row_loop(line.sub, step, body, piece * line.sub)

    def on_part(k, piece):
        if k == 0:
            if piece == 0:
                for p in range(1, n_dp):
                    small_copy(p, lax.rem(me + p, n_dp)).wait_recv()
            normalise(own, None, piece)
        else:

            def side(i, carry):
                shard = line.t + k * (2 * i - 1)

                @pl.when((shard >= 0) & (shard < size))
                def _():
                    normalise(tok, shard, piece)

                return carry

            lax.fori_loop(0, 2, side, 0)

    line.phase(gather=(tok, sems, own), on_part=on_part)
    line.drain_gather(tok, sems)
    for p in range(1, n_dp):
        small_copy(p, me).wait_send()


def first(small, own, part, n_dp, size, cid):
    rows, width = own.shape
    return pl.pallas_call(
        functools.partial(first_kernel, n_dp, size, part),
        out_shape=(
            jax.ShapeDtypeStruct((n_dp,) + small.shape, small.dtype),
            jax.ShapeDtypeStruct((size, rows, width), BF16),
        ),
        in_specs=[WHOLE, WHOLE],
        out_specs=(WHOLE, WHOLE),
        scratch_shapes=[
            pltpu.VMEM((size, rows, width), BF16),
            pltpu.SemaphoreType.DMA((n_dp,)),
            pltpu.SemaphoreType.DMA((n_dp,)),
        ]
        + line_sems(size),
        compiler_params=params(cid),
        name="first",
    )(small, own)


def middle_kernel(
    size, terms, cot, near, tok, valid, vecs, c_out, gm_done, mid_out, stats,
    gm_out, right, left, gs, gr, ss, sr, near_sem, out_sem,
):
    line = Line(size, tok.shape[0])
    rows = tok.shape[0]
    step = min(32, line.sub)
    own = pltpu.make_async_copy(cot, gm_out.at[line.t], near_sem.at[2])
    own.start()
    line.barrier()

    def keep(way):
        shard = line.t - 1 if way == 0 else line.t + 1
        return pltpu.make_async_copy(near.at[way], gm_out.at[shard], near_sem.at[way])

    def keep_all(act):
        for way in (0, 1):

            @pl.when(line._edge(1 - way))
            def _(way=way):
                act(keep(way))

    keep_all(lambda copy: copy.start())
    line.phase(
        gather=(gm_out, (gs, gr), None),
        scatter=(terms, (right, left), (ss, sr)),
        near=near,
        start=1,
    )
    own.wait()
    keep_all(lambda copy: copy.wait())
    stores = [
        pltpu.make_async_copy(gm_out.at[shard], gm_done.at[shard], out_sem.at[shard])
        for shard in range(size)
    ]
    for store in stores:
        store.start()
    stats[...] = jnp.zeros_like(stats)

    def body(at):
        attn = line.own_sum(terms, (right, left), at) + vecs[2:3, :]
        x = tok[at, :].astype(F32)
        mid = x + attn
        normed, _ = normal(mid)
        c_out[at, :] = (normed * vecs[3:4, :] + vecs[4:5, :]).astype(BF16)
        mid_out[at, :] = mid
        ok = valid[at, 0:1]
        stats[0:8, :] += fold(ok * x * x)
        stats[8:16, :] += fold(ok * attn * attn)
        stats[16:24, :] += fold(ok * mid * mid)

    for piece in range(SUBS):
        line.own_wait((right, left), (ss, sr), piece)
        row_loop(line.sub, step, body, piece * line.sub)
    for store in stores:
        store.wait()
    line.drain_gather(gm_out, (gs, gr), 1)
    line.drain_scatter((right, left), (ss, sr))


def middle(terms, cot, near, tok, valid, vecs, size, cid):
    rows, width = tok.shape
    full = (size, rows, width)
    return pl.pallas_call(
        functools.partial(middle_kernel, size),
        out_shape=(
            jax.ShapeDtypeStruct((rows, width), BF16),
            jax.ShapeDtypeStruct(full, BF16),
            jax.ShapeDtypeStruct((rows, width), F32),
            jax.ShapeDtypeStruct((24, width), F32),
        ),
        in_specs=[WHOLE, HBM, HBM, WHOLE, WHOLE, WHOLE],
        out_specs=(WHOLE, HBM, WHOLE, WHOLE),
        scratch_shapes=[pltpu.VMEM(full, BF16)] * 3
        + line_sems(size)
        + line_sems(size)
        + [pltpu.SemaphoreType.DMA((3,)), pltpu.SemaphoreType.DMA((size,))],
        compiler_params=params(cid),
        name="middle",
    )(terms, cot, near, tok, valid, vecs)


def back_middle_kernel(
    size, terms, landed, mlp_in, gm_in, mid_in, vecs, out_in, gz_done, gmid_out, ends, stats,
    go_out, gz_out, right, left, right2, left2, mlp, gm, mid, out_w,
    ss, sr, ms, mr, gs, gr, early_sem, load_sem, out_sem,
):
    rows = mid.shape[0]
    line = Line(size, rows)
    step = min(32, line.sub)
    early = line.early_start(landed, (right, left), early_sem)
    loads = [
        pltpu.make_async_copy(src, dst, load_sem.at[i])
        for i, (src, dst) in enumerate(
            ((gm_in, gm), (mid_in, mid), (mlp_in, mlp), (out_in, out_w))
        )
    ]
    for load in loads:
        load.start()
    line.barrier()
    line.early_sends(terms, (right, left), (ss, sr), early)
    for j in range(size - 1):
        for piece in range(SUBS):
            for way in (0, 1):
                line.scatter_step(
                    way, j, piece, terms, (right, left)[way], (ss, sr), None, True
                )
    for load in loads:
        load.wait()
    stats[...] = jnp.zeros_like(stats)

    def body(at):
        e = line.own_sum(terms, (right, left), at)
        normed, spread = normal(mid[at, :])
        gy = gm[at, :].astype(F32)
        gmid = gy + normal_back(e, normed, spread, vecs[3:4, :])
        gz_out[line.t, at, :] = gmid.astype(BF16)
        gmid_out[at, :] = gmid
        stats[0:8, :] += fold(e * normed)
        stats[8:16, :] += fold(e)
        stats[16:24, :] += fold(gmid)
        stats[24:32, :] += fold(gy)

    for piece in range(SUBS):
        line.own_wait((right, left), (ss, sr), piece)
        row_loop(line.sub, step, body, piece * line.sub)
        for way in (0, 1):
            line.gather_step(way, 0, piece, gz_out, (gs, gr), None)
    def store(shard):
        return pltpu.make_async_copy(gz_out.at[shard], gz_done.at[shard], out_sem.at[shard])

    def weigh(shard):
        store(shard).start()
        go_out[shard] = dot_t(gz_out[shard], out_w[...]).astype(BF16)

    def on_slot(k):
        def side(i, carry):
            shard = line.t + k * (2 * i - 1)

            @pl.when((shard >= 0) & (shard < size))
            def _():
                weigh(shard)

            return carry

        lax.fori_loop(0, 1 if k == 0 else 2, side, 0)

    on_slot(0)
    line.phase(
        gather=(gz_out, (gs, gr), None),
        scatter=(mlp, (right2, left2), (ms, mr)),
        on_slot=on_slot,
        ends=ends,
        start=1,
    )
    for shard in range(size):
        store(shard).wait()
    line.drain_scatter((right, left), (ss, sr), 0, True)
    line.drain_scatter((right2, left2), (ms, mr), 1)
    line.drain_gather(gz_out, (gs, gr))


def back_middle(terms, landed, mlp, gm, mid, vecs, out_w, size, cid):
    rows, width = mid.shape
    local = out_w.shape[0]
    full = (size, rows, width)
    return pl.pallas_call(
        functools.partial(back_middle_kernel, size),
        out_shape=(
            jax.ShapeDtypeStruct(full, BF16),
            jax.ShapeDtypeStruct((rows, width), F32),
            jax.ShapeDtypeStruct((2, rows, width), BF16),
            jax.ShapeDtypeStruct((32, width), F32),
            jax.ShapeDtypeStruct((size, rows, local), BF16),
        ),
        in_specs=[WHOLE, HBM, HBM, HBM, HBM, WHOLE, HBM],
        out_specs=(HBM, WHOLE, WHOLE, WHOLE, WHOLE),
        scratch_shapes=[pltpu.VMEM(full, BF16)] * 6
        + [
            pltpu.VMEM((rows, width), BF16),
            pltpu.VMEM((rows, width), F32),
            pltpu.VMEM((local, width), BF16),
        ]
        + line_sems(size)
        + line_sems(size)
        + line_sems(size)
        + [
            pltpu.SemaphoreType.DMA((2,)),
            pltpu.SemaphoreType.DMA((4,)),
            pltpu.SemaphoreType.DMA((size,)),
        ],
        compiler_params=params(cid),
        name="back_middle",
    )(terms, landed, mlp, gm, mid, vecs, out_w)


def finish_kernel(
    n_dp, size, shared, terms, first_landed, tok_in, gmid_in, mlp, landed, mid_in, valid, vecs,
    stats_a, stats_b, given, grad_out, y_out, reduced, rms, right, left, own_mlp, tok, ends,
    gmid, mid, stats, blocks, land, sums, land2, late, late_land,
    ss, sr, load_sem, early_sem, s1, r1, s2, r2, s3, r3,
):
    rows = tok.shape[0]
    line = Line(size, rows)
    step = min(32, line.sub)
    loads = [
        pltpu.make_async_copy(src, dst, load_sem.at[i])
        for i, (src, dst) in enumerate(
            (
                (mlp.at[line.t], own_mlp), (landed, ends), (mid_in, mid),
                (tok_in, tok), (gmid_in, gmid),
            )
        )
    ]
    early = line.early_start(first_landed, (right, left), early_sem)
    for load in loads:
        load.start()
    me = lax.axis_index("dp")
    entry = pltpu.get_barrier_semaphore()
    everyone = n_dp * size

    def place(q):
        return {"dp": lax.rem(me + q // size, n_dp), "tensor": lax.rem(line.t + q % size, size)}

    def greet(q, carry):
        pl.semaphore_signal(entry, device_id=place(q), device_id_type=MESH)
        return carry

    lax.fori_loop(1, everyone, greet, 0)
    pl.semaphore_wait(entry, everyone - 1)
    line.early_sends(terms, (right, left), (ss, sr), early)
    stats[...] = jnp.zeros_like(stats)

    def tail(at):
        zero = jnp.zeros((), F32)
        from_left = jnp.where(line.t > 0, ends[0, at, :].astype(F32), zero)
        from_right = jnp.where(line.t < size - 1, ends[1, at, :].astype(F32), zero)
        out = own_mlp[at, :].astype(F32) + from_left + from_right + vecs[5:6, :]
        y = mid[at, :] + out
        y_out[at, :] = y.astype(BF16)
        ok = valid[at, 0:1]
        stats[16:24, :] += fold(ok * out * out)
        stats[24:32, :] += fold(ok * y * y)

    per = tok.shape[1] // n_dp // 128

    def lanes(total, chunk):
        return total[:, chunk * 128 : (chunk + 1) * 128]

    def group_sum(source, group):
        return jnp.sum(source[8 * group : 8 * group + 8, :], axis=0, keepdims=True)

    def put_vector(dst, row, total):
        for d in range(n_dp):
            for r in range(per):
                dst[d, row + r : row + r + 1, :] = lanes(total, d * per + r)

    def put_square(dst, row, total):
        short = lanes(total, 0)
        for chunk in range(1, n_dp * per):
            short = short + lanes(total, chunk)
        for d in range(n_dp):
            dst[d, row : row + 1, :] = short

    def one(p):
        other = lax.rem(me + p, n_dp)
        return pltpu.make_async_remote_copy(
            src_ref=blocks.at[other],
            dst_ref=land.at[p],
            send_sem=s1.at[p],
            recv_sem=r1.at[p],
            device_id={"dp": other},
            device_id_type=MESH,
        )

    def two(p):
        return pltpu.make_async_remote_copy(
            src_ref=sums.at[pl.ds(0, shared)],
            dst_ref=land2.at[p],
            send_sem=s2.at[p],
            recv_sem=r2.at[p],
            device_id={"tensor": lax.rem(line.t + p, size)},
            device_id_type=MESH,
        )

    def three(q):
        target = place(q)
        return pltpu.make_async_remote_copy(
            src_ref=late.at[target["dp"]],
            dst_ref=late_land.at[q],
            send_sem=s3.at[q],
            recv_sem=r3.at[q],
            device_id=target,
            device_id_type=MESH,
        )

    for j in range(size - 1):
        for piece in range(SUBS):
            for way in (0, 1):
                line.scatter_step(
                    way, j, piece, terms, (right, left)[way], (ss, sr), None, True
                )
        if j == 0:
            for load in loads:
                load.wait()
            row_loop(rows, step, tail)
            blocks[:, 0:shared, :] = jnp.zeros((n_dp, shared, 128), F32)
            blocks[:, shared:, :] = given[...]
            for i, group in ((2, 2), (3, 0), (4, 1), (5, 3)):
                put_vector(blocks, i * per, group_sum(stats_b, group))
            for i in range(3):
                put_square(blocks, (6 + i) * per, group_sum(stats_a, i))
            count = jnp.sum(valid[...], axis=0, keepdims=True)
            for d in range(n_dp):
                blocks[d, 11 * per : 11 * per + 1, :] = count
            for p in range(1, n_dp):
                one(p).start()
    total = blocks[me]
    for p in range(1, n_dp):
        one(p).wait_recv()
        total = total + land[p]
    sums[...] = total
    for p in range(1, size):
        two(p).start()

    def body(at):
        e = line.own_sum(terms, (right, left), at)
        normed, spread = normal(tok[at, :].astype(F32))
        grad_out[at, :] = gmid[at, :] + normal_back(e, normed, spread, vecs[0:1, :])
        stats[0:8, :] += fold(e * normed)
        stats[8:16, :] += fold(e)

    for piece in range(SUBS):
        line.own_wait((right, left), (ss, sr), piece)
        row_loop(line.sub, step, body, piece * line.sub)
    late[...] = jnp.zeros_like(late)
    put_vector(late, 0, group_sum(stats, 0))
    put_vector(late, per, group_sum(stats, 1))
    put_square(late, 2 * per, group_sum(stats, 2))
    put_square(late, 2 * per + 1, group_sum(stats, 3))

    def send_late(q, carry):
        three(q).start()
        return carry

    lax.fori_loop(1, everyone, send_late, 0)
    reduced[...] = total
    top = sums[pl.ds(0, shared), :]
    for p in range(1, size):
        two(p).wait_recv()
        top = top + land2[p]
    reduced[pl.ds(0, shared), :] = top

    def take_late(q, held):
        three(q).wait_recv()
        return held + late_land[q]

    final = lax.fori_loop(1, everyone, take_late, late[me])
    reduced[0 : 2 * per, :] = final[0 : 2 * per, :]
    for i in (9, 10):
        row = 2 * per + i - 9
        reduced[i * per : i * per + 1, :] = final[row : row + 1, :]
    count = reduced[11 * per : 11 * per + 1, :] * jnp.float32(tok.shape[1])
    for i in range(5):
        row = (6 + i) * per
        square = jnp.sum(reduced[row : row + 1, :], keepdims=True)
        rms[i : i + 1, :] = jnp.sqrt(square / count)

    def sent_late(q, carry):
        three(q).wait_send()
        return carry

    lax.fori_loop(1, everyone, sent_late, 0)
    line.drain_scatter((right, left), (ss, sr), 0, True)
    for p in range(1, n_dp):
        one(p).wait_send()
    for p in range(1, size):
        two(p).wait_send()


def finish(
    terms, first_landed, tok, gmid, mlp, landed, mid, valid, vecs, stats_a, stats_b, given,
    shared, size, cid,
):
    rows, width = tok.shape
    n_dp = given.shape[0]
    lines = shared + given.shape[1]
    late = (-(-(2 * width // n_dp // 128 + 2) // 8) * 8, 128)
    full = (size, rows, width)
    return pl.pallas_call(
        functools.partial(finish_kernel, n_dp, size, shared),
        out_shape=(
            jax.ShapeDtypeStruct((rows, width), F32),
            jax.ShapeDtypeStruct((rows, width), BF16),
            jax.ShapeDtypeStruct((lines, 128), F32),
            jax.ShapeDtypeStruct((8, 128), F32),
        ),
        in_specs=[WHOLE] + [HBM] * 6 + [WHOLE] * 5,
        out_specs=(WHOLE,) * 4,
        scratch_shapes=[pltpu.VMEM(full, BF16)] * 2
        + [pltpu.VMEM((rows, width), BF16)] * 2
        + [pltpu.VMEM((2, rows, width), BF16)]
        + [pltpu.VMEM((rows, width), F32)] * 2
        + [
            pltpu.VMEM((32, width), F32),
            pltpu.VMEM((n_dp, lines, 128), F32),
            pltpu.VMEM((n_dp, lines, 128), F32),
            pltpu.VMEM((lines, 128), F32),
            pltpu.VMEM((size, shared, 128), F32),
            pltpu.VMEM((n_dp,) + late, F32),
            pltpu.VMEM((n_dp * size,) + late, F32),
        ]
        + line_sems(size)
        + [
            pltpu.SemaphoreType.DMA((5,)),
            pltpu.SemaphoreType.DMA((2,)),
            pltpu.SemaphoreType.DMA((n_dp,)),
            pltpu.SemaphoreType.DMA((n_dp,)),
            pltpu.SemaphoreType.DMA((size,)),
            pltpu.SemaphoreType.DMA((size,)),
            pltpu.SemaphoreType.DMA((n_dp * size,)),
            pltpu.SemaphoreType.DMA((n_dp * size,)),
        ],
        compiler_params=params(cid),
        name="finish",
    )(terms, first_landed, tok, gmid, mlp, landed, mid, valid, vecs, stats_a, stats_b, given)


BLOCK = 256
NEG = -1e30
SCALE = HD**-0.5


def dot(a, b):
    return jnp.dot(a, b, preferred_element_type=F32)


def dot_t(a, b):
    return lax.dot_general(a, b, (((1,), (1,)), ((), ())), preferred_element_type=F32)


def masked_scores(q, k, keys, first, bar):
    scores = dot_t(k, q) * SCALE + bar
    key_pos = lax.broadcasted_iota(jnp.int32, (keys, BLOCK), 0)
    query_pos = first + lax.broadcasted_iota(jnp.int32, (keys, BLOCK), 1)
    return jnp.where(key_pos <= query_pos, scores, NEG)


def head_cols(part, h, heads):
    return pl.ds(pl.multiple_of((part * heads + h) * HD, HD), HD)


def weight_loads(weights, cols, sem, part):
    n_dp, _, rows, local = weights.shape
    return [
        pltpu.make_async_copy(
            weights.at[d, part],
            cols.at[pl.ds(d * rows, rows), pl.ds(part * local, local)],
            sem.at[part, d],
        )
        for d in range(n_dp)
    ]


def front_kernel(
    size, heads, a, weights, shift, bar, out_w, cot, qkv, mixed_all, log_totals, terms, near,
    cols, gs, gr, load_sem,
):
    h = pl.program_id(0)
    rows = cot.shape[0]
    local = heads * HD
    line = Line(size, rows)

    @pl.when(h == 0)
    def _():
        for part in range(3):
            for load in weight_loads(weights, cols, load_sem, part):
                load.start()
        line.barrier()
        line.hop_start((cot, cot), near, (gs, gr))
        for part in range(3):
            for load in weight_loads(weights, cols, load_sem, part):
                load.wait()
            span = slice(part * local, (part + 1) * local)

            def product(at, span=span):
                qkv[at, span] = (dot(a[at, :], cols[:, span]) + shift[0:1, span]).astype(BF16)

            row_loop(LEN, min(256, LEN), product)

    at_q, at_k, at_v = (head_cols(part, h, heads) for part in range(3))
    value_cols = qkv[:, at_v].T
    for block in range(LEN // BLOCK):
        first, keys = block * BLOCK, (block + 1) * BLOCK
        here = slice(first, first + BLOCK)
        scores = masked_scores(qkv[here, at_q], qkv[0:keys, at_k], keys, first, bar[0:keys, 0:1])
        top = jnp.max(scores, axis=0, keepdims=True)
        powers = jnp.exp(scores - top)
        total = jnp.sum(powers, axis=0, keepdims=True)
        shares = (powers * (1.0 / total)).astype(BF16)
        mixed = dot(value_cols[:, 0:keys], shares)
        mixed_all[here, head_cols(0, h, heads)] = mixed.T.astype(BF16)
        log_totals[0, :, here] = jnp.broadcast_to(top + jnp.log(total), (8, BLOCK))

    @pl.when(h == heads - 1)
    def _():
        def project(at):
            terms[at, :] = dot(mixed_all[at, :], out_w[...]).astype(BF16)

        row_loop(LEN, min(256, LEN), project)
        line.hop_wait((cot, cot), near, (gs, gr))


def front(a, weights, shift, bar, out_w, cot, size, cid):
    n_dp, _, part, local = weights.shape
    width, local3 = n_dp * part, 3 * local
    heads = local // HD
    return pl.pallas_call(
        functools.partial(front_kernel, size, heads),
        grid=(heads,),
        out_shape=(
            jax.ShapeDtypeStruct((LEN, local3), BF16),
            jax.ShapeDtypeStruct((LEN, local), BF16),
            jax.ShapeDtypeStruct((heads, 8, LEN), F32),
            jax.ShapeDtypeStruct((LEN, width), BF16),
            jax.ShapeDtypeStruct((2,) + cot.shape, BF16),
        ),
        in_specs=[WHOLE, HBM, WHOLE, WHOLE, WHOLE, HBM],
        out_specs=(
            pl.BlockSpec((LEN, local3), lambda h: (0, 0)),
            pl.BlockSpec((LEN, local), lambda h: (0, 0)),
            pl.BlockSpec((1, 8, LEN), lambda h: (h, 0, 0)),
            pl.BlockSpec((LEN, width), lambda h: (0, 0)),
            HBM,
        ),
        scratch_shapes=[
            pltpu.VMEM((width, local3), BF16),
            pltpu.SemaphoreType.DMA((2,)),
            pltpu.SemaphoreType.DMA((2,)),
            pltpu.SemaphoreType.DMA((3, n_dp)),
        ],
        compiler_params=params(cid),
        name="front",
    )(a, weights, shift, bar, out_w, cot)


def attend_back_kernel(
    size, heads, q, k, v, go, bar, log_totals, weights, ends, out, sums, terms, landed,
    key_grad, value_grad, cols, gs, gr, load_sem,
):
    h = pl.program_id(0)
    line = Line(size, ends.shape[1])
    srcs = (ends.at[0], ends.at[1])
    loads = [load for part in range(3) for load in weight_loads(weights, cols, load_sem, part)]

    @pl.when(h == 0)
    def _():
        for load in loads:
            load.start()
        line.barrier()
        line.hop_start(srcs, landed, (gs, gr))

    key_cols = k[...].T
    query_sum = jnp.zeros((1, HD), F32)
    at_q, at_k, at_v = (head_cols(part, h, heads) for part in range(3))
    for block in range(LEN // BLOCK - 1, -1, -1):
        first, keys = block * BLOCK, (block + 1) * BLOCK
        here = slice(first, first + BLOCK)
        scores = masked_scores(q[here, :], k[0:keys, :], keys, first, bar[0:keys, 0:1])
        shares = jnp.exp(scores - log_totals[0, 0:1, here])
        share_grad = dot_t(v[0:keys, :], go[here, :])
        centre = jnp.sum(shares * share_grad, axis=0, keepdims=True)
        score_grad = (shares * (share_grad - centre)).astype(BF16)
        values = dot(shares.astype(BF16), go[here, :])
        keyed = dot(score_grad, q[here, :])
        if block == LEN // BLOCK - 1:
            value_grad[...] = values
            key_grad[...] = keyed
        else:
            value_grad[0:keys, :] += values
            key_grad[0:keys, :] += keyed
        query_grad = ((dot(key_cols[:, 0:keys], score_grad)) * SCALE).T.astype(BF16)
        out[here, at_q] = query_grad
        query_sum = query_sum + jnp.sum(query_grad.astype(F32), axis=0, keepdims=True)
    out[:, at_k] = (key_grad[...] * SCALE).astype(BF16)
    rounded = value_grad[...].astype(BF16)
    out[:, at_v] = rounded
    value_sum = jnp.sum(rounded.astype(F32), axis=0, keepdims=True)
    sums[0, 0:8, :] = jnp.broadcast_to(query_sum, (8, HD))
    sums[0, 8:16, :] = jnp.broadcast_to(value_sum, (8, HD))

    @pl.when(h == heads - 1)
    def _():
        for load in loads:
            load.wait()

        def product(at):
            terms[at, :] = dot_t(out[at, :], cols[...]).astype(BF16)

        row_loop(LEN, min(256, LEN), product)
        line.hop_wait(srcs, landed, (gs, gr))


def attend_back(qkv, go, bar, log_totals, weights, ends, size, cid):
    n_dp, _, part, local = weights.shape
    width, local3 = n_dp * part, 3 * local
    heads = local // HD

    def column(place):
        return pl.BlockSpec((LEN, HD), lambda h: (0, place * heads + h))

    return pl.pallas_call(
        functools.partial(attend_back_kernel, size, heads),
        grid=(heads,),
        out_shape=(
            jax.ShapeDtypeStruct((LEN, local3), BF16),
            jax.ShapeDtypeStruct((heads, 16, HD), F32),
            jax.ShapeDtypeStruct((LEN, width), BF16),
            jax.ShapeDtypeStruct(ends.shape, BF16),
        ),
        in_specs=[
            column(0), column(1), column(2), column(0),
            pl.BlockSpec((LEN, 128), lambda h: (0, 0)),
            pl.BlockSpec((1, 8, LEN), lambda h: (h, 0, 0)),
            HBM, HBM,
        ],
        out_specs=(
            pl.BlockSpec((LEN, local3), lambda h: (0, 0)),
            pl.BlockSpec((1, 16, HD), lambda h: (h, 0, 0)),
            pl.BlockSpec((LEN, width), lambda h: (0, 0)),
            HBM,
        ),
        scratch_shapes=[
            pltpu.VMEM((LEN, HD), F32),
            pltpu.VMEM((LEN, HD), F32),
            pltpu.VMEM((width, local3), BF16),
            pltpu.SemaphoreType.DMA((2,)),
            pltpu.SemaphoreType.DMA((2,)),
            pltpu.SemaphoreType.DMA((3, n_dp)),
        ],
        compiler_params=params(cid),
        name="attend_back",
    )(qkv, qkv, qkv, go, bar, log_totals, weights, ends)


def gelu_both(u):
    inner = 0.7978845608028654 * (u + 0.044715 * (u * u * u))
    th = jnp.tanh(inner)
    half = 0.5 * (1.0 + th)
    slope = half + 0.5 * u * (1.0 - th * th) * (
        0.7978845608028654 * (1.0 + 3 * 0.044715 * (u * u))
    )
    return u * half, slope


def hidden_kernel(
    n_dp, size, c_own, gm_in, up_in, down_in, bias,
    c_done, act_out, gu_out, mlp_out, back_out, sums, c_out, gm, up, down, act, gu, mlp, back, gs, gr, in_sem, out_sem,
):
    line = Line(size, c_own.shape[0])
    rows, width = c_own.shape
    units, part = down.shape[1], down.shape[2]
    block = min(512, units)
    loads = [
        pltpu.make_async_copy(up_in, up, in_sem.at[0]),
        pltpu.make_async_copy(down_in, down, in_sem.at[1]),
        pltpu.make_async_copy(gm_in, gm, in_sem.at[2]),
    ]
    for load in loads:
        load.start()
    line.barrier()
    for piece in range(SUBS):
        for way in (0, 1):
            line.gather_step(way, 0, piece, c_out, (gs, gr), c_own)
    c_out[pl.ds(line.t, 1)] = c_own[...][None]
    sums[...] = jnp.zeros_like(sums)
    for load in loads:
        load.wait()

    def stores(shard):
        pairs = (
            (c_out, c_done), (act, act_out), (gu, gu_out), (mlp, mlp_out), (back, back_out),
        )
        return [
            pltpu.make_async_copy(src.at[shard], dst.at[shard], out_sem.at[i, shard])
            for i, (src, dst) in enumerate(pairs)
        ]

    def work(shard):
        def unit_block(j, carry):
            at = pl.ds(pl.multiple_of(j * block, block), block)
            u = dot(c_out[shard], up[:, at]) + bias[0:1, at]
            grad = dot_t(gm[shard, :, 0:part], down[0, at, :])
            for d in range(1, n_dp):
                grad = grad + dot_t(gm[shard, :, d * part : (d + 1) * part], down[d, at, :])
            value, slope = gelu_both(u)
            act[shard, :, at] = value.astype(BF16)
            rounded = (grad * slope).astype(BF16)
            gu[shard, :, at] = rounded
            sums[:, at] += fold(rounded.astype(F32))
            return carry

        lax.fori_loop(0, units // block, unit_block, 0)

        def feature_block(d, carry):
            at = pl.ds(pl.multiple_of(d * part, part), part)
            mlp[shard, :, at] = dot(act[shard], down[d]).astype(BF16)
            back[shard, :, at] = dot_t(gu[shard], up[at, :]).astype(BF16)
            return carry

        lax.fori_loop(0, n_dp, feature_block, 0)
        for store in stores(shard):
            store.start()

    line.walk(c_out, (gs, gr), work)
    line.drain_gather(c_out, (gs, gr))
    for shard in range(size):
        for store in stores(shard):
            store.wait()


def hidden(c_own, gm, up, down, bias, size, cid):
    rows, width = c_own.shape
    n_dp, units, part = down.shape
    full, wide = (size, rows, width), (size, rows, units)
    return pl.pallas_call(
        functools.partial(hidden_kernel, n_dp, size),
        out_shape=(
            jax.ShapeDtypeStruct(full, BF16),
            jax.ShapeDtypeStruct(wide, BF16),
            jax.ShapeDtypeStruct(wide, BF16),
            jax.ShapeDtypeStruct(full, BF16),
            jax.ShapeDtypeStruct(full, BF16),
            jax.ShapeDtypeStruct((8, units), F32),
        ),
        in_specs=[WHOLE, HBM, HBM, HBM, WHOLE],
        out_specs=(HBM, HBM, HBM, HBM, HBM, WHOLE),
        scratch_shapes=[
            pltpu.VMEM(full, BF16),
            pltpu.VMEM(full, BF16),
            pltpu.VMEM((width, units), BF16),
            pltpu.VMEM((n_dp, units, part), BF16),
            pltpu.VMEM(wide, BF16),
            pltpu.VMEM(wide, BF16),
            pltpu.VMEM(full, BF16),
            pltpu.VMEM(full, BF16),
        ]
        + line_sems(size)
        + [pltpu.SemaphoreType.DMA((3,)), pltpu.SemaphoreType.DMA((5, size))],
        compiler_params=params(cid),
        name="hidden",
    )(c_own, gm, up, down, bias)


def cross(left, right):
    return lax.dot_general(left, right, (((0,), (0,)), ((), ())), preferred_element_type=F32)


def products_kernel(
    size, steps, act, gm, c, gu_in, terms, down_out, up_out, landed, gu, gs, gr, load_sem
):
    i = pl.program_id(0)
    line = Line(size, terms.shape[1])
    load = pltpu.make_async_copy(gu_in, gu, load_sem.at[0])
    hops = line.first_hops(terms, landed, (gs, gr))

    @pl.when(i == 0)
    def _():
        load.start()
        line.barrier()
        line.hops_start(hops)

    @pl.when(i < steps)
    def _():
        down_out[...] = cross(act[...], gm[...]).astype(BF16)

    @pl.when(i == steps)
    def _():
        load.wait()

    @pl.when(i >= steps)
    def _():
        up_out[...] = cross(c[...], gu[...]).astype(BF16)

    @pl.when(i == pl.num_programs(0) - 1)
    def _():
        line.hops_wait(hops)


def products(act, gm, c, gu, terms, size, cid):
    rows, units = act.shape
    width = gm.shape[1]
    steps, more = units // BLOCK, width // BLOCK
    return pl.pallas_call(
        functools.partial(products_kernel, size, steps),
        grid=(steps + more,),
        out_shape=(
            jax.ShapeDtypeStruct((units, width), BF16),
            jax.ShapeDtypeStruct((width, units), BF16),
            jax.ShapeDtypeStruct((2,) + terms.shape[1:], BF16),
        ),
        in_specs=[
            pl.BlockSpec((rows, BLOCK), lambda i: (0, jnp.minimum(i, steps - 1))),
            WHOLE,
            pl.BlockSpec((rows, BLOCK), lambda i: (0, jnp.maximum(i - steps, 0))),
            HBM,
            HBM,
        ],
        out_specs=(
            pl.BlockSpec((BLOCK, width), lambda i: (jnp.minimum(i, steps - 1), 0)),
            pl.BlockSpec((BLOCK, units), lambda i: (jnp.maximum(i - steps, 0), 0)),
            HBM,
        ),
        scratch_shapes=[
            pltpu.VMEM((rows, units), BF16),
            pltpu.SemaphoreType.DMA((2,)),
            pltpu.SemaphoreType.DMA((2,)),
            pltpu.SemaphoreType.DMA((1,)),
        ],
        compiler_params=params(cid),
        name="products",
    )(act, gm, c, gu, terms)


def head_products_kernel(size, gz, a, o, gqkv, terms, out, landed, gs, gr):
    i = pl.program_id(0)
    line = Line(size, terms.shape[1])
    hops = line.first_hops(terms, landed, (gs, gr))
    local = o.shape[1]

    @pl.when(i == 0)
    def _():
        line.barrier()
        line.hops_start(hops)

    out[:, 0:local] = cross(gz[...], o[...]).astype(BF16)
    out[:, local:] = cross(a[...], gqkv[...]).astype(BF16)

    @pl.when(i == pl.num_programs(0) - 1)
    def _():
        line.hops_wait(hops)


def head_products(gz, a, o, gqkv, terms, size, cid):
    rows, width = a.shape
    columns = o.shape[1] + gqkv.shape[1]
    return pl.pallas_call(
        functools.partial(head_products_kernel, size),
        grid=(width // BLOCK,),
        out_shape=(
            jax.ShapeDtypeStruct((width, columns), BF16),
            jax.ShapeDtypeStruct((2,) + terms.shape[1:], BF16),
        ),
        in_specs=[
            pl.BlockSpec((rows, BLOCK), lambda i: (0, i)),
            pl.BlockSpec((rows, BLOCK), lambda i: (0, i)),
            WHOLE,
            WHOLE,
            HBM,
        ],
        out_specs=(pl.BlockSpec((BLOCK, columns), lambda i: (i, 0)), HBM),
        scratch_shapes=[pltpu.SemaphoreType.DMA((2,)), pltpu.SemaphoreType.DMA((2,))],
        compiler_params=params(cid),
        name="head_products",
    )(gz, a, o, gqkv, terms)


def pad_to(x, count):
    return jnp.pad(x, ((0, 0), (0, count - x.shape[1])))


def shards(
    tokens, lengths, ln1_gain, ln1_bias, qkv_weight, qv_bias, out_weight, out_bias,
    ln2_gain, ln2_bias, up_weight, up_bias, down_weight, down_bias, cotangent,
):
    n_dp, n_t = lax.axis_size("dp"), lax.axis_size("tensor")
    rows, width = tokens.shape
    part = ln1_gain.shape[0]
    local = qkv_weight.shape[2]
    heads = local // HD
    units = up_weight.shape[1]
    hd_part = qv_bias.shape[2]
    t = lax.axis_index("tensor")
    length = lengths[0]

    pieces = [
        ln1_gain, ln1_bias, out_bias, ln2_gain, ln2_bias, down_bias,
        qv_bias.reshape(-1), up_bias.reshape(-1),
    ]
    packed = jnp.concatenate(pieces)
    count = packed.shape[0]
    lanes = -(-count // 2048) * 2048
    small = jnp.pad(packed, (0, lanes - count)).reshape(lanes // 128, 128)
    smalls, a = first(small, tokens, part, n_dp, n_t, 0)
    smalls, a = smalls.reshape(n_dp, lanes), a.reshape(n_t * rows, width)
    vecs = jnp.stack([smalls[:, i * part : (i + 1) * part].reshape(width) for i in range(6)])
    vecs = jnp.pad(vecs, ((0, 2), (0, 0))).astype(F32)
    at = 6 * part
    qv_all = smalls[:, at : at + 2 * heads * hd_part].reshape(n_dp, 2, heads, hd_part)
    qv_all = qv_all.transpose(1, 2, 0, 3).reshape(2, local).astype(F32)
    at += 2 * heads * hd_part
    up_all = smalls[:, at : at + units // n_dp].reshape(n_dp, units // 16, 16 // n_dp)
    up_shift = up_all.transpose(1, 0, 2).reshape(1, units).astype(F32)
    qkv_shift = jnp.concatenate([qv_all[0], jnp.zeros_like(qv_all[0]), qv_all[1]])

    qkv_full = lax.all_gather(
        qkv_weight.transpose(1, 0, 2).reshape(3 * part, local), "dp", axis=0, tiled=False
    ).reshape(n_dp, 3, part, local)
    out_full = lax.all_gather(out_weight, "dp", axis=1, tiled=True)
    up_full = lax.all_gather(up_weight, "dp", axis=0, tiled=True)
    down_blocks = lax.all_gather(down_weight, "dp", axis=0, tiled=False)

    own_pos = t * rows + jnp.arange(rows, dtype=jnp.int32)
    valid_own = (own_pos < length).astype(F32)
    valid = jnp.broadcast_to(valid_own[:, None], (rows, 128))
    positions = jnp.arange(LEN, dtype=jnp.int32)
    bar = jnp.broadcast_to(jnp.where(positions < length, 0.0, NEG)[:, None], (LEN, 128))
    gm_own = (cotangent.astype(F32) * valid_own[:, None]).astype(BF16)

    shift = jnp.broadcast_to(qkv_shift, (8, 3 * local))
    qkv, attended, log_totals, terms, near = front(
        a, qkv_full, shift, bar, out_full, gm_own, n_t, 7
    )
    terms = terms.reshape(n_t, rows, width)
    c_own, gm, mid, stats_a = middle(terms, gm_own, near, tokens, valid, vecs, n_t, 2)
    c, act, gu, mlp, back_terms, up_sums = hidden(
        c_own, gm, up_full, down_blocks, jnp.broadcast_to(up_shift, (8, units)), n_t, 6
    )
    c, gm = c.reshape(-1, width), gm.reshape(-1, width)
    act, gu = act.reshape(-1, units), gu.reshape(-1, units)

    down_grad, up_grad, early = products(act, gm, c, gu, back_terms, n_t, 9)
    down_out = lax.psum_scatter(down_grad, "dp", scatter_dimension=1, tiled=True)
    up_out = lax.psum_scatter(up_grad, "dp", scatter_dimension=0, tiled=True)
    gz, gmid, ends, stats_b, go = back_middle(
        back_terms, early, mlp, gm_own, mid, vecs, out_full, n_t, 3
    )
    gqkv, head_sums, last_terms, landed = attend_back(
        qkv, go.reshape(-1, local), bar, log_totals, qkv_full, ends, n_t, 8
    )
    last_terms = last_terms.reshape(n_t, rows, width)
    head_grad, last_early = head_products(
        gz.reshape(-1, width), a, attended, gqkv, last_terms, n_t, 10
    )
    last_early, head_grad, down_out, up_out = lax.optimization_barrier(
        (last_early, head_grad, down_out, up_out)
    )
    head_out = lax.psum_scatter(head_grad, "dp", scatter_dimension=0, tiled=True)
    out_out = head_out[:, :local].T
    qkv_out = head_out[:, local:].reshape(part, 3, local)
    up_blocks = jnp.sum(up_sums, axis=0).reshape(units // 16, n_dp, 16 // n_dp)
    up_blocks = up_blocks.transpose(1, 0, 2).reshape(n_dp, units // n_dp)
    qv_sums = jnp.stack([head_sums[:, 0], head_sums[:, 8]])
    qv_blocks = qv_sums.reshape(2, heads, n_dp, hd_part).transpose(2, 0, 1, 3)
    qv_blocks = qv_blocks.reshape(n_dp, 2 * heads * hd_part)
    low = jnp.concatenate([up_blocks, qv_blocks], axis=1)
    low_len = -(-low.shape[1] // 1024) * 1024
    given = pad_to(low, low_len).reshape(n_dp, low_len // 128, 128)
    shared = -(-(11 * part // 128 + 1) // 8) * 8
    top_len = shared * 128
    tokens_grad, output, reduced, rms = finish(
        last_terms, last_early, tokens, gmid, mlp, landed, mid, valid, vecs,
        stats_a, stats_b, given, shared, n_t, 4,
    )
    reduced = reduced.reshape(-1)
    outs = [reduced[i * part : (i + 1) * part] for i in range(6)]
    stream_rms = rms[:5, 0]
    at = top_len
    up_bias_out = reduced[at : at + units // n_dp].reshape(up_bias.shape)
    at += units // n_dp
    qv_bias_out = reduced[at : at + 2 * heads * hd_part].reshape(qv_bias.shape)

    return (
        output, tokens_grad, outs[0], outs[1],
        qkv_out.astype(F32), qv_bias_out, out_out.astype(F32), outs[2],
        outs[3], outs[4], up_out.astype(F32), up_bias_out,
        down_out.astype(F32), outs[5], stream_rms,
    )


def solution(mesh):
    vector = P("dp")
    rows = P(("dp", "tensor"), None)
    return jax.shard_map(
        shards,
        mesh=mesh,
        in_specs=(
            rows, vector, vector, vector, P("dp", None, "tensor"), P(None, "tensor", "dp"),
            P("tensor", "dp"), vector, vector, vector, P("dp", "tensor"), P("tensor", "dp"),
            P("tensor", "dp"), vector, rows,
        ),
        out_specs=(
            rows, rows, vector, vector, P("dp", None, "tensor"), P(None, "tensor", "dp"),
            P("tensor", "dp"), vector, vector, vector, P("dp", "tensor"), P("tensor", "dp"),
            P("tensor", "dp"), vector, P(),
        ),
        check_vma=False,
    )
```

```python
import functools

import jax
import jax.numpy as jnp
from jax import lax
from jax.experimental import pallas as pl
from jax.experimental.pallas import tpu as pltpu
from jax.sharding import PartitionSpec as P

HD = 128
LEN = 1024
EPS = 1e-05
MESH = pl.DeviceIdType.MESH
F32 = jnp.float32
BF16 = jnp.bfloat16
VMEM_CAP = 60 * 1024 * 1024
SUBS = 2
WHOLE = pl.BlockSpec(memory_space=pltpu.VMEM)
HBM = pl.BlockSpec(memory_space=pltpu.HBM)


class Line:
    def __init__(self, size, rows):
        self.size, self.rows, self.t = size, rows, lax.axis_index("tensor")
        self.sub = rows // SUBS

    def barrier(self):
        sem = pltpu.get_barrier_semaphore()
        pl.semaphore_wait(sem, self.greet(sem))

    def greet(self, sem):
        @pl.when(self.t > 0)
        def _():
            pl.semaphore_signal(sem, device_id={"tensor": self.t - 1}, device_id_type=MESH)

        @pl.when(self.t < self.size - 1)
        def _():
            pl.semaphore_signal(sem, device_id={"tensor": self.t + 1}, device_id_type=MESH)

        return jnp.where(self.t > 0, 1, 0) + jnp.where(self.t < self.size - 1, 1, 0)

    def _copy(self, src, dst, sems, way, shard, part):
        send, recv = sems
        target = self.t + 1 if way == 0 else self.t - 1
        return pltpu.make_async_remote_copy(
            src_ref=src,
            dst_ref=dst.at[shard, pl.ds(part * self.sub, self.sub)],
            send_sem=send.at[way, shard, part],
            recv_sem=recv.at[way, shard, part],
            device_id={"tensor": target},
            device_id_type=MESH,
        )

    def _rows(self, ref, shard, part):
        return ref.at[shard, pl.ds(part * self.sub, self.sub)]

    def _edge(self, way):
        return self.t < self.size - 1 if way == 0 else self.t > 0

    def hop(self, way, src, dst, sems):
        return pltpu.make_async_remote_copy(
            src_ref=src,
            dst_ref=dst.at[way],
            send_sem=sems[0].at[way],
            recv_sem=sems[1].at[way],
            device_id={"tensor": self.t + 1 if way == 0 else self.t - 1},
            device_id_type=MESH,
        )

    def hop_start(self, srcs, dst, sems):
        for way in (0, 1):

            @pl.when(self._edge(way))
            def _(way=way):
                self.hop(way, srcs[way], dst, sems).start()

    def hop_wait(self, srcs, dst, sems):
        for way in (0, 1):

            @pl.when(self._edge(1 - way))
            def _(way=way):
                self.hop(way, srcs[way], dst, sems).wait_recv()

        for way in (0, 1):

            @pl.when(self._edge(way))
            def _(way=way):
                self.hop(way, srcs[way], dst, sems).wait_send()

    def first_hops(self, terms, landed, sems):
        last = self.size - 1
        return [
            (self.t == sender, self.t == taker, self.hop(way, terms.at[shard], landed, sems))
            for way, sender, taker, shard in ((0, 0, 1, last), (1, last, last - 1, 0))
        ]

    def hops_start(self, hops):
        for sends, _, copy in hops:

            @pl.when(sends)
            def _(copy=copy):
                copy.start()

    def hops_wait(self, hops):
        for sends, takes, copy in hops:

            @pl.when(sends)
            def _(copy=copy):
                copy.wait_send()

            @pl.when(takes)
            def _(copy=copy):
                copy.wait_recv()

    def early_start(self, landed, bufs, sem):
        last = self.size - 1
        early = (
            pltpu.make_async_copy(landed.at[0], bufs[0].at[last], sem.at[0]),
            pltpu.make_async_copy(landed.at[1], bufs[1].at[0], sem.at[1]),
        )
        for copy, holder in zip(early, (1, last - 1)):

            @pl.when(self.t == holder)
            def _(copy=copy):
                copy.start()

        return early

    def gather_step(self, way, k, part, buf, sems, first, near=None):
        t, last = self.t, self.size - 1
        shard = t - k if way == 0 else t + k
        inside = (t >= k) if way == 0 else (t + k <= last)

        @pl.when(inside)
        def _():
            held = self._rows(buf, shard, part)
            if k > 1 or (k == 1 and near is None):
                self._copy(held, buf, sems, way, shard, part).wait_recv()

            @pl.when(self._edge(way))
            def _():
                src = held
                if k == 0 and first is not None:
                    src = first.at[pl.ds(part * self.sub, self.sub)]
                if k == 1 and near is not None:
                    src = near.at[way, pl.ds(part * self.sub, self.sub)]
                self._copy(src, buf, sems, way, shard, part).start()

    def relay(self, k, part, buf, sems):
        for way in (0, 1):
            shard = self.t - k if way == 0 else self.t + k
            inside = (self.t >= k) if way == 0 else (self.t + k <= self.size - 1)

            @pl.when(inside)
            def _(way=way, shard=shard):
                held = self._rows(buf, shard, part)
                self._copy(held, buf, sems, way, shard, part).wait_recv()

                @pl.when(self._edge(way))
                def _():
                    self._copy(held, buf, sems, way, shard, part).start()

    def walk(self, buf, sems, work):
        last_part = SUBS - 1

        def visit(m, carry):
            k = (m + 1) // 2
            shard = jnp.where(m % 2 == 1, self.t - k, self.t + k)

            @pl.when((shard >= 0) & (shard < self.size))
            def _():
                work(shard)

            @pl.when(m == 0)
            def _():
                for part in range(last_part):
                    self.relay(1, part, buf, sems)

            @pl.when(m % 2 == 0)
            def _():
                self.relay(k + 1, last_part, buf, sems)

            @pl.when(m % 2 == 1)
            def _():
                for part in range(last_part):
                    self.relay(k + 1, part, buf, sems)

            return carry

        lax.fori_loop(0, 2 * self.size - 1, visit, 0)

    def _second(self, way):
        return self.t == (1 if way == 0 else self.size - 2)

    def send_sum(self, way, shard, part, terms, buf, sems):
        step = min(32, self.sub)

        def add(i, carry):
            rows = pl.ds(part * self.sub + i * step, step)
            total = buf[shard, rows, :].astype(F32) + terms[shard, rows, :].astype(F32)
            buf[shard, rows, :] = total.astype(BF16)
            return carry

        lax.fori_loop(0, self.sub // step, add, 0)
        held = self._rows(buf, shard, part)
        self._copy(held, buf, sems, way, shard, part).start()

    def early_sends(self, terms, bufs, sems, early):
        for way in (0, 1):

            @pl.when(self._second(way))
            def _(way=way):
                early[way].wait()
                for part in range(SUBS):
                    shard = self.size - 1 if way == 0 else 0
                    self.send_sum(way, shard, part, terms, bufs[way], sems)

    def scatter_step(self, way, j, part, terms, buf, sems, ends=None, early=False):
        t, last = self.t, self.size - 1
        shard = last - j if way == 0 else j
        beyond = (shard > t) if way == 0 else (shard < t)
        starts = (t == 0) if way == 0 else (t == last)
        step = min(32, self.sub)
        if ends is None:
            goes, stays = beyond, None
        else:
            goes = (shard > t + 1) if way == 0 else (shard < t - 1)
            stays = (shard == t + 1) if way == 0 else (shard == t - 1)

        done = early and j == 0

        if not done:

            @pl.when(goes & starts)
            def _():
                self._copy(self._rows(terms, shard, part), buf, sems, way, shard, part).start()

        relays = goes & jnp.logical_not(starts)
        if done:
            relays = relays & jnp.logical_not(self._second(way))

        @pl.when(relays)
        def _():
            held = self._rows(buf, shard, part)
            self._copy(held, buf, sems, way, shard, part).wait_recv()
            self.send_sum(way, shard, part, terms, buf, sems)

        if stays is None:
            return

        @pl.when(stays & starts)
        def _():
            rows = pl.ds(part * self.sub, self.sub)
            ends[way, rows, :] = terms[shard, rows, :]

        @pl.when(stays & jnp.logical_not(starts))
        def _():
            held = self._rows(buf, shard, part)
            self._copy(held, buf, sems, way, shard, part).wait_recv()

            def add(i, carry):
                rows = pl.ds(part * self.sub + i * step, step)
                total = buf[shard, rows, :].astype(F32) + terms[shard, rows, :].astype(F32)
                ends[way, rows, :] = total.astype(BF16)
                return carry

            lax.fori_loop(0, self.sub // step, add, 0)

    def phase(
        self, gather=None, scatter=None, on_slot=None, near=None, ends=None, start=0, on_part=None
    ):
        n = self.size
        for k in range(start, n):
            for part in range(SUBS):
                for way in (0, 1):
                    if gather is not None:
                        self.gather_step(way, k, part, gather[0], gather[1], gather[2], near)
                    if scatter is not None:
                        if gather is None:
                            if k < n - 1:
                                self.scatter_step(way, k, part, scatter[0], scatter[1][way], scatter[2])
                        else:
                            behind = self.t if way == 0 else n - 1 - self.t
                            for b in range(k):

                                @pl.when(behind == b)
                                def _(b=b, k=k, part=part, way=way):
                                    self.scatter_step(
                                        way, k - 1 - b, part, scatter[0], scatter[1][way],
                                        scatter[2], ends,
                                    )
                if on_part is not None:
                    on_part(k, part)
            if on_slot is not None:
                on_slot(k)

    def own_wait(self, bufs, sems, part):
        for way in (0, 1):
            arrives = self.t > 0 if way == 0 else self.t < self.size - 1

            @pl.when(arrives)
            def _(way=way):
                held = self._rows(bufs[way], self.t, part)
                self._copy(held, bufs[way], sems, way, self.t, part).wait_recv()

    def own_sum(self, terms, bufs, rows):
        t = self.t
        zero = jnp.zeros((), F32)
        right = jnp.where(t > 0, bufs[0][t, rows, :].astype(F32), zero)
        left = jnp.where(t < self.size - 1, bufs[1][t, rows, :].astype(F32), zero)
        return terms[t, rows, :].astype(F32) + right + left

    def drain_gather(self, buf, sems, first=0):
        for way in (0, 1):
            for k in range(first, self.size):
                shard = self.t - k if way == 0 else self.t + k
                inside = (self.t >= k) if way == 0 else (self.t + k <= self.size - 1)

                @pl.when(inside & self._edge(way))
                def _(way=way, shard=shard):
                    for part in range(SUBS):
                        held = self._rows(buf, shard, part)
                        self._copy(held, buf, sems, way, shard, part).wait_send()

    def drain_scatter(self, bufs, sems, margin=0, early=False):
        for way in (0, 1):
            for j in range(self.size - 1):
                shard = self.size - 1 - j if way == 0 else j
                beyond = (shard > self.t + margin) if way == 0 else (shard < self.t - margin)
                if early and j == 0:
                    beyond = beyond & self._edge(1 - way)

                @pl.when(beyond)
                def _(way=way, shard=shard):
                    for part in range(SUBS):
                        held = self._rows(bufs[way], shard, part)
                        self._copy(held, bufs[way], sems, way, shard, part).wait_send()


def line_sems(size):
    return [pltpu.SemaphoreType.DMA((2, size, SUBS)), pltpu.SemaphoreType.DMA((2, size, SUBS))]


def fold(x):
    rows, width = x.shape
    return jnp.sum(x.reshape(rows // 8, 8, width), axis=0)


def normal(x):
    centre = x - jnp.mean(x, axis=-1, keepdims=True)
    spread = lax.rsqrt(jnp.mean(centre * centre, axis=-1, keepdims=True) + EPS)
    return centre * spread, spread


def normal_back(upstream, normed, spread, gain):
    scaled = upstream * gain
    mean_part = jnp.mean(scaled, axis=-1, keepdims=True)
    across = jnp.mean(scaled * normed, axis=-1, keepdims=True)
    return spread * (scaled - mean_part - normed * across)


def row_loop(rows, step, body, base=0):
    def one(i, carry):
        body(pl.ds(pl.multiple_of(base + i * step, step), step))
        return carry

    lax.fori_loop(0, rows // step, one, 0)


def params(collective_id=None):
    if collective_id is None:
        return pltpu.CompilerParams(vmem_limit_bytes=VMEM_CAP)
    return pltpu.CompilerParams(
        collective_id=collective_id, has_side_effects=True, vmem_limit_bytes=VMEM_CAP
    )


def first_kernel(n_dp, size, part, small, own, smalls, a_out, tok, send, recv, gs, gr):
    line = Line(size, own.shape[0])
    me = lax.axis_index("dp")
    rows, width = own.shape
    sem = pltpu.get_barrier_semaphore()
    for p in range(1, n_dp):
        pl.semaphore_signal(sem, device_id={"dp": lax.rem(me + p, n_dp)}, device_id_type=MESH)
    ends = line.greet(sem)
    pl.semaphore_wait(sem, ends + n_dp - 1)
    sems = (gs, gr)

    def small_copy(p, slot):
        return pltpu.make_async_remote_copy(
            src_ref=small,
            dst_ref=smalls.at[slot],
            send_sem=send.at[p],
            recv_sem=recv.at[slot],
            device_id={"dp": lax.rem(me + p, n_dp)},
            device_id_type=MESH,
        )

    for p in range(1, n_dp):
        small_copy(p, me).start()
    smalls[pl.ds(me, 1)] = small[...][None]
    step = min(32, line.sub)
    vec_rows = part // 128

    def normalise(source, shard, piece):
        gain = jnp.concatenate(
            [smalls[d, r : r + 1, :] for d in range(n_dp) for r in range(vec_rows)], axis=1
        ).astype(F32)
        shift = jnp.concatenate(
            [smalls[d, r : r + 1, :] for d in range(n_dp) for r in range(vec_rows, 2 * vec_rows)],
            axis=1,
        ).astype(F32)

        def body(at):
            x = source[at, :] if shard is None else source[shard, at, :]
            normed, _ = normal(x.astype(F32))
            to = line.t if shard is None else shard
            a_out[to, at, :] = (normed * gain + shift).astype(BF16)

        row_loop(line.sub, step, body, piece * line.sub)

    def on_part(k, piece):
        if k == 0:
            if piece == 0:
                for p in range(1, n_dp):
                    small_copy(p, lax.rem(me + p, n_dp)).wait_recv()
            normalise(own, None, piece)
        else:

            def side(i, carry):
                shard = line.t + k * (2 * i - 1)

                @pl.when((shard >= 0) & (shard < size))
                def _():
                    normalise(tok, shard, piece)

                return carry

            lax.fori_loop(0, 2, side, 0)

    line.phase(gather=(tok, sems, own), on_part=on_part)
    line.drain_gather(tok, sems)
    for p in range(1, n_dp):
        small_copy(p, me).wait_send()


def first(small, own, part, n_dp, size, cid):
    rows, width = own.shape
    return pl.pallas_call(
        functools.partial(first_kernel, n_dp, size, part),
        out_shape=(
            jax.ShapeDtypeStruct((n_dp,) + small.shape, small.dtype),
            jax.ShapeDtypeStruct((size, rows, width), BF16),
        ),
        in_specs=[WHOLE, WHOLE],
        out_specs=(WHOLE, WHOLE),
        scratch_shapes=[
            pltpu.VMEM((size, rows, width), BF16),
            pltpu.SemaphoreType.DMA((n_dp,)),
            pltpu.SemaphoreType.DMA((n_dp,)),
        ]
        + line_sems(size),
        compiler_params=params(cid),
        name="first",
    )(small, own)


def middle_kernel(
    size, terms, cot, near, tok, valid, vecs, c_out, gm_done, mid_out, stats,
    gm_out, right, left, gs, gr, ss, sr, near_sem, out_sem,
):
    line = Line(size, tok.shape[0])
    rows = tok.shape[0]
    step = min(32, line.sub)
    own = pltpu.make_async_copy(cot, gm_out.at[line.t], near_sem.at[2])
    own.start()
    line.barrier()

    def keep(way):
        shard = line.t - 1 if way == 0 else line.t + 1
        return pltpu.make_async_copy(near.at[way], gm_out.at[shard], near_sem.at[way])

    def keep_all(act):
        for way in (0, 1):

            @pl.when(line._edge(1 - way))
            def _(way=way):
                act(keep(way))

    keep_all(lambda copy: copy.start())
    line.phase(
        gather=(gm_out, (gs, gr), None),
        scatter=(terms, (right, left), (ss, sr)),
        near=near,
        start=1,
    )
    own.wait()
    keep_all(lambda copy: copy.wait())
    stores = [
        pltpu.make_async_copy(gm_out.at[shard], gm_done.at[shard], out_sem.at[shard])
        for shard in range(size)
    ]
    for store in stores:
        store.start()
    stats[...] = jnp.zeros_like(stats)

    def body(at):
        attn = line.own_sum(terms, (right, left), at) + vecs[2:3, :]
        x = tok[at, :].astype(F32)
        mid = x + attn
        normed, _ = normal(mid)
        c_out[at, :] = (normed * vecs[3:4, :] + vecs[4:5, :]).astype(BF16)
        mid_out[at, :] = mid
        ok = valid[at, 0:1]
        stats[0:8, :] += fold(ok * x * x)
        stats[8:16, :] += fold(ok * attn * attn)
        stats[16:24, :] += fold(ok * mid * mid)

    for piece in range(SUBS):
        line.own_wait((right, left), (ss, sr), piece)
        row_loop(line.sub, step, body, piece * line.sub)
    for store in stores:
        store.wait()
    line.drain_gather(gm_out, (gs, gr), 1)
    line.drain_scatter((right, left), (ss, sr))


def middle(terms, cot, near, tok, valid, vecs, size, cid):
    rows, width = tok.shape
    full = (size, rows, width)
    return pl.pallas_call(
        functools.partial(middle_kernel, size),
        out_shape=(
            jax.ShapeDtypeStruct((rows, width), BF16),
            jax.ShapeDtypeStruct(full, BF16),
            jax.ShapeDtypeStruct((rows, width), F32),
            jax.ShapeDtypeStruct((24, width), F32),
        ),
        in_specs=[WHOLE, HBM, HBM, WHOLE, WHOLE, WHOLE],
        out_specs=(WHOLE, HBM, WHOLE, WHOLE),
        scratch_shapes=[pltpu.VMEM(full, BF16)] * 3
        + line_sems(size)
        + line_sems(size)
        + [pltpu.SemaphoreType.DMA((3,)), pltpu.SemaphoreType.DMA((size,))],
        compiler_params=params(cid),
        name="middle",
    )(terms, cot, near, tok, valid, vecs)


def back_middle_kernel(
    size, terms, landed, mlp_in, gm_in, mid_in, vecs, out_in, o, gmid_out, ends, stats,
    go_out, grad_out, gz_out, right, left, right2, left2, mlp, gm, mid, out_w, grad,
    ss, sr, ms, mr, gs, gr, early_sem, load_sem,
):
    rows = mid.shape[0]
    line = Line(size, rows)
    step = min(32, line.sub)
    early = line.early_start(landed, (right, left), early_sem)
    loads = [
        pltpu.make_async_copy(src, dst, load_sem.at[i])
        for i, (src, dst) in enumerate(
            ((gm_in, gm), (mid_in, mid), (mlp_in, mlp), (out_in, out_w))
        )
    ]
    for load in loads:
        load.start()
    line.barrier()
    line.early_sends(terms, (right, left), (ss, sr), early)
    for j in range(size - 1):
        for piece in range(SUBS):
            for way in (0, 1):
                line.scatter_step(
                    way, j, piece, terms, (right, left)[way], (ss, sr), None, True
                )
    for load in loads:
        load.wait()
    stats[...] = jnp.zeros_like(stats)

    def body(at):
        e = line.own_sum(terms, (right, left), at)
        normed, spread = normal(mid[at, :])
        gy = gm[at, :].astype(F32)
        gmid = gy + normal_back(e, normed, spread, vecs[3:4, :])
        gz_out[line.t, at, :] = gmid.astype(BF16)
        gmid_out[at, :] = gmid
        stats[0:8, :] += fold(e * normed)
        stats[8:16, :] += fold(e)
        stats[16:24, :] += fold(gmid)
        stats[24:32, :] += fold(gy)

    for piece in range(SUBS):
        line.own_wait((right, left), (ss, sr), piece)
        row_loop(line.sub, step, body, piece * line.sub)
        for way in (0, 1):
            line.gather_step(way, 0, piece, gz_out, (gs, gr), None)
    width = mid.shape[1]
    block = min(512, width)

    def weigh(shard):
        go_out[shard] = dot_t(gz_out[shard], out_w[...]).astype(BF16)
        here = o[pl.ds(pl.multiple_of(shard * rows, rows), rows), :].T

        def column(j, carry):
            at = pl.ds(pl.multiple_of(j * block, block), block)
            grad[:, at] += dot(here, gz_out[shard, :, at])
            return carry

        lax.fori_loop(0, width // block, column, 0)

    def on_slot(k):
        def side(i, carry):
            shard = line.t + k * (2 * i - 1)

            @pl.when((shard >= 0) & (shard < size))
            def _():
                weigh(shard)

            return carry

        lax.fori_loop(0, 1 if k == 0 else 2, side, 0)

    grad[...] = jnp.zeros_like(grad)
    on_slot(0)
    line.phase(
        gather=(gz_out, (gs, gr), None),
        scatter=(mlp, (right2, left2), (ms, mr)),
        on_slot=on_slot,
        ends=ends,
        start=1,
    )
    grad_out[...] = grad[...].astype(BF16)
    line.drain_scatter((right, left), (ss, sr), 0, True)
    line.drain_scatter((right2, left2), (ms, mr), 1)
    line.drain_gather(gz_out, (gs, gr))


def back_middle(terms, landed, mlp, gm, mid, vecs, out_w, o, size, cid):
    rows, width = mid.shape
    local = out_w.shape[0]
    full = (size, rows, width)
    return pl.pallas_call(
        functools.partial(back_middle_kernel, size),
        out_shape=(
            jax.ShapeDtypeStruct((rows, width), F32),
            jax.ShapeDtypeStruct((2, rows, width), BF16),
            jax.ShapeDtypeStruct((32, width), F32),
            jax.ShapeDtypeStruct((size, rows, local), BF16),
            jax.ShapeDtypeStruct((local, width), BF16),
        ),
        in_specs=[WHOLE, HBM, HBM, HBM, HBM, WHOLE, HBM, WHOLE],
        out_specs=(WHOLE,) * 5,
        scratch_shapes=[pltpu.VMEM(full, BF16)] * 6
        + [
            pltpu.VMEM((rows, width), BF16),
            pltpu.VMEM((rows, width), F32),
            pltpu.VMEM((local, width), BF16),
            pltpu.VMEM((local, width), F32),
        ]
        + line_sems(size)
        + line_sems(size)
        + line_sems(size)
        + [
            pltpu.SemaphoreType.DMA((2,)),
            pltpu.SemaphoreType.DMA((4,)),
        ],
        compiler_params=params(cid),
        name="back_middle",
    )(terms, landed, mlp, gm, mid, vecs, out_w, o)


def finish_kernel(
    n_dp, size, shared, terms, first_landed, tok_in, gmid_in, mlp, landed, mid_in, valid, vecs,
    stats_a, stats_b, given, grad_out, y_out, reduced, rms, right, left, own_mlp, tok, ends,
    gmid, mid, stats, blocks, land, sums, land2, late, late_land,
    ss, sr, load_sem, early_sem, s1, r1, s2, r2, s3, r3,
):
    rows = tok.shape[0]
    line = Line(size, rows)
    step = min(32, line.sub)
    loads = [
        pltpu.make_async_copy(src, dst, load_sem.at[i])
        for i, (src, dst) in enumerate(
            (
                (mlp.at[line.t], own_mlp), (landed, ends), (mid_in, mid),
                (tok_in, tok), (gmid_in, gmid),
            )
        )
    ]
    early = line.early_start(first_landed, (right, left), early_sem)
    for load in loads:
        load.start()
    me = lax.axis_index("dp")
    entry = pltpu.get_barrier_semaphore()
    everyone = n_dp * size

    def place(q):
        return {"dp": lax.rem(me + q // size, n_dp), "tensor": lax.rem(line.t + q % size, size)}

    def greet(q, carry):
        pl.semaphore_signal(entry, device_id=place(q), device_id_type=MESH)
        return carry

    lax.fori_loop(1, everyone, greet, 0)
    pl.semaphore_wait(entry, everyone - 1)
    line.early_sends(terms, (right, left), (ss, sr), early)
    stats[...] = jnp.zeros_like(stats)

    def tail(at):
        zero = jnp.zeros((), F32)
        from_left = jnp.where(line.t > 0, ends[0, at, :].astype(F32), zero)
        from_right = jnp.where(line.t < size - 1, ends[1, at, :].astype(F32), zero)
        out = own_mlp[at, :].astype(F32) + from_left + from_right + vecs[5:6, :]
        y = mid[at, :] + out
        y_out[at, :] = y.astype(BF16)
        ok = valid[at, 0:1]
        stats[16:24, :] += fold(ok * out * out)
        stats[24:32, :] += fold(ok * y * y)

    per = tok.shape[1] // n_dp // 128

    def lanes(total, chunk):
        return total[:, chunk * 128 : (chunk + 1) * 128]

    def group_sum(source, group):
        return jnp.sum(source[8 * group : 8 * group + 8, :], axis=0, keepdims=True)

    def put_vector(dst, row, total):
        for d in range(n_dp):
            for r in range(per):
                dst[d, row + r : row + r + 1, :] = lanes(total, d * per + r)

    def put_square(dst, row, total):
        short = lanes(total, 0)
        for chunk in range(1, n_dp * per):
            short = short + lanes(total, chunk)
        for d in range(n_dp):
            dst[d, row : row + 1, :] = short

    def one(p):
        other = lax.rem(me + p, n_dp)
        return pltpu.make_async_remote_copy(
            src_ref=blocks.at[other],
            dst_ref=land.at[p],
            send_sem=s1.at[p],
            recv_sem=r1.at[p],
            device_id={"dp": other},
            device_id_type=MESH,
        )

    def two(p):
        return pltpu.make_async_remote_copy(
            src_ref=sums.at[pl.ds(0, shared)],
            dst_ref=land2.at[p],
            send_sem=s2.at[p],
            recv_sem=r2.at[p],
            device_id={"tensor": lax.rem(line.t + p, size)},
            device_id_type=MESH,
        )

    def three(q):
        target = place(q)
        return pltpu.make_async_remote_copy(
            src_ref=late.at[target["dp"]],
            dst_ref=late_land.at[q],
            send_sem=s3.at[q],
            recv_sem=r3.at[q],
            device_id=target,
            device_id_type=MESH,
        )

    for j in range(size - 1):
        for piece in range(SUBS):
            for way in (0, 1):
                line.scatter_step(
                    way, j, piece, terms, (right, left)[way], (ss, sr), None, True
                )
        if j == 0:
            for load in loads:
                load.wait()
            row_loop(rows, step, tail)
            blocks[:, 0:shared, :] = jnp.zeros((n_dp, shared, 128), F32)
            blocks[:, shared:, :] = given[...]
            for i, group in ((2, 2), (3, 0), (4, 1), (5, 3)):
                put_vector(blocks, i * per, group_sum(stats_b, group))
            for i in range(3):
                put_square(blocks, (6 + i) * per, group_sum(stats_a, i))
            count = jnp.sum(valid[...], axis=0, keepdims=True)
            for d in range(n_dp):
                blocks[d, 11 * per : 11 * per + 1, :] = count
            for p in range(1, n_dp):
                one(p).start()
    total = blocks[me]
    for p in range(1, n_dp):
        one(p).wait_recv()
        total = total + land[p]
    sums[...] = total
    for p in range(1, size):
        two(p).start()

    def body(at):
        e = line.own_sum(terms, (right, left), at)
        normed, spread = normal(tok[at, :].astype(F32))
        grad_out[at, :] = gmid[at, :] + normal_back(e, normed, spread, vecs[0:1, :])
        stats[0:8, :] += fold(e * normed)
        stats[8:16, :] += fold(e)

    for piece in range(SUBS):
        line.own_wait((right, left), (ss, sr), piece)
        row_loop(line.sub, step, body, piece * line.sub)
    late[...] = jnp.zeros_like(late)
    put_vector(late, 0, group_sum(stats, 0))
    put_vector(late, per, group_sum(stats, 1))
    put_square(late, 2 * per, group_sum(stats, 2))
    put_square(late, 2 * per + 1, group_sum(stats, 3))

    def send_late(q, carry):
        three(q).start()
        return carry

    lax.fori_loop(1, everyone, send_late, 0)
    reduced[...] = total
    top = sums[pl.ds(0, shared), :]
    for p in range(1, size):
        two(p).wait_recv()
        top = top + land2[p]
    reduced[pl.ds(0, shared), :] = top

    def take_late(q, held):
        three(q).wait_recv()
        return held + late_land[q]

    final = lax.fori_loop(1, everyone, take_late, late[me])
    reduced[0 : 2 * per, :] = final[0 : 2 * per, :]
    for i in (9, 10):
        row = 2 * per + i - 9
        reduced[i * per : i * per + 1, :] = final[row : row + 1, :]
    count = reduced[11 * per : 11 * per + 1, :] * jnp.float32(tok.shape[1])
    for i in range(5):
        row = (6 + i) * per
        square = jnp.sum(reduced[row : row + 1, :], keepdims=True)
        rms[i : i + 1, :] = jnp.sqrt(square / count)

    def sent_late(q, carry):
        three(q).wait_send()
        return carry

    lax.fori_loop(1, everyone, sent_late, 0)
    line.drain_scatter((right, left), (ss, sr), 0, True)
    for p in range(1, n_dp):
        one(p).wait_send()
    for p in range(1, size):
        two(p).wait_send()


def finish(
    terms, first_landed, tok, gmid, mlp, landed, mid, valid, vecs, stats_a, stats_b, given,
    shared, size, cid,
):
    rows, width = tok.shape
    n_dp = given.shape[0]
    lines = shared + given.shape[1]
    late = (-(-(2 * width // n_dp // 128 + 2) // 8) * 8, 128)
    full = (size, rows, width)
    return pl.pallas_call(
        functools.partial(finish_kernel, n_dp, size, shared),
        out_shape=(
            jax.ShapeDtypeStruct((rows, width), F32),
            jax.ShapeDtypeStruct((rows, width), BF16),
            jax.ShapeDtypeStruct((lines, 128), F32),
            jax.ShapeDtypeStruct((8, 128), F32),
        ),
        in_specs=[WHOLE] + [HBM] * 6 + [WHOLE] * 5,
        out_specs=(WHOLE,) * 4,
        scratch_shapes=[pltpu.VMEM(full, BF16)] * 2
        + [pltpu.VMEM((rows, width), BF16)] * 2
        + [pltpu.VMEM((2, rows, width), BF16)]
        + [pltpu.VMEM((rows, width), F32)] * 2
        + [
            pltpu.VMEM((32, width), F32),
            pltpu.VMEM((n_dp, lines, 128), F32),
            pltpu.VMEM((n_dp, lines, 128), F32),
            pltpu.VMEM((lines, 128), F32),
            pltpu.VMEM((size, shared, 128), F32),
            pltpu.VMEM((n_dp,) + late, F32),
            pltpu.VMEM((n_dp * size,) + late, F32),
        ]
        + line_sems(size)
        + [
            pltpu.SemaphoreType.DMA((5,)),
            pltpu.SemaphoreType.DMA((2,)),
            pltpu.SemaphoreType.DMA((n_dp,)),
            pltpu.SemaphoreType.DMA((n_dp,)),
            pltpu.SemaphoreType.DMA((size,)),
            pltpu.SemaphoreType.DMA((size,)),
            pltpu.SemaphoreType.DMA((n_dp * size,)),
            pltpu.SemaphoreType.DMA((n_dp * size,)),
        ],
        compiler_params=params(cid),
        name="finish",
    )(terms, first_landed, tok, gmid, mlp, landed, mid, valid, vecs, stats_a, stats_b, given)


BLOCK = 256
NEG = -1e30
SCALE = HD**-0.5


def dot(a, b):
    return jnp.dot(a, b, preferred_element_type=F32)


def dot_t(a, b):
    return lax.dot_general(a, b, (((1,), (1,)), ((), ())), preferred_element_type=F32)


def masked_scores(q, k, keys, first, bar):
    scores = dot_t(k, q) * SCALE + bar
    key_pos = lax.broadcasted_iota(jnp.int32, (keys, BLOCK), 0)
    query_pos = first + lax.broadcasted_iota(jnp.int32, (keys, BLOCK), 1)
    return jnp.where(key_pos <= query_pos, scores, NEG)


def head_cols(part, h, heads):
    return pl.ds(pl.multiple_of((part * heads + h) * HD, HD), HD)


def weight_loads(weights, cols, sem, part):
    n_dp, _, rows, local = weights.shape
    return [
        pltpu.make_async_copy(
            weights.at[d, part],
            cols.at[pl.ds(d * rows, rows), pl.ds(part * local, local)],
            sem.at[part, d],
        )
        for d in range(n_dp)
    ]


def front_kernel(
    size, heads, a, weights, shift, bar, out_w, cot, qkv, mixed_all, log_totals, terms, near,
    cols, gs, gr, load_sem,
):
    h = pl.program_id(0)
    rows = cot.shape[0]
    local = heads * HD
    line = Line(size, rows)

    @pl.when(h == 0)
    def _():
        for part in range(3):
            for load in weight_loads(weights, cols, load_sem, part):
                load.start()
        line.barrier()
        line.hop_start((cot, cot), near, (gs, gr))
        for part in range(3):
            for load in weight_loads(weights, cols, load_sem, part):
                load.wait()
            span = slice(part * local, (part + 1) * local)

            def product(at, span=span):
                qkv[at, span] = (dot(a[at, :], cols[:, span]) + shift[0:1, span]).astype(BF16)

            row_loop(LEN, min(256, LEN), product)

    at_q, at_k, at_v = (head_cols(part, h, heads) for part in range(3))
    value_cols = qkv[:, at_v].T
    for block in range(LEN // BLOCK):
        first, keys = block * BLOCK, (block + 1) * BLOCK
        here = slice(first, first + BLOCK)
        scores = masked_scores(qkv[here, at_q], qkv[0:keys, at_k], keys, first, bar[0:keys, 0:1])
        top = jnp.max(scores, axis=0, keepdims=True)
        powers = jnp.exp(scores - top)
        total = jnp.sum(powers, axis=0, keepdims=True)
        shares = (powers * (1.0 / total)).astype(BF16)
        mixed = dot(value_cols[:, 0:keys], shares)
        mixed_all[here, head_cols(0, h, heads)] = mixed.T.astype(BF16)
        log_totals[0, :, here] = jnp.broadcast_to(top + jnp.log(total), (8, BLOCK))

    @pl.when(h == heads - 1)
    def _():
        def project(at):
            terms[at, :] = dot(mixed_all[at, :], out_w[...]).astype(BF16)

        row_loop(LEN, min(256, LEN), project)
        line.hop_wait((cot, cot), near, (gs, gr))


def front(a, weights, shift, bar, out_w, cot, size, cid):
    n_dp, _, part, local = weights.shape
    width, local3 = n_dp * part, 3 * local
    heads = local // HD
    return pl.pallas_call(
        functools.partial(front_kernel, size, heads),
        grid=(heads,),
        out_shape=(
            jax.ShapeDtypeStruct((LEN, local3), BF16),
            jax.ShapeDtypeStruct((LEN, local), BF16),
            jax.ShapeDtypeStruct((heads, 8, LEN), F32),
            jax.ShapeDtypeStruct((LEN, width), BF16),
            jax.ShapeDtypeStruct((2,) + cot.shape, BF16),
        ),
        in_specs=[WHOLE, HBM, WHOLE, WHOLE, WHOLE, HBM],
        out_specs=(
            pl.BlockSpec((LEN, local3), lambda h: (0, 0)),
            pl.BlockSpec((LEN, local), lambda h: (0, 0)),
            pl.BlockSpec((1, 8, LEN), lambda h: (h, 0, 0)),
            pl.BlockSpec((LEN, width), lambda h: (0, 0)),
            HBM,
        ),
        scratch_shapes=[
            pltpu.VMEM((width, local3), BF16),
            pltpu.SemaphoreType.DMA((2,)),
            pltpu.SemaphoreType.DMA((2,)),
            pltpu.SemaphoreType.DMA((3, n_dp)),
        ],
        compiler_params=params(cid),
        name="front",
    )(a, weights, shift, bar, out_w, cot)


def attend_back_kernel(
    size, heads, q, k, v, go, bar, log_totals, weights, ends, out, sums, terms, landed,
    key_grad, value_grad, cols, gs, gr, load_sem,
):
    h = pl.program_id(0)
    line = Line(size, ends.shape[1])
    srcs = (ends.at[0], ends.at[1])
    loads = [load for part in range(3) for load in weight_loads(weights, cols, load_sem, part)]

    @pl.when(h == 0)
    def _():
        for load in loads:
            load.start()
        line.barrier()
        line.hop_start(srcs, landed, (gs, gr))

    key_cols = k[...].T
    query_sum = jnp.zeros((1, HD), F32)
    at_q, at_k, at_v = (head_cols(part, h, heads) for part in range(3))
    for block in range(LEN // BLOCK - 1, -1, -1):
        first, keys = block * BLOCK, (block + 1) * BLOCK
        here = slice(first, first + BLOCK)
        scores = masked_scores(q[here, :], k[0:keys, :], keys, first, bar[0:keys, 0:1])
        shares = jnp.exp(scores - log_totals[0, 0:1, here])
        share_grad = dot_t(v[0:keys, :], go[here, :])
        centre = jnp.sum(shares * share_grad, axis=0, keepdims=True)
        score_grad = (shares * (share_grad - centre)).astype(BF16)
        values = dot(shares.astype(BF16), go[here, :])
        keyed = dot(score_grad, q[here, :])
        if block == LEN // BLOCK - 1:
            value_grad[...] = values
            key_grad[...] = keyed
        else:
            value_grad[0:keys, :] += values
            key_grad[0:keys, :] += keyed
        query_grad = ((dot(key_cols[:, 0:keys], score_grad)) * SCALE).T.astype(BF16)
        out[here, at_q] = query_grad
        query_sum = query_sum + jnp.sum(query_grad.astype(F32), axis=0, keepdims=True)
    out[:, at_k] = (key_grad[...] * SCALE).astype(BF16)
    rounded = value_grad[...].astype(BF16)
    out[:, at_v] = rounded
    value_sum = jnp.sum(rounded.astype(F32), axis=0, keepdims=True)
    sums[0, 0:8, :] = jnp.broadcast_to(query_sum, (8, HD))
    sums[0, 8:16, :] = jnp.broadcast_to(value_sum, (8, HD))

    @pl.when(h == heads - 1)
    def _():
        for load in loads:
            load.wait()

        def product(at):
            terms[at, :] = dot_t(out[at, :], cols[...]).astype(BF16)

        row_loop(LEN, min(256, LEN), product)
        line.hop_wait(srcs, landed, (gs, gr))


def attend_back(qkv, go, bar, log_totals, weights, ends, size, cid):
    n_dp, _, part, local = weights.shape
    width, local3 = n_dp * part, 3 * local
    heads = local // HD

    def column(place):
        return pl.BlockSpec((LEN, HD), lambda h: (0, place * heads + h))

    return pl.pallas_call(
        functools.partial(attend_back_kernel, size, heads),
        grid=(heads,),
        out_shape=(
            jax.ShapeDtypeStruct((LEN, local3), BF16),
            jax.ShapeDtypeStruct((heads, 16, HD), F32),
            jax.ShapeDtypeStruct((LEN, width), BF16),
            jax.ShapeDtypeStruct(ends.shape, BF16),
        ),
        in_specs=[
            column(0), column(1), column(2), column(0),
            pl.BlockSpec((LEN, 128), lambda h: (0, 0)),
            pl.BlockSpec((1, 8, LEN), lambda h: (h, 0, 0)),
            HBM, HBM,
        ],
        out_specs=(
            pl.BlockSpec((LEN, local3), lambda h: (0, 0)),
            pl.BlockSpec((1, 16, HD), lambda h: (h, 0, 0)),
            pl.BlockSpec((LEN, width), lambda h: (0, 0)),
            HBM,
        ),
        scratch_shapes=[
            pltpu.VMEM((LEN, HD), F32),
            pltpu.VMEM((LEN, HD), F32),
            pltpu.VMEM((width, local3), BF16),
            pltpu.SemaphoreType.DMA((2,)),
            pltpu.SemaphoreType.DMA((2,)),
            pltpu.SemaphoreType.DMA((3, n_dp)),
        ],
        compiler_params=params(cid),
        name="attend_back",
    )(qkv, qkv, qkv, go, bar, log_totals, weights, ends)


def gelu_both(u):
    inner = 0.7978845608028654 * (u + 0.044715 * (u * u * u))
    th = jnp.tanh(inner)
    half = 0.5 * (1.0 + th)
    slope = half + 0.5 * u * (1.0 - th * th) * (
        0.7978845608028654 * (1.0 + 3 * 0.044715 * (u * u))
    )
    return u * half, slope


def hidden_kernel(
    n_dp, size, c_own, gm_in, up_in, down_in, bias,
    c_done, act_out, gu_out, mlp_out, back_out, sums, c_out, gm, up, down, act, gu, mlp, back, gs, gr, in_sem, out_sem,
):
    line = Line(size, c_own.shape[0])
    rows, width = c_own.shape
    units, part = down.shape[1], down.shape[2]
    block = min(512, units)
    loads = [
        pltpu.make_async_copy(up_in, up, in_sem.at[0]),
        pltpu.make_async_copy(down_in, down, in_sem.at[1]),
        pltpu.make_async_copy(gm_in, gm, in_sem.at[2]),
    ]
    for load in loads:
        load.start()
    line.barrier()
    for piece in range(SUBS):
        for way in (0, 1):
            line.gather_step(way, 0, piece, c_out, (gs, gr), c_own)
    c_out[pl.ds(line.t, 1)] = c_own[...][None]
    sums[...] = jnp.zeros_like(sums)
    for load in loads:
        load.wait()

    def stores(shard):
        pairs = (
            (c_out, c_done), (act, act_out), (gu, gu_out), (mlp, mlp_out), (back, back_out),
        )
        return [
            pltpu.make_async_copy(src.at[shard], dst.at[shard], out_sem.at[i, shard])
            for i, (src, dst) in enumerate(pairs)
        ]

    def work(shard):
        def unit_block(j, carry):
            at = pl.ds(pl.multiple_of(j * block, block), block)
            u = dot(c_out[shard], up[:, at]) + bias[0:1, at]
            grad = dot_t(gm[shard, :, 0:part], down[0, at, :])
            for d in range(1, n_dp):
                grad = grad + dot_t(gm[shard, :, d * part : (d + 1) * part], down[d, at, :])
            value, slope = gelu_both(u)
            act[shard, :, at] = value.astype(BF16)
            rounded = (grad * slope).astype(BF16)
            gu[shard, :, at] = rounded
            sums[:, at] += fold(rounded.astype(F32))
            return carry

        lax.fori_loop(0, units // block, unit_block, 0)

        def feature_block(d, carry):
            at = pl.ds(pl.multiple_of(d * part, part), part)
            mlp[shard, :, at] = dot(act[shard], down[d]).astype(BF16)
            back[shard, :, at] = dot_t(gu[shard], up[at, :]).astype(BF16)
            return carry

        lax.fori_loop(0, n_dp, feature_block, 0)
        for store in stores(shard):
            store.start()

    line.walk(c_out, (gs, gr), work)
    line.drain_gather(c_out, (gs, gr))
    for shard in range(size):
        for store in stores(shard):
            store.wait()


def hidden(c_own, gm, up, down, bias, size, cid):
    rows, width = c_own.shape
    n_dp, units, part = down.shape
    full, wide = (size, rows, width), (size, rows, units)
    return pl.pallas_call(
        functools.partial(hidden_kernel, n_dp, size),
        out_shape=(
            jax.ShapeDtypeStruct(full, BF16),
            jax.ShapeDtypeStruct(wide, BF16),
            jax.ShapeDtypeStruct(wide, BF16),
            jax.ShapeDtypeStruct(full, BF16),
            jax.ShapeDtypeStruct(full, BF16),
            jax.ShapeDtypeStruct((8, units), F32),
        ),
        in_specs=[WHOLE, HBM, HBM, HBM, WHOLE],
        out_specs=(HBM, HBM, HBM, HBM, HBM, WHOLE),
        scratch_shapes=[
            pltpu.VMEM(full, BF16),
            pltpu.VMEM(full, BF16),
            pltpu.VMEM((width, units), BF16),
            pltpu.VMEM((n_dp, units, part), BF16),
            pltpu.VMEM(wide, BF16),
            pltpu.VMEM(wide, BF16),
            pltpu.VMEM(full, BF16),
            pltpu.VMEM(full, BF16),
        ]
        + line_sems(size)
        + [pltpu.SemaphoreType.DMA((3,)), pltpu.SemaphoreType.DMA((5, size))],
        compiler_params=params(cid),
        name="hidden",
    )(c_own, gm, up, down, bias)


def cross(left, right):
    return lax.dot_general(left, right, (((0,), (0,)), ((), ())), preferred_element_type=F32)


def products_kernel(size, steps, gm, act, c, gu_in, terms, out, landed, gu, gs, gr, load_sem):
    i = pl.program_id(0)
    line = Line(size, terms.shape[1])
    load = pltpu.make_async_copy(gu_in, gu, load_sem.at[0])
    hops = line.first_hops(terms, landed, (gs, gr))

    @pl.when(i == 0)
    def _():
        load.start()
        line.barrier()
        line.hops_start(hops)

    @pl.when(i < steps)
    def _():
        out[...] = cross(gm[...], act[...]).astype(BF16)

    @pl.when(i == steps)
    def _():
        load.wait()

    @pl.when(i >= steps)
    def _():
        out[...] = cross(c[...], gu[...]).astype(BF16)

    @pl.when(i == pl.num_programs(0) - 1)
    def _():
        line.hops_wait(hops)


def products(act, gm, c, gu, terms, size, cid):
    rows, units = act.shape
    width = gm.shape[1]
    steps = width // BLOCK
    return pl.pallas_call(
        functools.partial(products_kernel, size, steps),
        grid=(2 * steps,),
        out_shape=(
            jax.ShapeDtypeStruct((width, 2 * units), BF16),
            jax.ShapeDtypeStruct((2,) + terms.shape[1:], BF16),
        ),
        in_specs=[
            pl.BlockSpec((rows, BLOCK), lambda i: (0, jnp.minimum(i, steps - 1))),
            WHOLE,
            pl.BlockSpec((rows, BLOCK), lambda i: (0, jnp.maximum(i - steps, 0))),
            HBM,
            HBM,
        ],
        out_specs=(pl.BlockSpec((BLOCK, units), lambda i: (i % steps, i // steps)), HBM),
        scratch_shapes=[
            pltpu.VMEM((rows, units), BF16),
            pltpu.SemaphoreType.DMA((2,)),
            pltpu.SemaphoreType.DMA((2,)),
            pltpu.SemaphoreType.DMA((1,)),
        ],
        compiler_params=params(cid),
        name="products",
    )(gm, act, c, gu, terms)


def head_products_kernel(size, a, gqkv, terms, out, landed, gs, gr):
    i = pl.program_id(0)
    line = Line(size, terms.shape[1])
    hops = line.first_hops(terms, landed, (gs, gr))

    @pl.when(i == 0)
    def _():
        line.barrier()
        line.hops_start(hops)

    out[...] = cross(a[...], gqkv[...]).astype(BF16)

    @pl.when(i == pl.num_programs(0) - 1)
    def _():
        line.hops_wait(hops)


def head_products(a, gqkv, terms, size, cid):
    rows, width = a.shape
    columns = gqkv.shape[1]
    return pl.pallas_call(
        functools.partial(head_products_kernel, size),
        grid=(width // BLOCK,),
        out_shape=(
            jax.ShapeDtypeStruct((width, columns), BF16),
            jax.ShapeDtypeStruct((2,) + terms.shape[1:], BF16),
        ),
        in_specs=[
            pl.BlockSpec((rows, BLOCK), lambda i: (0, i)),
            WHOLE,
            HBM,
        ],
        out_specs=(pl.BlockSpec((BLOCK, columns), lambda i: (i, 0)), HBM),
        scratch_shapes=[pltpu.SemaphoreType.DMA((2,)), pltpu.SemaphoreType.DMA((2,))],
        compiler_params=params(cid),
        name="head_products",
    )(a, gqkv, terms)


def pad_to(x, count):
    return jnp.pad(x, ((0, 0), (0, count - x.shape[1])))


def shards(
    tokens, lengths, ln1_gain, ln1_bias, qkv_weight, qv_bias, out_weight, out_bias,
    ln2_gain, ln2_bias, up_weight, up_bias, down_weight, down_bias, cotangent,
):
    n_dp, n_t = lax.axis_size("dp"), lax.axis_size("tensor")
    rows, width = tokens.shape
    part = ln1_gain.shape[0]
    local = qkv_weight.shape[2]
    heads = local // HD
    units = up_weight.shape[1]
    hd_part = qv_bias.shape[2]
    t = lax.axis_index("tensor")
    length = lengths[0]

    pieces = [
        ln1_gain, ln1_bias, out_bias, ln2_gain, ln2_bias, down_bias,
        qv_bias.reshape(-1), up_bias.reshape(-1),
    ]
    packed = jnp.concatenate(pieces)
    count = packed.shape[0]
    lanes = -(-count // 2048) * 2048
    small = jnp.pad(packed, (0, lanes - count)).reshape(lanes // 128, 128)
    smalls, a = first(small, tokens, part, n_dp, n_t, 0)
    smalls, a = smalls.reshape(n_dp, lanes), a.reshape(n_t * rows, width)
    vecs = jnp.stack([smalls[:, i * part : (i + 1) * part].reshape(width) for i in range(6)])
    vecs = jnp.pad(vecs, ((0, 2), (0, 0))).astype(F32)
    at = 6 * part
    qv_all = smalls[:, at : at + 2 * heads * hd_part].reshape(n_dp, 2, heads, hd_part)
    qv_all = qv_all.transpose(1, 2, 0, 3).reshape(2, local).astype(F32)
    at += 2 * heads * hd_part
    up_all = smalls[:, at : at + units // n_dp].reshape(n_dp, units // 16, 16 // n_dp)
    up_shift = up_all.transpose(1, 0, 2).reshape(1, units).astype(F32)
    qkv_shift = jnp.concatenate([qv_all[0], jnp.zeros_like(qv_all[0]), qv_all[1]])

    qkv_full = lax.all_gather(
        qkv_weight.transpose(1, 0, 2).reshape(3 * part, local), "dp", axis=0, tiled=False
    ).reshape(n_dp, 3, part, local)
    out_full = lax.all_gather(out_weight, "dp", axis=1, tiled=True)
    up_full = lax.all_gather(up_weight, "dp", axis=0, tiled=True)
    down_blocks = lax.all_gather(down_weight, "dp", axis=0, tiled=False)

    own_pos = t * rows + jnp.arange(rows, dtype=jnp.int32)
    valid_own = (own_pos < length).astype(F32)
    valid = jnp.broadcast_to(valid_own[:, None], (rows, 128))
    positions = jnp.arange(LEN, dtype=jnp.int32)
    bar = jnp.broadcast_to(jnp.where(positions < length, 0.0, NEG)[:, None], (LEN, 128))
    gm_own = (cotangent.astype(F32) * valid_own[:, None]).astype(BF16)

    shift = jnp.broadcast_to(qkv_shift, (8, 3 * local))
    qkv, attended, log_totals, terms, near = front(
        a, qkv_full, shift, bar, out_full, gm_own, n_t, 7
    )
    terms = terms.reshape(n_t, rows, width)
    c_own, gm, mid, stats_a = middle(terms, gm_own, near, tokens, valid, vecs, n_t, 2)
    c, act, gu, mlp, back_terms, up_sums = hidden(
        c_own, gm, up_full, down_blocks, jnp.broadcast_to(up_shift, (8, units)), n_t, 6
    )
    c, gm = c.reshape(-1, width), gm.reshape(-1, width)
    act, gu = act.reshape(-1, units), gu.reshape(-1, units)

    both_grad, early = products(act, gm, c, gu, back_terms, n_t, 9)
    both_out = lax.psum_scatter(both_grad, "dp", scatter_dimension=0, tiled=True)
    gmid, ends, stats_b, go, out_grad = back_middle(
        back_terms, early, mlp, gm_own, mid, vecs, out_full, attended, n_t, 3
    )
    go, out_grad, both_out = lax.optimization_barrier((go, out_grad, both_out))
    down_out, up_out = both_out[:, :units].T, both_out[:, units:]
    out_out = lax.psum_scatter(out_grad, "dp", scatter_dimension=1, tiled=True)
    gqkv, head_sums, last_terms, landed = attend_back(
        qkv, go.reshape(-1, local), bar, log_totals, qkv_full, ends, n_t, 8
    )
    last_terms = last_terms.reshape(n_t, rows, width)
    qkv_grad, last_early = head_products(a, gqkv, last_terms, n_t, 10)
    last_early, qkv_grad = lax.optimization_barrier((last_early, qkv_grad))
    qkv_out = lax.psum_scatter(qkv_grad, "dp", scatter_dimension=0, tiled=True)
    qkv_out = qkv_out.reshape(part, 3, local)

    up_blocks = jnp.sum(up_sums, axis=0).reshape(units // 16, n_dp, 16 // n_dp)
    up_blocks = up_blocks.transpose(1, 0, 2).reshape(n_dp, units // n_dp)
    qv_sums = jnp.stack([head_sums[:, 0], head_sums[:, 8]])
    qv_blocks = qv_sums.reshape(2, heads, n_dp, hd_part).transpose(2, 0, 1, 3)
    qv_blocks = qv_blocks.reshape(n_dp, 2 * heads * hd_part)
    low = jnp.concatenate([up_blocks, qv_blocks], axis=1)
    low_len = -(-low.shape[1] // 1024) * 1024
    given = pad_to(low, low_len).reshape(n_dp, low_len // 128, 128)
    shared = -(-(11 * part // 128 + 1) // 8) * 8
    top_len = shared * 128
    tokens_grad, output, reduced, rms = finish(
        last_terms, last_early, tokens, gmid, mlp, landed, mid, valid, vecs,
        stats_a, stats_b, given, shared, n_t, 4,
    )
    reduced = reduced.reshape(-1)
    outs = [reduced[i * part : (i + 1) * part] for i in range(6)]
    stream_rms = rms[:5, 0]
    at = top_len
    up_bias_out = reduced[at : at + units // n_dp].reshape(up_bias.shape)
    at += units // n_dp
    qv_bias_out = reduced[at : at + 2 * heads * hd_part].reshape(qv_bias.shape)

    return (
        output, tokens_grad, outs[0], outs[1],
        qkv_out.astype(F32), qv_bias_out, out_out.astype(F32), outs[2],
        outs[3], outs[4], up_out.astype(F32), up_bias_out,
        down_out.astype(F32), outs[5], stream_rms,
    )


def solution(mesh):
    vector = P("dp")
    rows = P(("dp", "tensor"), None)
    return jax.shard_map(
        shards,
        mesh=mesh,
        in_specs=(
            rows, vector, vector, vector, P("dp", None, "tensor"), P(None, "tensor", "dp"),
            P("tensor", "dp"), vector, vector, vector, P("dp", "tensor"), P("tensor", "dp"),
            P("tensor", "dp"), vector, rows,
        ),
        out_specs=(
            rows, rows, vector, vector, P("dp", None, "tensor"), P(None, "tensor", "dp"),
            P("tensor", "dp"), vector, vector, vector, P("dp", "tensor"), P("tensor", "dp"),
            P("tensor", "dp"), vector, P(),
        ),
        check_vma=False,
    )
```

```python
import functools

import jax
import jax.numpy as jnp
from jax import lax
from jax.experimental import pallas as pl
from jax.experimental.pallas import tpu as pltpu
from jax.sharding import PartitionSpec as P

HD = 128
LEN = 1024
EPS = 1e-05
MESH = pl.DeviceIdType.MESH
F32 = jnp.float32
BF16 = jnp.bfloat16
VMEM_CAP = 60 * 1024 * 1024
SUBS = 2
WHOLE = pl.BlockSpec(memory_space=pltpu.VMEM)
HBM = pl.BlockSpec(memory_space=pltpu.HBM)


class Line:
    def __init__(self, size, rows):
        self.size, self.rows, self.t = size, rows, lax.axis_index("tensor")
        self.sub = rows // SUBS

    def barrier(self):
        sem = pltpu.get_barrier_semaphore()
        pl.semaphore_wait(sem, self.greet(sem))

    def greet(self, sem):
        @pl.when(self.t > 0)
        def _():
            pl.semaphore_signal(sem, device_id={"tensor": self.t - 1}, device_id_type=MESH)

        @pl.when(self.t < self.size - 1)
        def _():
            pl.semaphore_signal(sem, device_id={"tensor": self.t + 1}, device_id_type=MESH)

        return jnp.where(self.t > 0, 1, 0) + jnp.where(self.t < self.size - 1, 1, 0)

    def _copy(self, src, dst, sems, way, shard, part):
        send, recv = sems
        target = self.t + 1 if way == 0 else self.t - 1
        return pltpu.make_async_remote_copy(
            src_ref=src,
            dst_ref=dst.at[shard, pl.ds(part * self.sub, self.sub)],
            send_sem=send.at[way, shard, part],
            recv_sem=recv.at[way, shard, part],
            device_id={"tensor": target},
            device_id_type=MESH,
        )

    def _rows(self, ref, shard, part):
        return ref.at[shard, pl.ds(part * self.sub, self.sub)]

    def _edge(self, way):
        return self.t < self.size - 1 if way == 0 else self.t > 0

    def hop(self, way, src, dst, sems):
        return pltpu.make_async_remote_copy(
            src_ref=src,
            dst_ref=dst.at[way],
            send_sem=sems[0].at[way],
            recv_sem=sems[1].at[way],
            device_id={"tensor": self.t + 1 if way == 0 else self.t - 1},
            device_id_type=MESH,
        )

    def hop_start(self, srcs, dst, sems):
        for way in (0, 1):

            @pl.when(self._edge(way))
            def _(way=way):
                self.hop(way, srcs[way], dst, sems).start()

    def hop_wait(self, srcs, dst, sems):
        for way in (0, 1):

            @pl.when(self._edge(1 - way))
            def _(way=way):
                self.hop(way, srcs[way], dst, sems).wait_recv()

        for way in (0, 1):

            @pl.when(self._edge(way))
            def _(way=way):
                self.hop(way, srcs[way], dst, sems).wait_send()

    def first_hops(self, terms, landed, sems):
        last = self.size - 1
        return [
            (self.t == sender, self.t == taker, self.hop(way, terms.at[shard], landed, sems))
            for way, sender, taker, shard in ((0, 0, 1, last), (1, last, last - 1, 0))
        ]

    def hops_start(self, hops):
        for sends, _, copy in hops:

            @pl.when(sends)
            def _(copy=copy):
                copy.start()

    def hops_wait(self, hops):
        for sends, takes, copy in hops:

            @pl.when(sends)
            def _(copy=copy):
                copy.wait_send()

            @pl.when(takes)
            def _(copy=copy):
                copy.wait_recv()

    def early_start(self, landed, bufs, sem):
        last = self.size - 1
        early = (
            pltpu.make_async_copy(landed.at[0], bufs[0].at[last], sem.at[0]),
            pltpu.make_async_copy(landed.at[1], bufs[1].at[0], sem.at[1]),
        )
        for copy, holder in zip(early, (1, last - 1)):

            @pl.when(self.t == holder)
            def _(copy=copy):
                copy.start()

        return early

    def gather_step(self, way, k, part, buf, sems, first, near=None):
        t, last = self.t, self.size - 1
        shard = t - k if way == 0 else t + k
        inside = (t >= k) if way == 0 else (t + k <= last)

        @pl.when(inside)
        def _():
            held = self._rows(buf, shard, part)
            if k > 1 or (k == 1 and near is None):
                self._copy(held, buf, sems, way, shard, part).wait_recv()

            @pl.when(self._edge(way))
            def _():
                src = held
                if k == 0 and first is not None:
                    src = first.at[pl.ds(part * self.sub, self.sub)]
                if k == 1 and near is not None:
                    src = near.at[way, pl.ds(part * self.sub, self.sub)]
                self._copy(src, buf, sems, way, shard, part).start()

    def relay(self, k, part, buf, sems):
        for way in (0, 1):
            shard = self.t - k if way == 0 else self.t + k
            inside = (self.t >= k) if way == 0 else (self.t + k <= self.size - 1)

            @pl.when(inside)
            def _(way=way, shard=shard):
                held = self._rows(buf, shard, part)
                self._copy(held, buf, sems, way, shard, part).wait_recv()

                @pl.when(self._edge(way))
                def _():
                    self._copy(held, buf, sems, way, shard, part).start()

    def walk(self, buf, sems, work):
        last_part = SUBS - 1

        def visit(m, carry):
            k = (m + 1) // 2
            shard = jnp.where(m % 2 == 1, self.t - k, self.t + k)

            @pl.when((shard >= 0) & (shard < self.size))
            def _():
                work(shard)

            @pl.when(m == 0)
            def _():
                for part in range(last_part):
                    self.relay(1, part, buf, sems)

            @pl.when(m % 2 == 0)
            def _():
                self.relay(k + 1, last_part, buf, sems)

            @pl.when(m % 2 == 1)
            def _():
                for part in range(last_part):
                    self.relay(k + 1, part, buf, sems)

            return carry

        lax.fori_loop(0, 2 * self.size - 1, visit, 0)

    def _second(self, way):
        return self.t == (1 if way == 0 else self.size - 2)

    def send_sum(self, way, shard, part, terms, buf, sems):
        step = min(32, self.sub)

        def add(i, carry):
            rows = pl.ds(part * self.sub + i * step, step)
            total = buf[shard, rows, :].astype(F32) + terms[shard, rows, :].astype(F32)
            buf[shard, rows, :] = total.astype(BF16)
            return carry

        lax.fori_loop(0, self.sub // step, add, 0)
        held = self._rows(buf, shard, part)
        self._copy(held, buf, sems, way, shard, part).start()

    def early_sends(self, terms, bufs, sems, early):
        for way in (0, 1):

            @pl.when(self._second(way))
            def _(way=way):
                early[way].wait()
                for part in range(SUBS):
                    shard = self.size - 1 if way == 0 else 0
                    self.send_sum(way, shard, part, terms, bufs[way], sems)

    def scatter_step(self, way, j, part, terms, buf, sems, ends=None, early=False):
        t, last = self.t, self.size - 1
        shard = last - j if way == 0 else j
        beyond = (shard > t) if way == 0 else (shard < t)
        starts = (t == 0) if way == 0 else (t == last)
        step = min(32, self.sub)
        if ends is None:
            goes, stays = beyond, None
        else:
            goes = (shard > t + 1) if way == 0 else (shard < t - 1)
            stays = (shard == t + 1) if way == 0 else (shard == t - 1)

        done = early and j == 0

        if not done:

            @pl.when(goes & starts)
            def _():
                self._copy(self._rows(terms, shard, part), buf, sems, way, shard, part).start()

        relays = goes & jnp.logical_not(starts)
        if done:
            relays = relays & jnp.logical_not(self._second(way))

        @pl.when(relays)
        def _():
            held = self._rows(buf, shard, part)
            self._copy(held, buf, sems, way, shard, part).wait_recv()
            self.send_sum(way, shard, part, terms, buf, sems)

        if stays is None:
            return

        @pl.when(stays & starts)
        def _():
            rows = pl.ds(part * self.sub, self.sub)
            ends[way, rows, :] = terms[shard, rows, :]

        @pl.when(stays & jnp.logical_not(starts))
        def _():
            held = self._rows(buf, shard, part)
            self._copy(held, buf, sems, way, shard, part).wait_recv()

            def add(i, carry):
                rows = pl.ds(part * self.sub + i * step, step)
                total = buf[shard, rows, :].astype(F32) + terms[shard, rows, :].astype(F32)
                ends[way, rows, :] = total.astype(BF16)
                return carry

            lax.fori_loop(0, self.sub // step, add, 0)

    def phase(
        self, gather=None, scatter=None, on_slot=None, near=None, ends=None, start=0, on_part=None
    ):
        n = self.size
        for k in range(start, n):
            for part in range(SUBS):
                for way in (0, 1):
                    if gather is not None:
                        self.gather_step(way, k, part, gather[0], gather[1], gather[2], near)
                    if scatter is not None:
                        if gather is None:
                            if k < n - 1:
                                self.scatter_step(way, k, part, scatter[0], scatter[1][way], scatter[2])
                        else:
                            behind = self.t if way == 0 else n - 1 - self.t
                            for b in range(k):

                                @pl.when(behind == b)
                                def _(b=b, k=k, part=part, way=way):
                                    self.scatter_step(
                                        way, k - 1 - b, part, scatter[0], scatter[1][way],
                                        scatter[2], ends,
                                    )
                if on_part is not None:
                    on_part(k, part)
            if on_slot is not None:
                on_slot(k)

    def own_wait(self, bufs, sems, part):
        for way in (0, 1):
            arrives = self.t > 0 if way == 0 else self.t < self.size - 1

            @pl.when(arrives)
            def _(way=way):
                held = self._rows(bufs[way], self.t, part)
                self._copy(held, bufs[way], sems, way, self.t, part).wait_recv()

    def own_sum(self, terms, bufs, rows):
        t = self.t
        zero = jnp.zeros((), F32)
        right = jnp.where(t > 0, bufs[0][t, rows, :].astype(F32), zero)
        left = jnp.where(t < self.size - 1, bufs[1][t, rows, :].astype(F32), zero)
        return terms[t, rows, :].astype(F32) + right + left

    def drain_gather(self, buf, sems, first=0):
        for way in (0, 1):
            for k in range(first, self.size):
                shard = self.t - k if way == 0 else self.t + k
                inside = (self.t >= k) if way == 0 else (self.t + k <= self.size - 1)

                @pl.when(inside & self._edge(way))
                def _(way=way, shard=shard):
                    for part in range(SUBS):
                        held = self._rows(buf, shard, part)
                        self._copy(held, buf, sems, way, shard, part).wait_send()

    def drain_scatter(self, bufs, sems, margin=0, early=False):
        for way in (0, 1):
            for j in range(self.size - 1):
                shard = self.size - 1 - j if way == 0 else j
                beyond = (shard > self.t + margin) if way == 0 else (shard < self.t - margin)
                if early and j == 0:
                    beyond = beyond & self._edge(1 - way)

                @pl.when(beyond)
                def _(way=way, shard=shard):
                    for part in range(SUBS):
                        held = self._rows(bufs[way], shard, part)
                        self._copy(held, bufs[way], sems, way, shard, part).wait_send()


def line_sems(size):
    return [pltpu.SemaphoreType.DMA((2, size, SUBS)), pltpu.SemaphoreType.DMA((2, size, SUBS))]


def fold(x):
    rows, width = x.shape
    return jnp.sum(x.reshape(rows // 8, 8, width), axis=0)


def normal(x):
    centre = x - jnp.mean(x, axis=-1, keepdims=True)
    spread = lax.rsqrt(jnp.mean(centre * centre, axis=-1, keepdims=True) + EPS)
    return centre * spread, spread


def normal_back(upstream, normed, spread, gain):
    scaled = upstream * gain
    mean_part = jnp.mean(scaled, axis=-1, keepdims=True)
    across = jnp.mean(scaled * normed, axis=-1, keepdims=True)
    return spread * (scaled - mean_part - normed * across)


def row_loop(rows, step, body, base=0):
    def one(i, carry):
        body(pl.ds(pl.multiple_of(base + i * step, step), step))
        return carry

    lax.fori_loop(0, rows // step, one, 0)


def params(collective_id=None):
    if collective_id is None:
        return pltpu.CompilerParams(vmem_limit_bytes=VMEM_CAP)
    return pltpu.CompilerParams(
        collective_id=collective_id, has_side_effects=True, vmem_limit_bytes=VMEM_CAP
    )


def first_kernel(n_dp, size, part, small, own, smalls, a_out, tok, send, recv, gs, gr):
    line = Line(size, own.shape[0])
    me = lax.axis_index("dp")
    rows, width = own.shape
    sem = pltpu.get_barrier_semaphore()
    for p in range(1, n_dp):
        pl.semaphore_signal(sem, device_id={"dp": lax.rem(me + p, n_dp)}, device_id_type=MESH)
    ends = line.greet(sem)
    pl.semaphore_wait(sem, ends + n_dp - 1)
    sems = (gs, gr)

    def small_copy(p, slot):
        return pltpu.make_async_remote_copy(
            src_ref=small,
            dst_ref=smalls.at[slot],
            send_sem=send.at[p],
            recv_sem=recv.at[slot],
            device_id={"dp": lax.rem(me + p, n_dp)},
            device_id_type=MESH,
        )

    for p in range(1, n_dp):
        small_copy(p, me).start()
    smalls[pl.ds(me, 1)] = small[...][None]
    step = min(32, line.sub)
    vec_rows = part // 128

    def normalise(source, shard, piece):
        gain = jnp.concatenate(
            [smalls[d, r : r + 1, :] for d in range(n_dp) for r in range(vec_rows)], axis=1
        ).astype(F32)
        shift = jnp.concatenate(
            [smalls[d, r : r + 1, :] for d in range(n_dp) for r in range(vec_rows, 2 * vec_rows)],
            axis=1,
        ).astype(F32)

        def body(at):
            x = source[at, :] if shard is None else source[shard, at, :]
            normed, _ = normal(x.astype(F32))
            to = line.t if shard is None else shard
            a_out[to, at, :] = (normed * gain + shift).astype(BF16)

        row_loop(line.sub, step, body, piece * line.sub)

    def on_part(k, piece):
        if k == 0:
            if piece == 0:
                for p in range(1, n_dp):
                    small_copy(p, lax.rem(me + p, n_dp)).wait_recv()
            normalise(own, None, piece)
        else:

            def side(i, carry):
                shard = line.t + k * (2 * i - 1)

                @pl.when((shard >= 0) & (shard < size))
                def _():
                    normalise(tok, shard, piece)

                return carry

            lax.fori_loop(0, 2, side, 0)

    line.phase(gather=(tok, sems, own), on_part=on_part)
    line.drain_gather(tok, sems)
    for p in range(1, n_dp):
        small_copy(p, me).wait_send()


def first(small, own, part, n_dp, size, cid):
    rows, width = own.shape
    return pl.pallas_call(
        functools.partial(first_kernel, n_dp, size, part),
        out_shape=(
            jax.ShapeDtypeStruct((n_dp,) + small.shape, small.dtype),
            jax.ShapeDtypeStruct((size, rows, width), BF16),
        ),
        in_specs=[WHOLE, WHOLE],
        out_specs=(WHOLE, WHOLE),
        scratch_shapes=[
            pltpu.VMEM((size, rows, width), BF16),
            pltpu.SemaphoreType.DMA((n_dp,)),
            pltpu.SemaphoreType.DMA((n_dp,)),
        ]
        + line_sems(size),
        compiler_params=params(cid),
        name="first",
    )(small, own)


def middle_kernel(
    size, terms, cot, near, tok, valid, vecs, c_out, gm_done, mid_out, stats,
    gm_out, right, left, gs, gr, ss, sr, near_sem, out_sem,
):
    line = Line(size, tok.shape[0])
    rows = tok.shape[0]
    step = min(32, line.sub)
    own = pltpu.make_async_copy(cot, gm_out.at[line.t], near_sem.at[2])
    own.start()
    line.barrier()

    def keep(way):
        shard = line.t - 1 if way == 0 else line.t + 1
        return pltpu.make_async_copy(near.at[way], gm_out.at[shard], near_sem.at[way])

    def keep_all(act):
        for way in (0, 1):

            @pl.when(line._edge(1 - way))
            def _(way=way):
                act(keep(way))

    keep_all(lambda copy: copy.start())
    line.phase(
        gather=(gm_out, (gs, gr), None),
        scatter=(terms, (right, left), (ss, sr)),
        near=near,
        start=1,
    )
    own.wait()
    keep_all(lambda copy: copy.wait())
    stores = [
        pltpu.make_async_copy(gm_out.at[shard], gm_done.at[shard], out_sem.at[shard])
        for shard in range(size)
    ]
    for store in stores:
        store.start()
    stats[...] = jnp.zeros_like(stats)

    def body(at):
        attn = line.own_sum(terms, (right, left), at) + vecs[2:3, :]
        x = tok[at, :].astype(F32)
        mid = x + attn
        normed, _ = normal(mid)
        c_out[at, :] = (normed * vecs[3:4, :] + vecs[4:5, :]).astype(BF16)
        mid_out[at, :] = mid
        ok = valid[at, 0:1]
        stats[0:8, :] += fold(ok * x * x)
        stats[8:16, :] += fold(ok * attn * attn)
        stats[16:24, :] += fold(ok * mid * mid)

    for piece in range(SUBS):
        line.own_wait((right, left), (ss, sr), piece)
        row_loop(line.sub, step, body, piece * line.sub)
    for store in stores:
        store.wait()
    line.drain_gather(gm_out, (gs, gr), 1)
    line.drain_scatter((right, left), (ss, sr))


def middle(terms, cot, near, tok, valid, vecs, size, cid):
    rows, width = tok.shape
    full = (size, rows, width)
    return pl.pallas_call(
        functools.partial(middle_kernel, size),
        out_shape=(
            jax.ShapeDtypeStruct((rows, width), BF16),
            jax.ShapeDtypeStruct(full, BF16),
            jax.ShapeDtypeStruct((rows, width), F32),
            jax.ShapeDtypeStruct((24, width), F32),
        ),
        in_specs=[WHOLE, HBM, HBM, WHOLE, WHOLE, WHOLE],
        out_specs=(WHOLE, HBM, WHOLE, WHOLE),
        scratch_shapes=[pltpu.VMEM(full, BF16)] * 3
        + line_sems(size)
        + line_sems(size)
        + [pltpu.SemaphoreType.DMA((3,)), pltpu.SemaphoreType.DMA((size,))],
        compiler_params=params(cid),
        name="middle",
    )(terms, cot, near, tok, valid, vecs)


def back_middle_kernel(
    size, terms, landed, mlp_in, gm_in, mid_in, vecs, out_in, o, gmid_out, ends, stats,
    go_out, grad_out, gz_out, right, left, right2, left2, mlp, gm, mid, out_w, grad,
    ss, sr, ms, mr, gs, gr, early_sem, load_sem,
):
    rows = mid.shape[0]
    line = Line(size, rows)
    step = min(32, line.sub)
    early = line.early_start(landed, (right, left), early_sem)
    loads = [
        pltpu.make_async_copy(src, dst, load_sem.at[i])
        for i, (src, dst) in enumerate(
            ((gm_in, gm), (mid_in, mid), (mlp_in, mlp), (out_in, out_w))
        )
    ]
    for load in loads:
        load.start()
    line.barrier()
    line.early_sends(terms, (right, left), (ss, sr), early)
    for j in range(size - 1):
        for piece in range(SUBS):
            for way in (0, 1):
                line.scatter_step(
                    way, j, piece, terms, (right, left)[way], (ss, sr), None, True
                )
    for load in loads:
        load.wait()
    stats[...] = jnp.zeros_like(stats)

    def body(at):
        e = line.own_sum(terms, (right, left), at)
        normed, spread = normal(mid[at, :])
        gy = gm[at, :].astype(F32)
        gmid = gy + normal_back(e, normed, spread, vecs[3:4, :])
        gz_out[line.t, at, :] = gmid.astype(BF16)
        gmid_out[at, :] = gmid
        stats[0:8, :] += fold(e * normed)
        stats[8:16, :] += fold(e)
        stats[16:24, :] += fold(gmid)
        stats[24:32, :] += fold(gy)

    for piece in range(SUBS):
        line.own_wait((right, left), (ss, sr), piece)
        row_loop(line.sub, step, body, piece * line.sub)
        for way in (0, 1):
            line.gather_step(way, 0, piece, gz_out, (gs, gr), None)
    width = mid.shape[1]
    block = min(512, width)

    def weigh(shard):
        go_out[shard] = dot_t(gz_out[shard], out_w[...]).astype(BF16)
        here = o[pl.ds(pl.multiple_of(shard * rows, rows), rows), :].T

        def column(j, carry):
            at = pl.ds(pl.multiple_of(j * block, block), block)
            grad[:, at] += dot(here, gz_out[shard, :, at])
            return carry

        lax.fori_loop(0, width // block, column, 0)

    def on_slot(k):
        def side(i, carry):
            shard = line.t + k * (2 * i - 1)

            @pl.when((shard >= 0) & (shard < size))
            def _():
                weigh(shard)

            return carry

        lax.fori_loop(0, 1 if k == 0 else 2, side, 0)

    grad[...] = jnp.zeros_like(grad)
    on_slot(0)
    line.phase(
        gather=(gz_out, (gs, gr), None),
        scatter=(mlp, (right2, left2), (ms, mr)),
        on_slot=on_slot,
        ends=ends,
        start=1,
    )
    grad_out[...] = grad[...].astype(BF16)
    line.drain_scatter((right, left), (ss, sr), 0, True)
    line.drain_scatter((right2, left2), (ms, mr), 1)
    line.drain_gather(gz_out, (gs, gr))


def back_middle(terms, landed, mlp, gm, mid, vecs, out_w, o, size, cid):
    rows, width = mid.shape
    local = out_w.shape[0]
    full = (size, rows, width)
    return pl.pallas_call(
        functools.partial(back_middle_kernel, size),
        out_shape=(
            jax.ShapeDtypeStruct((rows, width), F32),
            jax.ShapeDtypeStruct((2, rows, width), BF16),
            jax.ShapeDtypeStruct((32, width), F32),
            jax.ShapeDtypeStruct((size, rows, local), BF16),
            jax.ShapeDtypeStruct((local, width), BF16),
        ),
        in_specs=[WHOLE, HBM, HBM, HBM, HBM, WHOLE, HBM, WHOLE],
        out_specs=(WHOLE,) * 5,
        scratch_shapes=[pltpu.VMEM(full, BF16)] * 6
        + [
            pltpu.VMEM((rows, width), BF16),
            pltpu.VMEM((rows, width), F32),
            pltpu.VMEM((local, width), BF16),
            pltpu.VMEM((local, width), F32),
        ]
        + line_sems(size)
        + line_sems(size)
        + line_sems(size)
        + [
            pltpu.SemaphoreType.DMA((2,)),
            pltpu.SemaphoreType.DMA((4,)),
        ],
        compiler_params=params(cid),
        name="back_middle",
    )(terms, landed, mlp, gm, mid, vecs, out_w, o)


def finish_kernel(
    n_dp, size, shared, terms, first_landed, tok_in, gmid_in, mlp, landed, mid_in, valid, vecs,
    stats_a, stats_b, given, grad_out, y_out, reduced, rms, right, left, own_mlp, tok, ends,
    gmid, mid, stats, blocks, land, sums, land2, late, late_land, late_sums, late_land2,
    ss, sr, load_sem, early_sem, s1, r1, s2, r2, s3, r3, s4, r4,
):
    rows = tok.shape[0]
    line = Line(size, rows)
    step = min(32, line.sub)
    loads = [
        pltpu.make_async_copy(src, dst, load_sem.at[i])
        for i, (src, dst) in enumerate(
            (
                (mlp.at[line.t], own_mlp), (landed, ends), (mid_in, mid),
                (tok_in, tok), (gmid_in, gmid),
            )
        )
    ]
    early = line.early_start(first_landed, (right, left), early_sem)
    for load in loads:
        load.start()
    me = lax.axis_index("dp")
    entry = pltpu.get_barrier_semaphore()
    for p in range(1, n_dp):
        pl.semaphore_signal(entry, device_id={"dp": lax.rem(me + p, n_dp)}, device_id_type=MESH)
    for p in range(1, size):
        pl.semaphore_signal(
            entry, device_id={"tensor": lax.rem(line.t + p, size)}, device_id_type=MESH
        )
    pl.semaphore_wait(entry, n_dp + size - 2)
    line.early_sends(terms, (right, left), (ss, sr), early)
    stats[...] = jnp.zeros_like(stats)

    def tail(at):
        zero = jnp.zeros((), F32)
        from_left = jnp.where(line.t > 0, ends[0, at, :].astype(F32), zero)
        from_right = jnp.where(line.t < size - 1, ends[1, at, :].astype(F32), zero)
        out = own_mlp[at, :].astype(F32) + from_left + from_right + vecs[5:6, :]
        y = mid[at, :] + out
        y_out[at, :] = y.astype(BF16)
        ok = valid[at, 0:1]
        stats[16:24, :] += fold(ok * out * out)
        stats[24:32, :] += fold(ok * y * y)

    per = tok.shape[1] // n_dp // 128

    def lanes(total, chunk):
        return total[:, chunk * 128 : (chunk + 1) * 128]

    def group_sum(source, group):
        return jnp.sum(source[8 * group : 8 * group + 8, :], axis=0, keepdims=True)

    def put_vector(dst, row, total):
        for d in range(n_dp):
            for r in range(per):
                dst[d, row + r : row + r + 1, :] = lanes(total, d * per + r)

    def put_square(dst, row, total):
        short = lanes(total, 0)
        for chunk in range(1, n_dp * per):
            short = short + lanes(total, chunk)
        for d in range(n_dp):
            dst[d, row : row + 1, :] = short

    def one(p):
        other = lax.rem(me + p, n_dp)
        return pltpu.make_async_remote_copy(
            src_ref=blocks.at[other],
            dst_ref=land.at[p],
            send_sem=s1.at[p],
            recv_sem=r1.at[p],
            device_id={"dp": other},
            device_id_type=MESH,
        )

    def two(p):
        return pltpu.make_async_remote_copy(
            src_ref=sums.at[pl.ds(0, shared)],
            dst_ref=land2.at[p],
            send_sem=s2.at[p],
            recv_sem=r2.at[p],
            device_id={"tensor": lax.rem(line.t + p, size)},
            device_id_type=MESH,
        )

    def three(p):
        other = lax.rem(me + p, n_dp)
        return pltpu.make_async_remote_copy(
            src_ref=late.at[other],
            dst_ref=late_land.at[p],
            send_sem=s3.at[p],
            recv_sem=r3.at[p],
            device_id={"dp": other},
            device_id_type=MESH,
        )

    def four(p):
        return pltpu.make_async_remote_copy(
            src_ref=late_sums,
            dst_ref=late_land2.at[p],
            send_sem=s4.at[p],
            recv_sem=r4.at[p],
            device_id={"tensor": lax.rem(line.t + p, size)},
            device_id_type=MESH,
        )

    for j in range(size - 1):
        for piece in range(SUBS):
            for way in (0, 1):
                line.scatter_step(
                    way, j, piece, terms, (right, left)[way], (ss, sr), None, True
                )
        if j == 0:
            for load in loads:
                load.wait()
            row_loop(rows, step, tail)
            blocks[:, 0:shared, :] = jnp.zeros((n_dp, shared, 128), F32)
            blocks[:, shared:, :] = given[...]
            for i, group in ((2, 2), (3, 0), (4, 1), (5, 3)):
                put_vector(blocks, i * per, group_sum(stats_b, group))
            for i in range(3):
                put_square(blocks, (6 + i) * per, group_sum(stats_a, i))
            count = jnp.sum(valid[...], axis=0, keepdims=True)
            for d in range(n_dp):
                blocks[d, 11 * per : 11 * per + 1, :] = count
            for p in range(1, n_dp):
                one(p).start()
    total = blocks[me]
    for p in range(1, n_dp):
        one(p).wait_recv()
        total = total + land[p]
    sums[...] = total
    for p in range(1, size):
        two(p).start()

    def body(at):
        e = line.own_sum(terms, (right, left), at)
        normed, spread = normal(tok[at, :].astype(F32))
        grad_out[at, :] = gmid[at, :] + normal_back(e, normed, spread, vecs[0:1, :])
        stats[0:8, :] += fold(e * normed)
        stats[8:16, :] += fold(e)

    for piece in range(SUBS):
        line.own_wait((right, left), (ss, sr), piece)
        row_loop(line.sub, step, body, piece * line.sub)
    late[...] = jnp.zeros_like(late)
    put_vector(late, 0, group_sum(stats, 0))
    put_vector(late, per, group_sum(stats, 1))
    put_square(late, 2 * per, group_sum(stats, 2))
    put_square(late, 2 * per + 1, group_sum(stats, 3))

    for p in range(1, n_dp):
        three(p).start()
    reduced[...] = total
    top = sums[pl.ds(0, shared), :]
    for p in range(1, size):
        two(p).wait_recv()
        top = top + land2[p]
    reduced[pl.ds(0, shared), :] = top

    final = late[me]
    for p in range(1, n_dp):
        three(p).wait_recv()
        final = final + late_land[p]
    late_sums[...] = final
    for p in range(1, size):
        four(p).start()
    for p in range(1, size):
        four(p).wait_recv()
        final = final + late_land2[p]
    reduced[0 : 2 * per, :] = final[0 : 2 * per, :]
    for i in (9, 10):
        row = 2 * per + i - 9
        reduced[i * per : i * per + 1, :] = final[row : row + 1, :]
    count = reduced[11 * per : 11 * per + 1, :] * jnp.float32(tok.shape[1])
    for i in range(5):
        row = (6 + i) * per
        square = jnp.sum(reduced[row : row + 1, :], keepdims=True)
        rms[i : i + 1, :] = jnp.sqrt(square / count)

    for p in range(1, n_dp):
        three(p).wait_send()
    for p in range(1, size):
        four(p).wait_send()
    line.drain_scatter((right, left), (ss, sr), 0, True)
    for p in range(1, n_dp):
        one(p).wait_send()
    for p in range(1, size):
        two(p).wait_send()


def finish(
    terms, first_landed, tok, gmid, mlp, landed, mid, valid, vecs, stats_a, stats_b, given,
    shared, size, cid,
):
    rows, width = tok.shape
    n_dp = given.shape[0]
    lines = shared + given.shape[1]
    late = (-(-(2 * width // n_dp // 128 + 2) // 8) * 8, 128)
    full = (size, rows, width)
    return pl.pallas_call(
        functools.partial(finish_kernel, n_dp, size, shared),
        out_shape=(
            jax.ShapeDtypeStruct((rows, width), F32),
            jax.ShapeDtypeStruct((rows, width), BF16),
            jax.ShapeDtypeStruct((lines, 128), F32),
            jax.ShapeDtypeStruct((8, 128), F32),
        ),
        in_specs=[WHOLE] + [HBM] * 6 + [WHOLE] * 5,
        out_specs=(WHOLE,) * 4,
        scratch_shapes=[pltpu.VMEM(full, BF16)] * 2
        + [pltpu.VMEM((rows, width), BF16)] * 2
        + [pltpu.VMEM((2, rows, width), BF16)]
        + [pltpu.VMEM((rows, width), F32)] * 2
        + [
            pltpu.VMEM((32, width), F32),
            pltpu.VMEM((n_dp, lines, 128), F32),
            pltpu.VMEM((n_dp, lines, 128), F32),
            pltpu.VMEM((lines, 128), F32),
            pltpu.VMEM((size, shared, 128), F32),
            pltpu.VMEM((n_dp,) + late, F32),
            pltpu.VMEM((n_dp,) + late, F32),
            pltpu.VMEM(late, F32),
            pltpu.VMEM((size,) + late, F32),
        ]
        + line_sems(size)
        + [
            pltpu.SemaphoreType.DMA((5,)),
            pltpu.SemaphoreType.DMA((2,)),
            pltpu.SemaphoreType.DMA((n_dp,)),
            pltpu.SemaphoreType.DMA((n_dp,)),
            pltpu.SemaphoreType.DMA((size,)),
            pltpu.SemaphoreType.DMA((size,)),
            pltpu.SemaphoreType.DMA((n_dp,)),
            pltpu.SemaphoreType.DMA((n_dp,)),
            pltpu.SemaphoreType.DMA((size,)),
            pltpu.SemaphoreType.DMA((size,)),
        ],
        compiler_params=params(cid),
        name="finish",
    )(terms, first_landed, tok, gmid, mlp, landed, mid, valid, vecs, stats_a, stats_b, given)


BLOCK = 256
NEG = -1e30
SCALE = HD**-0.5


def dot(a, b):
    return jnp.dot(a, b, preferred_element_type=F32)


def dot_t(a, b):
    return lax.dot_general(a, b, (((1,), (1,)), ((), ())), preferred_element_type=F32)


def masked_scores(q, k, keys, first, bar):
    scores = dot_t(k, q) * SCALE + bar
    key_pos = lax.broadcasted_iota(jnp.int32, (keys, BLOCK), 0)
    query_pos = first + lax.broadcasted_iota(jnp.int32, (keys, BLOCK), 1)
    return jnp.where(key_pos <= query_pos, scores, NEG)


def head_cols(part, h, heads):
    return pl.ds(pl.multiple_of((part * heads + h) * HD, HD), HD)


def weight_loads(weights, cols, sem, part):
    n_dp, _, rows, local = weights.shape
    return [
        pltpu.make_async_copy(
            weights.at[d, part],
            cols.at[pl.ds(d * rows, rows), pl.ds(part * local, local)],
            sem.at[part, d],
        )
        for d in range(n_dp)
    ]


def front_kernel(
    size, heads, a, weights, shift, bar, out_w, cot, qkv, mixed_all, log_totals, terms, near,
    cols, gs, gr, load_sem,
):
    h = pl.program_id(0)
    rows = cot.shape[0]
    local = heads * HD
    line = Line(size, rows)

    @pl.when(h == 0)
    def _():
        for part in range(3):
            for load in weight_loads(weights, cols, load_sem, part):
                load.start()
        line.barrier()
        line.hop_start((cot, cot), near, (gs, gr))
        for part in range(3):
            for load in weight_loads(weights, cols, load_sem, part):
                load.wait()
            span = slice(part * local, (part + 1) * local)

            def product(at, span=span):
                qkv[at, span] = (dot(a[at, :], cols[:, span]) + shift[0:1, span]).astype(BF16)

            row_loop(LEN, min(256, LEN), product)

    at_q, at_k, at_v = (head_cols(part, h, heads) for part in range(3))
    value_cols = qkv[:, at_v].T
    for block in range(LEN // BLOCK):
        first, keys = block * BLOCK, (block + 1) * BLOCK
        here = slice(first, first + BLOCK)
        scores = masked_scores(qkv[here, at_q], qkv[0:keys, at_k], keys, first, bar[0:keys, 0:1])
        top = jnp.max(scores, axis=0, keepdims=True)
        powers = jnp.exp(scores - top)
        total = jnp.sum(powers, axis=0, keepdims=True)
        shares = (powers * (1.0 / total)).astype(BF16)
        mixed = dot(value_cols[:, 0:keys], shares)
        mixed_all[here, head_cols(0, h, heads)] = mixed.T.astype(BF16)
        log_totals[0, :, here] = jnp.broadcast_to(top + jnp.log(total), (8, BLOCK))

    @pl.when(h == heads - 1)
    def _():
        def project(at):
            terms[at, :] = dot(mixed_all[at, :], out_w[...]).astype(BF16)

        row_loop(LEN, min(256, LEN), project)
        line.hop_wait((cot, cot), near, (gs, gr))


def front(a, weights, shift, bar, out_w, cot, size, cid):
    n_dp, _, part, local = weights.shape
    width, local3 = n_dp * part, 3 * local
    heads = local // HD
    return pl.pallas_call(
        functools.partial(front_kernel, size, heads),
        grid=(heads,),
        out_shape=(
            jax.ShapeDtypeStruct((LEN, local3), BF16),
            jax.ShapeDtypeStruct((LEN, local), BF16),
            jax.ShapeDtypeStruct((heads, 8, LEN), F32),
            jax.ShapeDtypeStruct((LEN, width), BF16),
            jax.ShapeDtypeStruct((2,) + cot.shape, BF16),
        ),
        in_specs=[WHOLE, HBM, WHOLE, WHOLE, WHOLE, HBM],
        out_specs=(
            pl.BlockSpec((LEN, local3), lambda h: (0, 0)),
            pl.BlockSpec((LEN, local), lambda h: (0, 0)),
            pl.BlockSpec((1, 8, LEN), lambda h: (h, 0, 0)),
            pl.BlockSpec((LEN, width), lambda h: (0, 0)),
            HBM,
        ),
        scratch_shapes=[
            pltpu.VMEM((width, local3), BF16),
            pltpu.SemaphoreType.DMA((2,)),
            pltpu.SemaphoreType.DMA((2,)),
            pltpu.SemaphoreType.DMA((3, n_dp)),
        ],
        compiler_params=params(cid),
        name="front",
    )(a, weights, shift, bar, out_w, cot)


def attend_back_kernel(
    size, heads, q, k, v, go, bar, log_totals, weights, ends, out, sums, terms, landed,
    key_grad, value_grad, cols, gs, gr, load_sem,
):
    h = pl.program_id(0)
    line = Line(size, ends.shape[1])
    srcs = (ends.at[0], ends.at[1])
    loads = [load for part in range(3) for load in weight_loads(weights, cols, load_sem, part)]

    @pl.when(h == 0)
    def _():
        for load in loads:
            load.start()
        line.barrier()
        line.hop_start(srcs, landed, (gs, gr))

    key_cols = k[...].T
    query_sum = jnp.zeros((1, HD), F32)
    at_q, at_k, at_v = (head_cols(part, h, heads) for part in range(3))
    for block in range(LEN // BLOCK - 1, -1, -1):
        first, keys = block * BLOCK, (block + 1) * BLOCK
        here = slice(first, first + BLOCK)
        scores = masked_scores(q[here, :], k[0:keys, :], keys, first, bar[0:keys, 0:1])
        shares = jnp.exp(scores - log_totals[0, 0:1, here])
        share_grad = dot_t(v[0:keys, :], go[here, :])
        centre = jnp.sum(shares * share_grad, axis=0, keepdims=True)
        score_grad = (shares * (share_grad - centre)).astype(BF16)
        values = dot(shares.astype(BF16), go[here, :])
        keyed = dot(score_grad, q[here, :])
        if block == LEN // BLOCK - 1:
            value_grad[...] = values
            key_grad[...] = keyed
        else:
            value_grad[0:keys, :] += values
            key_grad[0:keys, :] += keyed
        query_grad = ((dot(key_cols[:, 0:keys], score_grad)) * SCALE).T.astype(BF16)
        out[here, at_q] = query_grad
        query_sum = query_sum + jnp.sum(query_grad.astype(F32), axis=0, keepdims=True)
    out[:, at_k] = (key_grad[...] * SCALE).astype(BF16)
    rounded = value_grad[...].astype(BF16)
    out[:, at_v] = rounded
    value_sum = jnp.sum(rounded.astype(F32), axis=0, keepdims=True)
    sums[0, 0:8, :] = jnp.broadcast_to(query_sum, (8, HD))
    sums[0, 8:16, :] = jnp.broadcast_to(value_sum, (8, HD))

    @pl.when(h == heads - 1)
    def _():
        for load in loads:
            load.wait()

        def product(at):
            terms[at, :] = dot_t(out[at, :], cols[...]).astype(BF16)

        row_loop(LEN, min(256, LEN), product)
        line.hop_wait(srcs, landed, (gs, gr))


def attend_back(qkv, go, bar, log_totals, weights, ends, size, cid):
    n_dp, _, part, local = weights.shape
    width, local3 = n_dp * part, 3 * local
    heads = local // HD

    def column(place):
        return pl.BlockSpec((LEN, HD), lambda h: (0, place * heads + h))

    return pl.pallas_call(
        functools.partial(attend_back_kernel, size, heads),
        grid=(heads,),
        out_shape=(
            jax.ShapeDtypeStruct((LEN, local3), BF16),
            jax.ShapeDtypeStruct((heads, 16, HD), F32),
            jax.ShapeDtypeStruct((LEN, width), BF16),
            jax.ShapeDtypeStruct(ends.shape, BF16),
        ),
        in_specs=[
            column(0), column(1), column(2), column(0),
            pl.BlockSpec((LEN, 128), lambda h: (0, 0)),
            pl.BlockSpec((1, 8, LEN), lambda h: (h, 0, 0)),
            HBM, HBM,
        ],
        out_specs=(
            pl.BlockSpec((LEN, local3), lambda h: (0, 0)),
            pl.BlockSpec((1, 16, HD), lambda h: (h, 0, 0)),
            pl.BlockSpec((LEN, width), lambda h: (0, 0)),
            HBM,
        ),
        scratch_shapes=[
            pltpu.VMEM((LEN, HD), F32),
            pltpu.VMEM((LEN, HD), F32),
            pltpu.VMEM((width, local3), BF16),
            pltpu.SemaphoreType.DMA((2,)),
            pltpu.SemaphoreType.DMA((2,)),
            pltpu.SemaphoreType.DMA((3, n_dp)),
        ],
        compiler_params=params(cid),
        name="attend_back",
    )(qkv, qkv, qkv, go, bar, log_totals, weights, ends)


def gelu_both(u):
    inner = 0.7978845608028654 * (u + 0.044715 * (u * u * u))
    th = jnp.tanh(inner)
    half = 0.5 * (1.0 + th)
    slope = half + 0.5 * u * (1.0 - th * th) * (
        0.7978845608028654 * (1.0 + 3 * 0.044715 * (u * u))
    )
    return u * half, slope


def hidden_kernel(
    n_dp, size, c_own, gm_in, up_in, down_in, bias,
    c_done, act_out, gu_out, mlp_out, back_out, sums, c_out, gm, up, down, act, gu, mlp, back, gs, gr, in_sem, out_sem,
):
    line = Line(size, c_own.shape[0])
    rows, width = c_own.shape
    units, part = down.shape[1], down.shape[2]
    block = min(512, units)
    loads = [
        pltpu.make_async_copy(up_in, up, in_sem.at[0]),
        pltpu.make_async_copy(down_in, down, in_sem.at[1]),
        pltpu.make_async_copy(gm_in, gm, in_sem.at[2]),
    ]
    for load in loads:
        load.start()
    line.barrier()
    for piece in range(SUBS):
        for way in (0, 1):
            line.gather_step(way, 0, piece, c_out, (gs, gr), c_own)
    c_out[pl.ds(line.t, 1)] = c_own[...][None]
    sums[...] = jnp.zeros_like(sums)
    for load in loads:
        load.wait()

    def stores(shard):
        pairs = (
            (c_out, c_done), (act, act_out), (gu, gu_out), (mlp, mlp_out), (back, back_out),
        )
        return [
            pltpu.make_async_copy(src.at[shard], dst.at[shard], out_sem.at[i, shard])
            for i, (src, dst) in enumerate(pairs)
        ]

    def work(shard):
        def unit_block(j, carry):
            at = pl.ds(pl.multiple_of(j * block, block), block)
            u = dot(c_out[shard], up[:, at]) + bias[0:1, at]
            grad = dot_t(gm[shard, :, 0:part], down[0, at, :])
            for d in range(1, n_dp):
                grad = grad + dot_t(gm[shard, :, d * part : (d + 1) * part], down[d, at, :])
            value, slope = gelu_both(u)
            act[shard, :, at] = value.astype(BF16)
            rounded = (grad * slope).astype(BF16)
            gu[shard, :, at] = rounded
            sums[:, at] += fold(rounded.astype(F32))
            return carry

        lax.fori_loop(0, units // block, unit_block, 0)

        def feature_block(d, carry):
            at = pl.ds(pl.multiple_of(d * part, part), part)
            mlp[shard, :, at] = dot(act[shard], down[d]).astype(BF16)
            back[shard, :, at] = dot_t(gu[shard], up[at, :]).astype(BF16)
            return carry

        lax.fori_loop(0, n_dp, feature_block, 0)
        for store in stores(shard):
            store.start()

    line.walk(c_out, (gs, gr), work)
    line.drain_gather(c_out, (gs, gr))
    for shard in range(size):
        for store in stores(shard):
            store.wait()


def hidden(c_own, gm, up, down, bias, size, cid):
    rows, width = c_own.shape
    n_dp, units, part = down.shape
    full, wide = (size, rows, width), (size, rows, units)
    return pl.pallas_call(
        functools.partial(hidden_kernel, n_dp, size),
        out_shape=(
            jax.ShapeDtypeStruct(full, BF16),
            jax.ShapeDtypeStruct(wide, BF16),
            jax.ShapeDtypeStruct(wide, BF16),
            jax.ShapeDtypeStruct(full, BF16),
            jax.ShapeDtypeStruct(full, BF16),
            jax.ShapeDtypeStruct((8, units), F32),
        ),
        in_specs=[WHOLE, HBM, HBM, HBM, WHOLE],
        out_specs=(HBM, HBM, HBM, HBM, HBM, WHOLE),
        scratch_shapes=[
            pltpu.VMEM(full, BF16),
            pltpu.VMEM(full, BF16),
            pltpu.VMEM((width, units), BF16),
            pltpu.VMEM((n_dp, units, part), BF16),
            pltpu.VMEM(wide, BF16),
            pltpu.VMEM(wide, BF16),
            pltpu.VMEM(full, BF16),
            pltpu.VMEM(full, BF16),
        ]
        + line_sems(size)
        + [pltpu.SemaphoreType.DMA((3,)), pltpu.SemaphoreType.DMA((5, size))],
        compiler_params=params(cid),
        name="hidden",
    )(c_own, gm, up, down, bias)


def cross(left, right):
    return lax.dot_general(left, right, (((0,), (0,)), ((), ())), preferred_element_type=F32)


def products_kernel(size, steps, gm, act, c, gu_in, terms, out, landed, gu, gs, gr, load_sem):
    i = pl.program_id(0)
    line = Line(size, terms.shape[1])
    load = pltpu.make_async_copy(gu_in, gu, load_sem.at[0])
    hops = line.first_hops(terms, landed, (gs, gr))

    @pl.when(i == 0)
    def _():
        load.start()
        line.barrier()
        line.hops_start(hops)

    @pl.when(i < steps)
    def _():
        out[...] = cross(gm[...], act[...]).astype(BF16)

    @pl.when(i == steps)
    def _():
        load.wait()

    @pl.when(i >= steps)
    def _():
        out[...] = cross(c[...], gu[...]).astype(BF16)

    @pl.when(i == pl.num_programs(0) - 1)
    def _():
        line.hops_wait(hops)


def products(act, gm, c, gu, terms, size, cid):
    rows, units = act.shape
    width = gm.shape[1]
    steps = width // BLOCK
    return pl.pallas_call(
        functools.partial(products_kernel, size, steps),
        grid=(2 * steps,),
        out_shape=(
            jax.ShapeDtypeStruct((width, 2 * units), BF16),
            jax.ShapeDtypeStruct((2,) + terms.shape[1:], BF16),
        ),
        in_specs=[
            pl.BlockSpec((rows, BLOCK), lambda i: (0, jnp.minimum(i, steps - 1))),
            WHOLE,
            pl.BlockSpec((rows, BLOCK), lambda i: (0, jnp.maximum(i - steps, 0))),
            HBM,
            HBM,
        ],
        out_specs=(pl.BlockSpec((BLOCK, units), lambda i: (i % steps, i // steps)), HBM),
        scratch_shapes=[
            pltpu.VMEM((rows, units), BF16),
            pltpu.SemaphoreType.DMA((2,)),
            pltpu.SemaphoreType.DMA((2,)),
            pltpu.SemaphoreType.DMA((1,)),
        ],
        compiler_params=params(cid),
        name="products",
    )(gm, act, c, gu, terms)


def head_products_kernel(size, a, gqkv, terms, out, landed, gs, gr):
    i = pl.program_id(0)
    line = Line(size, terms.shape[1])
    hops = line.first_hops(terms, landed, (gs, gr))

    @pl.when(i == 0)
    def _():
        line.barrier()
        line.hops_start(hops)

    out[...] = cross(a[...], gqkv[...]).astype(BF16)

    @pl.when(i == pl.num_programs(0) - 1)
    def _():
        line.hops_wait(hops)


def head_products(a, gqkv, terms, size, cid):
    rows, width = a.shape
    columns = gqkv.shape[1]
    return pl.pallas_call(
        functools.partial(head_products_kernel, size),
        grid=(width // BLOCK,),
        out_shape=(
            jax.ShapeDtypeStruct((width, columns), BF16),
            jax.ShapeDtypeStruct((2,) + terms.shape[1:], BF16),
        ),
        in_specs=[
            pl.BlockSpec((rows, BLOCK), lambda i: (0, i)),
            WHOLE,
            HBM,
        ],
        out_specs=(pl.BlockSpec((BLOCK, columns), lambda i: (i, 0)), HBM),
        scratch_shapes=[pltpu.SemaphoreType.DMA((2,)), pltpu.SemaphoreType.DMA((2,))],
        compiler_params=params(cid),
        name="head_products",
    )(a, gqkv, terms)


def pad_to(x, count):
    return jnp.pad(x, ((0, 0), (0, count - x.shape[1])))


def shards(
    tokens, lengths, ln1_gain, ln1_bias, qkv_weight, qv_bias, out_weight, out_bias,
    ln2_gain, ln2_bias, up_weight, up_bias, down_weight, down_bias, cotangent,
):
    n_dp, n_t = lax.axis_size("dp"), lax.axis_size("tensor")
    rows, width = tokens.shape
    part = ln1_gain.shape[0]
    local = qkv_weight.shape[2]
    heads = local // HD
    units = up_weight.shape[1]
    hd_part = qv_bias.shape[2]
    t = lax.axis_index("tensor")
    length = lengths[0]

    pieces = [
        ln1_gain, ln1_bias, out_bias, ln2_gain, ln2_bias, down_bias,
        qv_bias.reshape(-1), up_bias.reshape(-1),
    ]
    packed = jnp.concatenate(pieces)
    count = packed.shape[0]
    lanes = -(-count // 2048) * 2048
    small = jnp.pad(packed, (0, lanes - count)).reshape(lanes // 128, 128)
    smalls, a = first(small, tokens, part, n_dp, n_t, 0)
    smalls, a = smalls.reshape(n_dp, lanes), a.reshape(n_t * rows, width)
    vecs = jnp.stack([smalls[:, i * part : (i + 1) * part].reshape(width) for i in range(6)])
    vecs = jnp.pad(vecs, ((0, 2), (0, 0))).astype(F32)
    at = 6 * part
    qv_all = smalls[:, at : at + 2 * heads * hd_part].reshape(n_dp, 2, heads, hd_part)
    qv_all = qv_all.transpose(1, 2, 0, 3).reshape(2, local).astype(F32)
    at += 2 * heads * hd_part
    up_all = smalls[:, at : at + units // n_dp].reshape(n_dp, units // 16, 16 // n_dp)
    up_shift = up_all.transpose(1, 0, 2).reshape(1, units).astype(F32)
    qkv_shift = jnp.concatenate([qv_all[0], jnp.zeros_like(qv_all[0]), qv_all[1]])

    qkv_full = lax.all_gather(
        qkv_weight.transpose(1, 0, 2).reshape(3 * part, local), "dp", axis=0, tiled=False
    ).reshape(n_dp, 3, part, local)
    out_full = lax.all_gather(out_weight, "dp", axis=1, tiled=True)
    up_full = lax.all_gather(up_weight, "dp", axis=0, tiled=True)
    down_blocks = lax.all_gather(down_weight, "dp", axis=0, tiled=False)

    own_pos = t * rows + jnp.arange(rows, dtype=jnp.int32)
    valid_own = (own_pos < length).astype(F32)
    valid = jnp.broadcast_to(valid_own[:, None], (rows, 128))
    positions = jnp.arange(LEN, dtype=jnp.int32)
    bar = jnp.broadcast_to(jnp.where(positions < length, 0.0, NEG)[:, None], (LEN, 128))
    gm_own = (cotangent.astype(F32) * valid_own[:, None]).astype(BF16)

    shift = jnp.broadcast_to(qkv_shift, (8, 3 * local))
    qkv, attended, log_totals, terms, near = front(
        a, qkv_full, shift, bar, out_full, gm_own, n_t, 7
    )
    terms = terms.reshape(n_t, rows, width)
    c_own, gm, mid, stats_a = middle(terms, gm_own, near, tokens, valid, vecs, n_t, 2)
    c, act, gu, mlp, back_terms, up_sums = hidden(
        c_own, gm, up_full, down_blocks, jnp.broadcast_to(up_shift, (8, units)), n_t, 6
    )
    c, gm = c.reshape(-1, width), gm.reshape(-1, width)
    act, gu = act.reshape(-1, units), gu.reshape(-1, units)

    both_grad, early = products(act, gm, c, gu, back_terms, n_t, 9)
    both_out = lax.psum_scatter(both_grad, "dp", scatter_dimension=0, tiled=True)
    gmid, ends, stats_b, go, out_grad = back_middle(
        back_terms, early, mlp, gm_own, mid, vecs, out_full, attended, n_t, 3
    )
    go, out_grad, both_out = lax.optimization_barrier((go, out_grad, both_out))
    down_out, up_out = both_out[:, :units].T, both_out[:, units:]
    out_out = lax.psum_scatter(out_grad, "dp", scatter_dimension=1, tiled=True)
    gqkv, head_sums, last_terms, landed = attend_back(
        qkv, go.reshape(-1, local), bar, log_totals, qkv_full, ends, n_t, 8
    )
    last_terms = last_terms.reshape(n_t, rows, width)
    qkv_grad, last_early = head_products(a, gqkv, last_terms, n_t, 10)
    last_early, qkv_grad = lax.optimization_barrier((last_early, qkv_grad))
    qkv_out = lax.psum_scatter(qkv_grad, "dp", scatter_dimension=0, tiled=True)
    qkv_out = qkv_out.reshape(part, 3, local)

    up_blocks = jnp.sum(up_sums, axis=0).reshape(units // 16, n_dp, 16 // n_dp)
    up_blocks = up_blocks.transpose(1, 0, 2).reshape(n_dp, units // n_dp)
    qv_sums = jnp.stack([head_sums[:, 0], head_sums[:, 8]])
    qv_blocks = qv_sums.reshape(2, heads, n_dp, hd_part).transpose(2, 0, 1, 3)
    qv_blocks = qv_blocks.reshape(n_dp, 2 * heads * hd_part)
    low = jnp.concatenate([up_blocks, qv_blocks], axis=1)
    low_len = -(-low.shape[1] // 1024) * 1024
    given = pad_to(low, low_len).reshape(n_dp, low_len // 128, 128)
    shared = -(-(11 * part // 128 + 1) // 8) * 8
    top_len = shared * 128
    tokens_grad, output, reduced, rms = finish(
        last_terms, last_early, tokens, gmid, mlp, landed, mid, valid, vecs,
        stats_a, stats_b, given, shared, n_t, 4,
    )
    reduced = reduced.reshape(-1)
    outs = [reduced[i * part : (i + 1) * part] for i in range(6)]
    stream_rms = rms[:5, 0]
    at = top_len
    up_bias_out = reduced[at : at + units // n_dp].reshape(up_bias.shape)
    at += units // n_dp
    qv_bias_out = reduced[at : at + 2 * heads * hd_part].reshape(qv_bias.shape)

    return (
        output, tokens_grad, outs[0], outs[1],
        qkv_out.astype(F32), qv_bias_out, out_out.astype(F32), outs[2],
        outs[3], outs[4], up_out.astype(F32), up_bias_out,
        down_out.astype(F32), outs[5], stream_rms,
    )


def solution(mesh):
    vector = P("dp")
    rows = P(("dp", "tensor"), None)
    return jax.shard_map(
        shards,
        mesh=mesh,
        in_specs=(
            rows, vector, vector, vector, P("dp", None, "tensor"), P(None, "tensor", "dp"),
            P("tensor", "dp"), vector, vector, vector, P("dp", "tensor"), P("tensor", "dp"),
            P("tensor", "dp"), vector, rows,
        ),
        out_specs=(
            rows, rows, vector, vector, P("dp", None, "tensor"), P(None, "tensor", "dp"),
            P("tensor", "dp"), vector, vector, vector, P("dp", "tensor"), P("tensor", "dp"),
            P("tensor", "dp"), vector, P(),
        ),
        check_vma=False,
    )
```

```python
import functools

import jax
import jax.numpy as jnp
from jax import lax
from jax.experimental import pallas as pl
from jax.experimental.pallas import tpu as pltpu
from jax.sharding import PartitionSpec as P

HD = 128
LEN = 1024
EPS = 1e-05
MESH = pl.DeviceIdType.MESH
F32 = jnp.float32
BF16 = jnp.bfloat16
VMEM_CAP = 60 * 1024 * 1024
SUBS = 2
WHOLE = pl.BlockSpec(memory_space=pltpu.VMEM)
HBM = pl.BlockSpec(memory_space=pltpu.HBM)


class Line:
    def __init__(self, size, rows):
        self.size, self.rows, self.t = size, rows, lax.axis_index("tensor")
        self.sub = rows // SUBS

    def barrier(self):
        sem = pltpu.get_barrier_semaphore()
        pl.semaphore_wait(sem, self.greet(sem))

    def greet(self, sem):
        @pl.when(self.t > 0)
        def _():
            pl.semaphore_signal(sem, device_id={"tensor": self.t - 1}, device_id_type=MESH)

        @pl.when(self.t < self.size - 1)
        def _():
            pl.semaphore_signal(sem, device_id={"tensor": self.t + 1}, device_id_type=MESH)

        return jnp.where(self.t > 0, 1, 0) + jnp.where(self.t < self.size - 1, 1, 0)

    def _copy(self, src, dst, sems, way, shard, part):
        send, recv = sems
        target = self.t + 1 if way == 0 else self.t - 1
        return pltpu.make_async_remote_copy(
            src_ref=src,
            dst_ref=dst.at[shard, pl.ds(part * self.sub, self.sub)],
            send_sem=send.at[way, shard, part],
            recv_sem=recv.at[way, shard, part],
            device_id={"tensor": target},
            device_id_type=MESH,
        )

    def _rows(self, ref, shard, part):
        return ref.at[shard, pl.ds(part * self.sub, self.sub)]

    def _edge(self, way):
        return self.t < self.size - 1 if way == 0 else self.t > 0

    def hop(self, way, src, dst, sems):
        return pltpu.make_async_remote_copy(
            src_ref=src,
            dst_ref=dst.at[way],
            send_sem=sems[0].at[way],
            recv_sem=sems[1].at[way],
            device_id={"tensor": self.t + 1 if way == 0 else self.t - 1},
            device_id_type=MESH,
        )

    def hop_start(self, srcs, dst, sems):
        for way in (0, 1):

            @pl.when(self._edge(way))
            def _(way=way):
                self.hop(way, srcs[way], dst, sems).start()

    def hop_wait(self, srcs, dst, sems):
        for way in (0, 1):

            @pl.when(self._edge(1 - way))
            def _(way=way):
                self.hop(way, srcs[way], dst, sems).wait_recv()

        for way in (0, 1):

            @pl.when(self._edge(way))
            def _(way=way):
                self.hop(way, srcs[way], dst, sems).wait_send()

    def first_hops(self, terms, landed, sems):
        last = self.size - 1
        return [
            (self.t == sender, self.t == taker, self.hop(way, terms.at[shard], landed, sems))
            for way, sender, taker, shard in ((0, 0, 1, last), (1, last, last - 1, 0))
        ]

    def hops_start(self, hops):
        for sends, _, copy in hops:

            @pl.when(sends)
            def _(copy=copy):
                copy.start()

    def hops_wait(self, hops):
        for sends, takes, copy in hops:

            @pl.when(sends)
            def _(copy=copy):
                copy.wait_send()

            @pl.when(takes)
            def _(copy=copy):
                copy.wait_recv()

    def early_start(self, landed, bufs, sem):
        last = self.size - 1
        early = (
            pltpu.make_async_copy(landed.at[0], bufs[0].at[last], sem.at[0]),
            pltpu.make_async_copy(landed.at[1], bufs[1].at[0], sem.at[1]),
        )
        for copy, holder in zip(early, (1, last - 1)):

            @pl.when(self.t == holder)
            def _(copy=copy):
                copy.start()

        return early

    def gather_step(self, way, k, part, buf, sems, first, near=None):
        t, last = self.t, self.size - 1
        shard = t - k if way == 0 else t + k
        inside = (t >= k) if way == 0 else (t + k <= last)

        @pl.when(inside)
        def _():
            held = self._rows(buf, shard, part)
            if k > 1 or (k == 1 and near is None):
                self._copy(held, buf, sems, way, shard, part).wait_recv()

            @pl.when(self._edge(way))
            def _():
                src = held
                if k == 0 and first is not None:
                    src = first.at[pl.ds(part * self.sub, self.sub)]
                if k == 1 and near is not None:
                    src = near.at[way, pl.ds(part * self.sub, self.sub)]
                self._copy(src, buf, sems, way, shard, part).start()

    def relay(self, k, part, buf, sems):
        for way in (0, 1):
            shard = self.t - k if way == 0 else self.t + k
            inside = (self.t >= k) if way == 0 else (self.t + k <= self.size - 1)

            @pl.when(inside)
            def _(way=way, shard=shard):
                held = self._rows(buf, shard, part)
                self._copy(held, buf, sems, way, shard, part).wait_recv()

                @pl.when(self._edge(way))
                def _():
                    self._copy(held, buf, sems, way, shard, part).start()

    def walk(self, buf, sems, work):
        last_part = SUBS - 1

        def visit(m, carry):
            k = (m + 1) // 2
            shard = jnp.where(m % 2 == 1, self.t - k, self.t + k)

            @pl.when((shard >= 0) & (shard < self.size))
            def _():
                work(shard)

            @pl.when(m == 0)
            def _():
                for part in range(last_part):
                    self.relay(1, part, buf, sems)

            @pl.when(m % 2 == 0)
            def _():
                self.relay(k + 1, last_part, buf, sems)

            @pl.when(m % 2 == 1)
            def _():
                for part in range(last_part):
                    self.relay(k + 1, part, buf, sems)

            return carry

        lax.fori_loop(0, 2 * self.size - 1, visit, 0)

    def _second(self, way):
        return self.t == (1 if way == 0 else self.size - 2)

    def send_sum(self, way, shard, part, terms, buf, sems):
        step = min(32, self.sub)

        def add(i, carry):
            rows = pl.ds(part * self.sub + i * step, step)
            total = buf[shard, rows, :].astype(F32) + terms[shard, rows, :].astype(F32)
            buf[shard, rows, :] = total.astype(BF16)
            return carry

        lax.fori_loop(0, self.sub // step, add, 0)
        held = self._rows(buf, shard, part)
        self._copy(held, buf, sems, way, shard, part).start()

    def early_sends(self, terms, bufs, sems, early):
        for way in (0, 1):

            @pl.when(self._second(way))
            def _(way=way):
                early[way].wait()
                for part in range(SUBS):
                    shard = self.size - 1 if way == 0 else 0
                    self.send_sum(way, shard, part, terms, bufs[way], sems)

    def scatter_step(self, way, j, part, terms, buf, sems, ends=None, early=False):
        t, last = self.t, self.size - 1
        shard = last - j if way == 0 else j
        beyond = (shard > t) if way == 0 else (shard < t)
        starts = (t == 0) if way == 0 else (t == last)
        step = min(32, self.sub)
        if ends is None:
            goes, stays = beyond, None
        else:
            goes = (shard > t + 1) if way == 0 else (shard < t - 1)
            stays = (shard == t + 1) if way == 0 else (shard == t - 1)

        done = early and j == 0

        if not done:

            @pl.when(goes & starts)
            def _():
                self._copy(self._rows(terms, shard, part), buf, sems, way, shard, part).start()

        relays = goes & jnp.logical_not(starts)
        if done:
            relays = relays & jnp.logical_not(self._second(way))

        @pl.when(relays)
        def _():
            held = self._rows(buf, shard, part)
            self._copy(held, buf, sems, way, shard, part).wait_recv()
            self.send_sum(way, shard, part, terms, buf, sems)

        if stays is None:
            return

        @pl.when(stays & starts)
        def _():
            rows = pl.ds(part * self.sub, self.sub)
            ends[way, rows, :] = terms[shard, rows, :]

        @pl.when(stays & jnp.logical_not(starts))
        def _():
            held = self._rows(buf, shard, part)
            self._copy(held, buf, sems, way, shard, part).wait_recv()

            def add(i, carry):
                rows = pl.ds(part * self.sub + i * step, step)
                total = buf[shard, rows, :].astype(F32) + terms[shard, rows, :].astype(F32)
                ends[way, rows, :] = total.astype(BF16)
                return carry

            lax.fori_loop(0, self.sub // step, add, 0)

    def phase(
        self, gather=None, scatter=None, on_slot=None, near=None, ends=None, start=0, on_part=None
    ):
        n = self.size
        for k in range(start, n):
            for part in range(SUBS):
                for way in (0, 1):
                    if gather is not None:
                        self.gather_step(way, k, part, gather[0], gather[1], gather[2], near)
                    if scatter is not None:
                        if gather is None:
                            if k < n - 1:
                                self.scatter_step(way, k, part, scatter[0], scatter[1][way], scatter[2])
                        else:
                            behind = self.t if way == 0 else n - 1 - self.t
                            for b in range(k):

                                @pl.when(behind == b)
                                def _(b=b, k=k, part=part, way=way):
                                    self.scatter_step(
                                        way, k - 1 - b, part, scatter[0], scatter[1][way],
                                        scatter[2], ends,
                                    )
                if on_part is not None:
                    on_part(k, part)
            if on_slot is not None:
                on_slot(k)

    def own_wait(self, bufs, sems, part):
        for way in (0, 1):
            arrives = self.t > 0 if way == 0 else self.t < self.size - 1

            @pl.when(arrives)
            def _(way=way):
                held = self._rows(bufs[way], self.t, part)
                self._copy(held, bufs[way], sems, way, self.t, part).wait_recv()

    def own_sum(self, terms, bufs, rows):
        t = self.t
        zero = jnp.zeros((), F32)
        right = jnp.where(t > 0, bufs[0][t, rows, :].astype(F32), zero)
        left = jnp.where(t < self.size - 1, bufs[1][t, rows, :].astype(F32), zero)
        return terms[t, rows, :].astype(F32) + right + left

    def drain_gather(self, buf, sems, first=0):
        for way in (0, 1):
            for k in range(first, self.size):
                shard = self.t - k if way == 0 else self.t + k
                inside = (self.t >= k) if way == 0 else (self.t + k <= self.size - 1)

                @pl.when(inside & self._edge(way))
                def _(way=way, shard=shard):
                    for part in range(SUBS):
                        held = self._rows(buf, shard, part)
                        self._copy(held, buf, sems, way, shard, part).wait_send()

    def drain_scatter(self, bufs, sems, margin=0, early=False):
        for way in (0, 1):
            for j in range(self.size - 1):
                shard = self.size - 1 - j if way == 0 else j
                beyond = (shard > self.t + margin) if way == 0 else (shard < self.t - margin)
                if early and j == 0:
                    beyond = beyond & self._edge(1 - way)

                @pl.when(beyond)
                def _(way=way, shard=shard):
                    for part in range(SUBS):
                        held = self._rows(bufs[way], shard, part)
                        self._copy(held, bufs[way], sems, way, shard, part).wait_send()


def line_sems(size):
    return [pltpu.SemaphoreType.DMA((2, size, SUBS)), pltpu.SemaphoreType.DMA((2, size, SUBS))]


def fold(x):
    rows, width = x.shape
    return jnp.sum(x.reshape(rows // 8, 8, width), axis=0)


def normal(x):
    centre = x - jnp.mean(x, axis=-1, keepdims=True)
    spread = lax.rsqrt(jnp.mean(centre * centre, axis=-1, keepdims=True) + EPS)
    return centre * spread, spread


def normal_back(upstream, normed, spread, gain):
    scaled = upstream * gain
    mean_part = jnp.mean(scaled, axis=-1, keepdims=True)
    across = jnp.mean(scaled * normed, axis=-1, keepdims=True)
    return spread * (scaled - mean_part - normed * across)


def row_loop(rows, step, body, base=0):
    def one(i, carry):
        body(pl.ds(pl.multiple_of(base + i * step, step), step))
        return carry

    lax.fori_loop(0, rows // step, one, 0)


def params(collective_id=None):
    if collective_id is None:
        return pltpu.CompilerParams(vmem_limit_bytes=VMEM_CAP)
    return pltpu.CompilerParams(
        collective_id=collective_id, has_side_effects=True, vmem_limit_bytes=VMEM_CAP
    )


def first_kernel(n_dp, size, part, small, own, smalls, a_out, tok, send, recv, gs, gr):
    line = Line(size, own.shape[0])
    me = lax.axis_index("dp")
    rows, width = own.shape
    sem = pltpu.get_barrier_semaphore()
    for p in range(1, n_dp):
        pl.semaphore_signal(sem, device_id={"dp": lax.rem(me + p, n_dp)}, device_id_type=MESH)
    ends = line.greet(sem)
    pl.semaphore_wait(sem, ends + n_dp - 1)
    sems = (gs, gr)

    def small_copy(p, slot):
        return pltpu.make_async_remote_copy(
            src_ref=small,
            dst_ref=smalls.at[slot],
            send_sem=send.at[p],
            recv_sem=recv.at[slot],
            device_id={"dp": lax.rem(me + p, n_dp)},
            device_id_type=MESH,
        )

    for p in range(1, n_dp):
        small_copy(p, me).start()
    smalls[pl.ds(me, 1)] = small[...][None]
    step = min(32, line.sub)
    vec_rows = part // 128

    def normalise(source, shard, piece):
        gain = jnp.concatenate(
            [smalls[d, r : r + 1, :] for d in range(n_dp) for r in range(vec_rows)], axis=1
        ).astype(F32)
        shift = jnp.concatenate(
            [smalls[d, r : r + 1, :] for d in range(n_dp) for r in range(vec_rows, 2 * vec_rows)],
            axis=1,
        ).astype(F32)

        def body(at):
            x = source[at, :] if shard is None else source[shard, at, :]
            normed, _ = normal(x.astype(F32))
            to = line.t if shard is None else shard
            a_out[to, at, :] = (normed * gain + shift).astype(BF16)

        row_loop(line.sub, step, body, piece * line.sub)

    def on_part(k, piece):
        if k == 0:
            if piece == 0:
                for p in range(1, n_dp):
                    small_copy(p, lax.rem(me + p, n_dp)).wait_recv()
            normalise(own, None, piece)
        else:

            def side(i, carry):
                shard = line.t + k * (2 * i - 1)

                @pl.when((shard >= 0) & (shard < size))
                def _():
                    normalise(tok, shard, piece)

                return carry

            lax.fori_loop(0, 2, side, 0)

    line.phase(gather=(tok, sems, own), on_part=on_part)
    line.drain_gather(tok, sems)
    for p in range(1, n_dp):
        small_copy(p, me).wait_send()


def first(small, own, part, n_dp, size, cid):
    rows, width = own.shape
    return pl.pallas_call(
        functools.partial(first_kernel, n_dp, size, part),
        out_shape=(
            jax.ShapeDtypeStruct((n_dp,) + small.shape, small.dtype),
            jax.ShapeDtypeStruct((size, rows, width), BF16),
        ),
        in_specs=[WHOLE, WHOLE],
        out_specs=(WHOLE, WHOLE),
        scratch_shapes=[
            pltpu.VMEM((size, rows, width), BF16),
            pltpu.SemaphoreType.DMA((n_dp,)),
            pltpu.SemaphoreType.DMA((n_dp,)),
        ]
        + line_sems(size),
        compiler_params=params(cid),
        name="first",
    )(small, own)


def middle_kernel(
    size, terms, cot, near, tok, valid, vecs, c_out, gm_done, mid_out, stats,
    gm_out, right, left, gs, gr, ss, sr, near_sem, out_sem,
):
    line = Line(size, tok.shape[0])
    rows = tok.shape[0]
    step = min(32, line.sub)
    own = pltpu.make_async_copy(cot, gm_out.at[line.t], near_sem.at[2])
    own.start()
    line.barrier()

    def keep(way):
        shard = line.t - 1 if way == 0 else line.t + 1
        return pltpu.make_async_copy(near.at[way], gm_out.at[shard], near_sem.at[way])

    def keep_all(act):
        for way in (0, 1):

            @pl.when(line._edge(1 - way))
            def _(way=way):
                act(keep(way))

    keep_all(lambda copy: copy.start())
    line.phase(
        gather=(gm_out, (gs, gr), None),
        scatter=(terms, (right, left), (ss, sr)),
        near=near,
        start=1,
    )
    own.wait()
    keep_all(lambda copy: copy.wait())
    stores = [
        pltpu.make_async_copy(gm_out.at[shard], gm_done.at[shard], out_sem.at[shard])
        for shard in range(size)
    ]
    for store in stores:
        store.start()
    stats[...] = jnp.zeros_like(stats)

    def body(at):
        attn = line.own_sum(terms, (right, left), at) + vecs[2:3, :]
        x = tok[at, :].astype(F32)
        mid = x + attn
        normed, _ = normal(mid)
        c_out[at, :] = (normed * vecs[3:4, :] + vecs[4:5, :]).astype(BF16)
        mid_out[at, :] = mid
        ok = valid[at, 0:1]
        stats[0:8, :] += fold(ok * x * x)
        stats[8:16, :] += fold(ok * attn * attn)
        stats[16:24, :] += fold(ok * mid * mid)

    for piece in range(SUBS):
        line.own_wait((right, left), (ss, sr), piece)
        row_loop(line.sub, step, body, piece * line.sub)
    for store in stores:
        store.wait()
    line.drain_gather(gm_out, (gs, gr), 1)
    line.drain_scatter((right, left), (ss, sr))


def middle(terms, cot, near, tok, valid, vecs, size, cid):
    rows, width = tok.shape
    full = (size, rows, width)
    return pl.pallas_call(
        functools.partial(middle_kernel, size),
        out_shape=(
            jax.ShapeDtypeStruct((rows, width), BF16),
            jax.ShapeDtypeStruct(full, BF16),
            jax.ShapeDtypeStruct((rows, width), F32),
            jax.ShapeDtypeStruct((24, width), F32),
        ),
        in_specs=[WHOLE, HBM, HBM, WHOLE, WHOLE, WHOLE],
        out_specs=(WHOLE, HBM, WHOLE, WHOLE),
        scratch_shapes=[pltpu.VMEM(full, BF16)] * 3
        + line_sems(size)
        + line_sems(size)
        + [pltpu.SemaphoreType.DMA((3,)), pltpu.SemaphoreType.DMA((size,))],
        compiler_params=params(cid),
        name="middle",
    )(terms, cot, near, tok, valid, vecs)


def back_middle_kernel(
    size, terms, landed, mlp_in, gm_in, mid_in, vecs, out_in, gz_done, gmid_out, ends, stats,
    go_out, gz_out, right, left, right2, left2, mlp, gm, mid, out_w,
    ss, sr, ms, mr, gs, gr, early_sem, load_sem, out_sem,
):
    rows = mid.shape[0]
    line = Line(size, rows)
    step = min(32, line.sub)
    early = line.early_start(landed, (right, left), early_sem)
    loads = [
        pltpu.make_async_copy(src, dst, load_sem.at[i])
        for i, (src, dst) in enumerate(
            ((gm_in, gm), (mid_in, mid), (mlp_in, mlp), (out_in, out_w))
        )
    ]
    for load in loads:
        load.start()
    line.barrier()
    line.early_sends(terms, (right, left), (ss, sr), early)
    for j in range(size - 1):
        for piece in range(SUBS):
            for way in (0, 1):
                line.scatter_step(
                    way, j, piece, terms, (right, left)[way], (ss, sr), None, True
                )
    for load in loads:
        load.wait()
    stats[...] = jnp.zeros_like(stats)

    def body(at):
        e = line.own_sum(terms, (right, left), at)
        normed, spread = normal(mid[at, :])
        gy = gm[at, :].astype(F32)
        gmid = gy + normal_back(e, normed, spread, vecs[3:4, :])
        gz_out[line.t, at, :] = gmid.astype(BF16)
        gmid_out[at, :] = gmid
        stats[0:8, :] += fold(e * normed)
        stats[8:16, :] += fold(e)
        stats[16:24, :] += fold(gmid)
        stats[24:32, :] += fold(gy)

    for piece in range(SUBS):
        line.own_wait((right, left), (ss, sr), piece)
        row_loop(line.sub, step, body, piece * line.sub)
        for way in (0, 1):
            line.gather_step(way, 0, piece, gz_out, (gs, gr), None)
    def store(shard):
        return pltpu.make_async_copy(gz_out.at[shard], gz_done.at[shard], out_sem.at[shard])

    def weigh(shard):
        store(shard).start()
        go_out[shard] = dot_t(gz_out[shard], out_w[...]).astype(BF16)

    def on_slot(k):
        def side(i, carry):
            shard = line.t + k * (2 * i - 1)

            @pl.when((shard >= 0) & (shard < size))
            def _():
                weigh(shard)

            return carry

        lax.fori_loop(0, 1 if k == 0 else 2, side, 0)

    on_slot(0)
    line.phase(
        gather=(gz_out, (gs, gr), None),
        scatter=(mlp, (right2, left2), (ms, mr)),
        on_slot=on_slot,
        ends=ends,
        start=1,
    )
    for shard in range(size):
        store(shard).wait()
    line.drain_scatter((right, left), (ss, sr), 0, True)
    line.drain_scatter((right2, left2), (ms, mr), 1)
    line.drain_gather(gz_out, (gs, gr))


def back_middle(terms, landed, mlp, gm, mid, vecs, out_w, size, cid):
    rows, width = mid.shape
    local = out_w.shape[0]
    full = (size, rows, width)
    return pl.pallas_call(
        functools.partial(back_middle_kernel, size),
        out_shape=(
            jax.ShapeDtypeStruct(full, BF16),
            jax.ShapeDtypeStruct((rows, width), F32),
            jax.ShapeDtypeStruct((2, rows, width), BF16),
            jax.ShapeDtypeStruct((32, width), F32),
            jax.ShapeDtypeStruct((size, rows, local), BF16),
        ),
        in_specs=[WHOLE, HBM, HBM, HBM, HBM, WHOLE, HBM],
        out_specs=(HBM, WHOLE, WHOLE, WHOLE, WHOLE),
        scratch_shapes=[pltpu.VMEM(full, BF16)] * 6
        + [
            pltpu.VMEM((rows, width), BF16),
            pltpu.VMEM((rows, width), F32),
            pltpu.VMEM((local, width), BF16),
        ]
        + line_sems(size)
        + line_sems(size)
        + line_sems(size)
        + [
            pltpu.SemaphoreType.DMA((2,)),
            pltpu.SemaphoreType.DMA((4,)),
            pltpu.SemaphoreType.DMA((size,)),
        ],
        compiler_params=params(cid),
        name="back_middle",
    )(terms, landed, mlp, gm, mid, vecs, out_w)


def finish_kernel(
    n_dp, size, shared, terms, first_landed, tok_in, gmid_in, mlp, landed, mid_in, valid, vecs,
    stats_a, stats_b, given, grad_out, y_out, reduced, rms, right, left, own_mlp, tok, ends,
    gmid, mid, stats, blocks, land, sums, land2, late, late_land, late_sums, late_land2,
    ss, sr, load_sem, early_sem, s1, r1, s2, r2, s3, r3, s4, r4,
):
    rows = tok.shape[0]
    line = Line(size, rows)
    step = min(32, line.sub)
    loads = [
        pltpu.make_async_copy(src, dst, load_sem.at[i])
        for i, (src, dst) in enumerate(
            (
                (mlp.at[line.t], own_mlp), (landed, ends), (mid_in, mid),
                (tok_in, tok), (gmid_in, gmid),
            )
        )
    ]
    early = line.early_start(first_landed, (right, left), early_sem)
    for load in loads:
        load.start()
    me = lax.axis_index("dp")
    entry = pltpu.get_barrier_semaphore()
    for p in range(1, n_dp):
        pl.semaphore_signal(entry, device_id={"dp": lax.rem(me + p, n_dp)}, device_id_type=MESH)
    for p in range(1, size):
        pl.semaphore_signal(
            entry, device_id={"tensor": lax.rem(line.t + p, size)}, device_id_type=MESH
        )
    pl.semaphore_wait(entry, n_dp + size - 2)
    line.early_sends(terms, (right, left), (ss, sr), early)
    stats[...] = jnp.zeros_like(stats)

    def tail(at):
        zero = jnp.zeros((), F32)
        from_left = jnp.where(line.t > 0, ends[0, at, :].astype(F32), zero)
        from_right = jnp.where(line.t < size - 1, ends[1, at, :].astype(F32), zero)
        out = own_mlp[at, :].astype(F32) + from_left + from_right + vecs[5:6, :]
        y = mid[at, :] + out
        y_out[at, :] = y.astype(BF16)
        ok = valid[at, 0:1]
        stats[16:24, :] += fold(ok * out * out)
        stats[24:32, :] += fold(ok * y * y)

    per = tok.shape[1] // n_dp // 128

    def lanes(total, chunk):
        return total[:, chunk * 128 : (chunk + 1) * 128]

    def group_sum(source, group):
        return jnp.sum(source[8 * group : 8 * group + 8, :], axis=0, keepdims=True)

    def put_vector(dst, row, total):
        for d in range(n_dp):
            for r in range(per):
                dst[d, row + r : row + r + 1, :] = lanes(total, d * per + r)

    def put_square(dst, row, total):
        short = lanes(total, 0)
        for chunk in range(1, n_dp * per):
            short = short + lanes(total, chunk)
        for d in range(n_dp):
            dst[d, row : row + 1, :] = short

    def one(p):
        other = lax.rem(me + p, n_dp)
        return pltpu.make_async_remote_copy(
            src_ref=blocks.at[other],
            dst_ref=land.at[p],
            send_sem=s1.at[p],
            recv_sem=r1.at[p],
            device_id={"dp": other},
            device_id_type=MESH,
        )

    def two(p):
        return pltpu.make_async_remote_copy(
            src_ref=sums.at[pl.ds(0, shared)],
            dst_ref=land2.at[p],
            send_sem=s2.at[p],
            recv_sem=r2.at[p],
            device_id={"tensor": lax.rem(line.t + p, size)},
            device_id_type=MESH,
        )

    def three(p):
        other = lax.rem(me + p, n_dp)
        return pltpu.make_async_remote_copy(
            src_ref=late.at[other],
            dst_ref=late_land.at[p],
            send_sem=s3.at[p],
            recv_sem=r3.at[p],
            device_id={"dp": other},
            device_id_type=MESH,
        )

    def four(p):
        return pltpu.make_async_remote_copy(
            src_ref=late_sums,
            dst_ref=late_land2.at[p],
            send_sem=s4.at[p],
            recv_sem=r4.at[p],
            device_id={"tensor": lax.rem(line.t + p, size)},
            device_id_type=MESH,
        )

    for j in range(size - 1):
        for piece in range(SUBS):
            for way in (0, 1):
                line.scatter_step(
                    way, j, piece, terms, (right, left)[way], (ss, sr), None, True
                )
        if j == 0:
            for load in loads:
                load.wait()
            row_loop(rows, step, tail)
            blocks[:, 0:shared, :] = jnp.zeros((n_dp, shared, 128), F32)
            blocks[:, shared:, :] = given[...]
            for i, group in ((2, 2), (3, 0), (4, 1), (5, 3)):
                put_vector(blocks, i * per, group_sum(stats_b, group))
            for i in range(3):
                put_square(blocks, (6 + i) * per, group_sum(stats_a, i))
            count = jnp.sum(valid[...], axis=0, keepdims=True)
            for d in range(n_dp):
                blocks[d, 11 * per : 11 * per + 1, :] = count
            for p in range(1, n_dp):
                one(p).start()
    total = blocks[me]
    for p in range(1, n_dp):
        one(p).wait_recv()
        total = total + land[p]
    sums[...] = total
    for p in range(1, size):
        two(p).start()

    def body(at):
        e = line.own_sum(terms, (right, left), at)
        normed, spread = normal(tok[at, :].astype(F32))
        grad_out[at, :] = gmid[at, :] + normal_back(e, normed, spread, vecs[0:1, :])
        stats[0:8, :] += fold(e * normed)
        stats[8:16, :] += fold(e)

    for piece in range(SUBS):
        line.own_wait((right, left), (ss, sr), piece)
        row_loop(line.sub, step, body, piece * line.sub)
    late[...] = jnp.zeros_like(late)
    put_vector(late, 0, group_sum(stats, 0))
    put_vector(late, per, group_sum(stats, 1))
    put_square(late, 2 * per, group_sum(stats, 2))
    put_square(late, 2 * per + 1, group_sum(stats, 3))

    for p in range(1, n_dp):
        three(p).start()
    reduced[...] = total
    top = sums[pl.ds(0, shared), :]
    for p in range(1, size):
        two(p).wait_recv()
        top = top + land2[p]
    reduced[pl.ds(0, shared), :] = top

    final = late[me]
    for p in range(1, n_dp):
        three(p).wait_recv()
        final = final + late_land[p]
    late_sums[...] = final
    for p in range(1, size):
        four(p).start()
    for p in range(1, size):
        four(p).wait_recv()
        final = final + late_land2[p]
    reduced[0 : 2 * per, :] = final[0 : 2 * per, :]
    for i in (9, 10):
        row = 2 * per + i - 9
        reduced[i * per : i * per + 1, :] = final[row : row + 1, :]
    count = reduced[11 * per : 11 * per + 1, :] * jnp.float32(tok.shape[1])
    for i in range(5):
        row = (6 + i) * per
        square = jnp.sum(reduced[row : row + 1, :], keepdims=True)
        rms[i : i + 1, :] = jnp.sqrt(square / count)

    for p in range(1, n_dp):
        three(p).wait_send()
    for p in range(1, size):
        four(p).wait_send()
    line.drain_scatter((right, left), (ss, sr), 0, True)
    for p in range(1, n_dp):
        one(p).wait_send()
    for p in range(1, size):
        two(p).wait_send()


def finish(
    terms, first_landed, tok, gmid, mlp, landed, mid, valid, vecs, stats_a, stats_b, given,
    shared, size, cid,
):
    rows, width = tok.shape
    n_dp = given.shape[0]
    lines = shared + given.shape[1]
    late = (-(-(2 * width // n_dp // 128 + 2) // 8) * 8, 128)
    full = (size, rows, width)
    return pl.pallas_call(
        functools.partial(finish_kernel, n_dp, size, shared),
        out_shape=(
            jax.ShapeDtypeStruct((rows, width), F32),
            jax.ShapeDtypeStruct((rows, width), BF16),
            jax.ShapeDtypeStruct((lines, 128), F32),
            jax.ShapeDtypeStruct((8, 128), F32),
        ),
        in_specs=[WHOLE] + [HBM] * 6 + [WHOLE] * 5,
        out_specs=(WHOLE,) * 4,
        scratch_shapes=[pltpu.VMEM(full, BF16)] * 2
        + [pltpu.VMEM((rows, width), BF16)] * 2
        + [pltpu.VMEM((2, rows, width), BF16)]
        + [pltpu.VMEM((rows, width), F32)] * 2
        + [
            pltpu.VMEM((32, width), F32),
            pltpu.VMEM((n_dp, lines, 128), F32),
            pltpu.VMEM((n_dp, lines, 128), F32),
            pltpu.VMEM((lines, 128), F32),
            pltpu.VMEM((size, shared, 128), F32),
            pltpu.VMEM((n_dp,) + late, F32),
            pltpu.VMEM((n_dp,) + late, F32),
            pltpu.VMEM(late, F32),
            pltpu.VMEM((size,) + late, F32),
        ]
        + line_sems(size)
        + [
            pltpu.SemaphoreType.DMA((5,)),
            pltpu.SemaphoreType.DMA((2,)),
            pltpu.SemaphoreType.DMA((n_dp,)),
            pltpu.SemaphoreType.DMA((n_dp,)),
            pltpu.SemaphoreType.DMA((size,)),
            pltpu.SemaphoreType.DMA((size,)),
            pltpu.SemaphoreType.DMA((n_dp,)),
            pltpu.SemaphoreType.DMA((n_dp,)),
            pltpu.SemaphoreType.DMA((size,)),
            pltpu.SemaphoreType.DMA((size,)),
        ],
        compiler_params=params(cid),
        name="finish",
    )(terms, first_landed, tok, gmid, mlp, landed, mid, valid, vecs, stats_a, stats_b, given)


BLOCK = 256
NEG = -1e30
SCALE = HD**-0.5


def dot(a, b):
    return jnp.dot(a, b, preferred_element_type=F32)


def dot_t(a, b):
    return lax.dot_general(a, b, (((1,), (1,)), ((), ())), preferred_element_type=F32)


def masked_scores(q, k, keys, first, bar):
    scores = dot_t(k, q) * SCALE + bar
    key_pos = lax.broadcasted_iota(jnp.int32, (keys, BLOCK), 0)
    query_pos = first + lax.broadcasted_iota(jnp.int32, (keys, BLOCK), 1)
    return jnp.where(key_pos <= query_pos, scores, NEG)


def head_cols(part, h, heads):
    return pl.ds(pl.multiple_of((part * heads + h) * HD, HD), HD)


def weight_loads(weights, cols, sem, part):
    n_dp, _, rows, local = weights.shape
    return [
        pltpu.make_async_copy(
            weights.at[d, part],
            cols.at[pl.ds(d * rows, rows), pl.ds(part * local, local)],
            sem.at[part, d],
        )
        for d in range(n_dp)
    ]


def front_kernel(
    size, heads, a, weights, shift, bar, out_w, cot, qkv, mixed_all, log_totals, terms, near,
    cols, gs, gr, load_sem,
):
    h = pl.program_id(0)
    rows = cot.shape[0]
    local = heads * HD
    line = Line(size, rows)

    @pl.when(h == 0)
    def _():
        for part in range(3):
            for load in weight_loads(weights, cols, load_sem, part):
                load.start()
        line.barrier()
        line.hop_start((cot, cot), near, (gs, gr))
        for part in range(3):
            for load in weight_loads(weights, cols, load_sem, part):
                load.wait()
            span = slice(part * local, (part + 1) * local)

            def product(at, span=span):
                qkv[at, span] = (dot(a[at, :], cols[:, span]) + shift[0:1, span]).astype(BF16)

            row_loop(LEN, min(256, LEN), product)

    at_q, at_k, at_v = (head_cols(part, h, heads) for part in range(3))
    value_cols = qkv[:, at_v].T
    for block in range(LEN // BLOCK):
        first, keys = block * BLOCK, (block + 1) * BLOCK
        here = slice(first, first + BLOCK)
        scores = masked_scores(qkv[here, at_q], qkv[0:keys, at_k], keys, first, bar[0:keys, 0:1])
        top = jnp.max(scores, axis=0, keepdims=True)
        powers = jnp.exp(scores - top)
        total = jnp.sum(powers, axis=0, keepdims=True)
        shares = (powers * (1.0 / total)).astype(BF16)
        mixed = dot(value_cols[:, 0:keys], shares)
        mixed_all[here, head_cols(0, h, heads)] = mixed.T.astype(BF16)
        log_totals[0, :, here] = jnp.broadcast_to(top + jnp.log(total), (8, BLOCK))

    @pl.when(h == heads - 1)
    def _():
        def project(at):
            terms[at, :] = dot(mixed_all[at, :], out_w[...]).astype(BF16)

        row_loop(LEN, min(256, LEN), project)
        line.hop_wait((cot, cot), near, (gs, gr))


def front(a, weights, shift, bar, out_w, cot, size, cid):
    n_dp, _, part, local = weights.shape
    width, local3 = n_dp * part, 3 * local
    heads = local // HD
    return pl.pallas_call(
        functools.partial(front_kernel, size, heads),
        grid=(heads,),
        out_shape=(
            jax.ShapeDtypeStruct((LEN, local3), BF16),
            jax.ShapeDtypeStruct((LEN, local), BF16),
            jax.ShapeDtypeStruct((heads, 8, LEN), F32),
            jax.ShapeDtypeStruct((LEN, width), BF16),
            jax.ShapeDtypeStruct((2,) + cot.shape, BF16),
        ),
        in_specs=[WHOLE, HBM, WHOLE, WHOLE, WHOLE, HBM],
        out_specs=(
            pl.BlockSpec((LEN, local3), lambda h: (0, 0)),
            pl.BlockSpec((LEN, local), lambda h: (0, 0)),
            pl.BlockSpec((1, 8, LEN), lambda h: (h, 0, 0)),
            pl.BlockSpec((LEN, width), lambda h: (0, 0)),
            HBM,
        ),
        scratch_shapes=[
            pltpu.VMEM((width, local3), BF16),
            pltpu.SemaphoreType.DMA((2,)),
            pltpu.SemaphoreType.DMA((2,)),
            pltpu.SemaphoreType.DMA((3, n_dp)),
        ],
        compiler_params=params(cid),
        name="front",
    )(a, weights, shift, bar, out_w, cot)


def attend_back_kernel(
    size, heads, q, k, v, go, bar, log_totals, weights, ends, out, sums, terms, landed,
    key_grad, value_grad, cols, gs, gr, load_sem,
):
    h = pl.program_id(0)
    line = Line(size, ends.shape[1])
    srcs = (ends.at[0], ends.at[1])
    loads = [load for part in range(3) for load in weight_loads(weights, cols, load_sem, part)]

    @pl.when(h == 0)
    def _():
        for load in loads:
            load.start()
        line.barrier()
        line.hop_start(srcs, landed, (gs, gr))

    key_cols = k[...].T
    query_sum = jnp.zeros((1, HD), F32)
    at_q, at_k, at_v = (head_cols(part, h, heads) for part in range(3))
    for block in range(LEN // BLOCK - 1, -1, -1):
        first, keys = block * BLOCK, (block + 1) * BLOCK
        here = slice(first, first + BLOCK)
        scores = masked_scores(q[here, :], k[0:keys, :], keys, first, bar[0:keys, 0:1])
        shares = jnp.exp(scores - log_totals[0, 0:1, here])
        share_grad = dot_t(v[0:keys, :], go[here, :])
        centre = jnp.sum(shares * share_grad, axis=0, keepdims=True)
        score_grad = (shares * (share_grad - centre)).astype(BF16)
        values = dot(shares.astype(BF16), go[here, :])
        keyed = dot(score_grad, q[here, :])
        if block == LEN // BLOCK - 1:
            value_grad[...] = values
            key_grad[...] = keyed
        else:
            value_grad[0:keys, :] += values
            key_grad[0:keys, :] += keyed
        query_grad = ((dot(key_cols[:, 0:keys], score_grad)) * SCALE).T.astype(BF16)
        out[here, at_q] = query_grad
        query_sum = query_sum + jnp.sum(query_grad.astype(F32), axis=0, keepdims=True)
    out[:, at_k] = (key_grad[...] * SCALE).astype(BF16)
    rounded = value_grad[...].astype(BF16)
    out[:, at_v] = rounded
    value_sum = jnp.sum(rounded.astype(F32), axis=0, keepdims=True)
    sums[0, 0:8, :] = jnp.broadcast_to(query_sum, (8, HD))
    sums[0, 8:16, :] = jnp.broadcast_to(value_sum, (8, HD))

    @pl.when(h == heads - 1)
    def _():
        for load in loads:
            load.wait()

        def product(at):
            terms[at, :] = dot_t(out[at, :], cols[...]).astype(BF16)

        row_loop(LEN, min(256, LEN), product)
        line.hop_wait(srcs, landed, (gs, gr))


def attend_back(qkv, go, bar, log_totals, weights, ends, size, cid):
    n_dp, _, part, local = weights.shape
    width, local3 = n_dp * part, 3 * local
    heads = local // HD

    def column(place):
        return pl.BlockSpec((LEN, HD), lambda h: (0, place * heads + h))

    return pl.pallas_call(
        functools.partial(attend_back_kernel, size, heads),
        grid=(heads,),
        out_shape=(
            jax.ShapeDtypeStruct((LEN, local3), BF16),
            jax.ShapeDtypeStruct((heads, 16, HD), F32),
            jax.ShapeDtypeStruct((LEN, width), BF16),
            jax.ShapeDtypeStruct(ends.shape, BF16),
        ),
        in_specs=[
            column(0), column(1), column(2), column(0),
            pl.BlockSpec((LEN, 128), lambda h: (0, 0)),
            pl.BlockSpec((1, 8, LEN), lambda h: (h, 0, 0)),
            HBM, HBM,
        ],
        out_specs=(
            pl.BlockSpec((LEN, local3), lambda h: (0, 0)),
            pl.BlockSpec((1, 16, HD), lambda h: (h, 0, 0)),
            pl.BlockSpec((LEN, width), lambda h: (0, 0)),
            HBM,
        ),
        scratch_shapes=[
            pltpu.VMEM((LEN, HD), F32),
            pltpu.VMEM((LEN, HD), F32),
            pltpu.VMEM((width, local3), BF16),
            pltpu.SemaphoreType.DMA((2,)),
            pltpu.SemaphoreType.DMA((2,)),
            pltpu.SemaphoreType.DMA((3, n_dp)),
        ],
        compiler_params=params(cid),
        name="attend_back",
    )(qkv, qkv, qkv, go, bar, log_totals, weights, ends)


def gelu_both(u):
    inner = 0.7978845608028654 * (u + 0.044715 * (u * u * u))
    th = jnp.tanh(inner)
    half = 0.5 * (1.0 + th)
    slope = half + 0.5 * u * (1.0 - th * th) * (
        0.7978845608028654 * (1.0 + 3 * 0.044715 * (u * u))
    )
    return u * half, slope


def hidden_kernel(
    n_dp, size, c_own, gm_in, up_in, down_in, bias,
    c_done, act_out, gu_out, mlp_out, back_out, sums, c_out, gm, up, down, act, gu, mlp, back, gs, gr, in_sem, out_sem,
):
    line = Line(size, c_own.shape[0])
    rows, width = c_own.shape
    units, part = down.shape[1], down.shape[2]
    block = min(512, units)
    loads = [
        pltpu.make_async_copy(up_in, up, in_sem.at[0]),
        pltpu.make_async_copy(down_in, down, in_sem.at[1]),
        pltpu.make_async_copy(gm_in, gm, in_sem.at[2]),
    ]
    for load in loads:
        load.start()
    line.barrier()
    for piece in range(SUBS):
        for way in (0, 1):
            line.gather_step(way, 0, piece, c_out, (gs, gr), c_own)
    c_out[pl.ds(line.t, 1)] = c_own[...][None]
    sums[...] = jnp.zeros_like(sums)
    for load in loads:
        load.wait()

    def stores(shard):
        pairs = (
            (c_out, c_done), (act, act_out), (gu, gu_out), (mlp, mlp_out), (back, back_out),
        )
        return [
            pltpu.make_async_copy(src.at[shard], dst.at[shard], out_sem.at[i, shard])
            for i, (src, dst) in enumerate(pairs)
        ]

    def work(shard):
        def unit_block(j, carry):
            at = pl.ds(pl.multiple_of(j * block, block), block)
            u = dot(c_out[shard], up[:, at]) + bias[0:1, at]
            grad = dot_t(gm[shard, :, 0:part], down[0, at, :])
            for d in range(1, n_dp):
                grad = grad + dot_t(gm[shard, :, d * part : (d + 1) * part], down[d, at, :])
            value, slope = gelu_both(u)
            act[shard, :, at] = value.astype(BF16)
            rounded = (grad * slope).astype(BF16)
            gu[shard, :, at] = rounded
            sums[:, at] += fold(rounded.astype(F32))
            return carry

        lax.fori_loop(0, units // block, unit_block, 0)

        def feature_block(d, carry):
            at = pl.ds(pl.multiple_of(d * part, part), part)
            mlp[shard, :, at] = dot(act[shard], down[d]).astype(BF16)
            back[shard, :, at] = dot_t(gu[shard], up[at, :]).astype(BF16)
            return carry

        lax.fori_loop(0, n_dp, feature_block, 0)
        for store in stores(shard):
            store.start()

    line.walk(c_out, (gs, gr), work)
    line.drain_gather(c_out, (gs, gr))
    for shard in range(size):
        for store in stores(shard):
            store.wait()


def hidden(c_own, gm, up, down, bias, size, cid):
    rows, width = c_own.shape
    n_dp, units, part = down.shape
    full, wide = (size, rows, width), (size, rows, units)
    return pl.pallas_call(
        functools.partial(hidden_kernel, n_dp, size),
        out_shape=(
            jax.ShapeDtypeStruct(full, BF16),
            jax.ShapeDtypeStruct(wide, BF16),
            jax.ShapeDtypeStruct(wide, BF16),
            jax.ShapeDtypeStruct(full, BF16),
            jax.ShapeDtypeStruct(full, BF16),
            jax.ShapeDtypeStruct((8, units), F32),
        ),
        in_specs=[WHOLE, HBM, HBM, HBM, WHOLE],
        out_specs=(HBM, HBM, HBM, HBM, HBM, WHOLE),
        scratch_shapes=[
            pltpu.VMEM(full, BF16),
            pltpu.VMEM(full, BF16),
            pltpu.VMEM((width, units), BF16),
            pltpu.VMEM((n_dp, units, part), BF16),
            pltpu.VMEM(wide, BF16),
            pltpu.VMEM(wide, BF16),
            pltpu.VMEM(full, BF16),
            pltpu.VMEM(full, BF16),
        ]
        + line_sems(size)
        + [pltpu.SemaphoreType.DMA((3,)), pltpu.SemaphoreType.DMA((5, size))],
        compiler_params=params(cid),
        name="hidden",
    )(c_own, gm, up, down, bias)


def cross(left, right):
    return lax.dot_general(left, right, (((0,), (0,)), ((), ())), preferred_element_type=F32)


def products_kernel(
    size, steps, act, gm, c, gu_in, terms, down_out, up_out, landed, gu, gs, gr, load_sem
):
    i = pl.program_id(0)
    line = Line(size, terms.shape[1])
    load = pltpu.make_async_copy(gu_in, gu, load_sem.at[0])
    hops = line.first_hops(terms, landed, (gs, gr))

    @pl.when(i == 0)
    def _():
        load.start()
        line.barrier()
        line.hops_start(hops)

    @pl.when(i < steps)
    def _():
        down_out[...] = cross(act[...], gm[...]).astype(BF16)

    @pl.when(i == steps)
    def _():
        load.wait()

    @pl.when(i >= steps)
    def _():
        up_out[...] = cross(c[...], gu[...]).astype(BF16)

    @pl.when(i == pl.num_programs(0) - 1)
    def _():
        line.hops_wait(hops)


def products(act, gm, c, gu, terms, size, cid):
    rows, units = act.shape
    width = gm.shape[1]
    steps, more = units // BLOCK, width // BLOCK
    return pl.pallas_call(
        functools.partial(products_kernel, size, steps),
        grid=(steps + more,),
        out_shape=(
            jax.ShapeDtypeStruct((units, width), BF16),
            jax.ShapeDtypeStruct((width, units), BF16),
            jax.ShapeDtypeStruct((2,) + terms.shape[1:], BF16),
        ),
        in_specs=[
            pl.BlockSpec((rows, BLOCK), lambda i: (0, jnp.minimum(i, steps - 1))),
            WHOLE,
            pl.BlockSpec((rows, BLOCK), lambda i: (0, jnp.maximum(i - steps, 0))),
            HBM,
            HBM,
        ],
        out_specs=(
            pl.BlockSpec((BLOCK, width), lambda i: (jnp.minimum(i, steps - 1), 0)),
            pl.BlockSpec((BLOCK, units), lambda i: (jnp.maximum(i - steps, 0), 0)),
            HBM,
        ),
        scratch_shapes=[
            pltpu.VMEM((rows, units), BF16),
            pltpu.SemaphoreType.DMA((2,)),
            pltpu.SemaphoreType.DMA((2,)),
            pltpu.SemaphoreType.DMA((1,)),
        ],
        compiler_params=params(cid),
        name="products",
    )(act, gm, c, gu, terms)


def head_products_kernel(size, gz, a, o, gqkv, terms, out, landed, gs, gr):
    i = pl.program_id(0)
    line = Line(size, terms.shape[1])
    hops = line.first_hops(terms, landed, (gs, gr))
    local = o.shape[1]

    @pl.when(i == 0)
    def _():
        line.barrier()
        line.hops_start(hops)

    out[:, 0:local] = cross(gz[...], o[...]).astype(BF16)
    out[:, local:] = cross(a[...], gqkv[...]).astype(BF16)

    @pl.when(i == pl.num_programs(0) - 1)
    def _():
        line.hops_wait(hops)


def head_products(gz, a, o, gqkv, terms, size, cid):
    rows, width = a.shape
    columns = o.shape[1] + gqkv.shape[1]
    return pl.pallas_call(
        functools.partial(head_products_kernel, size),
        grid=(width // BLOCK,),
        out_shape=(
            jax.ShapeDtypeStruct((width, columns), BF16),
            jax.ShapeDtypeStruct((2,) + terms.shape[1:], BF16),
        ),
        in_specs=[
            pl.BlockSpec((rows, BLOCK), lambda i: (0, i)),
            pl.BlockSpec((rows, BLOCK), lambda i: (0, i)),
            WHOLE,
            WHOLE,
            HBM,
        ],
        out_specs=(pl.BlockSpec((BLOCK, columns), lambda i: (i, 0)), HBM),
        scratch_shapes=[pltpu.SemaphoreType.DMA((2,)), pltpu.SemaphoreType.DMA((2,))],
        compiler_params=params(cid),
        name="head_products",
    )(gz, a, o, gqkv, terms)


def pad_to(x, count):
    return jnp.pad(x, ((0, 0), (0, count - x.shape[1])))


def shards(
    tokens, lengths, ln1_gain, ln1_bias, qkv_weight, qv_bias, out_weight, out_bias,
    ln2_gain, ln2_bias, up_weight, up_bias, down_weight, down_bias, cotangent,
):
    n_dp, n_t = lax.axis_size("dp"), lax.axis_size("tensor")
    rows, width = tokens.shape
    part = ln1_gain.shape[0]
    local = qkv_weight.shape[2]
    heads = local // HD
    units = up_weight.shape[1]
    hd_part = qv_bias.shape[2]
    t = lax.axis_index("tensor")
    length = lengths[0]

    pieces = [
        ln1_gain, ln1_bias, out_bias, ln2_gain, ln2_bias, down_bias,
        qv_bias.reshape(-1), up_bias.reshape(-1),
    ]
    packed = jnp.concatenate(pieces)
    count = packed.shape[0]
    lanes = -(-count // 2048) * 2048
    small = jnp.pad(packed, (0, lanes - count)).reshape(lanes // 128, 128)
    smalls, a = first(small, tokens, part, n_dp, n_t, 0)
    smalls, a = smalls.reshape(n_dp, lanes), a.reshape(n_t * rows, width)
    vecs = jnp.stack([smalls[:, i * part : (i + 1) * part].reshape(width) for i in range(6)])
    vecs = jnp.pad(vecs, ((0, 2), (0, 0))).astype(F32)
    at = 6 * part
    qv_all = smalls[:, at : at + 2 * heads * hd_part].reshape(n_dp, 2, heads, hd_part)
    qv_all = qv_all.transpose(1, 2, 0, 3).reshape(2, local).astype(F32)
    at += 2 * heads * hd_part
    up_all = smalls[:, at : at + units // n_dp].reshape(n_dp, units // 16, 16 // n_dp)
    up_shift = up_all.transpose(1, 0, 2).reshape(1, units).astype(F32)
    qkv_shift = jnp.concatenate([qv_all[0], jnp.zeros_like(qv_all[0]), qv_all[1]])

    qkv_full = lax.all_gather(
        qkv_weight.transpose(1, 0, 2).reshape(3 * part, local), "dp", axis=0, tiled=False
    ).reshape(n_dp, 3, part, local)
    out_full = lax.all_gather(out_weight, "dp", axis=1, tiled=True)
    up_full = lax.all_gather(up_weight, "dp", axis=0, tiled=True)
    down_blocks = lax.all_gather(down_weight, "dp", axis=0, tiled=False)

    own_pos = t * rows + jnp.arange(rows, dtype=jnp.int32)
    valid_own = (own_pos < length).astype(F32)
    valid = jnp.broadcast_to(valid_own[:, None], (rows, 128))
    positions = jnp.arange(LEN, dtype=jnp.int32)
    bar = jnp.broadcast_to(jnp.where(positions < length, 0.0, NEG)[:, None], (LEN, 128))
    gm_own = (cotangent.astype(F32) * valid_own[:, None]).astype(BF16)

    shift = jnp.broadcast_to(qkv_shift, (8, 3 * local))
    qkv, attended, log_totals, terms, near = front(
        a, qkv_full, shift, bar, out_full, gm_own, n_t, 7
    )
    terms = terms.reshape(n_t, rows, width)
    c_own, gm, mid, stats_a = middle(terms, gm_own, near, tokens, valid, vecs, n_t, 2)
    c, act, gu, mlp, back_terms, up_sums = hidden(
        c_own, gm, up_full, down_blocks, jnp.broadcast_to(up_shift, (8, units)), n_t, 6
    )
    c, gm = c.reshape(-1, width), gm.reshape(-1, width)
    act, gu = act.reshape(-1, units), gu.reshape(-1, units)

    down_grad, up_grad, early = products(act, gm, c, gu, back_terms, n_t, 9)
    down_out = lax.psum_scatter(down_grad, "dp", scatter_dimension=1, tiled=True)
    up_out = lax.psum_scatter(up_grad, "dp", scatter_dimension=0, tiled=True)
    gz, gmid, ends, stats_b, go = back_middle(
        back_terms, early, mlp, gm_own, mid, vecs, out_full, n_t, 3
    )
    gqkv, head_sums, last_terms, landed = attend_back(
        qkv, go.reshape(-1, local), bar, log_totals, qkv_full, ends, n_t, 8
    )
    last_terms = last_terms.reshape(n_t, rows, width)
    head_grad, last_early = head_products(
        gz.reshape(-1, width), a, attended, gqkv, last_terms, n_t, 10
    )
    last_early, head_grad, down_out, up_out = lax.optimization_barrier(
        (last_early, head_grad, down_out, up_out)
    )
    head_out = lax.psum_scatter(head_grad, "dp", scatter_dimension=0, tiled=True)
    out_out = head_out[:, :local].T
    qkv_out = head_out[:, local:].reshape(part, 3, local)
    up_blocks = jnp.sum(up_sums, axis=0).reshape(units // 16, n_dp, 16 // n_dp)
    up_blocks = up_blocks.transpose(1, 0, 2).reshape(n_dp, units // n_dp)
    qv_sums = jnp.stack([head_sums[:, 0], head_sums[:, 8]])
    qv_blocks = qv_sums.reshape(2, heads, n_dp, hd_part).transpose(2, 0, 1, 3)
    qv_blocks = qv_blocks.reshape(n_dp, 2 * heads * hd_part)
    low = jnp.concatenate([up_blocks, qv_blocks], axis=1)
    low_len = -(-low.shape[1] // 1024) * 1024
    given = pad_to(low, low_len).reshape(n_dp, low_len // 128, 128)
    shared = -(-(11 * part // 128 + 1) // 8) * 8
    top_len = shared * 128
    tokens_grad, output, reduced, rms = finish(
        last_terms, last_early, tokens, gmid, mlp, landed, mid, valid, vecs,
        stats_a, stats_b, given, shared, n_t, 4,
    )
    reduced = reduced.reshape(-1)
    outs = [reduced[i * part : (i + 1) * part] for i in range(6)]
    stream_rms = rms[:5, 0]
    at = top_len
    up_bias_out = reduced[at : at + units // n_dp].reshape(up_bias.shape)
    at += units // n_dp
    qv_bias_out = reduced[at : at + 2 * heads * hd_part].reshape(qv_bias.shape)

    return (
        output, tokens_grad, outs[0], outs[1],
        qkv_out.astype(F32), qv_bias_out, out_out.astype(F32), outs[2],
        outs[3], outs[4], up_out.astype(F32), up_bias_out,
        down_out.astype(F32), outs[5], stream_rms,
    )


def solution(mesh):
    vector = P("dp")
    rows = P(("dp", "tensor"), None)
    return jax.shard_map(
        shards,
        mesh=mesh,
        in_specs=(
            rows, vector, vector, vector, P("dp", None, "tensor"), P(None, "tensor", "dp"),
            P("tensor", "dp"), vector, vector, vector, P("dp", "tensor"), P("tensor", "dp"),
            P("tensor", "dp"), vector, rows,
        ),
        out_specs=(
            rows, rows, vector, vector, P("dp", None, "tensor"), P(None, "tensor", "dp"),
            P("tensor", "dp"), vector, vector, vector, P("dp", "tensor"), P("tensor", "dp"),
            P("tensor", "dp"), vector, P(),
        ),
        check_vma=False,
    )
```
